32 devices in a mesh: dp: 8 (over y, x, core), mp: 4 (over z).
Axes of the slice: x: 2, y: 2, z: 4, core: 2. Of those that a mesh axis runs over, the one named last changes fastest.
Arguments:
- tokens: bfloat16 [49152, 768], P(('dp', 'mp')), may hold values from -6 to 6
- out_grad: bfloat16 [49152, 768], P(('dp', 'mp')), may hold values from -6 to 6
- live_images: int32 [32, 2], P(('dp', 'mp')), may hold values from 0 to 2, as said below
- first_gain: float32 [768], replicated, may hold values from 0.5 to 1.5
- first_shift: float32 [768], replicated, may hold values from -1.75 to 1.75
- project_in: bfloat16 [768, 3, 768], P(None, None, 'mp'), may hold values from -0.21875 to 0.21875
- query_value_bias: bfloat16 [2, 768], P(None, 'mp'), may hold values from -3 to 3
- project_out: bfloat16 [768, 768], P('mp'), may hold values from -1.75 to 1.75
- output_bias: float32 [768], replicated, may hold values from -1.75 to 1.75
- second_gain: float32 [768], replicated, may hold values from 0.5 to 1.5
- second_shift: float32 [768], replicated, may hold values from -1.75 to 1.75
- up_weight: bfloat16 [768, 3072], P(None, 'mp'), may hold values from -0.21875 to 0.21875
- up_bias: bfloat16 [3072], P('mp'), may hold values from -3 to 3
- down_weight: bfloat16 [3072, 768], P('mp'), may hold values from -0.109375 to 0.109375
- down_bias: float32 [768], replicated, may hold values from -1.75 to 1.75
Outputs:
- output: bfloat16 [49152, 768], P(('dp', 'mp'))
- input_grad: float32 [49152, 768], P(('dp', 'mp'))
- grad_first_gain: float32 [768], replicated
- grad_first_shift: float32 [768], replicated
- grad_project_in: float32 [768, 3, 768], P(None, None, 'mp')
- grad_query_value_bias: float32 [2, 768], P(None, 'mp')
- grad_project_out: float32 [768, 768], P('mp')
- grad_output_bias: float32 [768], replicated
- grad_second_gain: float32 [768], replicated
- grad_second_shift: float32 [768], replicated
- grad_up_weight: float32 [768, 3072], P(None, 'mp')
- grad_up_bias: float32 [3072], P('mp')
- grad_down_weight: float32 [3072, 768], P('mp')
- grad_down_bias: float32 [768], replicated
The draws below stay inside these ranges and needn't reach their ends.
Inputs may be any that keep to these rules, and one draw needn't show every extreme that they name: `live_images`: column 0 counts a device's live low-resolution images (1 to 2), column 1 its live high-resolution images (0 to 1); live images fill the first slots of their region; in every draw some device has all its low-resolution slots live and some device all its high-resolution slots.
All inputs are finite; a program needn't handle non-finite values.
Results may differ from the reference program's by a relative error of at most 0.012.
The reference program's roundings to bfloat16 on the way count: a program that leaves them out, or rounds other values in their place, can miss the bound.
Values may be sent and summed in bfloat16 or wider, within the bound.
A program may use at most 256 MiB of HBM per device.

```python
import jax
import jax.numpy as jnp
from jax import lax

D = 768
HEADS = 16
HEAD_DIM = 48
FF = 3072
HD = 768
SHORT_LEN = 256
LONG_LEN = 1024
SHORT_SLOTS = 2
LONG_SLOTS = 1
ROWS = 1536
NODES = 32
TOKENS = 49152


def draw_live_images(key, part):
    short_count = jax.random.randint(jax.random.fold_in(key, 11), (NODES,), 1, SHORT_SLOTS + 1)
    long_count = jax.random.randint(jax.random.fold_in(key, 12), (NODES,), 0, LONG_SLOTS + 1)
    full_short = jax.random.randint(jax.random.fold_in(key, 13), (), 0, NODES)
    full_long = jax.random.randint(jax.random.fold_in(key, 14), (), 0, NODES)
    short_count = short_count.at[full_short].set(SHORT_SLOTS)
    long_count = long_count.at[full_long].set(LONG_SLOTS)
    return jnp.stack([short_count, long_count], axis=1).astype(jnp.int32)


def level_of(rng, dims, pieces, smallest, high):
    factor_of, own = 1.0, jax.random.fold_in(rng, 6)
    for position, blocks in pieces:
        steps = jnp.exp(jax.random.uniform(jax.random.fold_in(own, position), (blocks,), jnp.float32, smallest / len(pieces), high / len(pieces)))
        factor_of = factor_of * jnp.repeat(steps, dims[position] // blocks).reshape([-1 if axis == position else 1 for axis in range(len(dims))])
    return factor_of


def noise(stream_key, dims, width, reach, shards=(), held_as=jnp.bfloat16):
    factor_of = level_of(stream_key, dims, shards, -0.22, 0.18) if shards else 1.0
    values = jax.random.normal(stream_key, dims, jnp.float32) * width * factor_of
    return jnp.minimum(jnp.maximum(values, -reach), reach).astype(held_as)


def setup_inputs(seed: int = 0) -> dict:
    key_of = jax.random.split(jax.random.key(seed), 16)
    return {
        "tokens": noise(key_of[0], (TOKENS, D), 1.0, 6.0, ((0, 32),)),
        "out_grad": noise(key_of[1], (TOKENS, D), 1.0, 6.0, ((0, 32),)),
        "live_images": draw_live_images(jax.random.fold_in(key_of[15], 71), 0),
        "first_gain": jnp.clip(1.0 + 0.1 * jax.random.normal(key_of[3], (D,), jnp.float32), 0.5, 1.5),
        "first_shift": noise(key_of[4], (D,), 0.3, 1.75, (), jnp.float32),
        "project_in": noise(key_of[5], (D, 3, HD), D ** -0.5, 0.21875, ((2, 4),)),
        "query_value_bias": noise(key_of[6], (2, HD), 0.5, 3.0, ((1, 4),)),
        "project_out": noise(key_of[7], (HD, D), (HD // 64) ** -0.5, 1.75, ((0, 4),)),
        "output_bias": noise(key_of[8], (D,), 0.3, 1.75, (), jnp.float32),
        "second_gain": jnp.clip(1.0 + 0.1 * jax.random.normal(key_of[9], (D,), jnp.float32), 0.5, 1.5),
        "second_shift": noise(key_of[10], (D,), 0.3, 1.75, (), jnp.float32),
        "up_weight": noise(key_of[11], (D, FF), D ** -0.5, 0.21875, ((1, 4),)),
        "up_bias": noise(key_of[12], (FF,), 0.5, 3.0, ((0, 4),)),
        "down_weight": noise(key_of[13], (FF, D), FF ** -0.5, 0.109375, ((0, 4),)),
        "down_bias": noise(key_of[14], (D,), 0.3, 1.75, (), jnp.float32),
    }


epsilon = 1e-05
highest = lax.Precision.HIGHEST

@jax.custom_vjp
def low(v):
    return lax.optimization_barrier(v.astype(jnp.bfloat16)).astype(jnp.float32)

@jax.custom_vjp
def low_back(v):
    return v

def low_keep(v):
    return (low(v), None)

def low_pass(kept, grad):
    return (grad,)

def back_keep(v):
    return (v, None)

def back_low(kept, grad):
    return (low(grad),)
low.defvjp(low_keep, low_pass)
low_back.defvjp(back_keep, back_low)

def layer_norm(rows_in, norm_gain, norm_shift):
    average = lax.optimization_barrier(jnp.mean(rows_in, axis=-1, keepdims=True))
    centred = rows_in - average
    variance = lax.optimization_barrier(jnp.mean(centred * centred, axis=-1, keepdims=True))
    return centred * lax.rsqrt(variance + epsilon) * norm_gain + norm_shift

def mix_images(query_img, key_img, value_img):
    scale = HEAD_DIM ** (-0.5)
    scores = low_back(jnp.einsum('nqhd,nkhd->nhqk', query_img, key_img, precision=highest) * scale)
    probs = low(jax.nn.softmax(scores, axis=-1))
    return jnp.einsum('nhqk,nkhd->nqhd', probs, value_img, precision=highest)

def mix_single(members):
    return mix_images(members[0][None], members[1][None], members[2][None])[0]

def alive_rows(live_images):
    row_index = jnp.arange(ROWS, dtype=jnp.int32)[None, :]
    short_rows = SHORT_SLOTS * SHORT_LEN
    short_slot = row_index // SHORT_LEN
    long_slot = (row_index - short_rows) // LONG_LEN
    is_live = jnp.where(row_index < short_rows, short_slot < live_images[:, 0:1], long_slot < live_images[:, 1:2])
    return is_live.astype(jnp.float32)[:, :, None]

def one_buffer(params, rows_in, alive):
    first_gain, first_shift, project_in, pair_bias, project_out, output_bias, second_gain, second_shift, up_weight, up_bias, down_weight, down_bias = params
    first = low(layer_norm(rows_in, first_gain, first_shift))
    projected = jnp.dot(first, project_in.reshape(D, 3 * HD), precision=highest).reshape(-1, 3, HD)
    query_rows = low(low_back(projected[:, 0] + pair_bias[0]))
    key_rows = low(low_back(projected[:, 1]))
    value_rows = low(low_back(projected[:, 2] + pair_bias[1]))
    short_rows = SHORT_SLOTS * SHORT_LEN
    shorts = [t[:short_rows].reshape(SHORT_SLOTS, SHORT_LEN, HEADS, HEAD_DIM) for t in (query_rows, key_rows, value_rows)]
    longs = [t[short_rows:].reshape(LONG_SLOTS, LONG_LEN, HEADS, HEAD_DIM) for t in (query_rows, key_rows, value_rows)]
    short_mixed = mix_images(shorts[0], shorts[1], shorts[2])
    long_mixed = lax.map(jax.checkpoint(mix_single), (longs[0], longs[1], longs[2]))
    mixed = jnp.concatenate([short_mixed.reshape(short_rows, HD), long_mixed.reshape(-1, HD)], axis=0)
    mixed = low(low_back(mixed))
    branch = low_back(jnp.dot(mixed, project_out, precision=highest))
    residual = rows_in + branch + output_bias
    second = low(layer_norm(residual, second_gain, second_shift))
    hidden = low_back(jnp.dot(second, up_weight, precision=highest) + up_bias)
    activated = low(jax.nn.gelu(hidden, approximate=False))
    feed = low_back(jnp.dot(activated, down_weight, precision=highest))
    return alive * (residual + feed + down_bias)

def reference(tokens, out_grad, live_images, first_gain, first_shift, project_in, query_value_bias, project_out, output_bias, second_gain, second_shift, up_weight, up_bias, down_weight, down_bias):
    alive = alive_rows(live_images)
    params = tuple((p.astype(jnp.float32) for p in (first_gain, first_shift, project_in, query_value_bias, project_out, output_bias, second_gain, second_shift, up_weight, up_bias, down_weight, down_bias)))

    def forward(inputs, *weights):
        blocks = inputs.reshape(NODES, ROWS, D)

        def step(carry, member):
            return (carry, one_buffer(weights, member[0], member[1]))
        _, results = lax.scan(jax.checkpoint(step), jnp.zeros((), jnp.float32), (blocks, alive))
        return results.reshape(-1, D)
    output, pull = jax.vjp(forward, tokens.astype(jnp.float32), *params)
    grads = pull(out_grad.astype(jnp.float32))
    return (output.astype(jnp.bfloat16), grads[0], grads[1], grads[2], grads[3], grads[4], grads[5], grads[6], grads[7], grads[8], grads[9], grads[10], grads[11], grads[12])
```

```python
import functools
import math

import jax
import jax.numpy as jnp
from jax import lax
from jax.experimental import pallas as pl
from jax.experimental.pallas import tpu as pltpu
from jax.sharding import PartitionSpec as P

HEAD_DIM = 48
SHORT_LEN = 256
LONG_LEN = 1024
SHORT_SLOTS = 2
LONG_SLOTS = 1
SHORT_ROWS = SHORT_SLOTS * SHORT_LEN
IMAGES = tuple((SHORT_LEN * i, SHORT_LEN) for i in range(SHORT_SLOTS)) + tuple(
    (SHORT_ROWS + LONG_LEN * i, LONG_LEN) for i in range(LONG_SLOTS)
)
SCALE = HEAD_DIM**-0.5
SCALE_LOG2 = SCALE * math.log2(math.e)
ALL = ("mp", "dp")
BF16 = jnp.bfloat16
F32 = jnp.float32
CHUNK = 512

epsilon = 1e-05


def layer_norm(rows_in, norm_gain, norm_shift):
    average = jnp.mean(rows_in, axis=-1, keepdims=True)
    centred = rows_in - average
    variance = jnp.mean(centred * centred, axis=-1, keepdims=True)
    return centred * lax.rsqrt(variance + epsilon) * norm_gain + norm_shift


def gelu_exact(values):
    return jax.nn.gelu(values, approximate=False)


def nn(left, right):
    return lax.dot_general(
        left, right, (((1,), (0,)), ((), ())), preferred_element_type=F32
    )


def nt(left, right):
    return lax.dot_general(
        left, right, (((1,), (1,)), ((), ())), preferred_element_type=F32
    )


def tn(left, right):
    return lax.dot_general(
        left, right, (((0,), (0,)), ((), ())), preferred_element_type=F32
    )


def live_mask(live_images, total_rows):
    row_index = lax.broadcasted_iota(jnp.int32, (total_rows, 1), 0)
    short_slot = row_index // SHORT_LEN
    long_slot = (row_index - SHORT_ROWS) // LONG_LEN
    return jnp.where(
        row_index < SHORT_ROWS, short_slot < live_images[0, 0], long_slot < live_images[0, 1]
    )


def attend_kernel(qkv_ref, mixed_ref, logsum_ref):
    for start, length in IMAGES:
        key_t = qkv_ref[48:96, start : start + length]
        value_t = qkv_ref[96:144, start : start + length]
        value_ones = jnp.concatenate([value_t, jnp.ones((16, length), BF16)], axis=0)
        key_rows = key_t.T
        chunk = min(CHUNK, length)
        for first in range(start, start + length, chunk):
            cols = slice(first, first + chunk)
            scores = nn(key_rows, qkv_ref[0:48, cols])
            top = jnp.max(scores, axis=0, keepdims=True)
            weights = jnp.exp2((scores - top) * SCALE_LOG2).astype(BF16)
            sums = nn(value_ones, weights)
            total = sums[48:49]
            mixed_ref[:, cols] = (sums[:48] / total).astype(BF16)
            logsum_ref[0, :, cols] = top * SCALE_LOG2 + jnp.log2(total)


def attend(qkv):
    heads, rows = qkv.shape[0] // 144, qkv.shape[1]
    return pl.pallas_call(
        attend_kernel,
        grid=(heads,),
        in_specs=[pl.BlockSpec((144, rows), lambda h: (h, 0))],
        out_specs=[
            pl.BlockSpec((48, rows), lambda h: (h, 0)),
            pl.BlockSpec((1, 1, rows), lambda h: (h, 0, 0)),
        ],
        out_shape=[
            jax.ShapeDtypeStruct((heads * 48, rows), BF16),
            jax.ShapeDtypeStruct((heads, 1, rows), F32),
        ],
        compiler_params=pltpu.CompilerParams(vmem_limit_bytes=40 << 20),
        cost_estimate=pl.CostEstimate(
            flops=18_000_000_000, bytes_accessed=9_500_000, transcendentals=19_000_000
        ),
        name="attend",
    )(qkv)


def attend_back_kernel(qkv_ref, back_ref, mixed_ref, logsum_ref, out_ref, held):
    for start, length in IMAGES:
        whole = slice(start, start + length)
        key_t = qkv_ref[48:96, whole]
        key_rows = key_t.T
        value_rows = qkv_ref[96:144, whole].T
        chunk = min(CHUNK, length)
        count = length // chunk
        for i in range(count):
            cols = slice(start + i * chunk, start + (i + 1) * chunk)
            query_t = qkv_ref[0:48, cols]
            back_t = back_ref[:, cols]
            inner = jnp.sum(
                back_t.astype(F32) * mixed_ref[:, cols].astype(F32), axis=0, keepdims=True
            )
            scores = nn(key_rows, query_t)
            probs = jnp.exp2(scores * SCALE_LOG2 - logsum_ref[0, :, cols])
            back_probs = nn(value_rows, back_t)
            back_scores = (probs * (back_probs - inner)).astype(BF16)
            out_ref[0:48, cols] = (nn(key_t, back_scores) * SCALE).astype(BF16)
            back_key = nt(query_t, back_scores)
            back_value = nt(back_t, probs.astype(BF16))
            if i > 0:
                back_key = back_key + held[0:48, 0:length]
                back_value = back_value + held[48:96, 0:length]
            if i < count - 1:
                held[0:48, 0:length] = back_key
                held[48:96, 0:length] = back_value
            else:
                out_ref[48:96, whole] = (back_key * SCALE).astype(BF16)
                out_ref[96:144, whole] = back_value.astype(BF16)


def attend_back(qkv, back_mixed, mixed, logsum):
    heads, rows = qkv.shape[0] // 144, qkv.shape[1]
    return pl.pallas_call(
        attend_back_kernel,
        grid=(heads,),
        in_specs=[
            pl.BlockSpec((144, rows), lambda h: (h, 0)),
            pl.BlockSpec((48, rows), lambda h: (h, 0)),
            pl.BlockSpec((48, rows), lambda h: (h, 0)),
            pl.BlockSpec((1, 1, rows), lambda h: (h, 0, 0)),
        ],
        out_specs=pl.BlockSpec((144, rows), lambda h: (h, 0)),
        out_shape=jax.ShapeDtypeStruct((heads * 144, rows), BF16),
        scratch_shapes=[pltpu.VMEM((96, LONG_LEN), F32)],
        compiler_params=pltpu.CompilerParams(vmem_limit_bytes=40 << 20),
        cost_estimate=pl.CostEstimate(
            flops=40_000_000_000, bytes_accessed=19_000_000, transcendentals=19_000_000
        ),
        name="attend_back",
    )(qkv, back_mixed, mixed, logsum)


def gather_rows(shard):
    parts = lax.axis_size("dp")
    size = shard.shape[0] // parts
    own = lax.dynamic_slice_in_dim(shard, lax.axis_index("dp") * size, size, 0)
    return lax.all_gather(own, ALL, axis=0, tiled=True)


def reduce_rows(partial):
    dp, mp = lax.axis_size("dp"), lax.axis_size("mp")
    width = partial.shape[1]
    blocks = partial.reshape(mp, dp, -1, width).transpose(1, 0, 2, 3).reshape(-1, width)
    summed = lax.psum_scatter(blocks, "dp", scatter_dimension=0, tiled=True)
    summed = lax.psum_scatter(summed, "mp", scatter_dimension=0, tiled=True)
    return lax.all_gather(summed, "dp", axis=0, tiled=True).astype(F32)


def local(
    tokens,
    out_grad,
    live_images,
    first_gain,
    first_shift,
    project_in,
    query_value_bias,
    project_out,
    output_bias,
    second_gain,
    second_shift,
    up_weight,
    up_bias,
    down_weight,
    down_bias,
):
    mp = lax.axis_size("mp")
    width = tokens.shape[1]
    own_heads = project_in.shape[2] // HEAD_DIM
    own_hidden = up_weight.shape[1]
    shard_in = (
        project_in.reshape(width, 3, own_heads, HEAD_DIM).transpose(2, 1, 3, 0).reshape(-1, width)
    )
    weight_in = gather_rows(shard_in)
    weight_out = gather_rows(project_out)
    weight_up = gather_rows(up_weight)
    weight_down = gather_rows(down_weight)
    pair_bias = query_value_bias.reshape(2, own_heads, HEAD_DIM)
    own_bias = jnp.stack([pair_bias[0], jnp.zeros_like(pair_bias[0]), pair_bias[1]], axis=1)
    biases = lax.all_gather(
        jnp.concatenate([own_bias.reshape(-1), up_bias])[None], "mp", axis=0, tiled=True
    )
    bias_in = biases[:, : 3 * own_heads * HEAD_DIM].reshape(-1, 1).astype(F32)
    bias_up = biases[:, 3 * own_heads * HEAD_DIM :].astype(F32)

    inputs = tokens.astype(F32)
    first_normed, first_pull = jax.vjp(layer_norm, inputs, first_gain, first_shift)
    first = first_normed.astype(BF16)
    qkv = (nt(weight_in, first) + bias_in).astype(BF16)
    mixed, logsum = attend(qkv)
    residual = inputs + tn(mixed, weight_out) + output_bias
    second_normed, second_pull = jax.vjp(layer_norm, residual, second_gain, second_shift)
    second = second_normed.astype(BF16)
    is_live = live_mask(live_images, tokens.shape[0])
    back_out = jnp.where(is_live, out_grad, jnp.zeros_like(out_grad))

    feed = residual + down_bias
    back_second = jnp.zeros_like(residual)
    grads_up, grads_up_bias, grads_down = [], [], []
    for j in range(mp):
        up_j = weight_up[j * width : (j + 1) * width]
        down_j = weight_down[j * own_hidden : (j + 1) * own_hidden]
        hidden = nn(second, up_j) + bias_up[j]
        activated, gelu_pull = jax.vjp(gelu_exact, hidden)
        act_low = activated.astype(BF16)
        feed = feed + nn(act_low, down_j)
        grads_down.append(tn(act_low, back_out).astype(BF16))
        back_hidden = gelu_pull(nt(back_out, down_j))[0].astype(BF16)
        grads_up.append(tn(second, back_hidden).astype(BF16))
        grads_up_bias.append(jnp.sum(back_hidden, axis=0, dtype=F32))
        back_second = back_second + nt(back_hidden, up_j)
    output = jnp.where(is_live, feed, 0.0).astype(BF16)
    grad_down = reduce_rows(jnp.concatenate(grads_down, axis=0))
    grad_up = reduce_rows(jnp.concatenate(grads_up, axis=0))
    grad_down_bias = jnp.sum(back_out, axis=0, dtype=F32)

    back_resid_norm, grad_second_gain, grad_second_shift = second_pull(back_second)
    back_residual = back_out.astype(F32) + back_resid_norm
    grad_output_bias = jnp.sum(back_residual, axis=0)
    back_branch = back_residual.astype(BF16)
    grad_out = reduce_rows(nn(mixed, back_branch).astype(BF16))
    back_mixed = nt(weight_out, back_branch).astype(BF16)
    back_qkv = attend_back(qkv, back_mixed, mixed, logsum)
    grad_bias_in = jnp.sum(back_qkv, axis=1, dtype=F32)
    grad_in = reduce_rows(nn(back_qkv, first).astype(BF16))
    back_inputs, grad_first_gain, grad_first_shift = first_pull(tn(back_qkv, weight_in))
    input_grad = back_residual + back_inputs

    small = [
        grad_first_gain,
        grad_first_shift,
        grad_output_bias,
        grad_second_gain,
        grad_second_shift,
        grad_down_bias,
    ]
    packed = lax.psum(
        jnp.concatenate(small + [grad_bias_in] + grads_up_bias).reshape(-1, 128), ALL
    ).reshape(-1)
    sums = [packed[i * width : (i + 1) * width] for i in range(len(small))]
    place = lax.axis_index("mp")
    begin = len(small) * width
    own_rows = 3 * own_heads * HEAD_DIM
    own_in = lax.dynamic_slice_in_dim(packed, begin + place * own_rows, own_rows)
    own_in = own_in.reshape(own_heads, 3, HEAD_DIM)
    grad_pair = jnp.stack([own_in[:, 0].reshape(-1), own_in[:, 2].reshape(-1)])
    begin = begin + mp * own_rows
    grad_up_bias = lax.dynamic_slice_in_dim(packed, begin + place * own_hidden, own_hidden)
    grad_in = (
        grad_in.reshape(own_heads, 3, HEAD_DIM, width).transpose(3, 1, 0, 2).reshape(width, 3, -1)
    )
    return (
        output,
        input_grad,
        sums[0],
        sums[1],
        grad_in,
        grad_pair,
        grad_out,
        sums[2],
        sums[3],
        sums[4],
        grad_up,
        grad_up_bias,
        grad_down,
        sums[5],
    )


def solution(mesh):
    rows = P(("dp", "mp"), None)
    return jax.shard_map(
        local,
        mesh=mesh,
        in_specs=(
            rows,
            rows,
            rows,
            P(),
            P(),
            P(None, None, "mp"),
            P(None, "mp"),
            P("mp", None),
            P(),
            P(),
            P(),
            P(None, "mp"),
            P("mp"),
            P("mp", None),
            P(),
        ),
        out_specs=(
            rows,
            rows,
            P(),
            P(),
            P(None, None, "mp"),
            P(None, "mp"),
            P("mp", None),
            P(),
            P(),
            P(),
            P(None, "mp"),
            P("mp"),
            P("mp", None),
            P(),
        ),
        check_vma=False,
    )
```

```python
import functools
import math

import jax
import jax.numpy as jnp
from jax import lax
from jax.experimental import pallas as pl
from jax.experimental.pallas import tpu as pltpu
from jax.sharding import PartitionSpec as P

HEAD_DIM = 48
SHORT_LEN = 256
LONG_LEN = 1024
SHORT_SLOTS = 2
LONG_SLOTS = 1
SHORT_ROWS = SHORT_SLOTS * SHORT_LEN
IMAGES = tuple((SHORT_LEN * i, SHORT_LEN) for i in range(SHORT_SLOTS)) + tuple(
    (SHORT_ROWS + LONG_LEN * i, LONG_LEN) for i in range(LONG_SLOTS)
)
SCALE = HEAD_DIM**-0.5
SCALE_LOG2 = SCALE * math.log2(math.e)
ALL = ("mp", "dp")
BF16 = jnp.bfloat16
F32 = jnp.float32
CHUNK = 512

epsilon = 1e-05


def layer_norm(rows_in, norm_gain, norm_shift):
    average = jnp.mean(rows_in, axis=-1, keepdims=True)
    centred = rows_in - average
    variance = jnp.mean(centred * centred, axis=-1, keepdims=True)
    return centred * lax.rsqrt(variance + epsilon) * norm_gain + norm_shift


def gelu_exact(values):
    return jax.nn.gelu(values, approximate=False)


def nn(left, right):
    return lax.dot_general(
        left, right, (((1,), (0,)), ((), ())), preferred_element_type=F32
    )


def nt(left, right):
    return lax.dot_general(
        left, right, (((1,), (1,)), ((), ())), preferred_element_type=F32
    )


def tn(left, right):
    return lax.dot_general(
        left, right, (((0,), (0,)), ((), ())), preferred_element_type=F32
    )


def live_mask(live_images, total_rows):
    row_index = lax.broadcasted_iota(jnp.int32, (total_rows, 1), 0)
    short_slot = row_index // SHORT_LEN
    long_slot = (row_index - SHORT_ROWS) // LONG_LEN
    return jnp.where(
        row_index < SHORT_ROWS, short_slot < live_images[0, 0], long_slot < live_images[0, 1]
    )


GROUP = 8
MESH = pl.DeviceIdType.MESH
IN_ROWS = 144
FF_PIECE = 216


def place():
    dp, mp = lax.axis_index("dp"), lax.axis_index("mp")
    g = lax.rem(dp, GROUP)
    return dp, dp - g, g // 4, lax.rem(g // 2, 2), lax.rem(g, 2), mp


def flip(bit):
    return 1 - bit


class Gather:
    def __init__(self, own, buffer, piece, split, send, recv):
        self.own, self.buffer, self.piece, self.split, self.send, self.recv = (
            own,
            buffer,
            piece,
            split,
            send,
            recv,
        )
        self.dp, self.base, self.y, self.x, self.core, self.mp = place()

    def device(self, y, x, core):
        return (self.base + 4 * y + 2 * x + core, self.mp)

    def view(self, ref, y, x, core, part=None):
        view = self.piece(ref, 2 * y + x, core)
        if part is None:
            return view
        rows = view.shape[0]
        return view.at[pl.ds(0, self.split)] if part == 0 else view.at[pl.ds(self.split, rows - self.split)]

    def copy(self, kind, slot):
        y, x, core = self.y, self.x, self.core
        mine = (y, x, core)
        buffer = self.buffer.at[slot]
        if kind == 0:
            ways = lax.axis_size("mp")
            hop = 1 if slot == 2 else slot
            src = self.view(self.buffer.at[1] if slot == 2 else self.own, *mine)
            dst = self.view(buffer, *mine)
            device = (self.dp, lax.rem(self.mp + ways - hop, ways))
        else:
            near_x, near_y = (y, flip(x), core), (flip(y), x, core)
            src, device = {
                1: (self.view(buffer, *mine), near_x),
                2: (self.view(buffer, *mine), near_y),
                3: (self.view(buffer, *near_x, 0), near_y),
                4: (self.view(buffer, *near_y, 1), near_x),
                5: (self.view(buffer, *mine), (y, x, flip(core))),
                6: (self.view(buffer, *near_x), (y, x, flip(core))),
                7: (self.view(buffer, *near_y), (y, x, flip(core))),
                8: (self.view(buffer, flip(y), flip(x), core), (y, x, flip(core))),
            }[kind]
            dst, device = src, self.device(*device)
        index = kind * 4 + slot
        return pltpu.make_async_remote_copy(
            src_ref=src,
            dst_ref=dst,
            send_sem=self.send.at[index],
            recv_sem=self.recv.at[index],
            device_id=device,
            device_id_type=MESH,
        )

    def start(self, slot, *kinds):
        for kind in kinds:
            self.copy(kind, slot).start()

    def arrived(self, slot, *kinds):
        for kind in kinds:
            self.copy(kind, slot).wait_recv()

    def along(self, slot):
        self.start(slot, 0)

    def spread(self, slot):
        self.arrived(slot, 0)
        self.start(slot, 1, 2, 5)

    def forward(self, slot):
        self.arrived(slot, 1)
        self.start(slot, 3, 6)
        self.arrived(slot, 2)
        self.start(slot, 4, 7)

    def last(self, slot):
        self.arrived(slot, 3, 4)
        self.start(slot, 8)

    def complete(self, slot):
        self.arrived(slot, 5, 6, 7, 8)

    def finish(self):
        for slot in (1, 2, 3):
            for kind in range(GATHER_KINDS):
                self.copy(kind, slot).wait_send()


GATHER_KINDS = 9


def in_piece(ref, chip, core):
    return ref.at[chip, :, pl.ds(pl.multiple_of(core * 384, 128), 384)]


def ff_piece(ref, chip, core):
    return ref.at[2 * chip + core]


def greet(partners):
    barrier = pltpu.get_barrier_semaphore()
    for partner in partners:
        pl.semaphore_signal(barrier, inc=1, device_id=partner, device_id_type=MESH)
    pl.semaphore_wait(barrier, len(partners))


def attend_head(qkv_ref, offset, mixed_ref, logsum_ref):
    for start, length in IMAGES:
        whole = slice(start, start + length)
        key_t = qkv_ref[pl.ds(offset + 48, 48), whole]
        value_t = qkv_ref[pl.ds(offset + 96, 48), whole]
        value_ones = jnp.concatenate([value_t, jnp.ones((16, length), BF16)], axis=0)
        key_rows = key_t.T
        chunk = min(CHUNK, length)
        for first in range(start, start + length, chunk):
            cols = slice(first, first + chunk)
            scores = nn(key_rows, qkv_ref[pl.ds(offset, 48), cols])
            top = jnp.max(scores, axis=0, keepdims=True)
            weights = jnp.exp2((scores - top) * SCALE_LOG2).astype(BF16)
            sums = nn(value_ones, weights)
            total = sums[48:49]
            mixed_ref[:, cols] = (sums[:48] / total).astype(BF16)
            logsum_ref[0, :, cols] = top * SCALE_LOG2 + jnp.log2(total)


def slot_order(step):
    turn = step // 4
    return turn + (turn // 2) * (1 - 2 * (turn % 2))


def attend_kernel(
    first_ref,
    in_own,
    ff_own,
    bias_own,
    qkv_ref,
    mixed_ref,
    logsum_ref,
    in_out,
    ff_all,
    bias_out,
    in_all,
    bias_all,
    in_send,
    in_recv,
    ff_send,
    ff_recv,
    bias_send,
    bias_recv,
    local_sem,
):
    step = pl.program_id(0)
    dp, base, y, x, core, mp = place()
    ways = lax.axis_size("mp")
    gather_in = Gather(in_own, in_all, in_piece, 64, in_send, in_recv)
    gather_ff = Gather(ff_own, ff_all, ff_piece, 112, ff_send, ff_recv)
    local_in = pltpu.make_async_copy(in_own, in_all.at[0], local_sem.at[0])
    local_bias = pltpu.make_async_copy(bias_own, bias_all.at[0], local_sem.at[1])
    local_ff = pltpu.make_async_copy(ff_own, ff_all.at[0], local_sem.at[2])
    out_in = pltpu.make_async_copy(in_all, in_out, local_sem.at[3])
    out_bias = pltpu.make_async_copy(bias_all, bias_out, local_sem.at[4])

    def bias_copy(slot):
        return pltpu.make_async_remote_copy(
            src_ref=bias_own,
            dst_ref=bias_all.at[slot],
            send_sem=bias_send.at[slot],
            recv_sem=bias_recv.at[slot],
            device_id=(dp, lax.rem(mp + ways - slot, ways)),
            device_id_type=MESH,
        )

    @pl.when(step == 0)
    def _():
        local_in.start()
        local_bias.start()
        greet(
            [
                (dp, lax.rem(mp + 1, ways)),
                (dp, lax.rem(mp + 2, ways)),
                (dp, lax.rem(mp + 3, ways)),
                (base + 4 * y + 2 * flip(x) + core, mp),
                (base + 4 * flip(y) + 2 * x + core, mp),
                (base + 4 * y + 2 * x + flip(core), mp),
            ]
        )
        gather_in.along(1)
        gather_in.along(3)
        for slot in (1, 2, 3):
            bias_copy(slot).start()
        local_ff.start()
        local_in.wait()
        local_bias.wait()

    @pl.when(step == 1)
    def _():
        gather_in.spread(1)
        gather_in.along(2)

    @pl.when(step == 2)
    def _():
        gather_in.forward(1)
        gather_in.spread(3)
        gather_ff.along(1)
        gather_ff.along(3)

    @pl.when(step == 3)
    def _():
        gather_in.last(1)
        gather_in.spread(2)
        gather_in.forward(3)
        for slot in (1, 2, 3):
            bias_copy(slot).wait()

    @pl.when(step == 4)
    def _():
        gather_in.complete(1)
        gather_in.last(3)
        gather_in.forward(2)

    @pl.when(step == 6)
    def _():
        gather_in.last(2)

    @pl.when(step == 8)
    def _():
        gather_in.complete(3)
        gather_ff.spread(1)
        gather_ff.along(2)
        gather_ff.spread(3)

    @pl.when(step == 12)
    def _():
        gather_in.complete(2)
        out_in.start()
        out_bias.start()
        gather_ff.spread(2)
        gather_ff.forward(1)

    @pl.when(step == 14)
    def _():
        gather_ff.forward(3)

    slot = slot_order(step)
    head = step % 4

    @pl.when(head == 0)
    def _():
        bias_t = bias_all[slot, :, 0:256].T
        for part in range(4):
            product = nt(in_all[slot, part], first_ref[...])
            qkv_ref[part * IN_ROWS : (part + 1) * IN_ROWS, :] = (
                product + bias_t[:IN_ROWS, part : part + 1]
            ).astype(BF16)

    attend_head(qkv_ref, pl.multiple_of(head * IN_ROWS, 16), mixed_ref, logsum_ref)

    @pl.when(step == 15)
    def _():
        gather_ff.last(1)
        gather_ff.last(3)
        gather_ff.forward(2)
        gather_ff.last(2)
        for slot in (1, 3, 2):
            gather_ff.complete(slot)
        local_ff.wait()
        out_in.wait()
        out_bias.wait()
        gather_in.finish()
        gather_ff.finish()


def attend(first, in_own, ff_own, bias_own):
    rows, width = first.shape
    heads = 16
    anywhere = pl.BlockSpec(memory_space=pl.ANY)
    dma = pltpu.SemaphoreType.DMA
    return pl.pallas_call(
        attend_kernel,
        grid=(heads,),
        in_specs=[pl.BlockSpec((rows, width), lambda s: (0, 0)), anywhere, anywhere, anywhere],
        out_specs=[
            pl.BlockSpec((4 * IN_ROWS, rows), lambda s: (slot_order(s), 0)),
            pl.BlockSpec((48, rows), lambda s: (slot_order(s) * 4 + s % 4, 0)),
            pl.BlockSpec((1, 1, rows), lambda s: (slot_order(s) * 4 + s % 4, 0, 0)),
            anywhere,
            anywhere,
            anywhere,
        ],
        out_shape=[
            jax.ShapeDtypeStruct((heads * IN_ROWS, rows), BF16),
            jax.ShapeDtypeStruct((heads * 48, rows), BF16),
            jax.ShapeDtypeStruct((heads, 1, rows), F32),
            jax.ShapeDtypeStruct((4, 4, IN_ROWS, width), BF16),
            jax.ShapeDtypeStruct((4, 8, FF_PIECE, width), BF16),
            jax.ShapeDtypeStruct((4, 8, 1024), F32),
        ],
        scratch_shapes=[
            pltpu.VMEM((4, 4, IN_ROWS, width), BF16),
            pltpu.VMEM((4, 8, 1024), F32),
            dma((4 * GATHER_KINDS,)),
            dma((4 * GATHER_KINDS,)),
            dma((4 * GATHER_KINDS,)),
            dma((4 * GATHER_KINDS,)),
            dma((4,)),
            dma((4,)),
            dma((5,)),
        ],
        compiler_params=pltpu.CompilerParams(
            vmem_limit_bytes=40 << 20, collective_id=0, has_side_effects=True
        ),
        cost_estimate=pl.CostEstimate(
            flops=30_000_000_000, bytes_accessed=30_000_000, transcendentals=19_000_000
        ),
        name="attend",
    )(first, in_own, ff_own, bias_own)


def attend_back_kernel(qkv_ref, back_ref, mixed_ref, logsum_ref, out_ref, held):
    for start, length in IMAGES:
        whole = slice(start, start + length)
        key_t = qkv_ref[48:96, whole]
        key_rows = key_t.T
        value_rows = qkv_ref[96:144, whole].T
        chunk = min(CHUNK, length)
        count = length // chunk
        for i in range(count):
            cols = slice(start + i * chunk, start + (i + 1) * chunk)
            query_t = qkv_ref[0:48, cols]
            back_t = back_ref[:, cols]
            inner = jnp.sum(
                back_t.astype(F32) * mixed_ref[:, cols].astype(F32), axis=0, keepdims=True
            )
            scores = nn(key_rows, query_t)
            probs = jnp.exp2(scores * SCALE_LOG2 - logsum_ref[0, :, cols])
            back_probs = nn(value_rows, back_t)
            back_scores = (probs * (back_probs - inner)).astype(BF16)
            out_ref[0:48, cols] = (nn(key_t, back_scores) * SCALE).astype(BF16)
            back_key = nt(query_t, back_scores)
            back_value = nt(back_t, probs.astype(BF16))
            if i > 0:
                back_key = back_key + held[0:48, 0:length]
                back_value = back_value + held[48:96, 0:length]
            if i < count - 1:
                held[0:48, 0:length] = back_key
                held[48:96, 0:length] = back_value
            else:
                out_ref[48:96, whole] = (back_key * SCALE).astype(BF16)
                out_ref[96:144, whole] = back_value.astype(BF16)


def attend_back(qkv, back_mixed, mixed, logsum):
    heads, rows = qkv.shape[0] // 144, qkv.shape[1]
    return pl.pallas_call(
        attend_back_kernel,
        grid=(heads,),
        in_specs=[
            pl.BlockSpec((144, rows), lambda h: (h, 0)),
            pl.BlockSpec((48, rows), lambda h: (h, 0)),
            pl.BlockSpec((48, rows), lambda h: (h, 0)),
            pl.BlockSpec((1, 1, rows), lambda h: (h, 0, 0)),
        ],
        out_specs=pl.BlockSpec((144, rows), lambda h: (h, 0)),
        out_shape=jax.ShapeDtypeStruct((heads * 144, rows), BF16),
        scratch_shapes=[pltpu.VMEM((96, LONG_LEN), F32)],
        compiler_params=pltpu.CompilerParams(vmem_limit_bytes=40 << 20),
        cost_estimate=pl.CostEstimate(
            flops=40_000_000_000, bytes_accessed=19_000_000, transcendentals=19_000_000
        ),
        name="attend_back",
    )(qkv, back_mixed, mixed, logsum)


def by_shard(slots):
    mp = lax.axis_size("mp")
    blocks = slots.reshape(mp, -1, *slots.shape[1:])
    twice = jnp.concatenate([blocks, blocks], axis=0)
    start = lax.rem(mp - lax.axis_index("mp"), mp)
    return lax.dynamic_slice_in_dim(twice, start, mp, 0).reshape(slots.shape)


def reduce_rows(partial):
    dp, mp = lax.axis_size("dp"), lax.axis_size("mp")
    width = partial.shape[1]
    partial = by_shard(partial)
    blocks = partial.reshape(mp, dp, -1, width).transpose(1, 0, 2, 3).reshape(-1, width)
    summed = lax.psum_scatter(blocks, "dp", scatter_dimension=0, tiled=True)
    summed = lax.psum_scatter(summed, "mp", scatter_dimension=0, tiled=True)
    return lax.all_gather(summed, "dp", axis=0, tiled=True).astype(F32)


def local(
    tokens,
    out_grad,
    live_images,
    first_gain,
    first_shift,
    project_in,
    query_value_bias,
    project_out,
    output_bias,
    second_gain,
    second_shift,
    up_weight,
    up_bias,
    down_weight,
    down_bias,
):
    mp = lax.axis_size("mp")
    width = tokens.shape[1]
    own_heads = project_in.shape[2] // HEAD_DIM
    own_hidden = up_weight.shape[1]
    in_own = project_in.reshape(width, 3, own_heads, HEAD_DIM).transpose(2, 1, 3, 0)
    in_own = in_own.reshape(own_heads, IN_ROWS, width)
    ff_own = jnp.concatenate(
        [
            up_weight.reshape(8, -1, width),
            down_weight.reshape(8, -1, width),
            project_out.reshape(8, -1, width),
        ],
        axis=1,
    )
    pair_bias = query_value_bias.astype(F32).reshape(2, own_heads, HEAD_DIM)
    own_bias = jnp.concatenate([pair_bias[0], jnp.zeros_like(pair_bias[0]), pair_bias[1]], axis=1)
    bias_own = jnp.zeros((8, 1024), F32)
    bias_own = lax.dynamic_update_slice(bias_own, own_bias, (0, 0))
    bias_own = lax.dynamic_update_slice(bias_own, up_bias.astype(F32)[None], (0, 256))

    inputs = tokens.astype(F32)
    first_normed, first_pull = jax.vjp(layer_norm, inputs, first_gain, first_shift)
    first = first_normed.astype(BF16)
    qkv, mixed, logsum, in_all, ff_all, bias_all = attend(first, in_own, ff_own, bias_own)
    weight_in = in_all.reshape(-1, width)
    weight_up = ff_all[:, :, 0:96].reshape(-1, width)
    weight_down = ff_all[:, :, 96:192].reshape(-1, width)
    weight_out = ff_all[:, :, 192:216].reshape(-1, width)
    bias_up = bias_all[:, 0, 256:]
    residual = inputs + tn(mixed, weight_out) + output_bias
    second_normed, second_pull = jax.vjp(layer_norm, residual, second_gain, second_shift)
    second = second_normed.astype(BF16)
    is_live = live_mask(live_images, tokens.shape[0])
    back_out = jnp.where(is_live, out_grad, jnp.zeros_like(out_grad))

    feed = residual + down_bias
    back_second = jnp.zeros_like(residual)
    grads_up, grads_up_bias, grads_down = [], [], []
    for j in range(mp):
        up_j = weight_up[j * width : (j + 1) * width]
        down_j = weight_down[j * own_hidden : (j + 1) * own_hidden]
        hidden = nn(second, up_j) + bias_up[j]
        activated, gelu_pull = jax.vjp(gelu_exact, hidden)
        act_low = activated.astype(BF16)
        feed = feed + nn(act_low, down_j)
        grads_down.append(tn(act_low, back_out).astype(BF16))
        back_hidden = gelu_pull(nt(back_out, down_j))[0].astype(BF16)
        grads_up.append(tn(second, back_hidden).astype(BF16))
        grads_up_bias.append(jnp.sum(back_hidden, axis=0, dtype=F32))
        back_second = back_second + nt(back_hidden, up_j)
    output = jnp.where(is_live, feed, 0.0).astype(BF16)
    grad_down = reduce_rows(jnp.concatenate(grads_down, axis=0))
    grad_up = reduce_rows(jnp.concatenate(grads_up, axis=0))
    grad_down_bias = jnp.sum(back_out, axis=0, dtype=F32)

    back_resid_norm, grad_second_gain, grad_second_shift = second_pull(back_second)
    back_residual = back_out.astype(F32) + back_resid_norm
    grad_output_bias = jnp.sum(back_residual, axis=0)
    back_branch = back_residual.astype(BF16)
    grad_out = reduce_rows(nn(mixed, back_branch).astype(BF16))
    back_mixed = nt(weight_out, back_branch).astype(BF16)
    back_qkv = attend_back(qkv, back_mixed, mixed, logsum)
    grad_bias_in = jnp.sum(back_qkv, axis=1, dtype=F32)
    grad_in = reduce_rows(nn(back_qkv, first).astype(BF16))
    back_inputs, grad_first_gain, grad_first_shift = first_pull(tn(back_qkv, weight_in))
    input_grad = back_residual + back_inputs

    small = [
        grad_first_gain,
        grad_first_shift,
        grad_output_bias,
        grad_second_gain,
        grad_second_shift,
        grad_down_bias,
    ]
    packed = lax.psum(
        jnp.concatenate(
            small + [by_shard(grad_bias_in), by_shard(jnp.concatenate(grads_up_bias))]
        ).reshape(-1, 128), ALL
    ).reshape(-1)
    sums = [packed[i * width : (i + 1) * width] for i in range(len(small))]
    place = lax.axis_index("mp")
    begin = len(small) * width
    own_rows = 3 * own_heads * HEAD_DIM
    own_in = lax.dynamic_slice_in_dim(packed, begin + place * own_rows, own_rows)
    own_in = own_in.reshape(own_heads, 3, HEAD_DIM)
    grad_pair = jnp.stack([own_in[:, 0].reshape(-1), own_in[:, 2].reshape(-1)])
    begin = begin + mp * own_rows
    grad_up_bias = lax.dynamic_slice_in_dim(packed, begin + place * own_hidden, own_hidden)
    grad_in = (
        grad_in.reshape(own_heads, 3, HEAD_DIM, width).transpose(3, 1, 0, 2).reshape(width, 3, -1)
    )
    return (
        output,
        input_grad,
        sums[0],
        sums[1],
        grad_in,
        grad_pair,
        grad_out,
        sums[2],
        sums[3],
        sums[4],
        grad_up,
        grad_up_bias,
        grad_down,
        sums[5],
    )


def solution(mesh):
    rows = P(("dp", "mp"), None)
    return jax.shard_map(
        local,
        mesh=mesh,
        in_specs=(
            rows,
            rows,
            rows,
            P(),
            P(),
            P(None, None, "mp"),
            P(None, "mp"),
            P("mp", None),
            P(),
            P(),
            P(),
            P(None, "mp"),
            P("mp"),
            P("mp", None),
            P(),
        ),
        out_specs=(
            rows,
            rows,
            P(),
            P(),
            P(None, None, "mp"),
            P(None, "mp"),
            P("mp", None),
            P(),
            P(),
            P(),
            P(None, "mp"),
            P("mp"),
            P("mp", None),
            P(),
        ),
        check_vma=False,
    )
```

```python
import functools
import math

import jax
import jax.numpy as jnp
from jax import lax
from jax.experimental import pallas as pl
from jax.experimental.pallas import tpu as pltpu
from jax.sharding import PartitionSpec as P

HEAD_DIM = 48
SHORT_LEN = 256
LONG_LEN = 1024
SHORT_SLOTS = 2
LONG_SLOTS = 1
SHORT_ROWS = SHORT_SLOTS * SHORT_LEN
IMAGES = tuple((SHORT_LEN * i, SHORT_LEN) for i in range(SHORT_SLOTS)) + tuple(
    (SHORT_ROWS + LONG_LEN * i, LONG_LEN) for i in range(LONG_SLOTS)
)
SCALE = HEAD_DIM**-0.5
SCALE_LOG2 = SCALE * math.log2(math.e)
BF16 = jnp.bfloat16
F32 = jnp.float32
CHUNK = 512

epsilon = 1e-05


def layer_norm(rows_in, norm_gain, norm_shift):
    average = jnp.mean(rows_in, axis=-1, keepdims=True)
    centred = rows_in - average
    variance = jnp.mean(centred * centred, axis=-1, keepdims=True)
    return centred * lax.rsqrt(variance + epsilon) * norm_gain + norm_shift


def nn(left, right):
    return lax.dot_general(
        left, right, (((1,), (0,)), ((), ())), preferred_element_type=F32
    )


def nt(left, right):
    return lax.dot_general(
        left, right, (((1,), (1,)), ((), ())), preferred_element_type=F32
    )


def tn(left, right):
    return lax.dot_general(
        left, right, (((0,), (0,)), ((), ())), preferred_element_type=F32
    )


GROUP = 8
MESH = pl.DeviceIdType.MESH
IN_ROWS = 144
HEAD_ROWS = 192


def place():
    dp, mp = lax.axis_index("dp"), lax.axis_index("mp")
    g = lax.rem(dp, GROUP)
    return dp, dp - g, g // 4, lax.rem(g // 2, 2), lax.rem(g, 2), mp


def flip(bit):
    return 1 - bit


class Gather:
    def __init__(self, own, buffer, piece, split, send, recv):
        self.own, self.buffer, self.piece, self.split, self.send, self.recv = (
            own,
            buffer,
            piece,
            split,
            send,
            recv,
        )
        self.dp, self.base, self.y, self.x, self.core, self.mp = place()

    def device(self, y, x, core):
        return (self.base + 4 * y + 2 * x + core, self.mp)

    def view(self, ref, y, x, core, part=None):
        view = self.piece(ref, 2 * y + x, core)
        if part is None:
            return view
        rows = view.shape[0]
        return view.at[pl.ds(0, self.split)] if part == 0 else view.at[pl.ds(self.split, rows - self.split)]

    def copy(self, kind, slot):
        y, x, core = self.y, self.x, self.core
        mine = (y, x, core)
        buffer = self.buffer.at[slot]
        if kind == 0:
            ways = lax.axis_size("mp")
            hop = 1 if slot == 2 else slot
            src = self.view(self.buffer.at[1] if slot == 2 else self.own, *mine)
            dst = self.view(buffer, *mine)
            device = (self.dp, lax.rem(self.mp + ways - hop, ways))
        else:
            return self.shared(kind, buffer, kind * 4 + slot)
        return self.remote(src, dst, device, kind * 4 + slot)

    def shared(self, kind, buffer, index):
        y, x, core = self.y, self.x, self.core
        mine, near_x, near_y = (y, x, core), (y, flip(x), core), (flip(y), x, core)
        moved, device = {
            1: lambda: (self.view(buffer, *mine), near_x),
            2: lambda: (self.view(buffer, *mine), near_y),
            3: lambda: (self.view(buffer, *near_x, 0), near_y),
            4: lambda: (self.view(buffer, *near_y, 1), near_x),
            5: lambda: (self.view(buffer, *mine), (y, x, flip(core))),
            6: lambda: (self.view(buffer, *near_x), (y, x, flip(core))),
            7: lambda: (self.view(buffer, *near_y), (y, x, flip(core))),
            8: lambda: (self.view(buffer, flip(y), flip(x), core), (y, x, flip(core))),
        }[kind]()
        return self.remote(moved, moved, self.device(*device), index)

    def remote(self, src, dst, device, index):
        return pltpu.make_async_remote_copy(
            src_ref=src,
            dst_ref=dst,
            send_sem=self.send.at[index],
            recv_sem=self.recv.at[index],
            device_id=device,
            device_id_type=MESH,
        )

    def start(self, slot, *kinds):
        for kind in kinds:
            self.copy(kind, slot).start()

    def arrived(self, slot, *kinds):
        for kind in kinds:
            self.copy(kind, slot).wait_recv()

    def along(self, slot):
        self.start(slot, 0)

    def spread(self, slot):
        self.arrived(slot, 0)
        self.start(slot, 1, 2, 5)

    def forward(self, slot):
        self.arrived(slot, 1)
        self.start(slot, 3, 6)
        self.arrived(slot, 2)
        self.start(slot, 4, 7)

    def last(self, slot):
        self.arrived(slot, 3, 4)
        self.start(slot, 8)

    def complete(self, slot):
        self.arrived(slot, 5, 6, 7, 8)

    def finish(self):
        for slot in (1, 2, 3):
            for kind in range(GATHER_KINDS):
                self.copy(kind, slot).wait_send()


GATHER_KINDS = 9


def in_piece(ref, chip, core):
    return ref.at[chip, :, pl.ds(pl.multiple_of(core * 384, 128), 384)]


def ff_piece(ref, chip, core):
    return ref.at[2 * chip + core]


def greet(partners):
    barrier = pltpu.get_barrier_semaphore()
    for partner in partners:
        pl.semaphore_signal(barrier, inc=1, device_id=partner, device_id_type=MESH)
    pl.semaphore_wait(barrier, len(partners))


def attend_head(qkv_ref, offset, mixed_ref, logsum_ref):
    for start, length in IMAGES:
        whole = slice(start, start + length)
        key_t = qkv_ref[pl.ds(offset + 48, 48), whole]
        value_t = qkv_ref[pl.ds(offset + 96, 48), whole]
        value_ones = jnp.concatenate([value_t, jnp.ones((16, length), BF16)], axis=0)
        key_rows = key_t.T
        chunk = min(CHUNK, length)
        for first in range(start, start + length, chunk):
            cols = slice(first, first + chunk)
            scores = nn(key_rows, qkv_ref[pl.ds(offset, 48), cols])
            top = jnp.max(scores, axis=0, keepdims=True)
            weights = jnp.exp2((scores - top) * SCALE_LOG2).astype(BF16)
            sums = nn(value_ones, weights)
            total = sums[48:49]
            mixed_ref[:, cols] = (sums[:48] / total).astype(BF16)
            logsum_ref[0, :, cols] = top * SCALE_LOG2 + jnp.log2(total)


def slot_order(step):
    turn = step // 4
    return turn + (turn // 2) * (1 - 2 * (turn % 2))


def attend_kernel(
    first_ref,
    in_own,
    ff_own,
    bias_own,
    qkv_ref,
    mixed_ref,
    logsum_ref,
    in_out,
    ff_all,
    bias_out,
    in_all,
    bias_all,
    in_send,
    in_recv,
    ff_send,
    ff_recv,
    bias_send,
    bias_recv,
    local_sem,
):
    step = pl.program_id(0)
    dp, base, y, x, core, mp = place()
    ways = lax.axis_size("mp")
    gather_in = Gather(in_own, in_all, in_piece, 96, in_send, in_recv)
    gather_ff = Gather(ff_own, ff_all, ff_piece, 96, ff_send, ff_recv)
    local_in = pltpu.make_async_copy(in_own, in_all.at[0], local_sem.at[0])
    local_bias = pltpu.make_async_copy(bias_own, bias_all.at[0], local_sem.at[1])
    local_ff = pltpu.make_async_copy(ff_own, ff_all.at[0], local_sem.at[2])
    out_in = pltpu.make_async_copy(in_all, in_out, local_sem.at[3])
    out_bias = pltpu.make_async_copy(bias_all, bias_out, local_sem.at[4])

    def bias_copy(slot):
        return pltpu.make_async_remote_copy(
            src_ref=bias_own,
            dst_ref=bias_all.at[slot],
            send_sem=bias_send.at[slot],
            recv_sem=bias_recv.at[slot],
            device_id=(dp, lax.rem(mp + ways - slot, ways)),
            device_id_type=MESH,
        )

    @pl.when(step == 0)
    def _():
        local_in.start()
        local_bias.start()
        greet(
            [
                (dp, lax.rem(mp + 1, ways)),
                (dp, lax.rem(mp + 2, ways)),
                (dp, lax.rem(mp + 3, ways)),
                (base + 4 * y + 2 * flip(x) + core, mp),
                (base + 4 * flip(y) + 2 * x + core, mp),
                (base + 4 * y + 2 * x + flip(core), mp),
            ]
        )
        gather_in.along(1)
        gather_in.along(3)
        for slot in (1, 2, 3):
            bias_copy(slot).start()
        local_ff.start()
        local_in.wait()
        local_bias.wait()

    @pl.when(step == 1)
    def _():
        gather_in.spread(1)
        gather_in.along(2)

    @pl.when(step == 2)
    def _():
        gather_in.forward(1)
        gather_in.spread(3)
        gather_ff.along(1)
        gather_ff.along(3)

    @pl.when(step == 3)
    def _():
        gather_in.last(1)
        gather_in.spread(2)
        gather_in.forward(3)
        for slot in (1, 2, 3):
            bias_copy(slot).wait()

    @pl.when(step == 4)
    def _():
        gather_in.complete(1)
        gather_in.last(3)
        gather_in.forward(2)

    @pl.when(step == 6)
    def _():
        gather_in.last(2)

    @pl.when(step == 8)
    def _():
        gather_in.complete(3)
        gather_ff.spread(1)
        gather_ff.along(2)
        gather_ff.spread(3)

    @pl.when(step == 12)
    def _():
        gather_in.complete(2)
        out_in.start()
        out_bias.start()
        gather_ff.spread(2)
        gather_ff.forward(1)

    @pl.when(step == 14)
    def _():
        gather_ff.forward(3)

    slot = slot_order(step)
    head = step % 4

    @pl.when(head == 0)
    def _():
        bias_t = bias_all[slot, :, 0:256].T
        for part in range(4):
            product = nt(in_all[slot, part, :IN_ROWS], first_ref[...])
            qkv_ref[part * IN_ROWS : (part + 1) * IN_ROWS, :] = (
                product + bias_t[:IN_ROWS, part : part + 1]
            ).astype(BF16)

    attend_head(qkv_ref, pl.multiple_of(head * IN_ROWS, 16), mixed_ref, logsum_ref)

    @pl.when(step == 15)
    def _():
        gather_ff.last(1)
        gather_ff.last(3)
        gather_ff.forward(2)
        gather_ff.last(2)
        for slot in (1, 3, 2):
            gather_ff.complete(slot)
        local_ff.wait()
        out_in.wait()
        out_bias.wait()
        gather_in.finish()
        gather_ff.finish()


def attend(first, in_own, ff_own, bias_own):
    rows, width = first.shape
    heads = 16
    anywhere = pl.BlockSpec(memory_space=pl.ANY)
    dma = pltpu.SemaphoreType.DMA
    return pl.pallas_call(
        attend_kernel,
        grid=(heads,),
        in_specs=[pl.BlockSpec((rows, width), lambda s: (0, 0)), anywhere, anywhere, anywhere],
        out_specs=[
            pl.BlockSpec((4 * IN_ROWS, rows), lambda s: (slot_order(s), 0)),
            pl.BlockSpec((48, rows), lambda s: (slot_order(s) * 4 + s % 4, 0)),
            pl.BlockSpec((1, 1, rows), lambda s: (slot_order(s) * 4 + s % 4, 0, 0)),
            anywhere,
            anywhere,
            anywhere,
        ],
        out_shape=[
            jax.ShapeDtypeStruct((heads * IN_ROWS, rows), BF16),
            jax.ShapeDtypeStruct((heads * 48, rows), BF16),
            jax.ShapeDtypeStruct((heads, 1, rows), F32),
            jax.ShapeDtypeStruct((4, 4, HEAD_ROWS, width), BF16),
            jax.ShapeDtypeStruct((4, 8, 192, width), BF16),
            jax.ShapeDtypeStruct((4, 8, 1024), F32),
        ],
        scratch_shapes=[
            pltpu.VMEM((4, 4, HEAD_ROWS, width), BF16),
            pltpu.VMEM((4, 8, 1024), F32),
            dma((4 * GATHER_KINDS,)),
            dma((4 * GATHER_KINDS,)),
            dma((4 * GATHER_KINDS,)),
            dma((4 * GATHER_KINDS,)),
            dma((4,)),
            dma((4,)),
            dma((5,)),
        ],
        compiler_params=pltpu.CompilerParams(
            vmem_limit_bytes=40 << 20, collective_id=0, has_side_effects=True
        ),
        cost_estimate=pl.CostEstimate(
            flops=30_000_000_000, bytes_accessed=30_000_000, transcendentals=19_000_000
        ),
        name="attend",
    )(first, in_own, ff_own, bias_own)


class Reduce:
    def __init__(self, slot, other, total, got, split, send, recv):
        self.slot, self.other, self.total, self.got, self.split = slot, other, total, got, split
        self.send, self.recv = send, recv
        self.dp, self.base, self.y, self.x, self.core, self.mp = place()

    def copy(self, kind):
        y, x, core = self.y, self.x, self.core
        first, late = pl.ds(0, self.split), pl.ds(self.split, self.total.shape[2] - self.split)
        got = self.got
        near = lambda y, x, core: (self.base + 4 * y + 2 * x + core, self.mp)
        to_x, to_y = near(y, flip(x), core), near(flip(y), x, core)
        src, dst, device = {
            0: lambda: (self.other, got[0], near(y, x, flip(core))),
            1: lambda: (self.total.at[:, flip(x), first], got[1], to_x),
            2: lambda: (self.total.at[flip(y), :, late], got[2], to_y),
            3: lambda: (self.total.at[flip(y), x, first], got[3], to_y),
            4: lambda: (self.total.at[y, flip(x), late], got[4], to_x),
            5: lambda: (
                self.total.at[y, x],
                got[5],
                (self.dp, lax.rem(self.mp + self.slot, lax.axis_size("mp"))),
            ),
        }[kind]()
        index = kind * 4 + self.slot
        return pltpu.make_async_remote_copy(
            src_ref=src,
            dst_ref=dst,
            send_sem=self.send.at[index],
            recv_sem=self.recv.at[index],
            device_id=device,
            device_id_type=MESH,
        )

    def cores(self):
        self.copy(0).start()

    def chips(self):
        self.copy(0).wait_recv()
        for y in range(2):
            for x in range(2):
                self.total[y, x] = add(self.total[y, x], self.got[0][y, x])
        self.copy(1).start()
        self.copy(2).start()

    def chips_again(self):
        x, y, split = self.x, self.y, self.split
        self.copy(1).wait_recv()
        for i in range(2):
            self.total[i, x, :split] = add(self.total[i, x, :split], self.got[1][i])
        self.copy(2).wait_recv()
        for i in range(2):
            self.total[y, i, split:] = add(self.total[y, i, split:], self.got[2][i])
        self.copy(3).start()
        self.copy(4).start()

    def along(self):
        x, y, split = self.x, self.y, self.split
        self.copy(3).wait_recv()
        self.total[y, x, :split] = add(self.total[y, x, :split], self.got[3][...])
        self.copy(4).wait_recv()
        self.total[y, x, split:] = add(self.total[y, x, split:], self.got[4][...])
        if self.slot:
            self.copy(5).start()

    def arrived(self):
        self.copy(5).wait_recv()

    def finish(self):
        for kind in range(6 if self.slot else 5):
            self.copy(kind).wait_send()


REDUCE_KINDS = 6


def add(left, right):
    return (left.astype(F32) + right.astype(F32)).astype(BF16)


def other_bit(index, bit):
    return index + bit * (1 - 2 * lax.rem(index // bit, 2))


def wider_bits():
    bits, bit = [], GROUP
    while bit < lax.axis_size("dp"):
        bits.append(bit)
        bit *= 2
    return bits


class Share:
    def __init__(self, pieces, split, send, recv):
        self.inner = Gather(None, None, ff_piece, split, send, recv)
        self.inner.buffer = pieces

    def copy(self, kind):
        return self.inner.shared(kind, self.inner.buffer, kind)

    def start(self, *kinds):
        for kind in kinds:
            self.copy(kind).start()

    def arrived(self, *kinds):
        for kind in kinds:
            self.copy(kind).wait_recv()

    def spread(self):
        self.start(1, 2, 5)

    def forward(self):
        self.arrived(1)
        self.start(3, 6)
        self.arrived(2)
        self.start(4, 7)

    def last(self):
        self.arrived(3, 4)
        self.start(8)

    def finish(self):
        self.arrived(5, 6, 7, 8)
        for kind in range(1, 9):
            self.copy(kind).wait_send()


class Total:
    def __init__(self, reduces, arrivals, final, wide, wide_send, wide_recv):
        self.reduces, self.arrivals, self.final = reduces, arrivals, final
        self.wide, self.wide_send, self.wide_recv = wide, wide_send, wide_recv

    def copy(self, i, bit):
        dp, mp = lax.axis_index("dp"), lax.axis_index("mp")
        return pltpu.make_async_remote_copy(
            src_ref=self.wide.at[2 * i],
            dst_ref=self.wide.at[2 * i + 1],
            send_sem=self.wide_send.at[i],
            recv_sem=self.wide_recv.at[i],
            device_id=(other_bit(dp, bit), mp),
            device_id_type=MESH,
        )

    def sum(self):
        own = self.reduces[0]
        total = own.total[own.y, own.x].astype(F32)
        for k in (1, 2, 3):
            self.reduces[k].arrived()
            total = total + self.arrivals[k - 1].astype(F32)
        for i, bit in enumerate(wider_bits()):
            self.wide[2 * i] = total.astype(BF16)
            self.copy(i, bit).start()
            self.copy(i, bit).wait()
            total = total + self.wide[2 * i + 1].astype(F32)
        self.final[4 * own.y + 2 * own.x + own.core] = total.astype(BF16)


def group_partners():
    dp, base, y, x, core, mp = place()
    ways = lax.axis_size("mp")
    return (
        [(dp, lax.rem(mp + k, ways)) for k in (1, 2, 3)]
        + [
            (base + 4 * y + 2 * flip(x) + core, mp),
            (base + 4 * flip(y) + 2 * x + core, mp),
            (base + 4 * y + 2 * x + flip(core), mp),
        ]
        + [(other_bit(dp, bit), mp) for bit in wider_bits()]
    )


def reduce_refs(scratch, slot):
    r1, r2a, r2b, r3a, r3b, r4 = scratch
    return [
        r1.at[slot],
        r2a.at[slot],
        r2b.at[slot],
        r3a.at[slot],
        r3b.at[slot],
        r4.at[max(slot - 1, 0)],
    ]


def reduce_scratch(rows, split, width):
    late = rows - split
    dma = pltpu.SemaphoreType.DMA
    wide = 6
    return [
        pltpu.VMEM((4, 2, 2, rows, width), BF16),
        pltpu.VMEM((4, 2, split, width), BF16),
        pltpu.VMEM((4, 2, late, width), BF16),
        pltpu.VMEM((4, split, width), BF16),
        pltpu.VMEM((4, late, width), BF16),
        pltpu.VMEM((3, rows, width), BF16),
        pltpu.VMEM((8, rows, width), BF16),
        pltpu.VMEM((2 * len(wider_bits()) or 1, rows, width), BF16),
        dma((4 * REDUCE_KINDS,)),
        dma((4 * REDUCE_KINDS,)),
        dma((GATHER_KINDS,)),
        dma((GATHER_KINDS,)),
        dma((wide,)),
        dma((wide,)),
    ]


def attend_back_head(qkv_ref, offset, back_ref, mixed_ref, logsum_ref, out_ref, held):
    for start, length in IMAGES:
        whole = slice(start, start + length)
        key_t = qkv_ref[pl.ds(offset + 48, 48), whole]
        key_rows = key_t.T
        value_rows = qkv_ref[pl.ds(offset + 96, 48), whole].T
        chunk = min(CHUNK, length)
        count = length // chunk
        for i in range(count):
            cols = slice(start + i * chunk, start + (i + 1) * chunk)
            query_t = qkv_ref[pl.ds(offset, 48), cols]
            back_t = back_ref[:, cols]
            inner = jnp.sum(
                back_t.astype(F32) * mixed_ref[:, cols].astype(F32), axis=0, keepdims=True
            )
            scores = nn(key_rows, query_t)
            probs = jnp.exp2(scores * SCALE_LOG2 - logsum_ref[0, :, cols])
            back_probs = nn(value_rows, back_t)
            back_scores = (probs * (back_probs - inner)).astype(BF16)
            out_ref[pl.ds(offset, 48), cols] = (nn(key_t, back_scores) * SCALE).astype(BF16)
            back_key = nt(query_t, back_scores)
            back_value = nt(back_t, probs.astype(BF16))
            if i > 0:
                back_key = back_key + held[0:48, 0:length]
                back_value = back_value + held[48:96, 0:length]
            if i < count - 1:
                held[0:48, 0:length] = back_key
                held[48:96, 0:length] = back_value
            else:
                out_ref[pl.ds(offset + 48, 48), whole] = (back_key * SCALE).astype(BF16)
                out_ref[pl.ds(offset + 96, 48), whole] = back_value.astype(BF16)


def attend_back_kernel(
    qkv_ref,
    back_ref,
    mixed_ref,
    logsum_ref,
    first_ref,
    out_grad_ref,
    ff_grad,
    out_ref,
    grad_ref,
    sums_ref,
    ff_out,
    held,
    total,
    *scratch,
):
    step = pl.program_id(0)
    head = step % 4
    *got, final, wide, send, recv, share_send, share_recv, wide_send, wide_recv, local = scratch
    dp, base, y, x, core, mp = place()

    def own(slot):
        src = ff_grad.at[slot, :, :, core]
        return pltpu.make_async_copy(src, total.at[slot], local.at[slot])

    reduces = [
        Reduce(
            slot,
            ff_grad.at[slot, :, :, flip(core)],
            total.at[slot],
            reduce_refs(got, slot),
            96,
            send,
            recv,
        )
        for slot in range(4)
    ]
    whole = Total(reduces, got[5], final, wide, wide_send, wide_recv)
    share = Share(final, 96, share_send, share_recv)

    @pl.when(step == 0)
    def _():
        for slot in range(4):
            own(slot).start()
        greet(group_partners())

    for turn, slot in enumerate((2, 1, 3, 0)):

        @pl.when(step == 3 * turn)
        def _(slot=slot):
            reduces[slot].cores()

        @pl.when(step == 3 * turn + 1)
        def _(slot=slot):
            own(slot).wait()
            reduces[slot].chips()

        @pl.when(step == 3 * turn + 3)
        def _(slot=slot):
            reduces[slot].chips_again()

        @pl.when(step == 3 * turn + 5)
        def _(slot=slot):
            reduces[slot].along()

    attend_back_head(
        qkv_ref, pl.multiple_of(head * IN_ROWS, 16), back_ref, mixed_ref, logsum_ref, out_ref, held
    )

    @pl.when(head == 3)
    def _():
        for part in range(4):
            rows = out_ref[part * IN_ROWS : (part + 1) * IN_ROWS, :]
            grad_ref[0, part, :IN_ROWS] = nn(rows, first_ref[...]).astype(BF16)
            grad_ref[0, part, IN_ROWS:] = out_grad_ref[0, part]
        sums_ref[0] = nt(jnp.ones((8, out_ref.shape[1]), BF16), out_ref[...])

    @pl.when(step == 15)
    def _():
        whole.sum()
        share.spread()
        share.forward()
        share.last()
        share.finish()
        for reduce in reduces:
            reduce.finish()
        result = pltpu.make_async_copy(final, ff_out, local.at[0])
        result.start()
        result.wait()


def attend_back(qkv, back_mixed, mixed, logsum, first, out_grad, ff_grad):
    rows, width = first.shape
    anywhere = pl.BlockSpec(memory_space=pl.ANY)
    return pl.pallas_call(
        attend_back_kernel,
        grid=(16,),
        in_specs=[
            pl.BlockSpec((4 * IN_ROWS, rows), lambda s: (s // 4, 0)),
            pl.BlockSpec((48, rows), lambda s: (s, 0)),
            pl.BlockSpec((48, rows), lambda s: (s, 0)),
            pl.BlockSpec((1, 1, rows), lambda s: (s, 0, 0)),
            pl.BlockSpec((rows, width), lambda s: (0, 0), pipeline_mode=pl.Buffered(1)),
            pl.BlockSpec((1, 4, 48, width), lambda s: (s // 4, 0, 0, 0)),
            anywhere,
        ],
        out_specs=[
            pl.BlockSpec((4 * IN_ROWS, rows), lambda s: (s // 4, 0)),
            pl.BlockSpec((1, 4, HEAD_ROWS, width), lambda s: (s // 4, 0, 0, 0)),
            pl.BlockSpec((1, 8, 4 * IN_ROWS), lambda s: (s // 4, 0, 0)),
            anywhere,
        ],
        out_shape=[
            jax.ShapeDtypeStruct((16 * IN_ROWS, rows), BF16),
            jax.ShapeDtypeStruct((4, 4, HEAD_ROWS, width), BF16),
            jax.ShapeDtypeStruct((4, 8, 4 * IN_ROWS), F32),
            jax.ShapeDtypeStruct((8, 192, width), BF16),
        ],
        scratch_shapes=[pltpu.VMEM((96, LONG_LEN), F32), pltpu.VMEM((4, 2, 2, 192, width), BF16)]
        + reduce_scratch(192, 96, width)
        + [pltpu.SemaphoreType.DMA((4,))],
        compiler_params=pltpu.CompilerParams(
            vmem_limit_bytes=58 << 20, collective_id=1, has_side_effects=True
        ),
        cost_estimate=pl.CostEstimate(
            flops=45_000_000_000, bytes_accessed=40_000_000, transcendentals=19_000_000
        ),
        name="attend_back",
    )(qkv, back_mixed, mixed, logsum, first, out_grad, ff_grad.reshape(4, 2, 2, 2, 192, width))


BLOCK = 256


def tail_kernel(
    back_qkv_ref,
    in_ref,
    tokens_ref,
    resid_ref,
    vector_ref,
    feed_small_ref,
    bias_sums_ref,
    in_grad,
    input_ref,
    small_ref,
    in_out,
    total,
    sums,
    sum_got,
    along_got,
    sum_send,
    sum_recv,
    along_send,
    along_recv,
    *scratch,
    blocks,
):
    step = pl.program_id(0)
    width = tokens_ref.shape[1]
    *got, final, wide, send, recv, share_send, share_recv, wide_send, wide_recv, local = scratch
    dp, base, y, x, core, mp = place()
    ways = lax.axis_size("mp")

    def own(slot):
        src = in_grad.at[slot, :, :, core]
        return pltpu.make_async_copy(src, total.at[slot], local.at[slot])

    reduces = [
        Reduce(
            slot,
            in_grad.at[slot, :, :, flip(core)],
            total.at[slot],
            reduce_refs(got, slot),
            48,
            send,
            recv,
        )
        for slot in range(4)
    ]
    whole = Total(reduces, got[5], final, wide, wide_send, wide_recv)
    share = Share(final, 48, share_send, share_recv)
    order = (2, 1, 3, 0)

    @pl.when(step == 0)
    def _():
        for slot in order:
            own(slot).start()
        greet(group_partners())
        for slot in order:
            reduces[slot].cores()
        for slot in order:
            own(slot).wait()
            reduces[slot].chips()
        sums[0] = jnp.zeros_like(sums[0])
        sums[0, 0:8, :] = feed_small_ref[...]
        for slot in range(4):
            sums[0, 8 + slot : 9 + slot, 0 : 4 * IN_ROWS] = bias_sums_ref[slot, 0:1]

    @pl.when(step == 2)
    def _():
        for slot in order:
            reduces[slot].chips_again()

    @pl.when(step == 4)
    def _():
        for slot in order:
            reduces[slot].along()

    inputs = tokens_ref[...].astype(F32)
    average = jnp.mean(inputs, axis=-1, keepdims=True)
    centred = inputs - average
    inverse = lax.rsqrt(jnp.mean(centred * centred, axis=-1, keepdims=True) + epsilon)
    scaled = centred * inverse
    back_first = None
    for slot in range(4):
        weight = in_ref[slot, :, :IN_ROWS].reshape(4 * IN_ROWS, width)
        part = tn(back_qkv_ref[slot * 4 * IN_ROWS : (slot + 1) * 4 * IN_ROWS, :], weight)
        back_first = part if slot == 0 else back_first + part
    sums[0, 12:13, :] += jnp.sum(back_first * scaled, axis=0, keepdims=True)
    sums[0, 13:14, :] += jnp.sum(back_first, axis=0, keepdims=True)
    back_norm = back_first * vector_ref[0:1, :]
    input_ref[...] = resid_ref[...] + inverse * (
        back_norm
        - jnp.mean(back_norm, axis=-1, keepdims=True)
        - scaled * jnp.mean(back_norm * scaled, axis=-1, keepdims=True)
    )

    @pl.when(step == blocks - 1)
    def _():
        bits = [1, 2, 4] + wider_bits()

        def sum_copy(i):
            return pltpu.make_async_remote_copy(
                src_ref=sums.at[i],
                dst_ref=sum_got.at[i],
                send_sem=sum_send.at[i],
                recv_sem=sum_recv.at[i],
                device_id=(other_bit(dp, bits[i]), mp),
                device_id_type=MESH,
            )

        def along_copy(slot):
            return pltpu.make_async_remote_copy(
                src_ref=sums.at[len(bits)],
                dst_ref=along_got.at[slot - 1],
                send_sem=along_send.at[slot - 1],
                recv_sem=along_recv.at[slot - 1],
                device_id=(dp, lax.rem(mp + slot, ways)),
                device_id_type=MESH,
            )

        sum_copy(0).start()
        whole.sum()
        share.spread()
        for i in range(len(bits)):
            sum_copy(i).wait_recv()
            sums[i + 1] = sums[i] + sum_got[i]
            if i + 1 < len(bits):
                sum_copy(i + 1).start()
            if i == 1:
                share.forward()
        for slot in (1, 2, 3):
            along_copy(slot).start()
        share.last()
        result = sums[len(bits)]
        small_ref[...] = result
        for slot in (1, 2, 3):
            along_copy(slot).wait_recv()
            more = along_got[slot - 1]
            small_ref[0:4, :] += more[0:4]
            small_ref[12:14, :] += more[12:14]
            small_ref[4:5, :] += more[4 + slot : 5 + slot]
            small_ref[8:9, :] += more[8 + slot : 9 + slot]
        share.finish()
        for i in range(len(bits)):
            sum_copy(i).wait_send()
        for slot in (1, 2, 3):
            along_copy(slot).wait_send()
        for reduce in reduces:
            reduce.finish()
        written = pltpu.make_async_copy(final, in_out, local.at[0])
        written.start()
        written.wait()


def tail(back_qkv, in_all, tokens, resid, vectors, feed_small, bias_sums, in_grad):
    rows, width = tokens.shape
    blocks = rows // BLOCK
    bits = 3 + len(wider_bits())
    anywhere = pl.BlockSpec(memory_space=pl.ANY)
    one = pl.Buffered(1)
    dma = pltpu.SemaphoreType.DMA
    return pl.pallas_call(
        functools.partial(tail_kernel, blocks=blocks),
        grid=(blocks,),
        in_specs=[
            pl.BlockSpec((16 * IN_ROWS, BLOCK), lambda s: (0, s)),
            pl.BlockSpec((4, 4, HEAD_ROWS, width), lambda s: (0, 0, 0, 0), pipeline_mode=one),
            pl.BlockSpec((BLOCK, width), lambda s: (s, 0)),
            pl.BlockSpec((BLOCK, width), lambda s: (s, 0)),
            pl.BlockSpec((8, width), lambda s: (0, 0)),
            pl.BlockSpec((8, width), lambda s: (0, 0)),
            pl.BlockSpec((4, 8, 4 * IN_ROWS), lambda s: (0, 0, 0)),
            anywhere,
        ],
        out_specs=[
            pl.BlockSpec((BLOCK, width), lambda s: (s, 0)),
            pl.BlockSpec((16, width), lambda s: (0, 0)),
            anywhere,
        ],
        out_shape=[
            jax.ShapeDtypeStruct((rows, width), F32),
            jax.ShapeDtypeStruct((16, width), F32),
            jax.ShapeDtypeStruct((8, 96, width), BF16),
        ],
        scratch_shapes=[
            pltpu.VMEM((4, 2, 2, 96, width), BF16),
            pltpu.VMEM((bits + 1, 16, width), F32),
            pltpu.VMEM((bits, 16, width), F32),
            pltpu.VMEM((3, 16, width), F32),
            dma((bits,)),
            dma((bits,)),
            dma((3,)),
            dma((3,)),
        ]
        + reduce_scratch(96, 48, width)
        + [dma((4,))],
        compiler_params=pltpu.CompilerParams(
            vmem_limit_bytes=50 << 20, collective_id=2, has_side_effects=True
        ),
        cost_estimate=pl.CostEstimate(
            flops=6_000_000_000, bytes_accessed=30_000_000, transcendentals=2000
        ),
        name="tail",
    )(back_qkv, in_all, tokens, resid, vectors, feed_small, bias_sums, in_grad)


def feed_kernel(live_ref, tokens_ref, grad_ref, mixed_ref, out_w_ref, ff_ref, bias_ref, vec_ref,
                output_ref, resid_ref, back_mixed_ref, ff_grad_ref, out_grad_ref, small_ref,
                second_t, back_t, act_s, hid_s, out_acc, *, blocks):
    step = pl.program_id(0)
    width = tokens_ref.shape[1]

    @pl.when(step == 0)
    def _():
        small_ref[...] = jnp.zeros_like(small_ref)
        second_t[width:, :] = jnp.ones((16, second_t.shape[1]), BF16)

    @pl.when(step < blocks)
    def _():
        row = step * BLOCK + lax.broadcasted_iota(jnp.int32, (BLOCK, 1), 0)
        limit = jnp.where(row < SHORT_ROWS, live_ref[0, 0] * SHORT_LEN, SHORT_ROWS + live_ref[0, 1] * LONG_LEN)
        is_live = row < limit
        out_w = out_w_ref[...].reshape(width, width)
        mixed = mixed_ref[...]
        residual = tokens_ref[...].astype(F32) + tn(mixed, out_w) + vec_ref[0:1, :]
        average = jnp.mean(residual, axis=-1, keepdims=True)
        centred = residual - average
        inverse = lax.rsqrt(jnp.mean(centred * centred, axis=-1, keepdims=True) + epsilon)
        scaled = centred * inverse
        gain = vec_ref[1:2, :]
        second = (scaled * gain + vec_ref[2:3, :]).astype(BF16)
        back = jnp.where(is_live, grad_ref[...].astype(F32), 0.0)
        back_low = back.astype(BF16)
        rows = pl.ds(pl.multiple_of(step * BLOCK, BLOCK), BLOCK)
        second_t[0:width, rows] = second.T
        back_t[:, rows] = back_low.T
        feed = None
        back_second = None
        for j in range(4):
            up = ff_ref[j, :, 0:96, :].reshape(width, width)
            down = ff_ref[j, :, 96:192, :].reshape(width, width)
            hidden = nn(second, up) + bias_ref[j, 0:1, 256:]
            half = 0.5 + 0.5 * lax.erf(hidden * (0.5 ** 0.5))
            act = (hidden * half).astype(BF16)
            slope = half + hidden * (jnp.exp(hidden * hidden * -0.5) * (1.0 / math.sqrt(2 * math.pi)))
            back_hid = (nt(back_low, down) * slope).astype(BF16)
            act_s[j, rows, :] = act
            hid_s[j, rows, :] = back_hid
            f = nn(act, down)
            b = nt(back_hid, up)
            feed = f if j == 0 else feed + f
            back_second = b if j == 0 else back_second + b
        output_ref[...] = jnp.where(is_live, residual + feed + vec_ref[3:4, :], 0.0).astype(BF16)
        small_ref[1:2, :] += jnp.sum(back_second * scaled, axis=0, keepdims=True)
        small_ref[2:3, :] += jnp.sum(back_second, axis=0, keepdims=True)
        small_ref[3:4, :] += jnp.sum(back, axis=0, keepdims=True)
        back_norm = back_second * gain
        back_resid = back + inverse * (
            back_norm - jnp.mean(back_norm, axis=-1, keepdims=True)
            - scaled * jnp.mean(back_norm * scaled, axis=-1, keepdims=True))
        small_ref[0:1, :] += jnp.sum(back_resid, axis=0, keepdims=True)
        resid_ref[...] = back_resid
        branch = back_resid.astype(BF16)
        back_mixed_ref[...] = nt(out_w, branch).astype(BF16)
        part = nn(mixed, branch)
        @pl.when(step == 0)
        def _():
            out_acc[...] = part
        @pl.when(step > 0)
        def _():
            out_acc[...] += part
        @pl.when(step == blocks - 1)
        def _():
            out_grad_ref[...] = out_acc[...].astype(BF16).reshape(out_grad_ref.shape)

    @pl.when(step >= blocks)
    def _():
        slot = step - blocks
        up = nn(second_t[...], hid_s[slot])
        ff_grad_ref[0, :, 0:96, :] = up[:width].astype(BF16).reshape(8, 96, width)
        small_ref[pl.ds(4 + slot, 1), :] = up[width:width + 1]
        down = nn(back_t[...], act_s[slot])
        ff_grad_ref[0, :, 96:192, :] = down.astype(BF16).reshape(8, 96, width)

def feed(live, tokens, out_grad, mixed, in_all, ff_all, bias_all, vectors):
    rows, width = tokens.shape
    blocks = rows // BLOCK
    blk = lambda s: (jnp.minimum(s, blocks - 1), 0)
    col = lambda s: (0, jnp.minimum(s, blocks - 1))
    one = pl.Buffered(1)
    return pl.pallas_call(
        functools.partial(feed_kernel, blocks=blocks),
        grid=(blocks + 4,),
        in_specs=[
            pl.BlockSpec(memory_space=pltpu.SMEM),
            pl.BlockSpec((BLOCK, width), blk),
            pl.BlockSpec((BLOCK, width), blk),
            pl.BlockSpec((width, BLOCK), col),
            pl.BlockSpec((4, 4, 48, width), lambda s: (0, 0, 3, 0), pipeline_mode=one),
            pl.BlockSpec((4, 8, 192, width), lambda s: (0, 0, 0, 0), pipeline_mode=one),
            pl.BlockSpec((4, 8, 1024), lambda s: (0, 0, 0), pipeline_mode=one),
            pl.BlockSpec((8, width), lambda s: (0, 0), pipeline_mode=one),
        ],
        out_specs=[
            pl.BlockSpec((BLOCK, width), blk),
            pl.BlockSpec((BLOCK, width), blk),
            pl.BlockSpec((width, BLOCK), col),
            pl.BlockSpec((1, 8, 192, width), lambda s: (jnp.maximum(s - blocks, 0), 0, 0, 0)),
            pl.BlockSpec((4, 4, 48, width), lambda s: (0, 0, 0, 0)),
            pl.BlockSpec((8, width), lambda s: (0, 0)),
        ],
        out_shape=[
            jax.ShapeDtypeStruct((rows, width), BF16),
            jax.ShapeDtypeStruct((rows, width), F32),
            jax.ShapeDtypeStruct((width, rows), BF16),
            jax.ShapeDtypeStruct((4, 8, 192, width), BF16),
            jax.ShapeDtypeStruct((4, 4, 48, width), BF16),
            jax.ShapeDtypeStruct((8, width), F32),
        ],
        scratch_shapes=[
            pltpu.VMEM((width + 16, rows), BF16),
            pltpu.VMEM((width, rows), BF16),
            pltpu.VMEM((4, rows, width), BF16),
            pltpu.VMEM((4, rows, width), BF16),
            pltpu.VMEM((width, width), F32),
        ],
        compiler_params=pltpu.CompilerParams(vmem_limit_bytes=60 << 20),
        cost_estimate=pl.CostEstimate(flops=50_000_000_000, bytes_accessed=45_000_000, transcendentals=10_000_000),
        name="feed",
    )(live, tokens, out_grad, mixed, in_all, ff_all, bias_all, vectors)


def local(
    tokens,
    out_grad,
    live_images,
    first_gain,
    first_shift,
    project_in,
    query_value_bias,
    project_out,
    output_bias,
    second_gain,
    second_shift,
    up_weight,
    up_bias,
    down_weight,
    down_bias,
):
    width = tokens.shape[1]
    own_heads = project_in.shape[2] // HEAD_DIM
    in_own = project_in.reshape(width, 3, own_heads, HEAD_DIM).transpose(2, 1, 3, 0)
    in_own = jnp.concatenate(
        [in_own.reshape(own_heads, IN_ROWS, width), project_out.reshape(own_heads, HEAD_DIM, width)],
        axis=1,
    )
    ff_own = jnp.concatenate(
        [up_weight.reshape(8, -1, width), down_weight.reshape(8, -1, width)], axis=1
    )
    pair_bias = query_value_bias.astype(F32).reshape(2, own_heads, HEAD_DIM)
    own_bias = jnp.concatenate([pair_bias[0], jnp.zeros_like(pair_bias[0]), pair_bias[1]], axis=1)
    bias_own = jnp.zeros((8, 1024), F32)
    bias_own = lax.dynamic_update_slice(bias_own, own_bias, (0, 0))
    bias_own = lax.dynamic_update_slice(bias_own, up_bias.astype(F32)[None], (0, 256))
    blank = jnp.zeros_like(first_gain)
    feed_vectors = jnp.stack([output_bias, second_gain, second_shift, down_bias] + [blank] * 4)
    tail_vectors = jnp.stack([first_gain] + [blank] * 7)

    first = layer_norm(tokens.astype(F32), first_gain, first_shift).astype(BF16)
    qkv, mixed, logsum, in_all, ff_all, bias_all = attend(first, in_own, ff_own, bias_own)
    output, resid, back_mixed, ff_grad, out_grads, feed_small = feed(
        live_images, tokens, out_grad, mixed, in_all, ff_all, bias_all, feed_vectors
    )
    back_qkv, in_grad, bias_sums, ff_sum = attend_back(
        qkv, back_mixed, mixed, logsum, first, out_grads, ff_grad
    )
    input_grad, small, in_sum = tail(
        back_qkv,
        in_all,
        tokens,
        resid,
        tail_vectors,
        feed_small,
        bias_sums,
        in_grad.reshape(4, 2, 2, 2, 96, width),
    )
    grad_up = ff_sum[:, :96].reshape(width, width).astype(F32)
    grad_down = ff_sum[:, 96:].reshape(width, width).astype(F32).T
    in_sum = in_sum.reshape(own_heads, HEAD_ROWS, width)
    grad_out = in_sum[:, IN_ROWS:].reshape(-1, width).astype(F32)
    grad_in = in_sum[:, :IN_ROWS].reshape(own_heads, 3, HEAD_DIM, width).astype(F32)
    grad_in = grad_in.transpose(3, 1, 0, 2).reshape(width, 3, -1)
    pair_sum = small[8, : 4 * IN_ROWS].reshape(own_heads, 3, HEAD_DIM)
    grad_pair = jnp.stack([pair_sum[:, 0].reshape(-1), pair_sum[:, 2].reshape(-1)])
    return (
        output,
        input_grad,
        small[12],
        small[13],
        grad_in,
        grad_pair,
        grad_out,
        small[0],
        small[1],
        small[2],
        grad_up,
        small[4],
        grad_down,
        small[3],
    )


def solution(mesh):
    rows = P(("dp", "mp"), None)
    return jax.shard_map(
        local,
        mesh=mesh,
        in_specs=(
            rows,
            rows,
            rows,
            P(),
            P(),
            P(None, None, "mp"),
            P(None, "mp"),
            P("mp", None),
            P(),
            P(),
            P(),
            P(None, "mp"),
            P("mp"),
            P("mp", None),
            P(),
        ),
        out_specs=(
            rows,
            rows,
            P(),
            P(),
            P(None, None, "mp"),
            P(None, "mp"),
            P("mp", None),
            P(),
            P(),
            P(),
            P(None, "mp"),
            P("mp"),
            P("mp", None),
            P(),
        ),
        check_vma=False,
    )
```

```python
import functools
import math

import jax
import jax.numpy as jnp
from jax import lax
from jax.experimental import pallas as pl
from jax.experimental.pallas import tpu as pltpu
from jax.sharding import PartitionSpec as P

HEAD_DIM = 48
SHORT_LEN = 256
LONG_LEN = 1024
SHORT_SLOTS = 2
LONG_SLOTS = 1
SHORT_ROWS = SHORT_SLOTS * SHORT_LEN
IMAGES = tuple((SHORT_LEN * i, SHORT_LEN) for i in range(SHORT_SLOTS)) + tuple(
    (SHORT_ROWS + LONG_LEN * i, LONG_LEN) for i in range(LONG_SLOTS)
)
SCALE = HEAD_DIM**-0.5
SCALE_LOG2 = SCALE * math.log2(math.e)
BF16 = jnp.bfloat16
F32 = jnp.float32
CHUNK = 512
BACK_CHUNK = 256

epsilon = 1e-05


def layer_norm(rows_in, norm_gain, norm_shift):
    average = jnp.mean(rows_in, axis=-1, keepdims=True)
    centred = rows_in - average
    variance = jnp.mean(centred * centred, axis=-1, keepdims=True)
    return centred * lax.rsqrt(variance + epsilon) * norm_gain + norm_shift


def nn(left, right):
    return lax.dot_general(
        left, right, (((1,), (0,)), ((), ())), preferred_element_type=F32
    )


def nt(left, right):
    return lax.dot_general(
        left, right, (((1,), (1,)), ((), ())), preferred_element_type=F32
    )


def tn(left, right):
    return lax.dot_general(
        left, right, (((0,), (0,)), ((), ())), preferred_element_type=F32
    )


GROUP = 8
MESH = pl.DeviceIdType.MESH
IN_ROWS = 144
HEAD_ROWS = 192


def place():
    dp, mp = lax.axis_index("dp"), lax.axis_index("mp")
    g = lax.rem(dp, GROUP)
    return dp, dp - g, g // 4, lax.rem(g // 2, 2), lax.rem(g, 2), mp


def flip(bit):
    return 1 - bit


class Gather:
    def __init__(self, own, buffers, piece, split, send, recv):
        self.own, self.buffers, self.piece, self.split = own, buffers, piece, split
        self.send, self.recv = send, recv
        self.dp, self.base, self.y, self.x, self.core, self.mp = place()

    def device(self, y, x, core):
        return (self.base + 4 * y + 2 * x + core, self.mp)

    def view(self, ref, y, x, core, part=None):
        view = self.piece(ref, 2 * y + x, core)
        if part is None:
            return view
        rows = view.shape[0]
        return view.at[pl.ds(0, self.split)] if part == 0 else view.at[pl.ds(self.split, rows - self.split)]

    def copy(self, kind, slot):
        y, x, core = self.y, self.x, self.core
        mine = (y, x, core)
        buffer = self.buffers[slot]
        if kind == 0:
            ways = lax.axis_size("mp")
            hop = 1 if slot == 2 else slot
            src = self.view(self.buffers[1] if slot == 2 else self.own, *mine)
            dst = self.view(buffer, *mine)
            device = (self.dp, lax.rem(self.mp + ways - hop, ways))
        else:
            return self.shared(kind, buffer, kind * 4 + slot)
        return self.remote(src, dst, device, kind * 4 + slot)

    def shared(self, kind, buffer, index):
        y, x, core = self.y, self.x, self.core
        mine, near_x, near_y = (y, x, core), (y, flip(x), core), (flip(y), x, core)
        moved, device = {
            1: lambda: (self.view(buffer, *mine), near_x),
            2: lambda: (self.view(buffer, *mine), near_y),
            3: lambda: (self.view(buffer, *near_x, 0), near_y),
            4: lambda: (self.view(buffer, *near_y, 1), near_x),
            5: lambda: (self.view(buffer, *mine), (y, x, flip(core))),
            6: lambda: (self.view(buffer, *near_x), (y, x, flip(core))),
            7: lambda: (self.view(buffer, *near_y), (y, x, flip(core))),
            8: lambda: (self.view(buffer, flip(y), flip(x), core), (y, x, flip(core))),
        }[kind]()
        return self.remote(moved, moved, self.device(*device), index)

    def remote(self, src, dst, device, index):
        return pltpu.make_async_remote_copy(
            src_ref=src,
            dst_ref=dst,
            send_sem=self.send.at[index],
            recv_sem=self.recv.at[index],
            device_id=device,
            device_id_type=MESH,
        )

    def start(self, slot, *kinds):
        for kind in kinds:
            self.copy(kind, slot).start()

    def arrived(self, slot, *kinds):
        for kind in kinds:
            self.copy(kind, slot).wait_recv()

    def along(self, slot):
        self.start(slot, 0)

    def spread(self, slot):
        self.arrived(slot, 0)
        self.start(slot, 1, 2, 5)

    def forward(self, slot):
        self.arrived(slot, 1)
        self.start(slot, 3, 6)
        self.arrived(slot, 2)
        self.start(slot, 4, 7)

    def last(self, slot):
        self.arrived(slot, 3, 4)
        self.start(slot, 8)

    def complete(self, slot):
        self.arrived(slot, 5, 6, 7, 8)

    def finish(self, *slots):
        for slot in slots:
            for kind in range(GATHER_KINDS):
                self.copy(kind, slot).wait_send()


GATHER_KINDS = 9


def in_piece(ref, chip, core):
    return ref.at[chip, :, pl.ds(pl.multiple_of(core * 384, 128), 384)]


def ff_piece(ref, chip, core):
    return ref.at[2 * chip + core]


def greet(partners):
    barrier = pltpu.get_barrier_semaphore()
    for partner in partners:
        pl.semaphore_signal(barrier, inc=1, device_id=partner, device_id_type=MESH)
    pl.semaphore_wait(barrier, len(partners))


def chunks_of(images, size):
    return [
        (start, length, first, min(size, length))
        for start, length in images
        for first in range(start, start + length, min(size, length))
    ]


def attend_head(qkv_ref, mixed_ref, logsum_ref):
    held = {}

    def score(start, length, first, chunk):
        if start not in held:
            whole = slice(start, start + length)
            value_t = qkv_ref[96:144, whole]
            held[start] = (
                qkv_ref[48:96, whole].T,
                jnp.concatenate([value_t, jnp.ones((16, length), BF16)], axis=0),
            )
        return nn(held[start][0], qkv_ref[0:48, first : first + chunk])

    def soften(scores):
        top = jnp.max(scores, axis=0, keepdims=True)
        return top, jnp.exp2((scores - top) * SCALE_LOG2).astype(BF16)

    def mix(item, top, weights):
        start, length, first, chunk = item
        cols = slice(first, first + chunk)
        sums = nn(held[start][1], weights)
        total = sums[48:49]
        mixed_ref[:, cols] = (sums[:48] / total).astype(BF16)
        logsum_ref[:, cols] = top * SCALE_LOG2 + jnp.log2(total)

    items = chunks_of(IMAGES, CHUNK)
    early, late = {0: score(*items[0])}, {}
    for i in range(len(items) + 1):
        if i + 1 < len(items):
            early[i + 1] = score(*items[i + 1])
        if i < len(items):
            late[i] = soften(early.pop(i))
        if i > 0:
            mix(items[i - 1], *late.pop(i - 1))


def hooks_of(table, step):
    def hook(name):
        for (at, where), actions in table.items():
            if where == name:

                @pl.when(step == at)
                def _(actions=actions):
                    for action in actions:
                        action()

    return hook


def group_partners(wide=False):
    dp, base, y, x, core, mp = place()
    ways = lax.axis_size("mp")
    return (
        [(dp, lax.rem(mp + k, ways)) for k in (1, 2, 3)]
        + [
            (base + 4 * y + 2 * flip(x) + core, mp),
            (base + 4 * flip(y) + 2 * x + core, mp),
            (base + 4 * y + 2 * x + flip(core), mp),
        ]
        + [(other_bit(dp, bit), mp) for bit in wider_bits() if wide]
    )


def attend_kernel(
    tokens_ref,
    vector_ref,
    in_own,
    out_own,
    ff_own,
    bias_own,
    qkv_ref,
    mixed_ref,
    logsum_ref,
    first_ref,
    in_out,
    ff_near,
    bias_out,
    in_all,
    bias_all,
    in_send,
    in_recv,
    ff_send,
    ff_recv,
    bias_send,
    bias_recv,
    own_sem,
    local_sem,
):
    step = pl.program_id(0)
    dp, base, y, x, core, mp = place()
    ways = lax.axis_size("mp")
    gin = Gather(in_all.at[0], [in_all.at[k] for k in range(4)], in_piece, 96, in_send, in_recv)
    gff = Gather(ff_own, [None, ff_near], ff_piece, 96, ff_send, ff_recv)
    own_copies = [
        pltpu.make_async_copy(
            in_own.at[part, pl.ds(head * 48, 48)] if part < 3 else out_own.at[pl.ds(head * 48, 48)],
            in_all.at[0, head, pl.ds(part * 48, 48)],
            own_sem.at[part * 4 + head],
        )
        for part in range(4)
        for head in range(4)
    ]
    local_bias = pltpu.make_async_copy(bias_own, bias_all.at[0], local_sem.at[1])
    out_in = pltpu.make_async_copy(in_all, in_out, local_sem.at[2])
    out_bias = pltpu.make_async_copy(bias_all, bias_out, local_sem.at[3])

    def bias_copy(slot):
        return pltpu.make_async_remote_copy(
            src_ref=bias_own,
            dst_ref=bias_all.at[slot],
            send_sem=bias_send.at[slot],
            recv_sem=bias_recv.at[slot],
            device_id=(dp, lax.rem(mp + ways - slot, ways)),
            device_id_type=MESH,
        )

    def begin():
        for copy in own_copies:
            copy.start()
        local_bias.start()
        greet(group_partners())
        for copy in own_copies:
            copy.wait()
        gin.along(1)
        gin.along(3)
        for slot in (1, 2, 3):
            bias_copy(slot).start()
        for rows in range(0, tokens_ref.shape[0], BLOCK):
            block = slice(rows, rows + BLOCK)
            first_ref[block] = layer_norm(
                tokens_ref[block].astype(F32), vector_ref[4:5], vector_ref[5:6]
            ).astype(BF16)
        local_bias.wait()

    def end():
        gff.complete(1)
        out_in.wait()
        out_bias.wait()
        for slot in (1, 2, 3):
            bias_copy(slot).wait_send()
        gin.finish(1, 2, 3)
        gff.finish(1)

    hook = hooks_of(
        {
            (0, "begin"): [begin],
            (0, "heads"): [lambda: gin.spread(1), lambda: gin.along(2), lambda: gff.along(1)],
            (0, 2): [lambda: gin.forward(1)],
            (0, 3): [lambda: gin.spread(3)],
            (0, "end"): [lambda: gin.last(1), lambda: gin.spread(2)],
            (1, "begin"): [
                lambda: [bias_copy(slot).wait_recv() for slot in (1, 2, 3)],
                lambda: gin.complete(1),
            ],
            (1, "heads"): [lambda: gin.forward(3)],
            (1, 2): [lambda: gin.last(3), lambda: gin.forward(2), lambda: gff.spread(1)],
            (1, "end"): [lambda: gin.last(2)],
            (2, "begin"): [lambda: gin.complete(3)],
            (2, 2): [lambda: gff.forward(1)],
            (2, "end"): [lambda: gff.last(1)],
            (3, "begin"): [lambda: gin.complete(2), out_in.start, out_bias.start],
            (3, "end"): [end],
        },
        step,
    )
    slot = slot_order(step)
    hook("begin")
    bias_t = bias_all[slot, :, 0:256].T
    for part in range(4):
        product = nt(in_all[slot, part, :IN_ROWS], first_ref[...])
        qkv_ref[part * IN_ROWS : (part + 1) * IN_ROWS, :] = (
            product + bias_t[:IN_ROWS, part : part + 1]
        ).astype(BF16)
    hook("heads")
    for head in range(4):
        if head:
            hook(head)
        attend_head(
            qkv_ref.at[pl.ds(head * IN_ROWS, IN_ROWS)],
            mixed_ref.at[pl.ds(head * 48, 48)],
            logsum_ref.at[head],
        )
    hook("end")


def slot_order(turn):
    return turn + (turn // 2) * (1 - 2 * (turn % 2))


def attend(tokens, vectors, in_own, out_own, ff_own, bias_own):
    rows, width = tokens.shape
    heads = 16
    anywhere = pl.BlockSpec(memory_space=pl.ANY)
    dma = pltpu.SemaphoreType.DMA
    return pl.pallas_call(
        attend_kernel,
        grid=(4,),
        in_specs=[
            pl.BlockSpec((rows, width), lambda s: (0, 0), pipeline_mode=pl.Buffered(1)),
            pl.BlockSpec((8, width), lambda s: (0, 0)),
            anywhere,
            anywhere,
            anywhere,
            anywhere,
        ],
        out_specs=[
            pl.BlockSpec((4 * IN_ROWS, rows), lambda s: (slot_order(s), 0)),
            pl.BlockSpec((4 * 48, rows), lambda s: (slot_order(s), 0)),
            pl.BlockSpec((4, 1, rows), lambda s: (slot_order(s), 0, 0)),
            pl.BlockSpec((rows, width), lambda s: (0, 0)),
            anywhere,
            anywhere,
            anywhere,
        ],
        out_shape=[
            jax.ShapeDtypeStruct((heads * IN_ROWS, rows), BF16),
            jax.ShapeDtypeStruct((heads * 48, rows), BF16),
            jax.ShapeDtypeStruct((heads, 1, rows), F32),
            jax.ShapeDtypeStruct((rows, width), BF16),
            jax.ShapeDtypeStruct((4, 4, HEAD_ROWS, width), BF16),
            jax.ShapeDtypeStruct((8, 192, width), BF16),
            jax.ShapeDtypeStruct((4, 8, 1024), F32),
        ],
        scratch_shapes=[
            pltpu.VMEM((4, 4, HEAD_ROWS, width), BF16),
            pltpu.VMEM((4, 8, 1024), F32),
            dma((4 * GATHER_KINDS,)),
            dma((4 * GATHER_KINDS,)),
            dma((4 * GATHER_KINDS,)),
            dma((4 * GATHER_KINDS,)),
            dma((4,)),
            dma((4,)),
            dma((16,)),
            dma((4,)),
        ],
        compiler_params=pltpu.CompilerParams(
            vmem_limit_bytes=62 << 20, collective_id=0, has_side_effects=True
        ),
        cost_estimate=pl.CostEstimate(
            flops=30_000_000_000, bytes_accessed=30_000_000, transcendentals=19_000_000
        ),
        name="attend",
    )(tokens, vectors, in_own, out_own, ff_own, bias_own)


class Reduce:
    def __init__(self, slot, other, total, got, split, send, recv):
        self.slot, self.other, self.total, self.got, self.split = slot, other, total, got, split
        self.send, self.recv = send, recv
        self.dp, self.base, self.y, self.x, self.core, self.mp = place()

    def copy(self, kind):
        y, x, core = self.y, self.x, self.core
        first, late = pl.ds(0, self.split), pl.ds(self.split, self.total.shape[2] - self.split)
        got = self.got
        near = lambda y, x, core: (self.base + 4 * y + 2 * x + core, self.mp)
        to_x, to_y = near(y, flip(x), core), near(flip(y), x, core)
        src, dst, device = {
            0: lambda: (self.other, got[0], near(y, x, flip(core))),
            1: lambda: (self.total.at[:, flip(x), first], got[1], to_x),
            2: lambda: (self.total.at[flip(y), :, late], got[2], to_y),
            3: lambda: (self.total.at[flip(y), x, first], got[3], to_y),
            4: lambda: (self.total.at[y, flip(x), late], got[4], to_x),
            5: lambda: (
                self.total.at[y, x],
                got[5],
                (self.dp, lax.rem(self.mp + self.slot, lax.axis_size("mp"))),
            ),
        }[kind]()
        index = kind * 4 + self.slot
        return pltpu.make_async_remote_copy(
            src_ref=src,
            dst_ref=dst,
            send_sem=self.send.at[index],
            recv_sem=self.recv.at[index],
            device_id=device,
            device_id_type=MESH,
        )

    def cores(self):
        self.copy(0).start()

    def chips(self):
        self.copy(0).wait_recv()
        for y in range(2):
            for x in range(2):
                self.total[y, x] = add(self.total[y, x], self.got[0][y, x])
        self.copy(1).start()
        self.copy(2).start()

    def chips_again(self):
        x, y, split = self.x, self.y, self.split
        self.copy(1).wait_recv()
        for i in range(2):
            self.total[i, x, :split] = add(self.total[i, x, :split], self.got[1][i])
        self.copy(2).wait_recv()
        for i in range(2):
            self.total[y, i, split:] = add(self.total[y, i, split:], self.got[2][i])
        self.copy(3).start()
        self.copy(4).start()

    def settle(self):
        x, y, split = self.x, self.y, self.split
        self.copy(3).wait_recv()
        self.total[y, x, :split] = add(self.total[y, x, :split], self.got[3][...])
        self.copy(4).wait_recv()
        self.total[y, x, split:] = add(self.total[y, x, split:], self.got[4][...])

    def along(self):
        self.settle()
        if self.slot:
            self.copy(5).start()

    def finish(self, kinds=6):
        for kind in range(kinds if self.slot else 5):
            self.copy(kind).wait_send()

    def result(self):
        if self.slot:
            self.copy(5).wait_recv()
            return self.got[5][...].astype(F32)
        return self.total[self.y, self.x].astype(F32)


REDUCE_KINDS = 6


def add(left, right):
    return (left.astype(F32) + right.astype(F32)).astype(BF16)


def other_bit(index, bit):
    return index + bit * (1 - 2 * lax.rem(index // bit, 2))


def wider_bits():
    bits, bit = [], GROUP
    while bit < lax.axis_size("dp"):
        bits.append(bit)
        bit *= 2
    return bits


class Share:
    def __init__(self, pieces, split, send, recv):
        self.inner = Gather(None, None, ff_piece, split, send, recv)
        self.pieces = pieces

    def copy(self, kind):
        return self.inner.shared(kind, self.pieces, kind)

    def start(self, *kinds):
        for kind in kinds:
            self.copy(kind).start()

    def arrived(self, *kinds):
        for kind in kinds:
            self.copy(kind).wait_recv()

    def spread(self):
        self.start(1, 2, 5)

    def forward(self):
        self.arrived(1)
        self.start(3, 6)
        self.arrived(2)
        self.start(4, 7)

    def last(self):
        self.arrived(3, 4)
        self.start(8)

    def finish(self):
        self.arrived(5, 6, 7, 8)
        for kind in range(1, 9):
            self.copy(kind).wait_send()


class Wide:
    def __init__(self, held, send, recv):
        self.held, self.send, self.recv = held, send, recv

    def copy(self, i, bit):
        dp, mp = lax.axis_index("dp"), lax.axis_index("mp")
        return pltpu.make_async_remote_copy(
            src_ref=self.held.at[2 * i],
            dst_ref=self.held.at[2 * i + 1],
            send_sem=self.send.at[i],
            recv_sem=self.recv.at[i],
            device_id=(other_bit(dp, bit), mp),
            device_id_type=MESH,
        )

    def sum(self, total):
        for i, bit in enumerate(wider_bits()):
            self.held[2 * i] = total.astype(BF16)
            self.copy(i, bit).start()
            self.copy(i, bit).wait()
            total = total + self.held[2 * i + 1].astype(F32)
        return total


def reduce_scratch(slots, rows, split, width):
    dma = pltpu.SemaphoreType.DMA
    late = rows - split
    return [
        pltpu.VMEM((slots, 2, 2, rows, width), BF16),
        pltpu.VMEM((slots, 2, split, width), BF16),
        pltpu.VMEM((slots, 2, late, width), BF16),
        pltpu.VMEM((slots, split, width), BF16),
        pltpu.VMEM((slots, late, width), BF16),
        pltpu.VMEM((slots, rows, width), BF16),
        dma((4 * REDUCE_KINDS,)),
        dma((4 * REDUCE_KINDS,)),
    ]


REDUCE_REFS = 8


def reduces_of(slots, other, total, scratch, split):
    *got, send, recv = scratch
    return {
        slot: Reduce(slot, other(i), total(i), [ref.at[i] for ref in got], split, send, recv)
        for i, slot in enumerate(slots)
    }


def share_scratch(rows, width):
    dma = pltpu.SemaphoreType.DMA
    wide = max(len(wider_bits()), 1)
    return [
        pltpu.VMEM((8, rows, width), BF16),
        pltpu.VMEM((2 * wide, rows, width), BF16),
        dma((GATHER_KINDS,)),
        dma((GATHER_KINDS,)),
        dma((wide,)),
        dma((wide,)),
    ]


SHARE_REFS = 6


def attend_back_head(qkv_ref, back_ref, mixed_ref, logsum_ref, out_ref, held):
    rows = {}

    def score(start, length, first, chunk):
        if start not in rows:
            whole = slice(start, start + length)
            key_t = qkv_ref[48:96, whole]
            rows[start] = (key_t, key_t.T, qkv_ref[96:144, whole].T)
        cols = slice(first, first + chunk)
        return (
            nn(rows[start][1], qkv_ref[0:48, cols]),
            nn(rows[start][2], back_ref[:, cols]),
        )

    def soften(item, scores, back_probs):
        cols = slice(item[2], item[2] + item[3])
        inner = jnp.sum(
            back_ref[:, cols].astype(F32) * mixed_ref[:, cols].astype(F32), axis=0, keepdims=True
        )
        probs = jnp.exp2(scores * SCALE_LOG2 - logsum_ref[:, cols])
        return probs.astype(BF16), (probs * (back_probs - inner)).astype(BF16)

    def pull(item, probs, back_scores):
        start, length, first, chunk = item
        cols, whole = slice(first, first + chunk), slice(start, start + length)
        query_t, back_t = qkv_ref[0:48, cols], back_ref[:, cols]
        out_ref[0:48, cols] = (nn(rows[start][0], back_scores) * SCALE).astype(BF16)
        back_key = nt(query_t, back_scores)
        back_value = nt(back_t, probs)
        if first > start:
            back_key = back_key + held[0:48, 0:length]
            back_value = back_value + held[48:96, 0:length]
        if first + chunk < start + length:
            held[0:48, 0:length] = back_key
            held[48:96, 0:length] = back_value
        else:
            out_ref[48:96, whole] = (back_key * SCALE).astype(BF16)
            out_ref[96:144, whole] = back_value.astype(BF16)

    items = chunks_of(IMAGES, BACK_CHUNK)
    early = {0: score(*items[0])}
    for i in range(len(items)):
        if i + 1 < len(items):
            early[i + 1] = score(*items[i + 1])
        pull(items[i], *soften(items[i], *early.pop(i)))


def attend_back_kernel(
    qkv_ref,
    back_ref,
    mixed_ref,
    logsum_ref,
    first_ref,
    out_grad_ref,
    ff_part_ref,
    ff_grad,
    out_ref,
    sums_ref,
    part_ref,
    piece_ref,
    ff_out,
    in_grad,
    held,
    ff_total,
    grads,
    local,
    *scratch,
):
    step = pl.program_id(0)
    dp, base, y, x, core, mp = place()
    ff_scratch, scratch = scratch[:REDUCE_REFS], scratch[REDUCE_REFS:]
    in_scratch, scratch = scratch[:REDUCE_REFS], scratch[REDUCE_REFS:]
    final, wide, share_send, share_recv, wide_send, wide_recv = scratch
    ff = reduces_of(
        (2, 3),
        lambda i: ff_grad.at[i, :, :, flip(core)],
        lambda i: ff_total.at[i],
        ff_scratch,
        96,
    )
    ins = reduces_of(
        (1, 2, 3),
        lambda i: grads.at[i + 1, :, :, flip(core)],
        lambda i: grads.at[i + 1, :, :, core],
        in_scratch,
        48,
    )
    share = Share(final, 96, share_send, share_recv)
    written = pltpu.make_async_copy(final, ff_out, local.at[2])
    in_written = pltpu.make_async_copy(grads.at[0], in_grad, local.at[3])

    def own(i):
        return pltpu.make_async_copy(
            ff_grad.at[i, :, :, core], ff_total.at[i], local.at[i]
        )

    def begin():
        own(0).start()
        own(1).start()
        greet(group_partners(True))
        ff[2].cores()
        ff[3].cores()

    def chips(slot):
        own(slot - 2).wait()
        ff[slot].chips()

    def finish_ff():
        total = ff_part_ref[...] + ff[2].result() + ff[3].result()
        total = Wide(wide, wide_send, wide_recv).sum(total)
        final[4 * y + 2 * x + core] = total.astype(BF16)
        share.spread()

    def end():
        in_written.start()
        share.finish()
        written.start()
        part_ref[...] = ins[1].result() + ins[2].result()
        ins[3].settle()
        piece_ref[...] = ins[3].total[y, x]
        for reduce in [*ff.values(), ins[1], ins[2]]:
            reduce.finish()
        ins[3].finish(5)
        written.wait()
        in_written.wait()

    hook = hooks_of(
        {
            (0, 0): [begin],
            (0, 1): [lambda: chips(2)],
            (0, 3): [ff[2].chips_again, lambda: chips(3)],
            (1, 0): [ins[2].cores],
            (1, 2): [ff[2].along],
            (1, 3): [ff[3].chips_again, ins[2].chips],
            (2, 0): [ff[3].along, ins[1].cores],
            (2, 1): [ins[2].chips_again, ins[1].chips],
            (2, 3): [finish_ff, ins[2].along, ins[1].chips_again],
            (3, 0): [ins[1].along, ins[3].cores],
            (3, 1): [share.forward, ins[3].chips],
            (3, 3): [share.last, ins[3].chips_again],
            (3, "end"): [end],
        },
        step,
    )
    for head in range(4):
        hook(head)
        attend_back_head(
            qkv_ref.at[pl.ds(head * IN_ROWS, IN_ROWS)],
            back_ref.at[pl.ds(head * 48, 48)],
            mixed_ref.at[pl.ds(head * 48, 48)],
            logsum_ref.at[head],
            out_ref.at[pl.ds(head * IN_ROWS, IN_ROWS)],
            held,
        )
    slot = back_order(step)
    for head in range(4):
        rows = out_ref[head * IN_ROWS : (head + 1) * IN_ROWS, :]
        grad = nn(rows, first_ref[...]).astype(BF16)
        grads[slot, head // 2, head % 2, 0] = grad[:96]
        grads[slot, head // 2, head % 2, 1, 0:48] = grad[96:]
        grads[slot, head // 2, head % 2, 1, 48:96] = out_grad_ref[0, head]
    sums_ref[0] = nt(jnp.ones((8, out_ref.shape[1]), BF16), out_ref[...])
    hook("end")


def back_order(turn):
    return 2 - turn + (turn // 2) * (3 - 2 * (turn // 3))


def attend_back(qkv, back_mixed, mixed, logsum, first, out_grad, ff_part, ff_grad):
    rows, width = first.shape
    anywhere = pl.BlockSpec(memory_space=pl.ANY)
    return pl.pallas_call(
        attend_back_kernel,
        grid=(4,),
        in_specs=[
            pl.BlockSpec((4 * IN_ROWS, rows), lambda s: (back_order(s), 0)),
            pl.BlockSpec((4 * 48, rows), lambda s: (back_order(s), 0)),
            pl.BlockSpec((4 * 48, rows), lambda s: (back_order(s), 0)),
            pl.BlockSpec((4, 1, rows), lambda s: (back_order(s), 0, 0)),
            pl.BlockSpec((rows, width), lambda s: (0, 0), pipeline_mode=pl.Buffered(1)),
            pl.BlockSpec((1, 4, 48, width), lambda s: (back_order(s), 0, 0, 0)),
            pl.BlockSpec((192, width), lambda s: (0, 0), pipeline_mode=pl.Buffered(1)),
            anywhere,
        ],
        out_specs=[
            pl.BlockSpec((4 * IN_ROWS, rows), lambda s: (back_order(s), 0)),
            pl.BlockSpec((1, 8, 4 * IN_ROWS), lambda s: (back_order(s), 0, 0)),
            pl.BlockSpec((96, width), lambda s: (0, 0)),
            pl.BlockSpec((96, width), lambda s: (0, 0)),
            anywhere,
            anywhere,
        ],
        out_shape=[
            jax.ShapeDtypeStruct((16 * IN_ROWS, rows), BF16),
            jax.ShapeDtypeStruct((4, 8, 4 * IN_ROWS), F32),
            jax.ShapeDtypeStruct((96, width), F32),
            jax.ShapeDtypeStruct((96, width), BF16),
            jax.ShapeDtypeStruct((8, 192, width), BF16),
            jax.ShapeDtypeStruct((2, 2, 2, 96, width), BF16),
        ],
        scratch_shapes=[
            pltpu.VMEM((96, LONG_LEN), F32),
            pltpu.VMEM((2, 2, 2, 192, width), BF16),
            pltpu.VMEM((4, 2, 2, 2, 96, width), BF16),
            pltpu.SemaphoreType.DMA((4,)),
        ]
        + reduce_scratch(2, 192, 96, width)
        + reduce_scratch(3, 96, 48, width)
        + share_scratch(192, width),
        compiler_params=pltpu.CompilerParams(
            vmem_limit_bytes=62 << 20, collective_id=1, has_side_effects=True
        ),
        cost_estimate=pl.CostEstimate(
            flops=45_000_000_000, bytes_accessed=40_000_000, transcendentals=19_000_000
        ),
        name="attend_back",
    )(qkv, back_mixed, mixed, logsum, first, out_grad, ff_part, ff_grad)


BLOCK = 256


def tail_kernel(
    back_qkv_ref,
    in_ref,
    tokens_ref,
    resid_ref,
    vector_ref,
    feed_small_ref,
    up_sums_ref,
    bias_sums_ref,
    part_ref,
    piece_ref,
    ff_ref,
    in_grad,
    input_ref,
    small_ref,
    up_ref,
    down_ref,
    in_ref_out,
    out_ref_out,
    total,
    piece_got,
    sums,
    sum_got,
    wide_got,
    along_got,
    sum_send,
    sum_recv,
    along_send,
    along_recv,
    piece_sem,
    local,
    *scratch,
    blocks,
):
    step = pl.program_id(0)
    width = tokens_ref.shape[1]
    dp, base, y, x, core, mp = place()
    ways = lax.axis_size("mp")
    final, wide, share_send, share_recv, wide_send, wide_recv = scratch[REDUCE_REFS:]
    reduce = reduces_of(
        (0,),
        lambda i: in_grad.at[:, :, flip(core)],
        lambda i: total,
        scratch[:REDUCE_REFS],
        48,
    )[0]
    share = Share(final, 48, share_send, share_recv)
    own = pltpu.make_async_copy(in_grad.at[:, :, core], total, local.at[0])

    piece = pltpu.make_async_remote_copy(
        src_ref=piece_ref,
        dst_ref=piece_got,
        send_sem=piece_sem.at[0],
        recv_sem=piece_sem.at[1],
        device_id=(dp, lax.rem(mp + 3, ways)),
        device_id_type=MESH,
    )

    def begin():
        own.start()
        greet(every_partner())
        reduce.cores()
        piece.start()
        sums[0] = jnp.zeros_like(sums[0])
        sums[0, 0:8, :] = feed_small_ref[...]
        sums[0, 4:6, :] = up_sums_ref[0:2, :]
        for slot in range(4):
            sums[0, 8 + slot : 9 + slot, 0 : 4 * IN_ROWS] = bias_sums_ref[slot, 0:1]
        own.wait()
        reduce.chips()

    def finish_in():
        piece.wait_recv()
        whole = part_ref[...] + reduce.result() + piece_got[...].astype(F32)
        whole = Wide(wide, wide_send, wide_recv).sum(whole)
        final[4 * y + 2 * x + core] = whole.astype(BF16)
        share.spread()

    def along():
        reduce.along()
        finish_in()

    def write_up():
        up_ref[...] = ff_ref[:, :96].reshape(width, width).astype(F32)

    def write_down():
        down_ref[...] = ff_ref[:, 96:].reshape(width, width).astype(F32).T

    hook = hooks_of(
        {
            (0, "begin"): [begin],
            (1, "end"): [reduce.chips_again],
            (2, "begin"): [write_up],
            (2, "end"): [along],
            (3, "begin"): [write_down],
            (4, "end"): [share.forward],
        },
        step,
    )
    hook("begin")
    inputs = tokens_ref[...].astype(F32)
    average = jnp.mean(inputs, axis=-1, keepdims=True)
    centred = inputs - average
    inverse = lax.rsqrt(jnp.mean(centred * centred, axis=-1, keepdims=True) + epsilon)
    scaled = centred * inverse
    back_first = None
    for slot in range(4):
        weight = in_ref[slot, :, :IN_ROWS].reshape(4 * IN_ROWS, width)
        part = tn(back_qkv_ref[slot * 4 * IN_ROWS : (slot + 1) * 4 * IN_ROWS, :], weight)
        back_first = part if slot == 0 else back_first + part
    sums[0, 12:13, :] += jnp.sum(back_first * scaled, axis=0, keepdims=True)
    sums[0, 13:14, :] += jnp.sum(back_first, axis=0, keepdims=True)
    back_norm = back_first * vector_ref[4:5, :]
    input_ref[...] = resid_ref[...] + inverse * (
        back_norm
        - jnp.mean(back_norm, axis=-1, keepdims=True)
        - scaled * jnp.mean(back_norm * scaled, axis=-1, keepdims=True)
    )

    hook("end")

    @pl.when(step == blocks - 1)
    def _():
        wide = wider_bits()
        near = range(1, GROUP)

        def near_copy(k):
            return pltpu.make_async_remote_copy(
                src_ref=sums.at[0],
                dst_ref=sum_got.at[k - 1],
                send_sem=sum_send.at[k - 1],
                recv_sem=sum_recv.at[k - 1],
                device_id=(base + near_index(y, x, core, k), mp),
                device_id_type=MESH,
            )

        def wide_copy(i):
            return pltpu.make_async_remote_copy(
                src_ref=sums.at[i + 1],
                dst_ref=wide_got.at[i],
                send_sem=sum_send.at[GROUP - 1 + i],
                recv_sem=sum_recv.at[GROUP - 1 + i],
                device_id=(other_bit(dp, wide[i]), mp),
                device_id_type=MESH,
            )

        def along_copy(slot):
            return pltpu.make_async_remote_copy(
                src_ref=sums.at[len(wide) + 1],
                dst_ref=along_got.at[slot - 1],
                send_sem=along_send.at[slot - 1],
                recv_sem=along_recv.at[slot - 1],
                device_id=(dp, lax.rem(mp + slot, ways)),
                device_id_type=MESH,
            )

        for k in near:
            near_copy(k).start()
        share.last()
        result = sums[0]
        for k in near:
            near_copy(k).wait_recv()
            result = result + sum_got[k - 1]
        sums[1] = result
        for i in range(len(wide)):
            wide_copy(i).start()
            wide_copy(i).wait_recv()
            sums[i + 2] = sums[i + 1] + wide_got[i]
        for slot in (1, 2, 3):
            along_copy(slot).start()
        share.finish()
        for head in range(4):
            low, high = final[2 * head].astype(F32), final[2 * head + 1].astype(F32)
            rows = slice(48 * head, 48 * head + 48)
            in_ref_out[0, rows], in_ref_out[1, rows] = low[:48], low[48:]
            in_ref_out[2, rows], out_ref_out[rows] = high[:48], high[48:]
        small_ref[...] = sums[len(wide) + 1]
        for slot in (1, 2, 3):
            along_copy(slot).wait_recv()
            more = along_got[slot - 1]
            small_ref[0:4, :] += more[0:4]
            small_ref[12:14, :] += more[12:14]
            small_ref[4:5, :] += more[4 + slot : 5 + slot]
            small_ref[8:9, :] += more[8 + slot : 9 + slot]
        for k in near:
            near_copy(k).wait_send()
        for i in range(len(wide)):
            wide_copy(i).wait_send()
        for slot in (1, 2, 3):
            along_copy(slot).wait_send()
        reduce.finish()
        piece.wait_send()


def near_index(y, x, core, k):
    y = flip(y) if k & 4 else y
    x = flip(x) if k & 2 else x
    core = flip(core) if k & 1 else core
    return 4 * y + 2 * x + core


def every_partner():
    dp, base, y, x, core, mp = place()
    ways = lax.axis_size("mp")
    return (
        [(dp, lax.rem(mp + k, ways)) for k in (1, 2, 3)]
        + [(base + near_index(y, x, core, k), mp) for k in range(1, GROUP)]
        + [(other_bit(dp, bit), mp) for bit in wider_bits()]
    )


def tail(
    back_qkv, in_all, tokens, resid, vectors, small_sums, bias_sums, in_part, piece, ff_sum, in_grad
):
    rows, width = tokens.shape
    blocks = rows // BLOCK
    bits = len(wider_bits())
    anywhere = pl.BlockSpec(memory_space=pl.ANY)
    one = pl.Buffered(1)
    dma = pltpu.SemaphoreType.DMA
    return pl.pallas_call(
        functools.partial(tail_kernel, blocks=blocks),
        grid=(blocks,),
        in_specs=[
            pl.BlockSpec((16 * IN_ROWS, BLOCK), lambda s: (0, s)),
            pl.BlockSpec((4, 4, HEAD_ROWS, width), lambda s: (0, 0, 0, 0), pipeline_mode=one),
            pl.BlockSpec((BLOCK, width), lambda s: (s, 0)),
            pl.BlockSpec((BLOCK, width), lambda s: (s, 0)),
            pl.BlockSpec((8, width), lambda s: (0, 0)),
            pl.BlockSpec((8, width), lambda s: (0, 0)),
            pl.BlockSpec((8, width), lambda s: (0, 0)),
            pl.BlockSpec((4, 8, 4 * IN_ROWS), lambda s: (0, 0, 0)),
            pl.BlockSpec((96, width), lambda s: (0, 0)),
            pl.BlockSpec((96, width), lambda s: (0, 0)),
            pl.BlockSpec((8, 192, width), lambda s: (0, 0, 0), pipeline_mode=one),
            anywhere,
        ],
        out_specs=[
            pl.BlockSpec((BLOCK, width), lambda s: (s, 0)),
            pl.BlockSpec((16, width), lambda s: (0, 0)),
            pl.BlockSpec((width, width), lambda s: (0, 0)),
            pl.BlockSpec((width, width), lambda s: (0, 0)),
            pl.BlockSpec((3, 192, width), lambda s: (0, 0, 0)),
            pl.BlockSpec((192, width), lambda s: (0, 0)),
        ],
        out_shape=[
            jax.ShapeDtypeStruct((rows, width), F32),
            jax.ShapeDtypeStruct((16, width), F32),
            jax.ShapeDtypeStruct((width, width), F32),
            jax.ShapeDtypeStruct((width, width), F32),
            jax.ShapeDtypeStruct((3, 192, width), F32),
            jax.ShapeDtypeStruct((192, width), F32),
        ],
        scratch_shapes=[
            pltpu.VMEM((2, 2, 96, width), BF16),
            pltpu.VMEM((96, width), BF16),
            pltpu.VMEM((bits + 2, 16, width), F32),
            pltpu.VMEM((GROUP - 1, 16, width), F32),
            pltpu.VMEM((max(bits, 1), 16, width), F32),
            pltpu.VMEM((3, 16, width), F32),
            dma((GROUP - 1 + bits,)),
            dma((GROUP - 1 + bits,)),
            dma((3,)),
            dma((3,)),
            dma((2,)),
            dma((1,)),
        ]
        + reduce_scratch(1, 96, 48, width)
        + share_scratch(96, width),
        compiler_params=pltpu.CompilerParams(
            vmem_limit_bytes=62 << 20, collective_id=2, has_side_effects=True
        ),
        cost_estimate=pl.CostEstimate(
            flops=6_000_000_000, bytes_accessed=30_000_000, transcendentals=2000
        ),
        name="tail",
    )(
        back_qkv,
        in_all,
        tokens,
        resid,
        vectors,
        *small_sums,
        bias_sums,
        in_part,
        piece,
        ff_sum,
        in_grad,
    )


FEED_BLOCKS = 6


def feed_rows(
    second, back_low, slots, ff_refs, bias_ref, act_s, hid_s, rows, width, feed, back_second
):
    for i, slot in enumerate(slots):
        up = ff_refs[i][:, 0:96, :].reshape(width, width)
        down = ff_refs[i][:, 96:192, :].reshape(width, width)
        hidden = nn(second, up) + bias_ref[slot, 0:1, 256:]
        half = 0.5 + 0.5 * lax.erf(hidden * (0.5**0.5))
        act = (hidden * half).astype(BF16)
        slope = half + hidden * (jnp.exp(hidden * hidden * -0.5) * (1.0 / math.sqrt(2 * math.pi)))
        back_hid = (nt(back_low, down) * slope).astype(BF16)
        act_s[i, rows, :] = act
        hid_s[i, rows, :] = back_hid
        fed, pulled = nn(act, down), nt(back_hid, up)
        feed = fed if feed is None else feed + fed
        back_second = pulled if back_second is None else back_second + pulled
    return feed, back_second


def normed(rows_in):
    average = jnp.mean(rows_in, axis=-1, keepdims=True)
    centred = rows_in - average
    inverse = lax.rsqrt(jnp.mean(centred * centred, axis=-1, keepdims=True) + epsilon)
    return centred * inverse, inverse


def live_back(live_ref, grad_ref, step):
    row = step * BLOCK + lax.broadcasted_iota(jnp.int32, (BLOCK, 1), 0)
    limit = jnp.where(
        row < SHORT_ROWS, live_ref[0, 0] * SHORT_LEN, SHORT_ROWS + live_ref[0, 1] * LONG_LEN
    )
    is_live = row < limit
    return is_live, jnp.where(is_live, grad_ref[...].astype(F32), 0.0)


def feed_grads(i, second_t, back_t, act_s, hid_s, ff_grad_ref, up_sum_ref, row, width):
    up = nn(second_t[...], hid_s[i])
    ff_grad_ref[0, :, 0:96, :] = up[:width].astype(BF16).reshape(8, 96, width)
    up_sum_ref[pl.ds(row, 1), :] = up[width : width + 1]
    down = nn(back_t[...], act_s[i])
    ff_grad_ref[0, :, 96:192, :] = down.astype(BF16).reshape(8, 96, width)


def feed_first_kernel(
    live_ref,
    tokens_ref,
    grad_ref,
    mixed_ref,
    out_w_ref,
    own_ref,
    near_ref,
    bias_ref,
    vec_ref,
    ff_own,
    ff_near,
    residual_ref,
    feed_ref,
    back_second_ref,
    ff_grad_ref,
    up_sum_ref,
    ff_late,
    second_t,
    back_t,
    act_s,
    hid_s,
    send,
    recv,
):
    step = pl.program_id(0)
    width = tokens_ref.shape[1]
    late = [None, ff_near, ff_late.at[0], ff_late.at[1]]
    gff = Gather(ff_own, late, ff_piece, 96, send, recv)

    def begin():
        greet(group_partners())
        gff.along(3)
        gff.along(2)
        up_sum_ref[...] = jnp.zeros_like(up_sum_ref)
        second_t[width:, :] = jnp.ones((16, second_t.shape[1]), BF16)

    def end():
        gff.complete(3)
        gff.complete(2)
        gff.finish(2, 3)

    hook = hooks_of(
        {
            (0, "begin"): [begin],
            (2, "begin"): [lambda: gff.spread(3)],
            (3, "begin"): [lambda: gff.spread(2)],
            (5, "begin"): [lambda: gff.forward(3)],
            (6, "begin"): [lambda: gff.last(3), lambda: gff.forward(2)],
            (7, "begin"): [lambda: gff.last(2)],
            (7, "end"): [end],
        },
        step,
    )
    hook("begin")

    @pl.when(step < FEED_BLOCKS)
    def _():
        out_w = out_w_ref[...].reshape(width, width)
        residual = tokens_ref[...].astype(F32) + tn(mixed_ref[...], out_w) + vec_ref[0:1, :]
        residual_ref[...] = residual
        scaled, _ = normed(residual)
        second = (scaled * vec_ref[1:2, :] + vec_ref[2:3, :]).astype(BF16)
        _, back = live_back(live_ref, grad_ref, step)
        back_low = back.astype(BF16)
        rows = pl.ds(pl.multiple_of(step * BLOCK, BLOCK), BLOCK)
        second_t[0:width, rows] = second.T
        back_t[:, rows] = back_low.T
        feed_ref[...], back_second_ref[...] = feed_rows(
            second,
            back_low,
            (0, 1),
            (own_ref, near_ref),
            bias_ref,
            act_s,
            hid_s,
            rows,
            width,
            None,
            None,
        )

    @pl.when(step >= FEED_BLOCKS)
    def _():
        i = step - FEED_BLOCKS
        feed_grads(i, second_t, back_t, act_s, hid_s, ff_grad_ref, up_sum_ref, i, width)

    hook("end")


def feed_last_kernel(
    live_ref,
    residual_ref,
    feed_ref,
    back_second_ref,
    grad_ref,
    mixed_ref,
    out_w_ref,
    ff_ref,
    bias_ref,
    vec_ref,
    ff_near_grad,
    output_ref,
    resid_ref,
    back_mixed_ref,
    ff_grad_ref,
    out_grad_ref,
    small_ref,
    part_ref,
    second_t,
    back_t,
    act_s,
    hid_s,
    out_acc,
    ff_total,
    local,
    *scratch,
):
    step = pl.program_id(0)
    width = residual_ref.shape[1]
    dp, base, y, x, core, mp = place()
    ff = reduces_of(
        (0, 1),
        lambda i: ff_near_grad.at[i, :, :, flip(core)],
        lambda i: ff_total.at[i],
        scratch,
        96,
    )

    def own(i):
        return pltpu.make_async_copy(ff_near_grad.at[i, :, :, core], ff_total.at[i], local.at[i])

    def begin():
        own(1).start()
        own(0).start()
        greet(group_partners())
        ff[1].cores()
        ff[0].cores()
        small_ref[...] = jnp.zeros_like(small_ref)
        second_t[width:, :] = jnp.ones((16, second_t.shape[1]), BF16)

    def chips(slot):
        own(slot).wait()
        ff[slot].chips()

    def end():
        part_ref[...] = ff[0].result() + ff[1].result()
        ff[0].finish()
        ff[1].finish()

    hook = hooks_of(
        {
            (0, "begin"): [begin],
            (1, "begin"): [lambda: chips(1)],
            (3, "begin"): [ff[1].chips_again, lambda: chips(0)],
            (5, "begin"): [ff[1].along],
            (6, "begin"): [ff[0].chips_again],
            (7, "begin"): [ff[0].along],
            (7, "end"): [end],
        },
        step,
    )
    hook("begin")

    @pl.when(step < FEED_BLOCKS)
    def _():
        out_w = out_w_ref[...].reshape(width, width)
        residual = residual_ref[...]
        scaled, inverse = normed(residual)
        gain = vec_ref[1:2, :]
        second = (scaled * gain + vec_ref[2:3, :]).astype(BF16)
        is_live, back = live_back(live_ref, grad_ref, step)
        back_low = back.astype(BF16)
        rows = pl.ds(pl.multiple_of(step * BLOCK, BLOCK), BLOCK)
        second_t[0:width, rows] = second.T
        back_t[:, rows] = back_low.T
        feed, back_second = feed_rows(
            second,
            back_low,
            (2, 3),
            (ff_ref.at[0], ff_ref.at[1]),
            bias_ref,
            act_s,
            hid_s,
            rows,
            width,
            feed_ref[...],
            back_second_ref[...],
        )
        output_ref[...] = jnp.where(is_live, residual + feed + vec_ref[3:4, :], 0.0).astype(BF16)
        small_ref[1:2, :] += jnp.sum(back_second * scaled, axis=0, keepdims=True)
        small_ref[2:3, :] += jnp.sum(back_second, axis=0, keepdims=True)
        small_ref[3:4, :] += jnp.sum(back, axis=0, keepdims=True)
        back_norm = back_second * gain
        back_resid = back + inverse * (
            back_norm
            - jnp.mean(back_norm, axis=-1, keepdims=True)
            - scaled * jnp.mean(back_norm * scaled, axis=-1, keepdims=True)
        )
        small_ref[0:1, :] += jnp.sum(back_resid, axis=0, keepdims=True)
        resid_ref[...] = back_resid
        branch = back_resid.astype(BF16)
        back_mixed_ref[...] = nt(out_w, branch).astype(BF16)
        part = nn(mixed_ref[...], branch)

        @pl.when(step == 0)
        def _():
            out_acc[...] = part

        @pl.when(step > 0)
        def _():
            out_acc[...] += part

        @pl.when(step == FEED_BLOCKS - 1)
        def _():
            out_grad_ref[...] = out_acc[...].astype(BF16).reshape(out_grad_ref.shape)

    @pl.when(step >= FEED_BLOCKS)
    def _():
        i = step - FEED_BLOCKS
        feed_grads(i, second_t, back_t, act_s, hid_s, ff_grad_ref, small_ref, 6 + i, width)

    hook("end")


def feed_first(live, tokens, out_grad, mixed, in_all, ff_near, bias_all, vectors, ff_own):
    rows, width = tokens.shape
    anywhere = pl.BlockSpec(memory_space=pl.ANY)
    one = pl.Buffered(1)
    last = FEED_BLOCKS - 1
    row = pl.BlockSpec((BLOCK, width), lambda s: (jnp.minimum(s, last), 0))
    return pl.pallas_call(
        feed_first_kernel,
        grid=(FEED_BLOCKS + 2,),
        in_specs=[
            pl.BlockSpec(memory_space=pltpu.SMEM),
            row,
            row,
            pl.BlockSpec((width, BLOCK), lambda s: (0, jnp.minimum(s, last))),
            pl.BlockSpec((4, 4, 48, width), lambda s: (0, 0, 3, 0), pipeline_mode=one),
            pl.BlockSpec((8, 192, width), lambda s: (0, 0, 0), pipeline_mode=one),
            pl.BlockSpec((8, 192, width), lambda s: (0, 0, 0), pipeline_mode=one),
            pl.BlockSpec((4, 8, 1024), lambda s: (0, 0, 0), pipeline_mode=one),
            pl.BlockSpec((8, width), lambda s: (0, 0), pipeline_mode=one),
            anywhere,
            anywhere,
        ],
        out_specs=[
            row,
            row,
            row,
            pl.BlockSpec(
                (1, 8, 192, width), lambda s: (jnp.maximum(s - FEED_BLOCKS, 0), 0, 0, 0)
            ),
            pl.BlockSpec((8, width), lambda s: (0, 0)),
            anywhere,
        ],
        out_shape=[
            jax.ShapeDtypeStruct((rows, width), F32),
            jax.ShapeDtypeStruct((rows, width), F32),
            jax.ShapeDtypeStruct((rows, width), F32),
            jax.ShapeDtypeStruct((2, 8, 192, width), BF16),
            jax.ShapeDtypeStruct((8, width), F32),
            jax.ShapeDtypeStruct((2, 8, 192, width), BF16),
        ],
        scratch_shapes=[
            pltpu.VMEM((width + 16, rows), BF16),
            pltpu.VMEM((width, rows), BF16),
            pltpu.VMEM((2, rows, width), BF16),
            pltpu.VMEM((2, rows, width), BF16),
            pltpu.SemaphoreType.DMA((4 * GATHER_KINDS,)),
            pltpu.SemaphoreType.DMA((4 * GATHER_KINDS,)),
        ],
        compiler_params=pltpu.CompilerParams(
            vmem_limit_bytes=62 << 20, collective_id=3, has_side_effects=True
        ),
        cost_estimate=pl.CostEstimate(
            flops=24_000_000_000, bytes_accessed=45_000_000, transcendentals=5_000_000
        ),
        name="feed_first",
    )(live, tokens, out_grad, mixed, in_all, ff_own, ff_near, bias_all, vectors, ff_own, ff_near)


def feed_last(
    live,
    residual,
    feed,
    back_second,
    out_grad,
    mixed,
    in_all,
    ff_late,
    bias_all,
    vectors,
    ff_near_grad,
):
    rows, width = out_grad.shape
    anywhere = pl.BlockSpec(memory_space=pl.ANY)
    one = pl.Buffered(1)
    last = FEED_BLOCKS - 1
    row = pl.BlockSpec((BLOCK, width), lambda s: (jnp.minimum(s, last), 0))
    column = pl.BlockSpec((width, BLOCK), lambda s: (0, jnp.minimum(s, last)))
    return pl.pallas_call(
        feed_last_kernel,
        grid=(FEED_BLOCKS + 2,),
        in_specs=[
            pl.BlockSpec(memory_space=pltpu.SMEM),
            row,
            row,
            row,
            row,
            column,
            pl.BlockSpec((4, 4, 48, width), lambda s: (0, 0, 3, 0), pipeline_mode=one),
            pl.BlockSpec((2, 8, 192, width), lambda s: (0, 0, 0, 0), pipeline_mode=one),
            pl.BlockSpec((4, 8, 1024), lambda s: (0, 0, 0), pipeline_mode=one),
            pl.BlockSpec((8, width), lambda s: (0, 0), pipeline_mode=one),
            anywhere,
        ],
        out_specs=[
            row,
            row,
            column,
            pl.BlockSpec(
                (1, 8, 192, width), lambda s: (jnp.maximum(s - FEED_BLOCKS, 0), 0, 0, 0)
            ),
            pl.BlockSpec((4, 4, 48, width), lambda s: (0, 0, 0, 0)),
            pl.BlockSpec((8, width), lambda s: (0, 0)),
            pl.BlockSpec((192, width), lambda s: (0, 0)),
        ],
        out_shape=[
            jax.ShapeDtypeStruct((rows, width), BF16),
            jax.ShapeDtypeStruct((rows, width), F32),
            jax.ShapeDtypeStruct((width, rows), BF16),
            jax.ShapeDtypeStruct((2, 8, 192, width), BF16),
            jax.ShapeDtypeStruct((4, 4, 48, width), BF16),
            jax.ShapeDtypeStruct((8, width), F32),
            jax.ShapeDtypeStruct((192, width), F32),
        ],
        scratch_shapes=[
            pltpu.VMEM((width + 16, rows), BF16),
            pltpu.VMEM((width, rows), BF16),
            pltpu.VMEM((2, rows, width), BF16),
            pltpu.VMEM((2, rows, width), BF16),
            pltpu.VMEM((width, width), F32),
            pltpu.VMEM((2, 2, 2, 192, width), BF16),
            pltpu.SemaphoreType.DMA((2,)),
        ]
        + reduce_scratch(2, 192, 96, width),
        compiler_params=pltpu.CompilerParams(
            vmem_limit_bytes=62 << 20, collective_id=4, has_side_effects=True
        ),
        cost_estimate=pl.CostEstimate(
            flops=28_000_000_000, bytes_accessed=55_000_000, transcendentals=5_000_000
        ),
        name="feed_last",
    )(
        live,
        residual,
        feed,
        back_second,
        out_grad,
        mixed,
        in_all,
        ff_late,
        bias_all,
        vectors,
        ff_near_grad.reshape(2, 2, 2, 2, 192, width),
    )


def local(
    tokens,
    out_grad,
    live_images,
    first_gain,
    first_shift,
    project_in,
    query_value_bias,
    project_out,
    output_bias,
    second_gain,
    second_shift,
    up_weight,
    up_bias,
    down_weight,
    down_bias,
):
    width = tokens.shape[1]
    own_heads = project_in.shape[2] // HEAD_DIM
    ff_own = jnp.concatenate(
        [up_weight.reshape(8, -1, width), down_weight.reshape(8, -1, width)], axis=1
    )
    pair_bias = query_value_bias.astype(F32).reshape(2, own_heads, HEAD_DIM)
    own_bias = jnp.concatenate([pair_bias[0], jnp.zeros_like(pair_bias[0]), pair_bias[1]], axis=1)
    bias_own = jnp.concatenate(
        [
            jnp.pad(own_bias, ((0, 8 - own_heads), (0, 256 - own_bias.shape[1]))),
            jnp.pad(up_bias.astype(F32)[None], ((0, 7), (0, 0))),
        ],
        axis=1,
    )
    row = lax.broadcasted_iota(jnp.int32, (8, width), 0)
    vectors = jnp.zeros((8, width), F32)
    for i, vector in enumerate(
        (output_bias, second_gain, second_shift, down_bias, first_gain, first_shift)
    ):
        vectors = jnp.where(row == i, vector[None], vectors)
    qkv, mixed, logsum, first, in_all, ff_near, bias_all = attend(
        tokens, vectors, project_in.transpose(1, 2, 0), project_out, ff_own, bias_own
    )
    residual, feed, back_second, near_grad, up_sums, ff_late = feed_first(
        live_images, tokens, out_grad, mixed, in_all, ff_near, bias_all, vectors, ff_own
    )
    output, resid, back_mixed, late_grad, out_grads, feed_small, ff_part = feed_last(
        live_images,
        residual,
        feed,
        back_second,
        out_grad,
        mixed,
        in_all,
        ff_late,
        bias_all,
        vectors,
        near_grad,
    )
    back_qkv, bias_sums, in_part, piece, ff_sum, in_grad = attend_back(
        qkv,
        back_mixed,
        mixed,
        logsum,
        first,
        out_grads,
        ff_part,
        late_grad.reshape(2, 2, 2, 2, 192, width),
    )
    input_grad, small, grad_up, grad_down, grad_in, grad_out = tail(
        back_qkv,
        in_all,
        tokens,
        resid,
        vectors,
        (feed_small, up_sums),
        bias_sums,
        in_part,
        piece,
        ff_sum,
        in_grad,
    )
    grad_in = grad_in.transpose(2, 0, 1)
    pair_sum = small[8, : 4 * IN_ROWS].reshape(own_heads, 3, HEAD_DIM)
    grad_pair = jnp.stack([pair_sum[:, 0].reshape(-1), pair_sum[:, 2].reshape(-1)])
    return (
        output,
        input_grad,
        small[12],
        small[13],
        grad_in,
        grad_pair,
        grad_out,
        small[0],
        small[1],
        small[2],
        grad_up,
        small[4],
        grad_down,
        small[3],
    )


def solution(mesh):
    rows = P(("dp", "mp"), None)
    return jax.shard_map(
        local,
        mesh=mesh,
        in_specs=(
            rows,
            rows,
            rows,
            P(),
            P(),
            P(None, None, "mp"),
            P(None, "mp"),
            P("mp", None),
            P(),
            P(),
            P(),
            P(None, "mp"),
            P("mp"),
            P("mp", None),
            P(),
        ),
        out_specs=(
            rows,
            rows,
            P(),
            P(),
            P(None, None, "mp"),
            P(None, "mp"),
            P("mp", None),
            P(),
            P(),
            P(),
            P(None, "mp"),
            P("mp"),
            P("mp", None),
            P(),
        ),
        check_vma=False,
    )
```

```python
import functools
import math

import jax
import jax.numpy as jnp
from jax import lax
from jax.experimental import pallas as pl
from jax.experimental.pallas import tpu as pltpu
from jax.sharding import PartitionSpec as P

HEAD_DIM = 48
SHORT_LEN = 256
LONG_LEN = 1024
SHORT_SLOTS = 2
LONG_SLOTS = 1
SHORT_ROWS = SHORT_SLOTS * SHORT_LEN
IMAGES = tuple((SHORT_LEN * i, SHORT_LEN) for i in range(SHORT_SLOTS)) + tuple(
    (SHORT_ROWS + LONG_LEN * i, LONG_LEN) for i in range(LONG_SLOTS)
)
SCALE = HEAD_DIM**-0.5
SCALE_LOG2 = SCALE * math.log2(math.e)
BF16 = jnp.bfloat16
F32 = jnp.float32
CHUNK = 512
BACK_CHUNK = 256

epsilon = 1e-05


def layer_norm(rows_in, norm_gain, norm_shift):
    average = jnp.mean(rows_in, axis=-1, keepdims=True)
    centred = rows_in - average
    variance = jnp.mean(centred * centred, axis=-1, keepdims=True)
    return centred * lax.rsqrt(variance + epsilon) * norm_gain + norm_shift


def nn(left, right):
    return lax.dot_general(
        left, right, (((1,), (0,)), ((), ())), preferred_element_type=F32
    )


def nt(left, right):
    return lax.dot_general(
        left, right, (((1,), (1,)), ((), ())), preferred_element_type=F32
    )


def tn(left, right):
    return lax.dot_general(
        left, right, (((0,), (0,)), ((), ())), preferred_element_type=F32
    )


GROUP = 8
MESH = pl.DeviceIdType.MESH
IN_ROWS = 144
HEAD_ROWS = 192


def place():
    dp, mp = lax.axis_index("dp"), lax.axis_index("mp")
    g = lax.rem(dp, GROUP)
    return dp, dp - g, g // 4, lax.rem(g // 2, 2), lax.rem(g, 2), mp


def flip(bit):
    return 1 - bit


class Gather:
    def __init__(self, own, buffers, piece, split, send, recv):
        self.own, self.buffers, self.piece, self.split = own, buffers, piece, split
        self.send, self.recv = send, recv
        self.dp, self.base, self.y, self.x, self.core, self.mp = place()

    def device(self, y, x, core):
        return (self.base + 4 * y + 2 * x + core, self.mp)

    def view(self, ref, y, x, core, part=None):
        view = self.piece(ref, 2 * y + x, core)
        if part is None:
            return view
        rows = view.shape[0]
        return view.at[pl.ds(0, self.split)] if part == 0 else view.at[pl.ds(self.split, rows - self.split)]

    def copy(self, kind, slot):
        y, x, core = self.y, self.x, self.core
        mine = (y, x, core)
        buffer = self.buffers[slot]
        if kind == 0:
            ways = lax.axis_size("mp")
            hop = 1 if slot == 2 else slot
            src = self.view(self.buffers[1] if slot == 2 else self.own, *mine)
            dst = self.view(buffer, *mine)
            device = (self.dp, lax.rem(self.mp + ways - hop, ways))
        else:
            return self.shared(kind, buffer, kind * 4 + slot)
        return self.remote(src, dst, device, kind * 4 + slot)

    def shared(self, kind, buffer, index):
        y, x, core = self.y, self.x, self.core
        mine, near_x, near_y = (y, x, core), (y, flip(x), core), (flip(y), x, core)
        moved, device = {
            1: lambda: (self.view(buffer, *mine), near_x),
            2: lambda: (self.view(buffer, *mine), near_y),
            3: lambda: (self.view(buffer, *near_x, 0), near_y),
            4: lambda: (self.view(buffer, *near_y, 1), near_x),
            5: lambda: (self.view(buffer, *mine), (y, x, flip(core))),
            6: lambda: (self.view(buffer, *near_x), (y, x, flip(core))),
            7: lambda: (self.view(buffer, *near_y), (y, x, flip(core))),
            8: lambda: (self.view(buffer, flip(y), flip(x), core), (y, x, flip(core))),
        }[kind]()
        return self.remote(moved, moved, self.device(*device), index)

    def remote(self, src, dst, device, index):
        return pltpu.make_async_remote_copy(
            src_ref=src,
            dst_ref=dst,
            send_sem=self.send.at[index],
            recv_sem=self.recv.at[index],
            device_id=device,
            device_id_type=MESH,
        )

    def start(self, slot, *kinds):
        for kind in kinds:
            self.copy(kind, slot).start()

    def arrived(self, slot, *kinds):
        for kind in kinds:
            self.copy(kind, slot).wait_recv()

    def along(self, slot):
        self.start(slot, 0)

    def spread(self, slot):
        self.arrived(slot, 0)
        self.start(slot, 1, 2, 5)

    def forward(self, slot):
        self.arrived(slot, 1)
        self.start(slot, 3, 6)
        self.arrived(slot, 2)
        self.start(slot, 4, 7)

    def last(self, slot):
        self.arrived(slot, 3, 4)
        self.start(slot, 8)

    def complete(self, slot):
        self.arrived(slot, 5, 6, 7, 8)

    def finish(self, *slots):
        for slot in slots:
            for kind in range(GATHER_KINDS):
                self.copy(kind, slot).wait_send()


GATHER_KINDS = 9


def in_piece(ref, chip, core):
    return ref.at[chip, :, pl.ds(pl.multiple_of(core * 384, 128), 384)]


def ff_piece(ref, chip, core):
    return ref.at[2 * chip + core]


def greet(partners):
    barrier = pltpu.get_barrier_semaphore()
    for partner in partners:
        pl.semaphore_signal(barrier, inc=1, device_id=partner, device_id_type=MESH)
    pl.semaphore_wait(barrier, len(partners))


def chunks_of(images, size):
    return [
        (start, length, first, min(size, length))
        for start, length in images
        for first in range(start, start + length, min(size, length))
    ]


def attend_head(qkv_ref, mixed_ref, logsum_ref):
    held = {}

    def score(start, length, first, chunk):
        if start not in held:
            whole = slice(start, start + length)
            value_t = qkv_ref[96:144, whole]
            held[start] = (
                qkv_ref[48:96, whole].T,
                jnp.concatenate([value_t, jnp.ones((16, length), BF16)], axis=0),
            )
        return nn(held[start][0], qkv_ref[0:48, first : first + chunk])

    def soften(scores):
        top = jnp.max(scores, axis=0, keepdims=True)
        return top, jnp.exp2((scores - top) * SCALE_LOG2).astype(BF16)

    def mix(item, top, weights):
        start, length, first, chunk = item
        cols = slice(first, first + chunk)
        sums = nn(held[start][1], weights)
        total = sums[48:49]
        mixed_ref[:, cols] = (sums[:48] / total).astype(BF16)
        logsum_ref[:, cols] = top * SCALE_LOG2 + jnp.log2(total)

    items = chunks_of(IMAGES, CHUNK)
    early, late = {0: score(*items[0])}, {}
    for i in range(len(items) + 1):
        if i + 1 < len(items):
            early[i + 1] = score(*items[i + 1])
        if i < len(items):
            late[i] = soften(early.pop(i))
        if i > 0:
            mix(items[i - 1], *late.pop(i - 1))


def hooks_of(table, step):
    def hook(name, head=None):
        for (at, where), actions in table.items():
            if where == name if head is None else isinstance(where, int):

                @pl.when(step == at if head is None else (step == at) & (head == where))
                def _(actions=actions):
                    for action in actions:
                        action()

    return hook


def group_partners(wide=False):
    dp, base, y, x, core, mp = place()
    ways = lax.axis_size("mp")
    return (
        [(dp, lax.rem(mp + k, ways)) for k in (1, 2, 3)]
        + [
            (base + 4 * y + 2 * flip(x) + core, mp),
            (base + 4 * flip(y) + 2 * x + core, mp),
            (base + 4 * y + 2 * x + flip(core), mp),
        ]
        + [(other_bit(dp, bit), mp) for bit in wider_bits() if wide]
    )


def attend_kernel(
    tokens_ref,
    vector_ref,
    in_own,
    out_own,
    ff_own,
    bias_own,
    qkv_ref,
    mixed_ref,
    logsum_ref,
    first_ref,
    in_out,
    ff_near,
    bias_out,
    in_all,
    bias_all,
    in_send,
    in_recv,
    ff_send,
    ff_recv,
    bias_send,
    bias_recv,
    own_sem,
    local_sem,
):
    step = pl.program_id(0)
    dp, base, y, x, core, mp = place()
    ways = lax.axis_size("mp")
    gin = Gather(in_all.at[0], [in_all.at[k] for k in range(4)], in_piece, 96, in_send, in_recv)
    gff = Gather(ff_own, [None, ff_near], ff_piece, 96, ff_send, ff_recv)
    own_copies = [
        pltpu.make_async_copy(
            in_own.at[part, pl.ds(head * 48, 48)] if part < 3 else out_own.at[pl.ds(head * 48, 48)],
            in_all.at[0, head, pl.ds(part * 48, 48)],
            own_sem.at[part * 4 + head],
        )
        for part in range(4)
        for head in range(4)
    ]
    local_bias = pltpu.make_async_copy(bias_own, bias_all.at[0], local_sem.at[1])
    out_in = pltpu.make_async_copy(in_all, in_out, local_sem.at[2])
    out_bias = pltpu.make_async_copy(bias_all, bias_out, local_sem.at[3])

    def bias_copy(slot):
        return pltpu.make_async_remote_copy(
            src_ref=bias_own,
            dst_ref=bias_all.at[slot],
            send_sem=bias_send.at[slot],
            recv_sem=bias_recv.at[slot],
            device_id=(dp, lax.rem(mp + ways - slot, ways)),
            device_id_type=MESH,
        )

    def begin():
        for copy in own_copies:
            copy.start()
        local_bias.start()
        greet(group_partners())
        for copy in own_copies:
            copy.wait()
        gin.along(1)
        gin.along(3)
        for slot in (1, 2, 3):
            bias_copy(slot).start()
        for rows in range(0, tokens_ref.shape[0], BLOCK):
            block = slice(rows, rows + BLOCK)
            first_ref[block] = layer_norm(
                tokens_ref[block].astype(F32), vector_ref[4:5], vector_ref[5:6]
            ).astype(BF16)
        local_bias.wait()

    def end():
        gff.complete(1)
        out_in.wait()
        out_bias.wait()
        for slot in (1, 2, 3):
            bias_copy(slot).wait_send()
        gin.finish(1, 2, 3)
        gff.finish(1)

    hook = hooks_of(
        {
            (0, "begin"): [begin],
            (0, "heads"): [lambda: gin.spread(1), lambda: gin.along(2), lambda: gff.along(1)],
            (0, 2): [lambda: gin.forward(1)],
            (0, 3): [lambda: gin.spread(3)],
            (0, "end"): [lambda: gin.last(1), lambda: gin.spread(2)],
            (1, "begin"): [
                lambda: [bias_copy(slot).wait_recv() for slot in (1, 2, 3)],
                lambda: gin.complete(1),
            ],
            (1, "heads"): [lambda: gin.forward(3)],
            (1, 2): [lambda: gin.last(3), lambda: gin.forward(2), lambda: gff.spread(1)],
            (1, "end"): [lambda: gin.last(2)],
            (2, "begin"): [lambda: gin.complete(3)],
            (2, 2): [lambda: gff.forward(1)],
            (2, "end"): [lambda: gff.last(1)],
            (3, "begin"): [lambda: gin.complete(2), out_in.start, out_bias.start],
            (3, "end"): [end],
        },
        step,
    )
    slot = slot_order(step)
    hook("begin")
    bias_t = bias_all[slot, :, 0:256].T
    for part in range(4):
        product = nt(in_all[slot, part, :IN_ROWS], first_ref[...])
        qkv_ref[part * IN_ROWS : (part + 1) * IN_ROWS, :] = (
            product + bias_t[:IN_ROWS, part : part + 1]
        ).astype(BF16)
    hook("heads")

    def one_head(head, carry):
        hook(None, head)
        attend_head(
            qkv_ref.at[pl.ds(pl.multiple_of(head * IN_ROWS, 16), IN_ROWS)],
            mixed_ref.at[pl.ds(pl.multiple_of(head * 48, 16), 48)],
            logsum_ref.at[head],
        )
        return carry

    lax.fori_loop(0, 4, one_head, 0)
    hook("end")


def slot_order(turn):
    return turn + (turn // 2) * (1 - 2 * (turn % 2))


def attend(tokens, vectors, in_own, out_own, ff_own, bias_own):
    rows, width = tokens.shape
    heads = 16
    anywhere = pl.BlockSpec(memory_space=pl.ANY)
    dma = pltpu.SemaphoreType.DMA
    return pl.pallas_call(
        attend_kernel,
        grid=(4,),
        in_specs=[
            pl.BlockSpec((rows, width), lambda s: (0, 0), pipeline_mode=pl.Buffered(1)),
            pl.BlockSpec((8, width), lambda s: (0, 0)),
            anywhere,
            anywhere,
            anywhere,
            anywhere,
        ],
        out_specs=[
            pl.BlockSpec((4 * IN_ROWS, rows), lambda s: (slot_order(s), 0)),
            pl.BlockSpec((4 * 48, rows), lambda s: (slot_order(s), 0)),
            pl.BlockSpec((4, 1, rows), lambda s: (slot_order(s), 0, 0)),
            pl.BlockSpec((rows, width), lambda s: (0, 0)),
            anywhere,
            anywhere,
            anywhere,
        ],
        out_shape=[
            jax.ShapeDtypeStruct((heads * IN_ROWS, rows), BF16),
            jax.ShapeDtypeStruct((heads * 48, rows), BF16),
            jax.ShapeDtypeStruct((heads, 1, rows), F32),
            jax.ShapeDtypeStruct((rows, width), BF16),
            jax.ShapeDtypeStruct((4, 4, HEAD_ROWS, width), BF16),
            jax.ShapeDtypeStruct((8, 192, width), BF16),
            jax.ShapeDtypeStruct((4, 8, 1024), F32),
        ],
        scratch_shapes=[
            pltpu.VMEM((4, 4, HEAD_ROWS, width), BF16),
            pltpu.VMEM((4, 8, 1024), F32),
            dma((4 * GATHER_KINDS,)),
            dma((4 * GATHER_KINDS,)),
            dma((4 * GATHER_KINDS,)),
            dma((4 * GATHER_KINDS,)),
            dma((4,)),
            dma((4,)),
            dma((16,)),
            dma((4,)),
        ],
        compiler_params=pltpu.CompilerParams(
            vmem_limit_bytes=62 << 20, collective_id=0, has_side_effects=True
        ),
        cost_estimate=pl.CostEstimate(
            flops=30_000_000_000, bytes_accessed=30_000_000, transcendentals=19_000_000
        ),
        name="attend",
    )(tokens, vectors, in_own, out_own, ff_own, bias_own)


class Reduce:
    def __init__(self, slot, other, total, got, split, send, recv):
        self.slot, self.other, self.total, self.got, self.split = slot, other, total, got, split
        self.send, self.recv = send, recv
        self.dp, self.base, self.y, self.x, self.core, self.mp = place()

    def copy(self, kind):
        y, x, core = self.y, self.x, self.core
        first, late = pl.ds(0, self.split), pl.ds(self.split, self.total.shape[2] - self.split)
        got = self.got
        near = lambda y, x, core: (self.base + 4 * y + 2 * x + core, self.mp)
        to_x, to_y = near(y, flip(x), core), near(flip(y), x, core)
        src, dst, device = {
            0: lambda: (self.other, got[0], near(y, x, flip(core))),
            1: lambda: (self.total.at[:, flip(x), first], got[1], to_x),
            2: lambda: (self.total.at[flip(y), :, late], got[2], to_y),
            3: lambda: (self.total.at[flip(y), x, first], got[3], to_y),
            4: lambda: (self.total.at[y, flip(x), late], got[4], to_x),
            5: lambda: (
                self.total.at[y, x],
                got[5],
                (self.dp, lax.rem(self.mp + self.slot, lax.axis_size("mp"))),
            ),
        }[kind]()
        index = kind * 4 + self.slot
        return pltpu.make_async_remote_copy(
            src_ref=src,
            dst_ref=dst,
            send_sem=self.send.at[index],
            recv_sem=self.recv.at[index],
            device_id=device,
            device_id_type=MESH,
        )

    def cores(self):
        self.copy(0).start()

    def chips(self):
        self.copy(0).wait_recv()
        for y in range(2):
            for x in range(2):
                self.total[y, x] = add(self.total[y, x], self.got[0][y, x])
        self.copy(1).start()
        self.copy(2).start()

    def chips_again(self):
        x, y, split = self.x, self.y, self.split
        self.copy(1).wait_recv()
        for i in range(2):
            self.total[i, x, :split] = add(self.total[i, x, :split], self.got[1][i])
        self.copy(2).wait_recv()
        for i in range(2):
            self.total[y, i, split:] = add(self.total[y, i, split:], self.got[2][i])
        self.copy(3).start()
        self.copy(4).start()

    def settle(self):
        x, y, split = self.x, self.y, self.split
        self.copy(3).wait_recv()
        self.total[y, x, :split] = add(self.total[y, x, :split], self.got[3][...])
        self.copy(4).wait_recv()
        self.total[y, x, split:] = add(self.total[y, x, split:], self.got[4][...])

    def along(self):
        self.settle()
        if self.slot:
            self.copy(5).start()

    def finish(self, kinds=6):
        for kind in range(kinds if self.slot else 5):
            self.copy(kind).wait_send()

    def result(self):
        if self.slot:
            self.copy(5).wait_recv()
            return self.got[5][...].astype(F32)
        return self.total[self.y, self.x].astype(F32)


REDUCE_KINDS = 6


def add(left, right):
    return (left.astype(F32) + right.astype(F32)).astype(BF16)


def other_bit(index, bit):
    return index + bit * (1 - 2 * lax.rem(index // bit, 2))


def wider_bits():
    bits, bit = [], GROUP
    while bit < lax.axis_size("dp"):
        bits.append(bit)
        bit *= 2
    return bits


class Share:
    def __init__(self, pieces, split, send, recv):
        self.inner = Gather(None, None, ff_piece, split, send, recv)
        self.pieces = pieces

    def copy(self, kind):
        return self.inner.shared(kind, self.pieces, kind)

    def start(self, *kinds):
        for kind in kinds:
            self.copy(kind).start()

    def arrived(self, *kinds):
        for kind in kinds:
            self.copy(kind).wait_recv()

    def spread(self):
        self.start(1, 2, 5)

    def forward(self):
        self.arrived(1)
        self.start(3, 6)
        self.arrived(2)
        self.start(4, 7)

    def last(self):
        self.arrived(3, 4)
        self.start(8)

    def finish(self):
        self.arrived(5, 6, 7, 8)
        for kind in range(1, 9):
            self.copy(kind).wait_send()


class Wide:
    def __init__(self, held, send, recv):
        self.held, self.send, self.recv = held, send, recv

    def copy(self, i, bit):
        dp, mp = lax.axis_index("dp"), lax.axis_index("mp")
        return pltpu.make_async_remote_copy(
            src_ref=self.held.at[2 * i],
            dst_ref=self.held.at[2 * i + 1],
            send_sem=self.send.at[i],
            recv_sem=self.recv.at[i],
            device_id=(other_bit(dp, bit), mp),
            device_id_type=MESH,
        )

    def sum(self, total):
        for i, bit in enumerate(wider_bits()):
            self.held[2 * i] = total.astype(BF16)
            self.copy(i, bit).start()
            self.copy(i, bit).wait()
            total = total + self.held[2 * i + 1].astype(F32)
        return total


def reduce_scratch(slots, rows, split, width):
    dma = pltpu.SemaphoreType.DMA
    late = rows - split
    return [
        pltpu.VMEM((slots, 2, 2, rows, width), BF16),
        pltpu.VMEM((slots, 2, split, width), BF16),
        pltpu.VMEM((slots, 2, late, width), BF16),
        pltpu.VMEM((slots, split, width), BF16),
        pltpu.VMEM((slots, late, width), BF16),
        pltpu.VMEM((slots, rows, width), BF16),
        dma((4 * REDUCE_KINDS,)),
        dma((4 * REDUCE_KINDS,)),
    ]


REDUCE_REFS = 8


def reduces_of(slots, other, total, scratch, split):
    *got, send, recv = scratch
    return {
        slot: Reduce(slot, other(i), total(i), [ref.at[i] for ref in got], split, send, recv)
        for i, slot in enumerate(slots)
    }


def share_scratch(rows, width):
    dma = pltpu.SemaphoreType.DMA
    wide = max(len(wider_bits()), 1)
    return [
        pltpu.VMEM((8, rows, width), BF16),
        pltpu.VMEM((2 * wide, rows, width), BF16),
        dma((GATHER_KINDS,)),
        dma((GATHER_KINDS,)),
        dma((wide,)),
        dma((wide,)),
    ]


SHARE_REFS = 6


def attend_back_head(qkv_ref, back_ref, mixed_ref, logsum_ref, out_ref, held):
    rows = {}

    def score(start, length, first, chunk):
        if start not in rows:
            whole = slice(start, start + length)
            key_t = qkv_ref[48:96, whole]
            rows[start] = (key_t, key_t.T, qkv_ref[96:144, whole].T)
        cols = slice(first, first + chunk)
        return (
            nn(rows[start][1], qkv_ref[0:48, cols]),
            nn(rows[start][2], back_ref[:, cols]),
        )

    def soften(item, scores, back_probs):
        cols = slice(item[2], item[2] + item[3])
        inner = jnp.sum(
            back_ref[:, cols].astype(F32) * mixed_ref[:, cols].astype(F32), axis=0, keepdims=True
        )
        probs = jnp.exp2(scores * SCALE_LOG2 - logsum_ref[:, cols])
        return probs.astype(BF16), (probs * (back_probs - inner)).astype(BF16)

    def pull(item, probs, back_scores):
        start, length, first, chunk = item
        cols, whole = slice(first, first + chunk), slice(start, start + length)
        query_t, back_t = qkv_ref[0:48, cols], back_ref[:, cols]
        out_ref[0:48, cols] = (nn(rows[start][0], back_scores) * SCALE).astype(BF16)
        back_key = nt(query_t, back_scores)
        back_value = nt(back_t, probs)
        if first > start:
            back_key = back_key + held[0:48, 0:length]
            back_value = back_value + held[48:96, 0:length]
        if first + chunk < start + length:
            held[0:48, 0:length] = back_key
            held[48:96, 0:length] = back_value
        else:
            out_ref[48:96, whole] = (back_key * SCALE).astype(BF16)
            out_ref[96:144, whole] = back_value.astype(BF16)

    items = chunks_of(IMAGES, BACK_CHUNK)
    early = {0: score(*items[0])}
    for i in range(len(items)):
        if i + 1 < len(items):
            early[i + 1] = score(*items[i + 1])
        pull(items[i], *soften(items[i], *early.pop(i)))


def attend_back_kernel(
    qkv_ref,
    back_ref,
    mixed_ref,
    logsum_ref,
    first_ref,
    out_grad_ref,
    ff_part_ref,
    in_ref,
    tokens_ref,
    resid_ref,
    vector_ref,
    feed_small_ref,
    up_sums_ref,
    ff_grad,
    input_ref,
    small_ref,
    up_out,
    down_out,
    in_out,
    out_out,
    held,
    ff_total,
    grads,
    back_qkv,
    turned,
    sums,
    sum_got,
    wide_got,
    along_got,
    sum_send,
    sum_recv,
    along_send,
    along_recv,
    local,
    *scratch,
    blocks,
):
    step = pl.program_id(0)
    width = tokens_ref.shape[1]
    dp, base, y, x, core, mp = place()
    ways = lax.axis_size("mp")
    ff_scratch, scratch = scratch[:REDUCE_REFS], scratch[REDUCE_REFS:]
    in_scratch, scratch = scratch[:REDUCE_REFS], scratch[REDUCE_REFS:]
    ff_final, ff_wide, *ff_sems = scratch[:SHARE_REFS]
    in_final, in_wide, *in_sems = scratch[SHARE_REFS:]
    ff = reduces_of(
        (2, 3),
        lambda i: ff_grad.at[i, :, :, flip(core)],
        lambda i: ff_total.at[i],
        ff_scratch,
        96,
    )
    ins = reduces_of(
        (0, 1, 2, 3),
        lambda i: grads.at[i, :, :, flip(core)],
        lambda i: grads.at[i, :, :, core],
        in_scratch,
        48,
    )
    ff_share = Share(ff_final, 96, *ff_sems[:2])
    in_share = Share(in_final, 48, *in_sems[:2])
    me = 4 * y + 2 * x + core

    def own(i):
        return pltpu.make_async_copy(ff_grad.at[i, :, :, core], ff_total.at[i], local.at[i])

    up_written = pltpu.make_async_copy(ff_final.at[:, pl.ds(0, 96)], up_out, local.at[2])
    down_written = pltpu.make_async_copy(turned, down_out, local.at[3])

    def in_written():
        copies = []
        for head in range(4):
            rows = pl.ds(48 * head, 48)
            for part in range(4):
                src = in_final.at[2 * head + part // 2, pl.ds(48 * (part % 2), 48)]
                dst = in_out.at[part, rows] if part < 3 else out_out.at[rows]
                copies.append(pltpu.make_async_copy(src, dst, local.at[4 + 4 * head + part]))
        return copies

    def begin():
        own(0).start()
        own(1).start()
        greet(every_partner())
        ff[2].cores()
        ff[3].cores()
        sums[0] = jnp.zeros_like(sums[0])
        sums[0, 0:8, :] = feed_small_ref[...]
        sums[0, 4:6, :] = up_sums_ref[0:2, :]

    def chips(slot):
        own(slot - 2).wait()
        ff[slot].chips()

    def finish_ff():
        total = ff_part_ref[...] + ff[2].result() + ff[3].result()
        ff_final[me] = Wide(ff_wide, *ff_sems[2:]).sum(total).astype(BF16)
        ff_share.spread()

    def write_ff():
        ff_share.finish()
        up_written.start()
        turned[...] = ff_final[:, 96:].reshape(width, width).T
        down_written.start()

    def finish_in():
        ins[0].along()
        total = ins[0].result() + ins[1].result() + ins[2].result() + ins[3].result()
        in_final[me] = Wide(in_wide, *in_sems[2:]).sum(total).astype(BF16)
        in_share.spread()

    wide = wider_bits()
    near = range(1, GROUP)

    def near_copy(k):
        return pltpu.make_async_remote_copy(
            src_ref=sums.at[0],
            dst_ref=sum_got.at[k - 1],
            send_sem=sum_send.at[k - 1],
            recv_sem=sum_recv.at[k - 1],
            device_id=(base + near_index(y, x, core, k), mp),
            device_id_type=MESH,
        )

    def wide_copy(i):
        return pltpu.make_async_remote_copy(
            src_ref=sums.at[i + 1],
            dst_ref=wide_got.at[i],
            send_sem=sum_send.at[GROUP - 1 + i],
            recv_sem=sum_recv.at[GROUP - 1 + i],
            device_id=(other_bit(dp, wide[i]), mp),
            device_id_type=MESH,
        )

    def along_copy(slot):
        return pltpu.make_async_remote_copy(
            src_ref=sums.at[len(wide) + 1],
            dst_ref=along_got.at[slot - 1],
            send_sem=along_send.at[slot - 1],
            recv_sem=along_recv.at[slot - 1],
            device_id=(dp, lax.rem(mp + slot, ways)),
            device_id_type=MESH,
        )

    def end():
        for k in near:
            near_copy(k).start()
        in_share.forward()
        result = sums[0]
        for k in near:
            near_copy(k).wait_recv()
            result = result + sum_got[k - 1]
        sums[1] = result
        for i in range(len(wide)):
            wide_copy(i).start()
            wide_copy(i).wait_recv()
            sums[i + 2] = sums[i + 1] + wide_got[i]
        for slot in (1, 2, 3):
            along_copy(slot).start()
        in_share.last()
        in_share.finish()
        for copy in in_written():
            copy.start()
        small_ref[...] = sums[len(wide) + 1]
        for slot in (1, 2, 3):
            along_copy(slot).wait_recv()
            more = along_got[slot - 1]
            small_ref[0:4, :] += more[0:4]
            small_ref[12:14, :] += more[12:14]
            small_ref[4:5, :] += more[4 + slot : 5 + slot]
            small_ref[8:9, :] += more[8 + slot : 9 + slot]
        for k in near:
            near_copy(k).wait_send()
        for i in range(len(wide)):
            wide_copy(i).wait_send()
        for slot in (1, 2, 3):
            along_copy(slot).wait_send()
        for reduce in [*ff.values(), *ins.values()]:
            reduce.finish()
        up_written.wait()
        down_written.wait()
        for copy in in_written():
            copy.wait()

    hook = hooks_of(
        {
            (0, 0): [begin],
            (0, 1): [lambda: chips(2)],
            (0, 3): [ff[2].chips_again, lambda: chips(3)],
            (1, 0): [ins[2].cores],
            (1, 2): [ff[2].along],
            (1, 3): [ff[3].chips_again, ins[2].chips],
            (2, 0): [ff[3].along, ins[1].cores],
            (2, 1): [ins[2].chips_again, ins[1].chips],
            (2, 3): [ins[2].along, ins[1].chips_again],
            (3, 0): [finish_ff, ins[1].along, ins[3].cores],
            (3, 1): [ins[3].chips],
            (3, 3): [ff_share.forward, ins[3].chips_again],
            (4, "begin"): [ins[0].cores, ins[3].along],
            (5, "begin"): [ins[0].chips, ff_share.last],
            (6, "begin"): [write_ff],
            (6, "end"): [ins[0].chips_again],
            (7, "end"): [finish_in],
            (9, "end"): [end],
        },
        step,
    )

    @pl.when(step < 4)
    def _():
        slot = back_order(step)

        def one_head(head, carry):
            hook(None, head)
            of_head = pl.ds(pl.multiple_of(head * IN_ROWS, 16), IN_ROWS)
            own_head = pl.ds(pl.multiple_of(head * 48, 16), 48)
            out_rows = pl.ds(pl.multiple_of((4 * slot + head) * IN_ROWS, 16), IN_ROWS)
            attend_back_head(
                qkv_ref.at[of_head],
                back_ref.at[own_head],
                mixed_ref.at[own_head],
                logsum_ref.at[head],
                back_qkv.at[out_rows],
                held,
            )
            return carry

        lax.fori_loop(0, 4, one_head, 0)

        for head in range(4):
            rows = back_qkv[pl.ds(pl.multiple_of((4 * slot + head) * IN_ROWS, 16), IN_ROWS), :]
            grad = nn(rows, first_ref[...]).astype(BF16)
            grads[slot, head // 2, head % 2, 0] = grad[:96]
            grads[slot, head // 2, head % 2, 1, 0:48] = grad[96:]
            grads[slot, head // 2, head % 2, 1, 48:96] = out_grad_ref[0, head]
        rows = back_qkv[pl.ds(pl.multiple_of(4 * slot * IN_ROWS, 16), 4 * IN_ROWS), :]
        row_sums = nt(jnp.ones((8, rows.shape[1]), BF16), rows)
        sums[0, pl.ds(8 + slot, 1), 0 : 4 * IN_ROWS] = row_sums[0:1]

    @pl.when(step >= 4)
    def _():
        hook("begin")
        inputs = tokens_ref[...].astype(F32)
        scaled, inverse = normed(inputs)
        cols = pl.ds(pl.multiple_of((step - 4) * BLOCK, BLOCK), BLOCK)
        back_first = None
        for slot in range(4):
            weight = in_ref[slot, :, :IN_ROWS].reshape(4 * IN_ROWS, width)
            part = tn(back_qkv[slot * 4 * IN_ROWS : (slot + 1) * 4 * IN_ROWS, cols], weight)
            back_first = part if slot == 0 else back_first + part
        sums[0, 12:13, :] += jnp.sum(back_first * scaled, axis=0, keepdims=True)
        sums[0, 13:14, :] += jnp.sum(back_first, axis=0, keepdims=True)
        back_norm = back_first * vector_ref[4:5, :]
        input_ref[...] = resid_ref[...] + inverse * (
            back_norm
            - jnp.mean(back_norm, axis=-1, keepdims=True)
            - scaled * jnp.mean(back_norm * scaled, axis=-1, keepdims=True)
        )
        hook("end")


def near_index(y, x, core, k):
    y = flip(y) if k & 4 else y
    x = flip(x) if k & 2 else x
    core = flip(core) if k & 1 else core
    return 4 * y + 2 * x + core


def every_partner():
    dp, base, y, x, core, mp = place()
    ways = lax.axis_size("mp")
    return (
        [(dp, lax.rem(mp + k, ways)) for k in (1, 2, 3)]
        + [(base + near_index(y, x, core, k), mp) for k in range(1, GROUP)]
        + [(other_bit(dp, bit), mp) for bit in wider_bits()]
    )


def back_order(turn):
    turn = jnp.minimum(turn, 3)
    return 2 - turn + (turn // 2) * (3 - 2 * (turn // 3))


BLOCK = 256


def attend_back(
    qkv,
    back_mixed,
    mixed,
    logsum,
    first,
    out_grad,
    ff_part,
    in_all,
    tokens,
    resid,
    vectors,
    feed_small,
    up_sums,
    ff_grad,
):
    rows, width = first.shape
    blocks = rows // BLOCK
    bits = len(wider_bits())
    anywhere = pl.BlockSpec(memory_space=pl.ANY)
    one = pl.Buffered(1)
    dma = pltpu.SemaphoreType.DMA
    row = pl.BlockSpec((BLOCK, width), lambda s: (jnp.maximum(s - 4, 0), 0))
    small = pl.BlockSpec((8, width), lambda s: (0, 0))
    return pl.pallas_call(
        functools.partial(attend_back_kernel, blocks=blocks),
        grid=(4 + blocks,),
        in_specs=[
            pl.BlockSpec((4 * IN_ROWS, rows), lambda s: (back_order(s), 0)),
            pl.BlockSpec((4 * 48, rows), lambda s: (back_order(s), 0)),
            pl.BlockSpec((4 * 48, rows), lambda s: (back_order(s), 0)),
            pl.BlockSpec((4, 1, rows), lambda s: (back_order(s), 0, 0)),
            pl.BlockSpec((rows, width), lambda s: (0, 0), pipeline_mode=one),
            pl.BlockSpec((1, 4, 48, width), lambda s: (back_order(s), 0, 0, 0)),
            pl.BlockSpec((192, width), lambda s: (0, 0), pipeline_mode=one),
            pl.BlockSpec((4, 4, HEAD_ROWS, width), lambda s: (0, 0, 0, 0), pipeline_mode=one),
            row,
            row,
            small,
            small,
            small,
            anywhere,
        ],
        out_specs=[
            row,
            pl.BlockSpec((16, width), lambda s: (0, 0)),
            anywhere,
            anywhere,
            anywhere,
            anywhere,
        ],
        out_shape=[
            jax.ShapeDtypeStruct((rows, width), F32),
            jax.ShapeDtypeStruct((16, width), F32),
            jax.ShapeDtypeStruct((8, 96, width), BF16),
            jax.ShapeDtypeStruct((width, width), BF16),
            jax.ShapeDtypeStruct((3, 192, width), BF16),
            jax.ShapeDtypeStruct((192, width), BF16),
        ],
        scratch_shapes=[
            pltpu.VMEM((96, LONG_LEN), F32),
            pltpu.VMEM((2, 2, 2, 192, width), BF16),
            pltpu.VMEM((4, 2, 2, 2, 96, width), BF16),
            pltpu.VMEM((16 * IN_ROWS, rows), BF16),
            pltpu.VMEM((width, width), BF16),
            pltpu.VMEM((bits + 2, 16, width), F32),
            pltpu.VMEM((GROUP - 1, 16, width), F32),
            pltpu.VMEM((max(bits, 1), 16, width), F32),
            pltpu.VMEM((3, 16, width), F32),
            dma((GROUP - 1 + bits,)),
            dma((GROUP - 1 + bits,)),
            dma((3,)),
            dma((3,)),
            dma((20,)),
        ]
        + reduce_scratch(2, 192, 96, width)
        + reduce_scratch(4, 96, 48, width)
        + share_scratch(192, width)
        + share_scratch(96, width),
        compiler_params=pltpu.CompilerParams(
            vmem_limit_bytes=62 << 20, collective_id=1, has_side_effects=True
        ),
        cost_estimate=pl.CostEstimate(
            flops=50_000_000_000, bytes_accessed=50_000_000, transcendentals=19_000_000
        ),
        name="attend_back",
    )(
        qkv,
        back_mixed,
        mixed,
        logsum,
        first,
        out_grad,
        ff_part,
        in_all,
        tokens,
        resid,
        vectors,
        feed_small,
        up_sums,
        ff_grad,
    )


FEED_BLOCKS = 6


def feed_rows(
    second, back_low, slots, ff_refs, bias_ref, act_s, hid_s, rows, width, feed, back_second
):
    for i, slot in enumerate(slots):
        up = ff_refs[i][:, 0:96, :].reshape(width, width)
        down = ff_refs[i][:, 96:192, :].reshape(width, width)
        hidden = nn(second, up) + bias_ref[slot, 0:1, 256:]
        half = 0.5 + 0.5 * lax.erf(hidden * (0.5**0.5))
        act = (hidden * half).astype(BF16)
        slope = half + hidden * (jnp.exp(hidden * hidden * -0.5) * (1.0 / math.sqrt(2 * math.pi)))
        back_hid = (nt(back_low, down) * slope).astype(BF16)
        act_s[i, rows, :] = act
        hid_s[i, rows, :] = back_hid
        fed, pulled = nn(act, down), nt(back_hid, up)
        feed = fed if feed is None else feed + fed
        back_second = pulled if back_second is None else back_second + pulled
    return feed, back_second


def normed(rows_in):
    average = jnp.mean(rows_in, axis=-1, keepdims=True)
    centred = rows_in - average
    inverse = lax.rsqrt(jnp.mean(centred * centred, axis=-1, keepdims=True) + epsilon)
    return centred * inverse, inverse


def live_back(live_ref, grad_ref, step):
    row = step * BLOCK + lax.broadcasted_iota(jnp.int32, (BLOCK, 1), 0)
    limit = jnp.where(
        row < SHORT_ROWS, live_ref[0, 0] * SHORT_LEN, SHORT_ROWS + live_ref[0, 1] * LONG_LEN
    )
    is_live = row < limit
    return is_live, jnp.where(is_live, grad_ref[...].astype(F32), 0.0)


def feed_grads(i, second_t, back_t, act_s, hid_s, ff_grad_ref, up_sum_ref, row, width):
    up = nn(second_t[...], hid_s[i])
    ff_grad_ref[0, :, 0:96, :] = up[:width].astype(BF16).reshape(8, 96, width)
    up_sum_ref[pl.ds(row, 1), :] = up[width : width + 1]
    down = nn(back_t[...], act_s[i])
    ff_grad_ref[0, :, 96:192, :] = down.astype(BF16).reshape(8, 96, width)


def feed_first_kernel(
    live_ref,
    tokens_ref,
    grad_ref,
    mixed_ref,
    out_w_ref,
    own_ref,
    near_ref,
    bias_ref,
    vec_ref,
    ff_own,
    ff_near,
    residual_ref,
    feed_ref,
    back_second_ref,
    ff_grad_ref,
    up_sum_ref,
    ff_late,
    second_t,
    back_t,
    act_s,
    hid_s,
    send,
    recv,
):
    step = pl.program_id(0)
    width = tokens_ref.shape[1]
    late = [None, ff_near, ff_late.at[0], ff_late.at[1]]
    gff = Gather(ff_own, late, ff_piece, 96, send, recv)

    def begin():
        greet(group_partners())
        gff.along(3)
        gff.along(2)
        up_sum_ref[...] = jnp.zeros_like(up_sum_ref)
        second_t[width:, :] = jnp.ones((16, second_t.shape[1]), BF16)

    def end():
        gff.complete(3)
        gff.complete(2)
        gff.finish(2, 3)

    hook = hooks_of(
        {
            (0, "begin"): [begin],
            (2, "begin"): [lambda: gff.spread(3)],
            (3, "begin"): [lambda: gff.spread(2)],
            (5, "begin"): [lambda: gff.forward(3)],
            (6, "begin"): [lambda: gff.last(3), lambda: gff.forward(2)],
            (7, "begin"): [lambda: gff.last(2)],
            (7, "end"): [end],
        },
        step,
    )
    hook("begin")

    @pl.when(step < FEED_BLOCKS)
    def _():
        out_w = out_w_ref[...].reshape(width, width)
        residual = tokens_ref[...].astype(F32) + tn(mixed_ref[...], out_w) + vec_ref[0:1, :]
        residual_ref[...] = residual
        scaled, _ = normed(residual)
        second = (scaled * vec_ref[1:2, :] + vec_ref[2:3, :]).astype(BF16)
        _, back = live_back(live_ref, grad_ref, step)
        back_low = back.astype(BF16)
        rows = pl.ds(pl.multiple_of(step * BLOCK, BLOCK), BLOCK)
        second_t[0:width, rows] = second.T
        back_t[:, rows] = back_low.T
        feed_ref[...], back_second_ref[...] = feed_rows(
            second,
            back_low,
            (0, 1),
            (own_ref, near_ref),
            bias_ref,
            act_s,
            hid_s,
            rows,
            width,
            None,
            None,
        )

    @pl.when(step >= FEED_BLOCKS)
    def _():
        i = step - FEED_BLOCKS
        feed_grads(i, second_t, back_t, act_s, hid_s, ff_grad_ref, up_sum_ref, i, width)

    hook("end")


def feed_last_kernel(
    live_ref,
    residual_ref,
    feed_ref,
    back_second_ref,
    grad_ref,
    mixed_ref,
    out_w_ref,
    ff_ref,
    bias_ref,
    vec_ref,
    ff_near_grad,
    output_ref,
    resid_ref,
    back_mixed_ref,
    ff_grad_ref,
    out_grad_ref,
    small_ref,
    part_ref,
    second_t,
    back_t,
    act_s,
    hid_s,
    out_acc,
    ff_total,
    local,
    *scratch,
):
    step = pl.program_id(0)
    width = residual_ref.shape[1]
    dp, base, y, x, core, mp = place()
    ff = reduces_of(
        (0, 1),
        lambda i: ff_near_grad.at[i, :, :, flip(core)],
        lambda i: ff_total.at[i],
        scratch,
        96,
    )

    def own(i):
        return pltpu.make_async_copy(ff_near_grad.at[i, :, :, core], ff_total.at[i], local.at[i])

    def begin():
        own(1).start()
        own(0).start()
        greet(group_partners())
        ff[1].cores()
        ff[0].cores()
        small_ref[...] = jnp.zeros_like(small_ref)
        second_t[width:, :] = jnp.ones((16, second_t.shape[1]), BF16)

    def chips(slot):
        own(slot).wait()
        ff[slot].chips()

    def end():
        part_ref[...] = ff[0].result() + ff[1].result()
        ff[0].finish()
        ff[1].finish()

    hook = hooks_of(
        {
            (0, "begin"): [begin],
            (1, "begin"): [lambda: chips(1)],
            (3, "begin"): [ff[1].chips_again, lambda: chips(0)],
            (5, "begin"): [ff[1].along],
            (6, "begin"): [ff[0].chips_again],
            (7, "begin"): [ff[0].along],
            (7, "end"): [end],
        },
        step,
    )
    hook("begin")

    @pl.when(step < FEED_BLOCKS)
    def _():
        out_w = out_w_ref[...].reshape(width, width)
        residual = residual_ref[...]
        scaled, inverse = normed(residual)
        gain = vec_ref[1:2, :]
        second = (scaled * gain + vec_ref[2:3, :]).astype(BF16)
        is_live, back = live_back(live_ref, grad_ref, step)
        back_low = back.astype(BF16)
        rows = pl.ds(pl.multiple_of(step * BLOCK, BLOCK), BLOCK)
        second_t[0:width, rows] = second.T
        back_t[:, rows] = back_low.T
        feed, back_second = feed_rows(
            second,
            back_low,
            (2, 3),
            (ff_ref.at[0], ff_ref.at[1]),
            bias_ref,
            act_s,
            hid_s,
            rows,
            width,
            feed_ref[...],
            back_second_ref[...],
        )
        output_ref[...] = jnp.where(is_live, residual + feed + vec_ref[3:4, :], 0.0).astype(BF16)
        small_ref[1:2, :] += jnp.sum(back_second * scaled, axis=0, keepdims=True)
        small_ref[2:3, :] += jnp.sum(back_second, axis=0, keepdims=True)
        small_ref[3:4, :] += jnp.sum(back, axis=0, keepdims=True)
        back_norm = back_second * gain
        back_resid = back + inverse * (
            back_norm
            - jnp.mean(back_norm, axis=-1, keepdims=True)
            - scaled * jnp.mean(back_norm * scaled, axis=-1, keepdims=True)
        )
        small_ref[0:1, :] += jnp.sum(back_resid, axis=0, keepdims=True)
        resid_ref[...] = back_resid
        branch = back_resid.astype(BF16)
        back_mixed_ref[...] = nt(out_w, branch).astype(BF16)
        part = nn(mixed_ref[...], branch)

        @pl.when(step == 0)
        def _():
            out_acc[...] = part

        @pl.when(step > 0)
        def _():
            out_acc[...] += part

        @pl.when(step == FEED_BLOCKS - 1)
        def _():
            out_grad_ref[...] = out_acc[...].astype(BF16).reshape(out_grad_ref.shape)

    @pl.when(step >= FEED_BLOCKS)
    def _():
        i = step - FEED_BLOCKS
        feed_grads(i, second_t, back_t, act_s, hid_s, ff_grad_ref, small_ref, 6 + i, width)

    hook("end")


def feed_first(live, tokens, out_grad, mixed, in_all, ff_near, bias_all, vectors, ff_own):
    rows, width = tokens.shape
    anywhere = pl.BlockSpec(memory_space=pl.ANY)
    one = pl.Buffered(1)
    last = FEED_BLOCKS - 1
    row = pl.BlockSpec((BLOCK, width), lambda s: (jnp.minimum(s, last), 0))
    return pl.pallas_call(
        feed_first_kernel,
        grid=(FEED_BLOCKS + 2,),
        in_specs=[
            pl.BlockSpec(memory_space=pltpu.SMEM),
            row,
            row,
            pl.BlockSpec((width, BLOCK), lambda s: (0, jnp.minimum(s, last))),
            pl.BlockSpec((4, 4, 48, width), lambda s: (0, 0, 3, 0), pipeline_mode=one),
            pl.BlockSpec((8, 192, width), lambda s: (0, 0, 0), pipeline_mode=one),
            pl.BlockSpec((8, 192, width), lambda s: (0, 0, 0), pipeline_mode=one),
            pl.BlockSpec((4, 8, 1024), lambda s: (0, 0, 0), pipeline_mode=one),
            pl.BlockSpec((8, width), lambda s: (0, 0), pipeline_mode=one),
            anywhere,
            anywhere,
        ],
        out_specs=[
            row,
            row,
            row,
            pl.BlockSpec(
                (1, 8, 192, width), lambda s: (jnp.maximum(s - FEED_BLOCKS, 0), 0, 0, 0)
            ),
            pl.BlockSpec((8, width), lambda s: (0, 0)),
            anywhere,
        ],
        out_shape=[
            jax.ShapeDtypeStruct((rows, width), F32),
            jax.ShapeDtypeStruct((rows, width), F32),
            jax.ShapeDtypeStruct((rows, width), F32),
            jax.ShapeDtypeStruct((2, 8, 192, width), BF16),
            jax.ShapeDtypeStruct((8, width), F32),
            jax.ShapeDtypeStruct((2, 8, 192, width), BF16),
        ],
        scratch_shapes=[
            pltpu.VMEM((width + 16, rows), BF16),
            pltpu.VMEM((width, rows), BF16),
            pltpu.VMEM((2, rows, width), BF16),
            pltpu.VMEM((2, rows, width), BF16),
            pltpu.SemaphoreType.DMA((4 * GATHER_KINDS,)),
            pltpu.SemaphoreType.DMA((4 * GATHER_KINDS,)),
        ],
        compiler_params=pltpu.CompilerParams(
            vmem_limit_bytes=62 << 20, collective_id=3, has_side_effects=True
        ),
        cost_estimate=pl.CostEstimate(
            flops=24_000_000_000, bytes_accessed=45_000_000, transcendentals=5_000_000
        ),
        name="feed_first",
    )(live, tokens, out_grad, mixed, in_all, ff_own, ff_near, bias_all, vectors, ff_own, ff_near)


def feed_last(
    live,
    residual,
    feed,
    back_second,
    out_grad,
    mixed,
    in_all,
    ff_late,
    bias_all,
    vectors,
    ff_near_grad,
):
    rows, width = out_grad.shape
    anywhere = pl.BlockSpec(memory_space=pl.ANY)
    one = pl.Buffered(1)
    last = FEED_BLOCKS - 1
    row = pl.BlockSpec((BLOCK, width), lambda s: (jnp.minimum(s, last), 0))
    column = pl.BlockSpec((width, BLOCK), lambda s: (0, jnp.minimum(s, last)))
    return pl.pallas_call(
        feed_last_kernel,
        grid=(FEED_BLOCKS + 2,),
        in_specs=[
            pl.BlockSpec(memory_space=pltpu.SMEM),
            row,
            row,
            row,
            row,
            column,
            pl.BlockSpec((4, 4, 48, width), lambda s: (0, 0, 3, 0), pipeline_mode=one),
            pl.BlockSpec((2, 8, 192, width), lambda s: (0, 0, 0, 0), pipeline_mode=one),
            pl.BlockSpec((4, 8, 1024), lambda s: (0, 0, 0), pipeline_mode=one),
            pl.BlockSpec((8, width), lambda s: (0, 0), pipeline_mode=one),
            anywhere,
        ],
        out_specs=[
            row,
            row,
            column,
            pl.BlockSpec(
                (1, 8, 192, width), lambda s: (jnp.maximum(s - FEED_BLOCKS, 0), 0, 0, 0)
            ),
            pl.BlockSpec((4, 4, 48, width), lambda s: (0, 0, 0, 0)),
            pl.BlockSpec((8, width), lambda s: (0, 0)),
            pl.BlockSpec((192, width), lambda s: (0, 0)),
        ],
        out_shape=[
            jax.ShapeDtypeStruct((rows, width), BF16),
            jax.ShapeDtypeStruct((rows, width), F32),
            jax.ShapeDtypeStruct((width, rows), BF16),
            jax.ShapeDtypeStruct((2, 8, 192, width), BF16),
            jax.ShapeDtypeStruct((4, 4, 48, width), BF16),
            jax.ShapeDtypeStruct((8, width), F32),
            jax.ShapeDtypeStruct((192, width), F32),
        ],
        scratch_shapes=[
            pltpu.VMEM((width + 16, rows), BF16),
            pltpu.VMEM((width, rows), BF16),
            pltpu.VMEM((2, rows, width), BF16),
            pltpu.VMEM((2, rows, width), BF16),
            pltpu.VMEM((width, width), F32),
            pltpu.VMEM((2, 2, 2, 192, width), BF16),
            pltpu.SemaphoreType.DMA((2,)),
        ]
        + reduce_scratch(2, 192, 96, width),
        compiler_params=pltpu.CompilerParams(
            vmem_limit_bytes=62 << 20, collective_id=4, has_side_effects=True
        ),
        cost_estimate=pl.CostEstimate(
            flops=28_000_000_000, bytes_accessed=55_000_000, transcendentals=5_000_000
        ),
        name="feed_last",
    )(
        live,
        residual,
        feed,
        back_second,
        out_grad,
        mixed,
        in_all,
        ff_late,
        bias_all,
        vectors,
        ff_near_grad.reshape(2, 2, 2, 2, 192, width),
    )


def local(
    tokens,
    out_grad,
    live_images,
    first_gain,
    first_shift,
    project_in,
    query_value_bias,
    project_out,
    output_bias,
    second_gain,
    second_shift,
    up_weight,
    up_bias,
    down_weight,
    down_bias,
):
    width = tokens.shape[1]
    own_heads = project_in.shape[2] // HEAD_DIM
    ff_own = jnp.concatenate(
        [up_weight.reshape(8, -1, width), down_weight.reshape(8, -1, width)], axis=1
    )
    pair_bias = query_value_bias.astype(F32).reshape(2, own_heads, HEAD_DIM)
    own_bias = jnp.concatenate([pair_bias[0], jnp.zeros_like(pair_bias[0]), pair_bias[1]], axis=1)
    bias_own = jnp.concatenate(
        [
            jnp.pad(own_bias, ((0, 8 - own_heads), (0, 256 - own_bias.shape[1]))),
            jnp.pad(up_bias.astype(F32)[None], ((0, 7), (0, 0))),
        ],
        axis=1,
    )
    row = lax.broadcasted_iota(jnp.int32, (8, width), 0)
    vectors = jnp.zeros((8, width), F32)
    for i, vector in enumerate(
        (output_bias, second_gain, second_shift, down_bias, first_gain, first_shift)
    ):
        vectors = jnp.where(row == i, vector[None], vectors)
    qkv, mixed, logsum, first, in_all, ff_near, bias_all = attend(
        tokens, vectors, project_in.transpose(1, 2, 0), project_out, ff_own, bias_own
    )
    residual, feed, back_second, near_grad, up_sums, ff_late = feed_first(
        live_images, tokens, out_grad, mixed, in_all, ff_near, bias_all, vectors, ff_own
    )
    output, resid, back_mixed, late_grad, out_grads, feed_small, ff_part = feed_last(
        live_images,
        residual,
        feed,
        back_second,
        out_grad,
        mixed,
        in_all,
        ff_late,
        bias_all,
        vectors,
        near_grad,
    )
    input_grad, small, grad_up, grad_down, grad_in, grad_out = attend_back(
        qkv,
        back_mixed,
        mixed,
        logsum,
        first,
        out_grads,
        ff_part,
        in_all,
        tokens,
        resid,
        vectors,
        feed_small,
        up_sums,
        late_grad.reshape(2, 2, 2, 2, 192, width),
    )
    grad_up = grad_up.reshape(width, width).astype(F32)
    grad_down, grad_out = grad_down.astype(F32), grad_out.astype(F32)
    grad_in = grad_in.astype(F32).transpose(2, 0, 1)
    pair_sum = small[8, : 4 * IN_ROWS].reshape(own_heads, 3, HEAD_DIM)
    grad_pair = jnp.stack([pair_sum[:, 0].reshape(-1), pair_sum[:, 2].reshape(-1)])
    return (
        output,
        input_grad,
        small[12],
        small[13],
        grad_in,
        grad_pair,
        grad_out,
        small[0],
        small[1],
        small[2],
        grad_up,
        small[4],
        grad_down,
        small[3],
    )


def solution(mesh):
    rows = P(("dp", "mp"), None)
    return jax.shard_map(
        local,
        mesh=mesh,
        in_specs=(
            rows,
            rows,
            rows,
            P(),
            P(),
            P(None, None, "mp"),
            P(None, "mp"),
            P("mp", None),
            P(),
            P(),
            P(),
            P(None, "mp"),
            P("mp"),
            P("mp", None),
            P(),
        ),
        out_specs=(
            rows,
            rows,
            P(),
            P(),
            P(None, None, "mp"),
            P(None, "mp"),
            P("mp", None),
            P(),
            P(),
            P(),
            P(None, "mp"),
            P("mp"),
            P("mp", None),
            P(),
        ),
        check_vma=False,
    )
```

```python
import functools
import math

import jax
import jax.numpy as jnp
from jax import lax
from jax.experimental import pallas as pl
from jax.experimental.pallas import tpu as pltpu
from jax.sharding import PartitionSpec as P

HEAD_DIM = 48
SHORT_LEN = 256
LONG_LEN = 1024
SHORT_SLOTS = 2
LONG_SLOTS = 1
SHORT_ROWS = SHORT_SLOTS * SHORT_LEN
IMAGES = tuple((SHORT_LEN * i, SHORT_LEN) for i in range(SHORT_SLOTS)) + tuple(
    (SHORT_ROWS + LONG_LEN * i, LONG_LEN) for i in range(LONG_SLOTS)
)
SCALE = HEAD_DIM**-0.5
SCALE_LOG2 = SCALE * math.log2(math.e)
BF16 = jnp.bfloat16
F32 = jnp.float32
CHUNK = 512
BACK_CHUNK = 256

epsilon = 1e-05


def layer_norm(rows_in, norm_gain, norm_shift):
    average = jnp.mean(rows_in, axis=-1, keepdims=True)
    centred = rows_in - average
    variance = jnp.mean(centred * centred, axis=-1, keepdims=True)
    return centred * lax.rsqrt(variance + epsilon) * norm_gain + norm_shift


def nn(left, right):
    return lax.dot_general(
        left, right, (((1,), (0,)), ((), ())), preferred_element_type=F32
    )


def nt(left, right):
    return lax.dot_general(
        left, right, (((1,), (1,)), ((), ())), preferred_element_type=F32
    )


def tn(left, right):
    return lax.dot_general(
        left, right, (((0,), (0,)), ((), ())), preferred_element_type=F32
    )


GROUP = 8
MESH = pl.DeviceIdType.MESH
IN_ROWS = 144
HEAD_ROWS = 192


def place():
    dp, mp = lax.axis_index("dp"), lax.axis_index("mp")
    g = lax.rem(dp, GROUP)
    return dp, dp - g, g // 4, lax.rem(g // 2, 2), lax.rem(g, 2), mp


def flip(bit):
    return 1 - bit


class Gather:
    def __init__(self, own, buffers, piece, split, send, recv, pieces=None):
        self.own, self.buffers, self.piece, self.split = own, buffers, piece, split
        self.pieces = pieces or {}
        self.send, self.recv = send, recv
        self.dp, self.base, self.y, self.x, self.core, self.mp = place()

    def device(self, y, x, core):
        return (self.base + 4 * y + 2 * x + core, self.mp)

    def view(self, ref, y, x, core, part=None):
        view = self.piece(ref, 2 * y + x, core)
        if part is None:
            return view
        rows = view.shape[0]
        return view.at[pl.ds(0, self.split)] if part == 0 else view.at[pl.ds(self.split, rows - self.split)]

    def copy(self, kind, slot):
        y, x, core = self.y, self.x, self.core
        mine = (y, x, core)
        buffer = self.buffers[slot]
        if kind == 0:
            ways = lax.axis_size("mp")
            hop = 1 if slot == 2 else slot
            src = self.view(self.buffers[1] if slot == 2 else self.own, *mine)
            dst = self.pieces[slot] if slot in self.pieces else self.view(buffer, *mine)
            device = (self.dp, lax.rem(self.mp + ways - hop, ways))
        else:
            return self.shared(kind, buffer, kind * 4 + slot, self.pieces.get(slot))
        return self.remote(src, dst, device, kind * 4 + slot)

    def shared(self, kind, buffer, index, piece=None):
        y, x, core = self.y, self.x, self.core
        mine, near_x, near_y = (y, x, core), (y, flip(x), core), (flip(y), x, core)
        moved, device = {
            1: lambda: (self.view(buffer, *mine), near_x),
            2: lambda: (self.view(buffer, *mine), near_y),
            3: lambda: (self.view(buffer, *near_x, 0), near_y),
            4: lambda: (self.view(buffer, *near_y, 1), near_x),
            5: lambda: (self.view(buffer, *mine), (y, x, flip(core))),
            6: lambda: (self.view(buffer, *near_x), (y, x, flip(core))),
            7: lambda: (self.view(buffer, *near_y), (y, x, flip(core))),
            8: lambda: (self.view(buffer, flip(y), flip(x), core), (y, x, flip(core))),
        }[kind]()
        src = moved if piece is None or kind not in (1, 2, 5) else piece
        return self.remote(src, moved, self.device(*device), index)

    def remote(self, src, dst, device, index):
        return pltpu.make_async_remote_copy(
            src_ref=src,
            dst_ref=dst,
            send_sem=self.send.at[index],
            recv_sem=self.recv.at[index],
            device_id=device,
            device_id_type=MESH,
        )

    def start(self, slot, *kinds):
        for kind in kinds:
            self.copy(kind, slot).start()

    def arrived(self, slot, *kinds):
        for kind in kinds:
            self.copy(kind, slot).wait_recv()

    def along(self, slot):
        self.start(slot, 0)

    def spread(self, slot):
        if slot not in self.pieces:
            self.arrived(slot, 0)
        self.start(slot, 1, 2, 5)

    def forward(self, slot):
        self.arrived(slot, 1)
        self.start(slot, 3, 6)
        self.arrived(slot, 2)
        self.start(slot, 4, 7)

    def last(self, slot):
        self.arrived(slot, 3, 4)
        self.start(slot, 8)

    def complete(self, slot):
        self.arrived(slot, 5, 6, 7, 8)

    def finish(self, slots, kinds=range(9)):
        for slot in slots:
            for kind in kinds:
                self.copy(kind, slot).wait_send()


GATHER_KINDS = 9


def in_piece(ref, chip, core):
    return ref.at[chip, :, pl.ds(pl.multiple_of(core * 384, 128), 384)]


def ff_piece(ref, chip, core):
    return ref.at[2 * chip + core]


def greet(partners):
    barrier = pltpu.get_barrier_semaphore()
    for partner in partners:
        pl.semaphore_signal(barrier, inc=1, device_id=partner, device_id_type=MESH)
    pl.semaphore_wait(barrier, len(partners))


def chunks_of(images, size):
    return [
        (start, length, first, min(size, length))
        for start, length in images
        for first in range(start, start + length, min(size, length))
    ]


def attend_head(qkv_ref, mixed_ref, logsum_ref):
    held = {}

    def score(start, length, first, chunk):
        if start not in held:
            whole = slice(start, start + length)
            value_t = qkv_ref[96:144, whole]
            held[start] = (
                qkv_ref[48:96, whole].T,
                jnp.concatenate([value_t, jnp.ones((16, length), BF16)], axis=0),
            )
        return nn(held[start][0], qkv_ref[0:48, first : first + chunk])

    def soften(scores):
        top = jnp.max(scores, axis=0, keepdims=True)
        return top, jnp.exp2((scores - top) * SCALE_LOG2).astype(BF16)

    def mix(item, top, weights):
        start, length, first, chunk = item
        cols = slice(first, first + chunk)
        sums = nn(held[start][1], weights)
        total = sums[48:49]
        mixed_ref[:, cols] = (sums[:48] / total).astype(BF16)
        logsum_ref[:, cols] = top * SCALE_LOG2 + jnp.log2(total)

    items = chunks_of(IMAGES, CHUNK)
    early, late = {0: score(*items[0])}, {}
    for i in range(len(items) + 1):
        if i + 1 < len(items):
            early[i + 1] = score(*items[i + 1])
        if i < len(items):
            late[i] = soften(early.pop(i))
        if i > 0:
            mix(items[i - 1], *late.pop(i - 1))


def hooks_of(table, step):
    def hook(name, head=None):
        for (at, where), actions in table.items():
            if where == name if head is None else isinstance(where, int):

                @pl.when(step == at if head is None else (step == at) & (head == where))
                def _(actions=actions):
                    for action in actions:
                        action()

    return hook


def group_partners(wide=False):
    dp, base, y, x, core, mp = place()
    ways = lax.axis_size("mp")
    return (
        [(dp, lax.rem(mp + k, ways)) for k in (1, 2, 3)]
        + [
            (base + 4 * y + 2 * flip(x) + core, mp),
            (base + 4 * flip(y) + 2 * x + core, mp),
            (base + 4 * y + 2 * x + flip(core), mp),
        ]
        + [(other_bit(dp, bit), mp) for bit in wider_bits() if wide]
    )


def attend_kernel(
    tokens_ref,
    vector_ref,
    in_own,
    out_own,
    ff_own,
    bias_own,
    qkv_ref,
    mixed_ref,
    logsum_ref,
    first_ref,
    in_out,
    ff_near,
    ff_pieces,
    bias_out,
    in_all,
    bias_all,
    in_send,
    in_recv,
    ff_send,
    ff_recv,
    bias_send,
    bias_recv,
    own_sem,
    local_sem,
):
    step = pl.program_id(0)
    dp, base, y, x, core, mp = place()
    ways = lax.axis_size("mp")
    gin = Gather(in_all.at[0], [in_all.at[k] for k in range(4)], in_piece, 96, in_send, in_recv)
    gff = Gather(
        ff_own,
        [None, ff_near, None, None],
        ff_piece,
        96,
        ff_send,
        ff_recv,
        {2: ff_pieces.at[0], 3: ff_pieces.at[1]},
    )
    own_copies = [
        pltpu.make_async_copy(
            in_own.at[part, pl.ds(head * 48, 48)] if part < 3 else out_own.at[pl.ds(head * 48, 48)],
            in_all.at[0, head, pl.ds(part * 48, 48)],
            own_sem.at[part * 4 + head],
        )
        for part in range(4)
        for head in range(4)
    ]
    local_bias = pltpu.make_async_copy(bias_own, bias_all.at[0], local_sem.at[1])
    out_in = pltpu.make_async_copy(in_all, in_out, local_sem.at[2])
    out_bias = pltpu.make_async_copy(bias_all, bias_out, local_sem.at[3])

    def bias_copy(slot):
        return pltpu.make_async_remote_copy(
            src_ref=bias_own,
            dst_ref=bias_all.at[slot],
            send_sem=bias_send.at[slot],
            recv_sem=bias_recv.at[slot],
            device_id=(dp, lax.rem(mp + ways - slot, ways)),
            device_id_type=MESH,
        )

    def begin():
        for copy in own_copies:
            copy.start()
        local_bias.start()
        greet(group_partners())
        for copy in own_copies:
            copy.wait()
        gin.along(1)
        for rows in range(0, tokens_ref.shape[0], BLOCK):
            block = slice(rows, rows + BLOCK)
            first_ref[block] = layer_norm(
                tokens_ref[block].astype(F32), vector_ref[4:5], vector_ref[5:6]
            ).astype(BF16)
        local_bias.wait()

    def end():
        gff.complete(1)
        gff.arrived(2, 0)
        gff.arrived(3, 0)
        out_in.wait()
        out_bias.wait()
        for slot in (1, 2, 3):
            bias_copy(slot).wait_send()
        gin.finish((1, 2, 3))
        gff.finish((1,))
        gff.finish((2, 3), (0,))

    hook = hooks_of(
        {
            (0, "begin"): [begin],
            (0, "heads"): [
                lambda: gin.spread(1),
                lambda: gin.along(3),
                lambda: gin.along(2),
                lambda: [bias_copy(slot).start() for slot in (1, 2, 3)],
            ],
            (0, 2): [lambda: gin.forward(1)],
            (0, "end"): [lambda: gin.last(1), lambda: gin.spread(3)],
            (1, "begin"): [
                lambda: [bias_copy(slot).wait_recv() for slot in (1, 2, 3)],
                lambda: gin.complete(1),
            ],
            (1, "heads"): [lambda: gin.spread(2), lambda: gff.along(1)],
            (1, 1): [lambda: gin.forward(3)],
            (1, 3): [lambda: gin.last(3), lambda: gin.forward(2)],
            (2, "begin"): [lambda: gin.last(2), lambda: gin.complete(3)],
            (2, "heads"): [lambda: gff.spread(1), lambda: gff.along(3), lambda: gff.along(2)],
            (3, "begin"): [
                lambda: gin.complete(2),
                out_in.start,
                out_bias.start,
                lambda: gff.forward(1),
            ],
            (3, 2): [lambda: gff.last(1)],
            (3, "end"): [end],
        },
        step,
    )
    slot = slot_order(step)
    hook("begin")
    bias_t = bias_all[slot, :, 0:256].T
    for part in range(4):
        product = nt(in_all[slot, part, :IN_ROWS], first_ref[...])
        qkv_ref[part * IN_ROWS : (part + 1) * IN_ROWS, :] = (
            product + bias_t[:IN_ROWS, part : part + 1]
        ).astype(BF16)
    hook("heads")

    def one_head(head, carry):
        hook(None, head)
        attend_head(
            qkv_ref.at[pl.ds(pl.multiple_of(head * IN_ROWS, 16), IN_ROWS)],
            mixed_ref.at[pl.ds(pl.multiple_of(head * 48, 16), 48)],
            logsum_ref.at[head],
        )
        return carry

    lax.fori_loop(0, 4, one_head, 0)
    hook("end")


def slot_order(turn):
    return turn + (turn // 2) * (1 - 2 * (turn % 2))


def attend(tokens, vectors, in_own, out_own, ff_own, bias_own):
    rows, width = tokens.shape
    heads = 16
    anywhere = pl.BlockSpec(memory_space=pl.ANY)
    dma = pltpu.SemaphoreType.DMA
    return pl.pallas_call(
        attend_kernel,
        grid=(4,),
        in_specs=[
            pl.BlockSpec((rows, width), lambda s: (0, 0), pipeline_mode=pl.Buffered(1)),
            pl.BlockSpec((8, width), lambda s: (0, 0)),
            anywhere,
            anywhere,
            anywhere,
            anywhere,
        ],
        out_specs=[
            pl.BlockSpec((4 * IN_ROWS, rows), lambda s: (slot_order(s), 0)),
            pl.BlockSpec((4 * 48, rows), lambda s: (slot_order(s), 0)),
            pl.BlockSpec((4, 1, rows), lambda s: (slot_order(s), 0, 0)),
            pl.BlockSpec((rows, width), lambda s: (0, 0)),
            anywhere,
            anywhere,
            anywhere,
            anywhere,
        ],
        out_shape=[
            jax.ShapeDtypeStruct((heads * IN_ROWS, rows), BF16),
            jax.ShapeDtypeStruct((heads * 48, rows), BF16),
            jax.ShapeDtypeStruct((heads, 1, rows), F32),
            jax.ShapeDtypeStruct((rows, width), BF16),
            jax.ShapeDtypeStruct((4, 4, HEAD_ROWS, width), BF16),
            jax.ShapeDtypeStruct((8, 192, width), BF16),
            jax.ShapeDtypeStruct((2, 192, width), BF16),
            jax.ShapeDtypeStruct((4, 8, 1024), F32),
        ],
        scratch_shapes=[
            pltpu.VMEM((4, 4, HEAD_ROWS, width), BF16),
            pltpu.VMEM((4, 8, 1024), F32),
            dma((4 * GATHER_KINDS,)),
            dma((4 * GATHER_KINDS,)),
            dma((4 * GATHER_KINDS,)),
            dma((4 * GATHER_KINDS,)),
            dma((4,)),
            dma((4,)),
            dma((16,)),
            dma((4,)),
        ],
        compiler_params=pltpu.CompilerParams(
            vmem_limit_bytes=62 << 20, collective_id=0, has_side_effects=True
        ),
        cost_estimate=pl.CostEstimate(
            flops=30_000_000_000, bytes_accessed=30_000_000, transcendentals=19_000_000
        ),
        name="attend",
    )(tokens, vectors, in_own, out_own, ff_own, bias_own)


class Reduce:
    def __init__(self, slot, other, total, got, split, send, recv):
        self.slot, self.other, self.total, self.got, self.split = slot, other, total, got, split
        self.send, self.recv = send, recv
        self.dp, self.base, self.y, self.x, self.core, self.mp = place()

    def copy(self, kind):
        y, x, core = self.y, self.x, self.core
        first, late = pl.ds(0, self.split), pl.ds(self.split, self.total.shape[2] - self.split)
        got = self.got
        near = lambda y, x, core: (self.base + 4 * y + 2 * x + core, self.mp)
        to_x, to_y = near(y, flip(x), core), near(flip(y), x, core)
        src, dst, device = {
            0: lambda: (self.other, got[0], near(y, x, flip(core))),
            1: lambda: (self.total.at[:, flip(x), first], got[1], to_x),
            2: lambda: (self.total.at[flip(y), :, late], got[2], to_y),
            3: lambda: (self.total.at[flip(y), x, first], got[3], to_y),
            4: lambda: (self.total.at[y, flip(x), late], got[4], to_x),
            5: lambda: (
                self.total.at[y, x],
                got[5],
                (self.dp, lax.rem(self.mp + self.slot, lax.axis_size("mp"))),
            ),
        }[kind]()
        index = kind * 4 + self.slot
        return pltpu.make_async_remote_copy(
            src_ref=src,
            dst_ref=dst,
            send_sem=self.send.at[index],
            recv_sem=self.recv.at[index],
            device_id=device,
            device_id_type=MESH,
        )

    def cores(self):
        self.copy(0).start()

    def chips(self):
        self.copy(0).wait_recv()
        for y in range(2):
            for x in range(2):
                self.total[y, x] = add(self.total[y, x], self.got[0][y, x])
        self.copy(1).start()
        self.copy(2).start()

    def chips_again(self):
        x, y, split = self.x, self.y, self.split
        self.copy(1).wait_recv()
        for i in range(2):
            self.total[i, x, :split] = add(self.total[i, x, :split], self.got[1][i])
        self.copy(2).wait_recv()
        for i in range(2):
            self.total[y, i, split:] = add(self.total[y, i, split:], self.got[2][i])
        self.copy(3).start()
        self.copy(4).start()

    def settle(self):
        x, y, split = self.x, self.y, self.split
        self.copy(3).wait_recv()
        self.total[y, x, :split] = add(self.total[y, x, :split], self.got[3][...])
        self.copy(4).wait_recv()
        self.total[y, x, split:] = add(self.total[y, x, split:], self.got[4][...])

    def along(self):
        self.settle()
        if self.slot:
            self.copy(5).start()

    def finish(self, kinds=6):
        for kind in range(kinds if self.slot else 5):
            self.copy(kind).wait_send()

    def result(self):
        if self.slot:
            self.copy(5).wait_recv()
            return self.got[5][...].astype(F32)
        return self.total[self.y, self.x].astype(F32)


REDUCE_KINDS = 6


def add(left, right):
    return (left.astype(F32) + right.astype(F32)).astype(BF16)


def other_bit(index, bit):
    return index + bit * (1 - 2 * lax.rem(index // bit, 2))


def wider_bits():
    bits, bit = [], GROUP
    while bit < lax.axis_size("dp"):
        bits.append(bit)
        bit *= 2
    return bits


class Share:
    def __init__(self, pieces, split, send, recv):
        self.inner = Gather(None, None, ff_piece, split, send, recv)
        self.pieces = pieces

    def copy(self, kind):
        return self.inner.shared(kind, self.pieces, kind)

    def start(self, *kinds):
        for kind in kinds:
            self.copy(kind).start()

    def arrived(self, *kinds):
        for kind in kinds:
            self.copy(kind).wait_recv()

    def spread(self):
        self.start(1, 2, 5)

    def forward(self):
        self.arrived(1)
        self.start(3, 6)
        self.arrived(2)
        self.start(4, 7)

    def last(self):
        self.arrived(3, 4)
        self.start(8)

    def finish(self):
        self.arrived(5, 6, 7, 8)
        for kind in range(1, 9):
            self.copy(kind).wait_send()


class Wide:
    def __init__(self, held, send, recv):
        self.held, self.send, self.recv = held, send, recv

    def copy(self, i, bit):
        dp, mp = lax.axis_index("dp"), lax.axis_index("mp")
        return pltpu.make_async_remote_copy(
            src_ref=self.held.at[2 * i],
            dst_ref=self.held.at[2 * i + 1],
            send_sem=self.send.at[i],
            recv_sem=self.recv.at[i],
            device_id=(other_bit(dp, bit), mp),
            device_id_type=MESH,
        )

    def sum(self, total):
        for i, bit in enumerate(wider_bits()):
            self.held[2 * i] = total.astype(BF16)
            self.copy(i, bit).start()
            self.copy(i, bit).wait()
            total = total + self.held[2 * i + 1].astype(F32)
        return total


def reduce_scratch(slots, rows, split, width):
    dma = pltpu.SemaphoreType.DMA
    late = rows - split
    return [
        pltpu.VMEM((slots, 2, 2, rows, width), BF16),
        pltpu.VMEM((slots, 2, split, width), BF16),
        pltpu.VMEM((slots, 2, late, width), BF16),
        pltpu.VMEM((slots, split, width), BF16),
        pltpu.VMEM((slots, late, width), BF16),
        pltpu.VMEM((slots, rows, width), BF16),
        dma((4 * REDUCE_KINDS,)),
        dma((4 * REDUCE_KINDS,)),
    ]


REDUCE_REFS = 8


def reduces_of(slots, other, total, scratch, split):
    *got, send, recv = scratch
    return {
        slot: Reduce(slot, other(i), total(i), [ref.at[i] for ref in got], split, send, recv)
        for i, slot in enumerate(slots)
    }


def share_scratch(rows, width):
    dma = pltpu.SemaphoreType.DMA
    wide = max(len(wider_bits()), 1)
    return [
        pltpu.VMEM((8, rows, width), BF16),
        pltpu.VMEM((2 * wide, rows, width), BF16),
        dma((GATHER_KINDS,)),
        dma((GATHER_KINDS,)),
        dma((wide,)),
        dma((wide,)),
    ]


SHARE_REFS = 6


class Sums:
    def __init__(self, direct, held, got, along_got, send, recv, along_send, along_recv):
        self.direct, self.held, self.got, self.along_got = direct, held, got, along_got
        self.send, self.recv, self.along_send, self.along_recv = send, recv, along_send, along_recv
        self.dp, self.base, self.y, self.x, self.core, self.mp = place()
        self.bits = ([] if direct else [1, 2, 4]) + wider_bits()
        self.near = GROUP - 1 if direct else 0

    def copy(self, src, index, device):
        return pltpu.make_async_remote_copy(
            src_ref=self.held.at[src],
            dst_ref=self.got.at[index],
            send_sem=self.send.at[index],
            recv_sem=self.recv.at[index],
            device_id=(device, self.mp),
            device_id_type=MESH,
        )

    def near_copy(self, k):
        return self.copy(0, k, self.base + near_index(self.y, self.x, self.core, k + 1))

    def bit_copy(self, i):
        first = 1 if self.direct else 0
        return self.copy(first + i, self.near + i, other_bit(self.dp, self.bits[i]))

    def along_copy(self, slot):
        return pltpu.make_async_remote_copy(
            src_ref=self.held.at[self.last()],
            dst_ref=self.along_got.at[slot - 1],
            send_sem=self.along_send.at[slot - 1],
            recv_sem=self.along_recv.at[slot - 1],
            device_id=(self.dp, lax.rem(self.mp + slot, lax.axis_size("mp"))),
            device_id_type=MESH,
        )

    def last(self):
        return len(self.bits) + (1 if self.direct else 0)

    def start(self):
        if self.direct:
            for k in range(self.near):
                self.near_copy(k).start()
        else:
            self.bit_copy(0).start()

    def step(self, i):
        first = 1 if self.direct else 0
        self.bit_copy(i).wait_recv()
        self.held[first + i + 1] = self.held[first + i] + self.got[self.near + i]
        if i + 1 < len(self.bits):
            self.bit_copy(i + 1).start()

    def join(self, begin=0):
        if self.direct:
            total = self.held[0]
            for k in range(self.near):
                self.near_copy(k).wait_recv()
                total = total + self.got[k]
            self.held[1] = total
            if self.bits:
                self.bit_copy(0).start()
        for i in range(begin, len(self.bits)):
            self.step(i)
        for slot in (1, 2, 3):
            self.along_copy(slot).start()

    def result(self):
        return self.held[self.last()]

    def arrived(self, slot):
        self.along_copy(slot).wait_recv()
        return self.along_got[slot - 1]

    def finish(self):
        for k in range(self.near):
            self.near_copy(k).wait_send()
        for i in range(len(self.bits)):
            self.bit_copy(i).wait_send()
        for slot in (1, 2, 3):
            self.along_copy(slot).wait_send()


SUMS_REFS = 7


def sums_scratch(direct, rows, width):
    dma = pltpu.SemaphoreType.DMA
    stages = (GROUP - 1 if direct else 3) + len(wider_bits())
    return [
        pltpu.VMEM(((1 if direct else 3) + len(wider_bits()) + 1, rows, width), F32),
        pltpu.VMEM((stages, rows, width), F32),
        pltpu.VMEM((3, rows, width), F32),
        dma((stages,)),
        dma((stages,)),
        dma((3,)),
        dma((3,)),
    ]


def attend_back_head(qkv_ref, back_ref, mixed_ref, logsum_ref, out_ref, held):
    rows = {}

    def score(start, length, first, chunk):
        if start not in rows:
            whole = slice(start, start + length)
            key_t = qkv_ref[48:96, whole]
            rows[start] = (key_t, key_t.T, qkv_ref[96:144, whole].T)
        cols = slice(first, first + chunk)
        return (
            nn(rows[start][1], qkv_ref[0:48, cols]),
            nn(rows[start][2], back_ref[:, cols]),
        )

    def soften(item, scores, back_probs):
        cols = slice(item[2], item[2] + item[3])
        inner = jnp.sum(
            back_ref[:, cols].astype(F32) * mixed_ref[:, cols].astype(F32), axis=0, keepdims=True
        )
        probs = jnp.exp2(scores * SCALE_LOG2 - logsum_ref[:, cols])
        return probs.astype(BF16), (probs * (back_probs - inner)).astype(BF16)

    def pull(item, probs, back_scores):
        start, length, first, chunk = item
        cols, whole = slice(first, first + chunk), slice(start, start + length)
        query_t, back_t = qkv_ref[0:48, cols], back_ref[:, cols]
        out_ref[0:48, cols] = (nn(rows[start][0], back_scores) * SCALE).astype(BF16)
        back_key = nt(query_t, back_scores)
        back_value = nt(back_t, probs)
        if first > start:
            back_key = back_key + held[0:48, 0:length]
            back_value = back_value + held[48:96, 0:length]
        if first + chunk < start + length:
            held[0:48, 0:length] = back_key
            held[48:96, 0:length] = back_value
        else:
            out_ref[48:96, whole] = (back_key * SCALE).astype(BF16)
            out_ref[96:144, whole] = back_value.astype(BF16)

    items = chunks_of(IMAGES, BACK_CHUNK)
    early = {0: score(*items[0])}
    for i in range(len(items)):
        if i + 1 < len(items):
            early[i + 1] = score(*items[i + 1])
        pull(items[i], *soften(items[i], *early.pop(i)))


def attend_back_kernel(
    qkv_ref,
    back_ref,
    mixed_ref,
    logsum_ref,
    first_any,
    out_grad_ref,
    ff_part_ref,
    in_any,
    tokens_ref,
    resid_ref,
    vector_ref,
    feed_small_ref,
    up_sums_ref,
    ff_grad,
    input_ref,
    small_ref,
    up_out,
    down_out,
    in_out,
    out_out,
    held,
    ff_total,
    grads,
    back_qkv,
    turned,
    first_ref,
    in_ref,
    local,
    *scratch,
    blocks,
):
    step = pl.program_id(0)
    width = tokens_ref.shape[1]
    dp, base, y, x, core, mp = place()
    early, scratch = Sums(False, *scratch[:SUMS_REFS]), scratch[SUMS_REFS:]
    late, scratch = Sums(True, *scratch[:SUMS_REFS]), scratch[SUMS_REFS:]
    sums, late_sums = early.held, late.held
    ff_scratch, scratch = scratch[:REDUCE_REFS], scratch[REDUCE_REFS:]
    in_scratch, scratch = scratch[:REDUCE_REFS], scratch[REDUCE_REFS:]
    ff_final, ff_wide, *ff_sems = scratch[:SHARE_REFS]
    in_final, in_wide, *in_sems = scratch[SHARE_REFS:]
    ff = reduces_of(
        (2, 3),
        lambda i: ff_grad.at[i, :, :, flip(core)],
        lambda i: ff_total.at[i],
        ff_scratch,
        96,
    )
    ins = reduces_of(
        (0, 1, 2, 3),
        lambda i: grads.at[i, :, :, flip(core)],
        lambda i: grads.at[i, :, :, core],
        in_scratch,
        48,
    )
    ff_share = Share(ff_final, 96, *ff_sems[:2])
    in_share = Share(in_final, 48, *in_sems[:2])
    me = 4 * y + 2 * x + core

    def own(i):
        return pltpu.make_async_copy(ff_grad.at[i, :, :, core], ff_total.at[i], local.at[i])

    up_written = pltpu.make_async_copy(ff_final.at[:, pl.ds(0, 96)], up_out, local.at[2])
    down_written = pltpu.make_async_copy(turned, down_out, local.at[3])

    def in_written():
        copies = []
        for head in range(4):
            rows = pl.ds(48 * head, 48)
            for part in range(4):
                src = in_final.at[2 * head + part // 2, pl.ds(48 * (part % 2), 48)]
                dst = in_out.at[part, rows] if part < 3 else out_out.at[rows]
                copies.append(pltpu.make_async_copy(src, dst, local.at[4 + 4 * head + part]))
        return copies

    first_read = pltpu.make_async_copy(first_any, first_ref, local.at[20])
    in_read = pltpu.make_async_copy(in_any, in_ref, local.at[21])

    def begin():
        own(0).start()
        own(1).start()
        first_read.start()
        in_read.start()
        greet(every_partner())
        ff[2].cores()
        ff[3].cores()
        sums[0] = jnp.zeros_like(sums[0])
        late_sums[0] = jnp.zeros_like(late_sums[0])
        sums[0, 0:8, :] = feed_small_ref[...]
        sums[0, 4:6, :] = up_sums_ref[0:2, :]

    def chips(slot):
        own(slot - 2).wait()
        ff[slot].chips()

    def finish_ff():
        total = ff_part_ref[...] + ff[2].result() + ff[3].result()
        ff_final[me] = Wide(ff_wide, *ff_sems[2:]).sum(total).astype(BF16)
        ff_share.spread()

    def write_ff():
        ff_share.finish()
        up_written.start()
        turned[...] = ff_final[:, 96:].reshape(width, width).T
        down_written.start()

    def finish_in():
        ins[0].along()
        total = ins[0].result() + ins[1].result() + ins[2].result() + ins[3].result()
        in_final[me] = Wide(in_wide, *in_sems[2:]).sum(total).astype(BF16)
        in_share.spread()

    def late_start():
        late.start()
        in_share.forward()

    def end_early():
        small_ref[0:12] = early.result()[0:12]
        for slot in (1, 2, 3):
            more = early.arrived(slot)
            small_ref[0:4] += more[0:4]
            small_ref[4:5] += more[4 + slot : 5 + slot]
            small_ref[8:9] += more[8 + slot : 9 + slot]

    def end():
        late_start()
        late.join()
        in_share.last()
        in_share.finish()
        for copy in in_written():
            copy.start()
        total = late.result() + late.arrived(1) + late.arrived(2) + late.arrived(3)
        third = width // 3
        for i in range(3):
            part = slice(third * i, third * (i + 1))
            small_ref[12:13, part] = total[i : i + 1]
            small_ref[13:14, part] = total[3 + i : 4 + i]
        early.finish()
        late.finish()
        for reduce in [*ff.values(), *ins.values()]:
            reduce.finish()
        up_written.wait()
        down_written.wait()
        for copy in in_written():
            copy.wait()

    hook = hooks_of(
        {
            (0, 0): [begin],
            (0, "grads"): [first_read.wait],
            (0, 1): [lambda: chips(2)],
            (0, 3): [ff[2].chips_again, lambda: chips(3)],
            (1, 0): [ins[2].cores],
            (1, 2): [ff[2].along],
            (1, 3): [ff[3].chips_again, ins[2].chips],
            (2, 0): [ff[3].along, ins[1].cores],
            (2, 1): [ins[2].chips_again, ins[1].chips],
            (2, 3): [ins[2].along, ins[1].chips_again],
            (3, 0): [finish_ff, ins[1].along, ins[3].cores],
            (3, 1): [ins[3].chips],
            (3, 3): [ff_share.forward, ins[3].chips_again],
            (4, "begin"): [in_read.wait, ins[0].cores, early.start, ins[3].along],
            (5, "begin"): [ins[0].chips, ff_share.last, lambda: early.step(0)],
            (6, "begin"): [write_ff, lambda: early.step(1)],
            (6, "end"): [ins[0].chips_again],
            (7, "begin"): [lambda: early.join(2)],
            (7, "end"): [finish_in],
            (9, "begin"): [end_early],
            (9, "end"): [end],
        },
        step,
    )

    @pl.when(step < 4)
    def _():
        slot = back_order(step)

        def one_head(head, carry):
            hook(None, head)
            of_head = pl.ds(pl.multiple_of(head * IN_ROWS, 16), IN_ROWS)
            own_head = pl.ds(pl.multiple_of(head * 48, 16), 48)
            out_rows = pl.ds(pl.multiple_of((4 * slot + head) * IN_ROWS, 16), IN_ROWS)
            attend_back_head(
                qkv_ref.at[of_head],
                back_ref.at[own_head],
                mixed_ref.at[own_head],
                logsum_ref.at[head],
                back_qkv.at[out_rows],
                held,
            )
            return carry

        lax.fori_loop(0, 4, one_head, 0)
        hook("grads")
        for head in range(4):
            rows = back_qkv[pl.ds(pl.multiple_of((4 * slot + head) * IN_ROWS, 16), IN_ROWS), :]
            grad = nn(rows, first_ref[...]).astype(BF16)
            grads[slot, head // 2, head % 2, 0] = grad[:96]
            grads[slot, head // 2, head % 2, 1, 0:48] = grad[96:]
            grads[slot, head // 2, head % 2, 1, 48:96] = out_grad_ref[0, head]
        rows = back_qkv[pl.ds(pl.multiple_of(4 * slot * IN_ROWS, 16), 4 * IN_ROWS), :]
        row_sums = nt(jnp.ones((8, rows.shape[1]), BF16), rows)
        sums[0, pl.ds(8 + slot, 1), 0 : 4 * IN_ROWS] = row_sums[0:1]

    @pl.when(step >= 4)
    def _():
        hook("begin")
        inputs = tokens_ref[...].astype(F32)
        scaled, inverse = normed(inputs)
        cols = pl.ds(pl.multiple_of((step - 4) * BLOCK, BLOCK), BLOCK)
        back_first = None
        for slot in range(4):
            weight = in_ref[slot, :, :IN_ROWS].reshape(4 * IN_ROWS, width)
            part = tn(back_qkv[slot * 4 * IN_ROWS : (slot + 1) * 4 * IN_ROWS, cols], weight)
            back_first = part if slot == 0 else back_first + part
        gain_sum = jnp.sum(back_first * scaled, axis=0, keepdims=True)
        shift_sum = jnp.sum(back_first, axis=0, keepdims=True)
        third = width // 3
        for i in range(3):
            part = slice(third * i, third * (i + 1))
            late_sums[0, i : i + 1] += gain_sum[:, part]
            late_sums[0, 3 + i : 4 + i] += shift_sum[:, part]
        back_norm = back_first * vector_ref[4:5, :]
        input_ref[...] = resid_ref[...] + inverse * (
            back_norm
            - jnp.mean(back_norm, axis=-1, keepdims=True)
            - scaled * jnp.mean(back_norm * scaled, axis=-1, keepdims=True)
        )
        hook("end")


def near_index(y, x, core, k):
    y = flip(y) if k & 4 else y
    x = flip(x) if k & 2 else x
    core = flip(core) if k & 1 else core
    return 4 * y + 2 * x + core


def every_partner():
    dp, base, y, x, core, mp = place()
    ways = lax.axis_size("mp")
    return (
        [(dp, lax.rem(mp + k, ways)) for k in (1, 2, 3)]
        + [(base + near_index(y, x, core, k), mp) for k in range(1, GROUP)]
        + [(other_bit(dp, bit), mp) for bit in wider_bits()]
    )


def back_order(turn):
    turn = jnp.minimum(turn, 3)
    return 2 - turn + (turn // 2) * (3 - 2 * (turn // 3))


BLOCK = 256


def attend_back(
    qkv,
    back_mixed,
    mixed,
    logsum,
    first,
    out_grad,
    ff_part,
    in_all,
    tokens,
    resid,
    vectors,
    feed_small,
    up_sums,
    ff_grad,
):
    rows, width = first.shape
    blocks = rows // BLOCK
    anywhere = pl.BlockSpec(memory_space=pl.ANY)
    one = pl.Buffered(1)
    dma = pltpu.SemaphoreType.DMA
    row = pl.BlockSpec((BLOCK, width), lambda s: (jnp.maximum(s - 4, 0), 0))
    small = pl.BlockSpec((8, width), lambda s: (0, 0))
    return pl.pallas_call(
        functools.partial(attend_back_kernel, blocks=blocks),
        grid=(4 + blocks,),
        in_specs=[
            pl.BlockSpec((4 * IN_ROWS, rows), lambda s: (back_order(s), 0)),
            pl.BlockSpec((4 * 48, rows), lambda s: (back_order(s), 0)),
            pl.BlockSpec((4 * 48, rows), lambda s: (back_order(s), 0)),
            pl.BlockSpec((4, 1, rows), lambda s: (back_order(s), 0, 0)),
            anywhere,
            pl.BlockSpec((1, 4, 48, width), lambda s: (back_order(s), 0, 0, 0)),
            pl.BlockSpec((192, width), lambda s: (0, 0), pipeline_mode=one),
            anywhere,
            row,
            row,
            small,
            small,
            small,
            anywhere,
        ],
        out_specs=[
            row,
            pl.BlockSpec((16, width), lambda s: (0, 0)),
            anywhere,
            anywhere,
            anywhere,
            anywhere,
        ],
        out_shape=[
            jax.ShapeDtypeStruct((rows, width), F32),
            jax.ShapeDtypeStruct((16, width), F32),
            jax.ShapeDtypeStruct((8, 96, width), BF16),
            jax.ShapeDtypeStruct((width, width), BF16),
            jax.ShapeDtypeStruct((3, 192, width), BF16),
            jax.ShapeDtypeStruct((192, width), BF16),
        ],
        scratch_shapes=[
            pltpu.VMEM((96, LONG_LEN), F32),
            pltpu.VMEM((2, 2, 2, 192, width), BF16),
            pltpu.VMEM((4, 2, 2, 2, 96, width), BF16),
            pltpu.VMEM((16 * IN_ROWS, rows), BF16),
            pltpu.VMEM((width, width), BF16),
            pltpu.VMEM((rows, width), BF16),
            pltpu.VMEM((4, 4, HEAD_ROWS, width), BF16),
            dma((22,)),
        ]
        + sums_scratch(False, 16, width)
        + sums_scratch(True, 8, width // 3)
        + reduce_scratch(2, 192, 96, width)
        + reduce_scratch(4, 96, 48, width)
        + share_scratch(192, width)
        + share_scratch(96, width),
        compiler_params=pltpu.CompilerParams(
            vmem_limit_bytes=62 << 20, collective_id=1, has_side_effects=True
        ),
        cost_estimate=pl.CostEstimate(
            flops=50_000_000_000, bytes_accessed=50_000_000, transcendentals=19_000_000
        ),
        name="attend_back",
    )(
        qkv,
        back_mixed,
        mixed,
        logsum,
        first,
        out_grad,
        ff_part,
        in_all,
        tokens,
        resid,
        vectors,
        feed_small,
        up_sums,
        ff_grad,
    )


FEED_BLOCKS = 6


def feed_rows(
    second, back_low, slots, ff_refs, bias_ref, act_s, hid_s, rows, width, feed, back_second
):
    for i, slot in enumerate(slots):
        up = ff_refs[i][:, 0:96, :].reshape(width, width)
        down = ff_refs[i][:, 96:192, :].reshape(width, width)
        hidden = nn(second, up) + bias_ref[slot, 0:1, 256:]
        half = 0.5 + 0.5 * lax.erf(hidden * (0.5**0.5))
        act = (hidden * half).astype(BF16)
        slope = half + hidden * (jnp.exp(hidden * hidden * -0.5) * (1.0 / math.sqrt(2 * math.pi)))
        back_hid = (nt(back_low, down) * slope).astype(BF16)
        act_s[i, rows, :] = act
        hid_s[i, rows, :] = back_hid
        fed, pulled = nn(act, down), nt(back_hid, up)
        feed = fed if feed is None else feed + fed
        back_second = pulled if back_second is None else back_second + pulled
    return feed, back_second


def normed(rows_in):
    average = jnp.mean(rows_in, axis=-1, keepdims=True)
    centred = rows_in - average
    inverse = lax.rsqrt(jnp.mean(centred * centred, axis=-1, keepdims=True) + epsilon)
    return centred * inverse, inverse


def live_back(live_ref, grad_ref, step):
    row = step * BLOCK + lax.broadcasted_iota(jnp.int32, (BLOCK, 1), 0)
    limit = jnp.where(
        row < SHORT_ROWS, live_ref[0, 0] * SHORT_LEN, SHORT_ROWS + live_ref[0, 1] * LONG_LEN
    )
    is_live = row < limit
    return is_live, jnp.where(is_live, grad_ref[...].astype(F32), 0.0)


def feed_grads(i, second_t, back_t, act_s, hid_s, ff_grad_ref, up_sum_ref, row, width):
    up = nn(second_t[...], hid_s[i])
    ff_grad_ref[0, :, 0:96, :] = up[:width].astype(BF16).reshape(8, 96, width)
    up_sum_ref[pl.ds(row, 1), :] = up[width : width + 1]
    down = nn(back_t[...], act_s[i])
    ff_grad_ref[0, :, 96:192, :] = down.astype(BF16).reshape(8, 96, width)


def feed_first_kernel(
    live_ref,
    tokens_ref,
    grad_ref,
    mixed_ref,
    out_w_ref,
    own_ref,
    near_ref,
    bias_ref,
    vec_ref,
    pieces_ref,
    residual_ref,
    feed_ref,
    back_second_ref,
    ff_grad_ref,
    up_sum_ref,
    ff_late,
    second_t,
    back_t,
    act_s,
    hid_s,
    send,
    recv,
    local,
):
    step = pl.program_id(0)
    width = tokens_ref.shape[1]
    gff = Gather(
        None,
        [None, None, ff_late.at[0], ff_late.at[1]],
        ff_piece,
        96,
        send,
        recv,
        {2: pieces_ref.at[0], 3: pieces_ref.at[1]},
    )
    mine = pltpu.make_async_copy(
        pieces_ref, ff_late.at[:, 4 * gff.y + 2 * gff.x + gff.core], local.at[0]
    )

    def begin():
        greet(group_partners())
        gff.spread(3)
        mine.start()
        up_sum_ref[...] = jnp.zeros_like(up_sum_ref)
        second_t[width:, :] = jnp.ones((16, second_t.shape[1]), BF16)

    def end():
        gff.complete(3)
        gff.complete(2)
        gff.finish((2, 3), range(1, 9))
        mine.wait()

    hook = hooks_of(
        {
            (0, "begin"): [begin],
            (2, "begin"): [lambda: gff.forward(3), lambda: gff.spread(2)],
            (4, "begin"): [lambda: gff.last(3)],
            (5, "begin"): [lambda: gff.forward(2)],
            (7, "begin"): [lambda: gff.last(2)],
            (7, "end"): [end],
        },
        step,
    )
    hook("begin")

    @pl.when(step < FEED_BLOCKS)
    def _():
        out_w = out_w_ref[...].reshape(width, width)
        residual = tokens_ref[...].astype(F32) + tn(mixed_ref[...], out_w) + vec_ref[0:1, :]
        residual_ref[...] = residual
        scaled, _ = normed(residual)
        second = (scaled * vec_ref[1:2, :] + vec_ref[2:3, :]).astype(BF16)
        _, back = live_back(live_ref, grad_ref, step)
        back_low = back.astype(BF16)
        rows = pl.ds(pl.multiple_of(step * BLOCK, BLOCK), BLOCK)
        second_t[0:width, rows] = second.T
        back_t[:, rows] = back_low.T
        feed_ref[...], back_second_ref[...] = feed_rows(
            second,
            back_low,
            (0, 1),
            (own_ref, near_ref),
            bias_ref,
            act_s,
            hid_s,
            rows,
            width,
            None,
            None,
        )

    @pl.when(step >= FEED_BLOCKS)
    def _():
        i = step - FEED_BLOCKS
        feed_grads(i, second_t, back_t, act_s, hid_s, ff_grad_ref, up_sum_ref, i, width)

    hook("end")


def feed_last_kernel(
    live_ref,
    residual_ref,
    feed_ref,
    back_second_ref,
    grad_ref,
    mixed_ref,
    out_w_ref,
    ff_ref,
    bias_ref,
    vec_ref,
    ff_near_grad,
    output_ref,
    resid_ref,
    back_mixed_ref,
    ff_grad_ref,
    out_grad_ref,
    small_ref,
    part_ref,
    second_t,
    back_t,
    act_s,
    hid_s,
    out_acc,
    ff_total,
    local,
    *scratch,
):
    step = pl.program_id(0)
    width = residual_ref.shape[1]
    dp, base, y, x, core, mp = place()
    ff = reduces_of(
        (0, 1),
        lambda i: ff_near_grad.at[i, :, :, flip(core)],
        lambda i: ff_total.at[i],
        scratch,
        96,
    )

    def own(i):
        return pltpu.make_async_copy(ff_near_grad.at[i, :, :, core], ff_total.at[i], local.at[i])

    def begin():
        own(1).start()
        own(0).start()
        greet(group_partners())
        ff[1].cores()
        ff[0].cores()
        small_ref[...] = jnp.zeros_like(small_ref)
        second_t[width:, :] = jnp.ones((16, second_t.shape[1]), BF16)

    def chips(slot):
        own(slot).wait()
        ff[slot].chips()

    def end():
        part_ref[...] = ff[0].result() + ff[1].result()
        ff[0].finish()
        ff[1].finish()

    hook = hooks_of(
        {
            (0, "begin"): [begin],
            (1, "begin"): [lambda: chips(1)],
            (3, "begin"): [ff[1].chips_again, lambda: chips(0)],
            (5, "begin"): [ff[1].along],
            (6, "begin"): [ff[0].chips_again],
            (7, "begin"): [ff[0].along],
            (7, "end"): [end],
        },
        step,
    )
    hook("begin")

    @pl.when(step < FEED_BLOCKS)
    def _():
        out_w = out_w_ref[...].reshape(width, width)
        residual = residual_ref[...]
        scaled, inverse = normed(residual)
        gain = vec_ref[1:2, :]
        second = (scaled * gain + vec_ref[2:3, :]).astype(BF16)
        is_live, back = live_back(live_ref, grad_ref, step)
        back_low = back.astype(BF16)
        rows = pl.ds(pl.multiple_of(step * BLOCK, BLOCK), BLOCK)
        second_t[0:width, rows] = second.T
        back_t[:, rows] = back_low.T
        feed, back_second = feed_rows(
            second,
            back_low,
            (2, 3),
            (ff_ref.at[0], ff_ref.at[1]),
            bias_ref,
            act_s,
            hid_s,
            rows,
            width,
            feed_ref[...],
            back_second_ref[...],
        )
        output_ref[...] = jnp.where(is_live, residual + feed + vec_ref[3:4, :], 0.0).astype(BF16)
        small_ref[1:2, :] += jnp.sum(back_second * scaled, axis=0, keepdims=True)
        small_ref[2:3, :] += jnp.sum(back_second, axis=0, keepdims=True)
        small_ref[3:4, :] += jnp.sum(back, axis=0, keepdims=True)
        back_norm = back_second * gain
        back_resid = back + inverse * (
            back_norm
            - jnp.mean(back_norm, axis=-1, keepdims=True)
            - scaled * jnp.mean(back_norm * scaled, axis=-1, keepdims=True)
        )
        small_ref[0:1, :] += jnp.sum(back_resid, axis=0, keepdims=True)
        resid_ref[...] = back_resid
        branch = back_resid.astype(BF16)
        back_mixed_ref[...] = nt(out_w, branch).astype(BF16)
        part = nn(mixed_ref[...], branch)

        @pl.when(step == 0)
        def _():
            out_acc[...] = part

        @pl.when(step > 0)
        def _():
            out_acc[...] += part

        @pl.when(step == FEED_BLOCKS - 1)
        def _():
            out_grad_ref[...] = out_acc[...].astype(BF16).reshape(out_grad_ref.shape)

    @pl.when(step >= FEED_BLOCKS)
    def _():
        i = step - FEED_BLOCKS
        feed_grads(i, second_t, back_t, act_s, hid_s, ff_grad_ref, small_ref, 6 + i, width)

    hook("end")


def feed_first(
    live, tokens, out_grad, mixed, in_all, ff_own, ff_near, bias_all, vectors, ff_pieces
):
    rows, width = tokens.shape
    anywhere = pl.BlockSpec(memory_space=pl.ANY)
    one = pl.Buffered(1)
    last = FEED_BLOCKS - 1
    row = pl.BlockSpec((BLOCK, width), lambda s: (jnp.minimum(s, last), 0))
    return pl.pallas_call(
        feed_first_kernel,
        grid=(FEED_BLOCKS + 2,),
        in_specs=[
            pl.BlockSpec(memory_space=pltpu.SMEM),
            row,
            row,
            pl.BlockSpec((width, BLOCK), lambda s: (0, jnp.minimum(s, last))),
            pl.BlockSpec((4, 4, 48, width), lambda s: (0, 0, 3, 0), pipeline_mode=one),
            pl.BlockSpec((8, 192, width), lambda s: (0, 0, 0), pipeline_mode=one),
            pl.BlockSpec((8, 192, width), lambda s: (0, 0, 0), pipeline_mode=one),
            pl.BlockSpec((4, 8, 1024), lambda s: (0, 0, 0), pipeline_mode=one),
            pl.BlockSpec((8, width), lambda s: (0, 0), pipeline_mode=one),
            pl.BlockSpec((2, 192, width), lambda s: (0, 0, 0), pipeline_mode=one),
        ],
        out_specs=[
            row,
            row,
            row,
            pl.BlockSpec(
                (1, 8, 192, width), lambda s: (jnp.maximum(s - FEED_BLOCKS, 0), 0, 0, 0)
            ),
            pl.BlockSpec((8, width), lambda s: (0, 0)),
            anywhere,
        ],
        out_shape=[
            jax.ShapeDtypeStruct((rows, width), F32),
            jax.ShapeDtypeStruct((rows, width), F32),
            jax.ShapeDtypeStruct((rows, width), F32),
            jax.ShapeDtypeStruct((2, 8, 192, width), BF16),
            jax.ShapeDtypeStruct((8, width), F32),
            jax.ShapeDtypeStruct((2, 8, 192, width), BF16),
        ],
        scratch_shapes=[
            pltpu.VMEM((width + 16, rows), BF16),
            pltpu.VMEM((width, rows), BF16),
            pltpu.VMEM((2, rows, width), BF16),
            pltpu.VMEM((2, rows, width), BF16),
            pltpu.SemaphoreType.DMA((4 * GATHER_KINDS,)),
            pltpu.SemaphoreType.DMA((4 * GATHER_KINDS,)),
            pltpu.SemaphoreType.DMA((1,)),
        ],
        compiler_params=pltpu.CompilerParams(
            vmem_limit_bytes=62 << 20, collective_id=3, has_side_effects=True
        ),
        cost_estimate=pl.CostEstimate(
            flops=24_000_000_000, bytes_accessed=45_000_000, transcendentals=5_000_000
        ),
        name="feed_first",
    )(live, tokens, out_grad, mixed, in_all, ff_own, ff_near, bias_all, vectors, ff_pieces)


def feed_last(
    live,
    residual,
    feed,
    back_second,
    out_grad,
    mixed,
    in_all,
    ff_late,
    bias_all,
    vectors,
    ff_near_grad,
):
    rows, width = out_grad.shape
    anywhere = pl.BlockSpec(memory_space=pl.ANY)
    one = pl.Buffered(1)
    last = FEED_BLOCKS - 1
    row = pl.BlockSpec((BLOCK, width), lambda s: (jnp.minimum(s, last), 0))
    column = pl.BlockSpec((width, BLOCK), lambda s: (0, jnp.minimum(s, last)))
    return pl.pallas_call(
        feed_last_kernel,
        grid=(FEED_BLOCKS + 2,),
        in_specs=[
            pl.BlockSpec(memory_space=pltpu.SMEM),
            row,
            row,
            row,
            row,
            column,
            pl.BlockSpec((4, 4, 48, width), lambda s: (0, 0, 3, 0), pipeline_mode=one),
            pl.BlockSpec((2, 8, 192, width), lambda s: (0, 0, 0, 0), pipeline_mode=one),
            pl.BlockSpec((4, 8, 1024), lambda s: (0, 0, 0), pipeline_mode=one),
            pl.BlockSpec((8, width), lambda s: (0, 0), pipeline_mode=one),
            anywhere,
        ],
        out_specs=[
            row,
            row,
            column,
            pl.BlockSpec(
                (1, 8, 192, width), lambda s: (jnp.maximum(s - FEED_BLOCKS, 0), 0, 0, 0)
            ),
            pl.BlockSpec((4, 4, 48, width), lambda s: (0, 0, 0, 0)),
            pl.BlockSpec((8, width), lambda s: (0, 0)),
            pl.BlockSpec((192, width), lambda s: (0, 0)),
        ],
        out_shape=[
            jax.ShapeDtypeStruct((rows, width), BF16),
            jax.ShapeDtypeStruct((rows, width), F32),
            jax.ShapeDtypeStruct((width, rows), BF16),
            jax.ShapeDtypeStruct((2, 8, 192, width), BF16),
            jax.ShapeDtypeStruct((4, 4, 48, width), BF16),
            jax.ShapeDtypeStruct((8, width), F32),
            jax.ShapeDtypeStruct((192, width), F32),
        ],
        scratch_shapes=[
            pltpu.VMEM((width + 16, rows), BF16),
            pltpu.VMEM((width, rows), BF16),
            pltpu.VMEM((2, rows, width), BF16),
            pltpu.VMEM((2, rows, width), BF16),
            pltpu.VMEM((width, width), F32),
            pltpu.VMEM((2, 2, 2, 192, width), BF16),
            pltpu.SemaphoreType.DMA((2,)),
        ]
        + reduce_scratch(2, 192, 96, width),
        compiler_params=pltpu.CompilerParams(
            vmem_limit_bytes=62 << 20, collective_id=4, has_side_effects=True
        ),
        cost_estimate=pl.CostEstimate(
            flops=28_000_000_000, bytes_accessed=55_000_000, transcendentals=5_000_000
        ),
        name="feed_last",
    )(
        live,
        residual,
        feed,
        back_second,
        out_grad,
        mixed,
        in_all,
        ff_late,
        bias_all,
        vectors,
        ff_near_grad.reshape(2, 2, 2, 2, 192, width),
    )


def local(
    tokens,
    out_grad,
    live_images,
    first_gain,
    first_shift,
    project_in,
    query_value_bias,
    project_out,
    output_bias,
    second_gain,
    second_shift,
    up_weight,
    up_bias,
    down_weight,
    down_bias,
):
    width = tokens.shape[1]
    own_heads = project_in.shape[2] // HEAD_DIM
    ff_own = jnp.concatenate(
        [up_weight.reshape(8, -1, width), down_weight.reshape(8, -1, width)], axis=1
    )
    pair_bias = query_value_bias.astype(F32).reshape(2, own_heads, HEAD_DIM)
    own_bias = jnp.concatenate([pair_bias[0], jnp.zeros_like(pair_bias[0]), pair_bias[1]], axis=1)
    bias_own = jnp.concatenate(
        [
            jnp.pad(own_bias, ((0, 8 - own_heads), (0, 256 - own_bias.shape[1]))),
            jnp.pad(up_bias.astype(F32)[None], ((0, 7), (0, 0))),
        ],
        axis=1,
    )
    row = lax.broadcasted_iota(jnp.int32, (8, width), 0)
    vectors = jnp.zeros((8, width), F32)
    for i, vector in enumerate(
        (output_bias, second_gain, second_shift, down_bias, first_gain, first_shift)
    ):
        vectors = jnp.where(row == i, vector[None], vectors)
    qkv, mixed, logsum, first, in_all, ff_near, ff_pieces, bias_all = attend(
        tokens, vectors, project_in.transpose(1, 2, 0), project_out, ff_own, bias_own
    )
    residual, feed, back_second, near_grad, up_sums, ff_late = feed_first(
        live_images,
        tokens,
        out_grad,
        mixed,
        in_all,
        ff_own,
        ff_near,
        bias_all,
        vectors,
        ff_pieces,
    )
    output, resid, back_mixed, late_grad, out_grads, feed_small, ff_part = feed_last(
        live_images,
        residual,
        feed,
        back_second,
        out_grad,
        mixed,
        in_all,
        ff_late,
        bias_all,
        vectors,
        near_grad,
    )
    input_grad, small, grad_up, grad_down, grad_in, grad_out = attend_back(
        qkv,
        back_mixed,
        mixed,
        logsum,
        first,
        out_grads,
        ff_part,
        in_all,
        tokens,
        resid,
        vectors,
        feed_small,
        up_sums,
        late_grad.reshape(2, 2, 2, 2, 192, width),
    )
    grad_up = grad_up.reshape(width, width).astype(F32)
    grad_down, grad_out = grad_down.astype(F32), grad_out.astype(F32)
    grad_in = grad_in.astype(F32).transpose(2, 0, 1)
    pair_sum = small[8, : 4 * IN_ROWS].reshape(own_heads, 3, HEAD_DIM)
    grad_pair = jnp.stack([pair_sum[:, 0].reshape(-1), pair_sum[:, 2].reshape(-1)])
    return (
        output,
        input_grad,
        small[12],
        small[13],
        grad_in,
        grad_pair,
        grad_out,
        small[0],
        small[1],
        small[2],
        grad_up,
        small[4],
        grad_down,
        small[3],
    )


def solution(mesh):
    rows = P(("dp", "mp"), None)
    return jax.shard_map(
        local,
        mesh=mesh,
        in_specs=(
            rows,
            rows,
            rows,
            P(),
            P(),
            P(None, None, "mp"),
            P(None, "mp"),
            P("mp", None),
            P(),
            P(),
            P(),
            P(None, "mp"),
            P("mp"),
            P("mp", None),
            P(),
        ),
        out_specs=(
            rows,
            rows,
            P(),
            P(),
            P(None, None, "mp"),
            P(None, "mp"),
            P("mp", None),
            P(),
            P(),
            P(),
            P(None, "mp"),
            P("mp"),
            P("mp", None),
            P(),
        ),
        check_vma=False,
    )
```

```python
import functools
import math

import jax
import jax.numpy as jnp
from jax import lax
from jax.experimental import pallas as pl
from jax.experimental.pallas import tpu as pltpu
from jax.sharding import PartitionSpec as P

HEAD_DIM = 48
SHORT_LEN = 256
LONG_LEN = 1024
SHORT_SLOTS = 2
LONG_SLOTS = 1
SHORT_ROWS = SHORT_SLOTS * SHORT_LEN
IMAGES = tuple((SHORT_LEN * i, SHORT_LEN) for i in range(SHORT_SLOTS)) + tuple(
    (SHORT_ROWS + LONG_LEN * i, LONG_LEN) for i in range(LONG_SLOTS)
)
SCALE = HEAD_DIM**-0.5
SCALE_LOG2 = SCALE * math.log2(math.e)
BF16 = jnp.bfloat16
F32 = jnp.float32
CHUNK = 512
BACK_CHUNK = 256

epsilon = 1e-05


def layer_norm(rows_in, norm_gain, norm_shift):
    average = jnp.mean(rows_in, axis=-1, keepdims=True)
    centred = rows_in - average
    variance = jnp.mean(centred * centred, axis=-1, keepdims=True)
    return centred * lax.rsqrt(variance + epsilon) * norm_gain + norm_shift


def nn(left, right):
    return lax.dot_general(
        left, right, (((1,), (0,)), ((), ())), preferred_element_type=F32
    )


def nt(left, right):
    return lax.dot_general(
        left, right, (((1,), (1,)), ((), ())), preferred_element_type=F32
    )


def tn(left, right):
    return lax.dot_general(
        left, right, (((0,), (0,)), ((), ())), preferred_element_type=F32
    )


GROUP = 8
MESH = pl.DeviceIdType.MESH
IN_ROWS = 144
HEAD_ROWS = 192


def place():
    dp, mp = lax.axis_index("dp"), lax.axis_index("mp")
    g = lax.rem(dp, GROUP)
    return dp, dp - g, g // 4, lax.rem(g // 2, 2), lax.rem(g, 2), mp


def flip(bit):
    return 1 - bit


class Gather:
    def __init__(self, own, buffers, piece, split, send, recv, pieces=None):
        self.own, self.buffers, self.piece, self.split = own, buffers, piece, split
        self.pieces = pieces or {}
        self.send, self.recv = send, recv
        self.dp, self.base, self.y, self.x, self.core, self.mp = place()

    def device(self, y, x, core):
        return (self.base + 4 * y + 2 * x + core, self.mp)

    def view(self, ref, y, x, core, part=None):
        view = self.piece(ref, 2 * y + x, core)
        if part is None:
            return view
        rows = view.shape[0]
        return view.at[pl.ds(0, self.split)] if part == 0 else view.at[pl.ds(self.split, rows - self.split)]

    def copy(self, kind, slot):
        y, x, core = self.y, self.x, self.core
        mine = (y, x, core)
        buffer = self.buffers[slot]
        if kind in (0, 9):
            ways = lax.axis_size("mp")
            hop = 1 if slot == 2 else slot
            dst = self.pieces[slot] if slot in self.pieces else self.view(buffer, *mine)
            if slot == 2:
                src = self.view(self.buffers[1], *mine)
            elif isinstance(self.own, tuple):
                src = self.view(self.own[kind // 9], *mine)
                dst = dst.at[pl.ds(96 * (kind // 9), 96)]
            else:
                src = self.view(self.own, *mine)
            device = (self.dp, lax.rem(self.mp + ways - hop, ways))
        else:
            return self.shared(kind, buffer, kind * 4 + slot, self.pieces.get(slot))
        return self.remote(src, dst, device, kind * 4 + slot)

    def shared(self, kind, buffer, index, piece=None):
        y, x, core = self.y, self.x, self.core
        mine, near_x, near_y = (y, x, core), (y, flip(x), core), (flip(y), x, core)
        moved, device = {
            1: lambda: (self.view(buffer, *mine), near_x),
            2: lambda: (self.view(buffer, *mine), near_y),
            3: lambda: (self.view(buffer, *near_x, 0), near_y),
            4: lambda: (self.view(buffer, *near_y, 1), near_x),
            5: lambda: (self.view(buffer, *mine), (y, x, flip(core))),
            6: lambda: (self.view(buffer, *near_x), (y, x, flip(core))),
            7: lambda: (self.view(buffer, *near_y), (y, x, flip(core))),
            8: lambda: (self.view(buffer, flip(y), flip(x), core), (y, x, flip(core))),
        }[kind]()
        src = moved if piece is None or kind not in (1, 2, 5) else piece
        return self.remote(src, moved, self.device(*device), index)

    def remote(self, src, dst, device, index):
        return pltpu.make_async_remote_copy(
            src_ref=src,
            dst_ref=dst,
            send_sem=self.send.at[index],
            recv_sem=self.recv.at[index],
            device_id=device,
            device_id_type=MESH,
        )

    def start(self, slot, *kinds):
        for kind in kinds:
            self.copy(kind, slot).start()

    def arrived(self, slot, *kinds):
        for kind in kinds:
            self.copy(kind, slot).wait_recv()

    def along_kinds(self, slot):
        return (0, 9) if isinstance(self.own, tuple) and slot != 2 else (0,)

    def along(self, slot):
        self.start(slot, *self.along_kinds(slot))

    def spread(self, slot):
        if slot not in self.pieces:
            self.arrived(slot, *self.along_kinds(slot))
        self.start(slot, 1, 2, 5)

    def forward(self, slot):
        self.arrived(slot, 1)
        self.start(slot, 3, 6)
        self.arrived(slot, 2)
        self.start(slot, 4, 7)

    def last(self, slot):
        self.arrived(slot, 3, 4)
        self.start(slot, 8)

    def complete(self, slot):
        self.arrived(slot, 5, 6, 7, 8)

    def finish(self, slots, kinds=range(9)):
        for slot in slots:
            for kind in kinds:
                self.copy(kind, slot).wait_send()


GATHER_KINDS = 10


def in_piece(ref, chip, core):
    return ref.at[chip, :, pl.ds(pl.multiple_of(core * 384, 128), 384)]


def ff_piece(ref, chip, core):
    return ref.at[2 * chip + core]


def signal(partners):
    barrier = pltpu.get_barrier_semaphore()
    for partner in partners:
        pl.semaphore_signal(barrier, inc=1, device_id=partner, device_id_type=MESH)


def meet(partners):
    pl.semaphore_wait(pltpu.get_barrier_semaphore(), len(partners))


def chunks_of(images, size):
    return [
        (start, length, first, min(size, length))
        for start, length in images
        for first in range(start, start + length, min(size, length))
    ]


def attend_head(qkv_ref, mixed_ref, logsum_ref):
    held = {}

    def score(start, length, first, chunk):
        if start not in held:
            whole = slice(start, start + length)
            value_t = qkv_ref[96:144, whole]
            held[start] = (
                qkv_ref[48:96, whole].T,
                jnp.concatenate([value_t, jnp.ones((16, length), BF16)], axis=0),
            )
        return nn(held[start][0], qkv_ref[0:48, first : first + chunk])

    def soften(scores):
        top = jnp.max(scores, axis=0, keepdims=True)
        return top, jnp.exp2((scores - top) * SCALE_LOG2).astype(BF16)

    def mix(item, top, weights):
        start, length, first, chunk = item
        cols = slice(first, first + chunk)
        sums = nn(held[start][1], weights)
        total = sums[48:49]
        mixed_ref[:, cols] = (sums[:48] / total).astype(BF16)
        logsum_ref[:, cols] = top * SCALE_LOG2 + jnp.log2(total)

    items = chunks_of(IMAGES, CHUNK)
    early, late = {0: score(*items[0])}, {}
    for i in range(len(items) + 1):
        if i + 1 < len(items):
            early[i + 1] = score(*items[i + 1])
        if i < len(items):
            late[i] = soften(early.pop(i))
        if i > 0:
            mix(items[i - 1], *late.pop(i - 1))


def hooks_of(table, step):
    def hook(name, head=None):
        for (at, where), actions in table.items():
            if where == name if head is None else isinstance(where, int):

                @pl.when(step == at if head is None else (step == at) & (head == where))
                def _(actions=actions):
                    for action in actions:
                        action()

    return hook


def group_partners(wide=False):
    dp, base, y, x, core, mp = place()
    ways = lax.axis_size("mp")
    return (
        [(dp, lax.rem(mp + k, ways)) for k in (1, 2, 3)]
        + [
            (base + 4 * y + 2 * flip(x) + core, mp),
            (base + 4 * flip(y) + 2 * x + core, mp),
            (base + 4 * y + 2 * x + flip(core), mp),
        ]
        + [(other_bit(dp, bit), mp) for bit in wider_bits() if wide]
    )


def attend_kernel(
    tokens_ref,
    vector_ref,
    in_own,
    out_own,
    up_own,
    down_own,
    bias_own,
    qkv_ref,
    mixed_ref,
    logsum_ref,
    first_ref,
    in_out,
    ff_near,
    ff_pieces,
    bias_out,
    in_all,
    bias_all,
    in_send,
    in_recv,
    ff_send,
    ff_recv,
    bias_send,
    bias_recv,
    own_sem,
    local_sem,
):
    step = pl.program_id(0)
    dp, base, y, x, core, mp = place()
    ways = lax.axis_size("mp")
    gin = Gather(in_all.at[0], [in_all.at[k] for k in range(4)], in_piece, 96, in_send, in_recv)
    gff = Gather(
        (up_own, down_own),
        [None, ff_near, None, None],
        ff_piece,
        96,
        ff_send,
        ff_recv,
        {2: ff_pieces.at[0], 3: ff_pieces.at[1]},
    )
    own_copies = [
        pltpu.make_async_copy(
            in_own.at[part, pl.ds(head * 48, 48)] if part < 3 else out_own.at[pl.ds(head * 48, 48)],
            in_all.at[0, head, pl.ds(part * 48, 48)],
            own_sem.at[part * 4 + head],
        )
        for part in range(4)
        for head in range(4)
    ]
    local_bias = pltpu.make_async_copy(bias_own, bias_all.at[0], local_sem.at[1])
    out_in = pltpu.make_async_copy(in_all, in_out, local_sem.at[2])
    out_bias = pltpu.make_async_copy(bias_all, bias_out, local_sem.at[3])

    def bias_copy(slot):
        return pltpu.make_async_remote_copy(
            src_ref=bias_own,
            dst_ref=bias_all.at[slot],
            send_sem=bias_send.at[slot],
            recv_sem=bias_recv.at[slot],
            device_id=(dp, lax.rem(mp + ways - slot, ways)),
            device_id_type=MESH,
        )

    def begin():
        for copy in own_copies:
            copy.start()
        local_bias.start()
        signal(group_partners())
        for i, rows in enumerate(range(0, tokens_ref.shape[0], BLOCK)):
            if i == 2:
                meet(group_partners())
                for copy in own_copies:
                    copy.wait()
                gin.along(1)
            block = slice(rows, rows + BLOCK)
            first_ref[block] = layer_norm(
                tokens_ref[block].astype(F32), vector_ref[4:5], vector_ref[5:6]
            ).astype(BF16)
        local_bias.wait()

    def end():
        gff.complete(1)
        gff.arrived(2, 0)
        gff.arrived(3, 0, 9)
        out_in.wait()
        out_bias.wait()
        for slot in (1, 2, 3):
            bias_copy(slot).wait_send()
        gin.finish((1, 2, 3))
        gff.finish((1,), range(10))
        gff.finish((2,), (0,))
        gff.finish((3,), (0, 9))

    hook = hooks_of(
        {
            (0, "begin"): [begin],
            (0, "heads"): [
                lambda: gin.spread(1),
                lambda: gin.along(3),
                lambda: gin.along(2),
                lambda: [bias_copy(slot).start() for slot in (1, 2, 3)],
            ],
            (0, 2): [lambda: gin.forward(1)],
            (0, "end"): [lambda: gin.last(1), lambda: gin.spread(3)],
            (1, "begin"): [
                lambda: [bias_copy(slot).wait_recv() for slot in (1, 2, 3)],
                lambda: gin.complete(1),
            ],
            (1, "heads"): [lambda: gin.spread(2), lambda: gff.along(1)],
            (1, 1): [lambda: gin.forward(3)],
            (1, 3): [lambda: gin.last(3), lambda: gin.forward(2)],
            (2, "begin"): [lambda: gin.last(2), lambda: gin.complete(3)],
            (2, "heads"): [lambda: gff.spread(1), lambda: gff.along(3), lambda: gff.along(2)],
            (3, "begin"): [
                lambda: gin.complete(2),
                out_in.start,
                out_bias.start,
                lambda: gff.forward(1),
            ],
            (3, 2): [lambda: gff.last(1)],
            (3, "end"): [end],
        },
        step,
    )
    slot = slot_order(step)
    hook("begin")
    bias_t = bias_all[slot, :, 0:256].T
    for part in range(4):
        product = nt(in_all[slot, part, :IN_ROWS], first_ref[...])
        qkv_ref[part * IN_ROWS : (part + 1) * IN_ROWS, :] = (
            product + bias_t[:IN_ROWS, part : part + 1]
        ).astype(BF16)
    hook("heads")

    def one_head(head, carry):
        hook(None, head)
        attend_head(
            qkv_ref.at[pl.ds(pl.multiple_of(head * IN_ROWS, 16), IN_ROWS)],
            mixed_ref.at[pl.ds(pl.multiple_of(head * 48, 16), 48)],
            logsum_ref.at[head],
        )
        return carry

    lax.fori_loop(0, 4, one_head, 0)
    hook("end")


def slot_order(turn):
    return turn + (turn // 2) * (1 - 2 * (turn % 2))


def attend(tokens, vectors, in_own, out_own, up_own, down_own, bias_own):
    rows, width = tokens.shape
    heads = 16
    anywhere = pl.BlockSpec(memory_space=pl.ANY)
    dma = pltpu.SemaphoreType.DMA
    return pl.pallas_call(
        attend_kernel,
        grid=(4,),
        in_specs=[
            pl.BlockSpec((rows, width), lambda s: (0, 0), pipeline_mode=pl.Buffered(1)),
            pl.BlockSpec((8, width), lambda s: (0, 0)),
            anywhere,
            anywhere,
            anywhere,
            anywhere,
            anywhere,
        ],
        out_specs=[
            pl.BlockSpec((4 * IN_ROWS, rows), lambda s: (slot_order(s), 0)),
            pl.BlockSpec((4 * 48, rows), lambda s: (slot_order(s), 0)),
            pl.BlockSpec((4, 1, rows), lambda s: (slot_order(s), 0, 0)),
            pl.BlockSpec((rows, width), lambda s: (0, 0)),
            anywhere,
            anywhere,
            anywhere,
            anywhere,
        ],
        out_shape=[
            jax.ShapeDtypeStruct((heads * IN_ROWS, rows), BF16),
            jax.ShapeDtypeStruct((heads * 48, rows), BF16),
            jax.ShapeDtypeStruct((heads, 1, rows), F32),
            jax.ShapeDtypeStruct((rows, width), BF16),
            jax.ShapeDtypeStruct((4, 4, HEAD_ROWS, width), BF16),
            jax.ShapeDtypeStruct((8, 192, width), BF16),
            jax.ShapeDtypeStruct((2, 192, width), BF16),
            jax.ShapeDtypeStruct((4, 8, 1024), F32),
        ],
        scratch_shapes=[
            pltpu.VMEM((4, 4, HEAD_ROWS, width), BF16),
            pltpu.VMEM((4, 8, 1024), F32),
            dma((4 * GATHER_KINDS,)),
            dma((4 * GATHER_KINDS,)),
            dma((4 * GATHER_KINDS,)),
            dma((4 * GATHER_KINDS,)),
            dma((4,)),
            dma((4,)),
            dma((16,)),
            dma((4,)),
        ],
        compiler_params=pltpu.CompilerParams(
            vmem_limit_bytes=62 << 20, collective_id=0, has_side_effects=True
        ),
        cost_estimate=pl.CostEstimate(
            flops=30_000_000_000, bytes_accessed=30_000_000, transcendentals=19_000_000
        ),
        name="attend",
    )(tokens, vectors, in_own, out_own, up_own, down_own, bias_own)


class Reduce:
    def __init__(self, slot, other, total, got, split, send, recv):
        self.slot, self.other, self.total, self.got, self.split = slot, other, total, got, split
        self.send, self.recv = send, recv
        self.dp, self.base, self.y, self.x, self.core, self.mp = place()

    def copy(self, kind):
        y, x, core = self.y, self.x, self.core
        first, late = pl.ds(0, self.split), pl.ds(self.split, self.total.shape[2] - self.split)
        got = self.got
        near = lambda y, x, core: (self.base + 4 * y + 2 * x + core, self.mp)
        to_x, to_y = near(y, flip(x), core), near(flip(y), x, core)
        src, dst, device = {
            0: lambda: (self.other, got[0], near(y, x, flip(core))),
            1: lambda: (self.total.at[:, flip(x), first], got[1], to_x),
            2: lambda: (self.total.at[flip(y), :, late], got[2], to_y),
            3: lambda: (self.total.at[flip(y), x, first], got[3], to_y),
            4: lambda: (self.total.at[y, flip(x), late], got[4], to_x),
            5: lambda: (
                self.total.at[y, x],
                got[5],
                (self.dp, lax.rem(self.mp + self.slot, lax.axis_size("mp"))),
            ),
        }[kind]()
        index = kind * 4 + self.slot
        return pltpu.make_async_remote_copy(
            src_ref=src,
            dst_ref=dst,
            send_sem=self.send.at[index],
            recv_sem=self.recv.at[index],
            device_id=device,
            device_id_type=MESH,
        )

    def cores(self):
        self.copy(0).start()

    def chips(self):
        self.copy(0).wait_recv()
        for y in range(2):
            for x in range(2):
                self.total[y, x] = add(self.total[y, x], self.got[0][y, x])
        self.copy(1).start()
        self.copy(2).start()

    def chips_again(self):
        x, y, split = self.x, self.y, self.split
        self.copy(1).wait_recv()
        for i in range(2):
            self.total[i, x, :split] = add(self.total[i, x, :split], self.got[1][i])
        self.copy(2).wait_recv()
        for i in range(2):
            self.total[y, i, split:] = add(self.total[y, i, split:], self.got[2][i])
        self.copy(3).start()
        self.copy(4).start()

    def settle(self):
        x, y, split = self.x, self.y, self.split
        self.copy(3).wait_recv()
        self.total[y, x, :split] = add(self.total[y, x, :split], self.got[3][...])
        self.copy(4).wait_recv()
        self.total[y, x, split:] = add(self.total[y, x, split:], self.got[4][...])

    def along(self):
        self.settle()
        if self.slot:
            self.copy(5).start()

    def finish(self, kinds=6):
        for kind in range(kinds if self.slot else 5):
            self.copy(kind).wait_send()

    def result(self):
        if self.slot:
            self.copy(5).wait_recv()
            return self.got[5][...].astype(F32)
        return self.total[self.y, self.x].astype(F32)


REDUCE_KINDS = 6


def add(left, right):
    return (left.astype(F32) + right.astype(F32)).astype(BF16)


def other_bit(index, bit):
    return index + bit * (1 - 2 * lax.rem(index // bit, 2))


def wider_bits():
    bits, bit = [], GROUP
    while bit < lax.axis_size("dp"):
        bits.append(bit)
        bit *= 2
    return bits


class Share:
    def __init__(self, pieces, split, send, recv):
        self.inner = Gather(None, None, ff_piece, split, send, recv)
        self.pieces = pieces

    def copy(self, kind):
        return self.inner.shared(kind, self.pieces, kind)

    def start(self, *kinds):
        for kind in kinds:
            self.copy(kind).start()

    def arrived(self, *kinds):
        for kind in kinds:
            self.copy(kind).wait_recv()

    def spread(self):
        self.start(1, 2, 5)

    def forward(self):
        self.arrived(1)
        self.start(3, 6)
        self.arrived(2)
        self.start(4, 7)

    def last(self):
        self.arrived(3, 4)
        self.start(8)

    def finish(self):
        self.arrived(5, 6, 7, 8)
        for kind in range(1, 9):
            self.copy(kind).wait_send()


class Wide:
    def __init__(self, held, send, recv):
        self.held, self.send, self.recv = held, send, recv

    def copy(self, i, bit):
        dp, mp = lax.axis_index("dp"), lax.axis_index("mp")
        return pltpu.make_async_remote_copy(
            src_ref=self.held.at[2 * i],
            dst_ref=self.held.at[2 * i + 1],
            send_sem=self.send.at[i],
            recv_sem=self.recv.at[i],
            device_id=(other_bit(dp, bit), mp),
            device_id_type=MESH,
        )

    def sum(self, total):
        for i, bit in enumerate(wider_bits()):
            self.held[2 * i] = total.astype(BF16)
            self.copy(i, bit).start()
            self.copy(i, bit).wait()
            total = total + self.held[2 * i + 1].astype(F32)
        return total


def reduce_scratch(slots, rows, split, width):
    dma = pltpu.SemaphoreType.DMA
    late = rows - split
    return [
        pltpu.VMEM((slots, 2, 2, rows, width), BF16),
        pltpu.VMEM((slots, 2, split, width), BF16),
        pltpu.VMEM((slots, 2, late, width), BF16),
        pltpu.VMEM((slots, split, width), BF16),
        pltpu.VMEM((slots, late, width), BF16),
        pltpu.VMEM((slots, rows, width), BF16),
        dma((4 * REDUCE_KINDS,)),
        dma((4 * REDUCE_KINDS,)),
    ]


REDUCE_REFS = 8


def reduces_of(slots, other, total, scratch, split):
    *got, send, recv = scratch
    return {
        slot: Reduce(slot, other(i), total(i), [ref.at[i] for ref in got], split, send, recv)
        for i, slot in enumerate(slots)
    }


def share_scratch(rows, width):
    dma = pltpu.SemaphoreType.DMA
    wide = max(len(wider_bits()), 1)
    return [
        pltpu.VMEM((8, rows, width), BF16),
        pltpu.VMEM((2 * wide, rows, width), BF16),
        dma((GATHER_KINDS,)),
        dma((GATHER_KINDS,)),
        dma((wide,)),
        dma((wide,)),
    ]


SHARE_REFS = 6


class Sums:
    def __init__(self, direct, held, got, along_got, send, recv, along_send, along_recv):
        self.direct, self.held, self.got, self.along_got = direct, held, got, along_got
        self.send, self.recv, self.along_send, self.along_recv = send, recv, along_send, along_recv
        self.dp, self.base, self.y, self.x, self.core, self.mp = place()
        self.bits = ([] if direct else [1, 2, 4]) + wider_bits()
        self.near = GROUP - 1 if direct else 0

    def copy(self, src, index, device):
        return pltpu.make_async_remote_copy(
            src_ref=self.held.at[src],
            dst_ref=self.got.at[index],
            send_sem=self.send.at[index],
            recv_sem=self.recv.at[index],
            device_id=(device, self.mp),
            device_id_type=MESH,
        )

    def near_copy(self, k):
        return self.copy(0, k, self.base + near_index(self.y, self.x, self.core, k + 1))

    def bit_copy(self, i):
        first = 1 if self.direct else 0
        return self.copy(first + i, self.near + i, other_bit(self.dp, self.bits[i]))

    def along_copy(self, slot):
        return pltpu.make_async_remote_copy(
            src_ref=self.held.at[self.last()],
            dst_ref=self.along_got.at[slot - 1],
            send_sem=self.along_send.at[slot - 1],
            recv_sem=self.along_recv.at[slot - 1],
            device_id=(self.dp, lax.rem(self.mp + slot, lax.axis_size("mp"))),
            device_id_type=MESH,
        )

    def last(self):
        return len(self.bits) + (1 if self.direct else 0)

    def start(self):
        if self.direct:
            for k in range(self.near):
                self.near_copy(k).start()
        else:
            self.bit_copy(0).start()

    def step(self, i):
        first = 1 if self.direct else 0
        self.bit_copy(i).wait_recv()
        self.held[first + i + 1] = self.held[first + i] + self.got[self.near + i]
        if i + 1 < len(self.bits):
            self.bit_copy(i + 1).start()

    def join(self, begin=0):
        if self.direct:
            total = self.held[0]
            for k in range(self.near):
                self.near_copy(k).wait_recv()
                total = total + self.got[k]
            self.held[1] = total
            if self.bits:
                self.bit_copy(0).start()
        for i in range(begin, len(self.bits)):
            self.step(i)
        for slot in (1, 2, 3):
            self.along_copy(slot).start()

    def result(self):
        return self.held[self.last()]

    def arrived(self, slot):
        self.along_copy(slot).wait_recv()
        return self.along_got[slot - 1]

    def finish(self):
        for k in range(self.near):
            self.near_copy(k).wait_send()
        for i in range(len(self.bits)):
            self.bit_copy(i).wait_send()
        for slot in (1, 2, 3):
            self.along_copy(slot).wait_send()


SUMS_REFS = 7


def sums_scratch(direct, rows, width):
    dma = pltpu.SemaphoreType.DMA
    stages = (GROUP - 1 if direct else 3) + len(wider_bits())
    return [
        pltpu.VMEM(((1 if direct else 3) + len(wider_bits()) + 1, rows, width), F32),
        pltpu.VMEM((stages, rows, width), F32),
        pltpu.VMEM((3, rows, width), F32),
        dma((stages,)),
        dma((stages,)),
        dma((3,)),
        dma((3,)),
    ]


def attend_back_head(qkv_ref, back_ref, mixed_ref, logsum_ref, out_ref, held):
    rows = {}

    def score(start, length, first, chunk):
        if start not in rows:
            whole = slice(start, start + length)
            key_t = qkv_ref[48:96, whole]
            rows[start] = (key_t, key_t.T, qkv_ref[96:144, whole].T)
        cols = slice(first, first + chunk)
        return (
            nn(rows[start][1], qkv_ref[0:48, cols]),
            nn(rows[start][2], back_ref[:, cols]),
        )

    def soften(item, scores, back_probs):
        cols = slice(item[2], item[2] + item[3])
        inner = jnp.sum(
            back_ref[:, cols].astype(F32) * mixed_ref[:, cols].astype(F32), axis=0, keepdims=True
        )
        probs = jnp.exp2(scores * SCALE_LOG2 - logsum_ref[:, cols])
        return probs.astype(BF16), (probs * (back_probs - inner)).astype(BF16)

    def pull(item, probs, back_scores):
        start, length, first, chunk = item
        cols, whole = slice(first, first + chunk), slice(start, start + length)
        query_t, back_t = qkv_ref[0:48, cols], back_ref[:, cols]
        out_ref[0:48, cols] = (nn(rows[start][0], back_scores) * SCALE).astype(BF16)
        back_key = nt(query_t, back_scores)
        back_value = nt(back_t, probs)
        if first > start:
            back_key = back_key + held[0:48, 0:length]
            back_value = back_value + held[48:96, 0:length]
        if first + chunk < start + length:
            held[0:48, 0:length] = back_key
            held[48:96, 0:length] = back_value
        else:
            out_ref[48:96, whole] = (back_key * SCALE).astype(BF16)
            out_ref[96:144, whole] = back_value.astype(BF16)

    items = chunks_of(IMAGES, BACK_CHUNK)
    early = {0: score(*items[0])}
    for i in range(len(items)):
        if i + 1 < len(items):
            early[i + 1] = score(*items[i + 1])
        pull(items[i], *soften(items[i], *early.pop(i)))


def attend_back_kernel(
    qkv_ref,
    back_ref,
    mixed_ref,
    logsum_ref,
    first_any,
    out_grad_ref,
    ff_part_ref,
    in_any,
    tokens_ref,
    resid_ref,
    vector_ref,
    feed_small_ref,
    up_sums_ref,
    ff_grad,
    input_ref,
    small_ref,
    up_out,
    down_out,
    in_out,
    out_out,
    held,
    ff_total,
    grads,
    back_qkv,
    turned,
    first_ref,
    in_ref,
    local,
    *scratch,
    blocks,
):
    step = pl.program_id(0)
    width = tokens_ref.shape[1]
    dp, base, y, x, core, mp = place()
    early, scratch = Sums(False, *scratch[:SUMS_REFS]), scratch[SUMS_REFS:]
    late, scratch = Sums(True, *scratch[:SUMS_REFS]), scratch[SUMS_REFS:]
    sums, late_sums = early.held, late.held
    ff_scratch, scratch = scratch[:REDUCE_REFS], scratch[REDUCE_REFS:]
    in_scratch, scratch = scratch[:REDUCE_REFS], scratch[REDUCE_REFS:]
    ff_final, ff_wide, *ff_sems = scratch[:SHARE_REFS]
    in_final, in_wide, *in_sems = scratch[SHARE_REFS:]
    ff = reduces_of(
        (2, 3),
        lambda i: ff_grad.at[i, :, :, flip(core)],
        lambda i: ff_total.at[i],
        ff_scratch,
        96,
    )
    ins = reduces_of(
        (0, 1, 2, 3),
        lambda i: grads.at[i, :, :, flip(core)],
        lambda i: grads.at[i, :, :, core],
        in_scratch,
        48,
    )
    ff_share = Share(ff_final, 96, *ff_sems[:2])
    in_share = Share(in_final, 48, *in_sems[:2])
    me = 4 * y + 2 * x + core

    def own(i):
        return pltpu.make_async_copy(ff_grad.at[i, :, :, core], ff_total.at[i], local.at[i])

    up_written = pltpu.make_async_copy(ff_final.at[:, pl.ds(0, 96)], up_out, local.at[2])
    down_written = pltpu.make_async_copy(turned, down_out, local.at[3])

    def in_written():
        copies = []
        for head in range(4):
            rows = pl.ds(48 * head, 48)
            for part in range(4):
                src = in_final.at[2 * head + part // 2, pl.ds(48 * (part % 2), 48)]
                dst = in_out.at[part, rows] if part < 3 else out_out.at[rows]
                copies.append(pltpu.make_async_copy(src, dst, local.at[4 + 4 * head + part]))
        return copies

    first_read = pltpu.make_async_copy(first_any, first_ref, local.at[20])
    in_read = pltpu.make_async_copy(in_any, in_ref, local.at[21])

    def begin():
        own(0).start()
        own(1).start()
        first_read.start()
        in_read.start()
        signal(every_partner())
        sums[0] = jnp.zeros_like(sums[0])
        late_sums[0] = jnp.zeros_like(late_sums[0])
        sums[0, 0:8, :] = feed_small_ref[...]
        sums[0, 4:6, :] = up_sums_ref[0:2, :]

    def chips(slot):
        own(slot - 2).wait()
        ff[slot].chips()

    def finish_ff():
        total = ff_part_ref[...] + ff[2].result() + ff[3].result()
        ff_final[me] = Wide(ff_wide, *ff_sems[2:]).sum(total).astype(BF16)
        ff_share.spread()

    def write_ff():
        ff_share.finish()
        up_written.start()
        turned[...] = ff_final[:, 96:].reshape(width, width).T
        down_written.start()

    def finish_in():
        ins[0].along()
        total = ins[0].result() + ins[1].result() + ins[2].result() + ins[3].result()
        in_final[me] = Wide(in_wide, *in_sems[2:]).sum(total).astype(BF16)
        in_share.spread()

    def late_start():
        late.start()
        in_share.forward()

    def end_early():
        small_ref[0:12] = early.result()[0:12]
        for slot in (1, 2, 3):
            more = early.arrived(slot)
            small_ref[0:4] += more[0:4]
            small_ref[4:5] += more[4 + slot : 5 + slot]
            small_ref[8:9] += more[8 + slot : 9 + slot]

    def end():
        late_start()
        late.join()
        in_share.last()
        in_share.finish()
        for copy in in_written():
            copy.start()
        total = late.result() + late.arrived(1) + late.arrived(2) + late.arrived(3)
        third = width // 3
        for i in range(3):
            part = slice(third * i, third * (i + 1))
            small_ref[12:13, part] = total[i : i + 1]
            small_ref[13:14, part] = total[3 + i : 4 + i]
        early.finish()
        late.finish()
        for reduce in [*ff.values(), *ins.values()]:
            reduce.finish()
        up_written.wait()
        down_written.wait()
        for copy in in_written():
            copy.wait()

    hook = hooks_of(
        {
            (0, 0): [begin],
            (0, "grads"): [first_read.wait],
            (0, 1): [lambda: meet(every_partner()), ff[2].cores, ff[3].cores],
            (0, 2): [lambda: chips(2)],
            (1, 0): [ff[2].chips_again, lambda: chips(3), ins[2].cores],
            (1, 2): [ff[2].along],
            (1, 3): [ff[3].chips_again, ins[2].chips],
            (2, 0): [ff[3].along, ins[1].cores],
            (2, 1): [ins[2].chips_again, ins[1].chips],
            (2, 3): [ins[2].along, ins[1].chips_again],
            (3, 0): [finish_ff, ins[1].along, ins[3].cores],
            (3, 1): [ins[3].chips],
            (3, 3): [ff_share.forward, ins[3].chips_again],
            (4, "begin"): [in_read.wait, ins[0].cores, early.start, ins[3].along],
            (5, "begin"): [ins[0].chips, ff_share.last, lambda: early.step(0)],
            (6, "begin"): [write_ff, lambda: early.step(1)],
            (6, "end"): [ins[0].chips_again],
            (7, "begin"): [lambda: early.join(2)],
            (7, "end"): [finish_in],
            (9, "begin"): [end_early],
            (9, "end"): [end],
        },
        step,
    )

    @pl.when(step < 4)
    def _():
        slot = back_order(step)

        def one_head(head, carry):
            hook(None, head)
            of_head = pl.ds(pl.multiple_of(head * IN_ROWS, 16), IN_ROWS)
            own_head = pl.ds(pl.multiple_of(head * 48, 16), 48)
            out_rows = pl.ds(pl.multiple_of((4 * slot + head) * IN_ROWS, 16), IN_ROWS)
            attend_back_head(
                qkv_ref.at[of_head],
                back_ref.at[own_head],
                mixed_ref.at[own_head],
                logsum_ref.at[head],
                back_qkv.at[out_rows],
                held,
            )
            return carry

        lax.fori_loop(0, 4, one_head, 0)
        hook("grads")
        for head in range(4):
            rows = back_qkv[pl.ds(pl.multiple_of((4 * slot + head) * IN_ROWS, 16), IN_ROWS), :]
            grad = nn(rows, first_ref[...]).astype(BF16)
            grads[slot, head // 2, head % 2, 0] = grad[:96]
            grads[slot, head // 2, head % 2, 1, 0:48] = grad[96:]
            grads[slot, head // 2, head % 2, 1, 48:96] = out_grad_ref[0, head]
        rows = back_qkv[pl.ds(pl.multiple_of(4 * slot * IN_ROWS, 16), 4 * IN_ROWS), :]
        row_sums = nt(jnp.ones((8, rows.shape[1]), BF16), rows)
        sums[0, pl.ds(8 + slot, 1), 0 : 4 * IN_ROWS] = row_sums[0:1]

    @pl.when(step >= 4)
    def _():
        hook("begin")
        inputs = tokens_ref[...].astype(F32)
        scaled, inverse = normed(inputs)
        cols = pl.ds(pl.multiple_of((step - 4) * BLOCK, BLOCK), BLOCK)
        back_first = None
        for slot in range(4):
            weight = in_ref[slot, :, :IN_ROWS].reshape(4 * IN_ROWS, width)
            part = tn(back_qkv[slot * 4 * IN_ROWS : (slot + 1) * 4 * IN_ROWS, cols], weight)
            back_first = part if slot == 0 else back_first + part
        gain_sum = jnp.sum(back_first * scaled, axis=0, keepdims=True)
        shift_sum = jnp.sum(back_first, axis=0, keepdims=True)
        third = width // 3
        for i in range(3):
            part = slice(third * i, third * (i + 1))
            late_sums[0, i : i + 1] += gain_sum[:, part]
            late_sums[0, 3 + i : 4 + i] += shift_sum[:, part]
        back_norm = back_first * vector_ref[4:5, :]
        input_ref[...] = resid_ref[...] + inverse * (
            back_norm
            - jnp.mean(back_norm, axis=-1, keepdims=True)
            - scaled * jnp.mean(back_norm * scaled, axis=-1, keepdims=True)
        )
        hook("end")


def near_index(y, x, core, k):
    y = flip(y) if k & 4 else y
    x = flip(x) if k & 2 else x
    core = flip(core) if k & 1 else core
    return 4 * y + 2 * x + core


def every_partner():
    dp, base, y, x, core, mp = place()
    ways = lax.axis_size("mp")
    return (
        [(dp, lax.rem(mp + k, ways)) for k in (1, 2, 3)]
        + [(base + near_index(y, x, core, k), mp) for k in range(1, GROUP)]
        + [(other_bit(dp, bit), mp) for bit in wider_bits()]
    )


def back_order(turn):
    turn = jnp.minimum(turn, 3)
    return 2 - turn + (turn // 2) * (3 - 2 * (turn // 3))


BLOCK = 256


def attend_back(
    qkv,
    back_mixed,
    mixed,
    logsum,
    first,
    out_grad,
    ff_part,
    in_all,
    tokens,
    resid,
    vectors,
    feed_small,
    up_sums,
    ff_grad,
):
    rows, width = first.shape
    blocks = rows // BLOCK
    anywhere = pl.BlockSpec(memory_space=pl.ANY)
    one = pl.Buffered(1)
    dma = pltpu.SemaphoreType.DMA
    row = pl.BlockSpec((BLOCK, width), lambda s: (jnp.maximum(s - 4, 0), 0))
    small = pl.BlockSpec((8, width), lambda s: (0, 0))
    return pl.pallas_call(
        functools.partial(attend_back_kernel, blocks=blocks),
        grid=(4 + blocks,),
        in_specs=[
            pl.BlockSpec((4 * IN_ROWS, rows), lambda s: (back_order(s), 0)),
            pl.BlockSpec((4 * 48, rows), lambda s: (back_order(s), 0)),
            pl.BlockSpec((4 * 48, rows), lambda s: (back_order(s), 0)),
            pl.BlockSpec((4, 1, rows), lambda s: (back_order(s), 0, 0)),
            anywhere,
            pl.BlockSpec((1, 4, 48, width), lambda s: (back_order(s), 0, 0, 0)),
            pl.BlockSpec((192, width), lambda s: (0, 0), pipeline_mode=one),
            anywhere,
            row,
            row,
            small,
            small,
            small,
            anywhere,
        ],
        out_specs=[
            row,
            pl.BlockSpec((16, width), lambda s: (0, 0)),
            anywhere,
            anywhere,
            anywhere,
            anywhere,
        ],
        out_shape=[
            jax.ShapeDtypeStruct((rows, width), F32),
            jax.ShapeDtypeStruct((16, width), F32),
            jax.ShapeDtypeStruct((8, 96, width), BF16),
            jax.ShapeDtypeStruct((width, width), BF16),
            jax.ShapeDtypeStruct((3, 192, width), BF16),
            jax.ShapeDtypeStruct((192, width), BF16),
        ],
        scratch_shapes=[
            pltpu.VMEM((96, LONG_LEN), F32),
            pltpu.VMEM((2, 2, 2, 192, width), BF16),
            pltpu.VMEM((4, 2, 2, 2, 96, width), BF16),
            pltpu.VMEM((16 * IN_ROWS, rows), BF16),
            pltpu.VMEM((width, width), BF16),
            pltpu.VMEM((rows, width), BF16),
            pltpu.VMEM((4, 4, HEAD_ROWS, width), BF16),
            dma((22,)),
        ]
        + sums_scratch(False, 16, width)
        + sums_scratch(True, 8, width // 3)
        + reduce_scratch(2, 192, 96, width)
        + reduce_scratch(4, 96, 48, width)
        + share_scratch(192, width)
        + share_scratch(96, width),
        compiler_params=pltpu.CompilerParams(
            vmem_limit_bytes=62 << 20, collective_id=1, has_side_effects=True
        ),
        cost_estimate=pl.CostEstimate(
            flops=50_000_000_000, bytes_accessed=50_000_000, transcendentals=19_000_000
        ),
        name="attend_back",
    )(
        qkv,
        back_mixed,
        mixed,
        logsum,
        first,
        out_grad,
        ff_part,
        in_all,
        tokens,
        resid,
        vectors,
        feed_small,
        up_sums,
        ff_grad,
    )


FEED_BLOCKS = 6


def feed_rows(
    second, back_low, slots, ff_refs, bias_ref, act_s, hid_s, rows, width, feed, back_second
):
    for i, slot in enumerate(slots):
        if isinstance(ff_refs[i], tuple):
            up, down = ff_refs[i][0][...], ff_refs[i][1][...]
        else:
            up = ff_refs[i][:, 0:96, :].reshape(width, width)
            down = ff_refs[i][:, 96:192, :].reshape(width, width)
        hidden = nn(second, up) + bias_ref[slot, 0:1, 256:]
        half = 0.5 + 0.5 * lax.erf(hidden * (0.5**0.5))
        act = (hidden * half).astype(BF16)
        slope = half + hidden * (jnp.exp(hidden * hidden * -0.5) * (1.0 / math.sqrt(2 * math.pi)))
        back_hid = (nt(back_low, down) * slope).astype(BF16)
        act_s[i, rows, :] = act
        hid_s[i, rows, :] = back_hid
        fed, pulled = nn(act, down), nt(back_hid, up)
        feed = fed if feed is None else feed + fed
        back_second = pulled if back_second is None else back_second + pulled
    return feed, back_second


def normed(rows_in):
    average = jnp.mean(rows_in, axis=-1, keepdims=True)
    centred = rows_in - average
    inverse = lax.rsqrt(jnp.mean(centred * centred, axis=-1, keepdims=True) + epsilon)
    return centred * inverse, inverse


def live_back(live_ref, grad_ref, step):
    row = step * BLOCK + lax.broadcasted_iota(jnp.int32, (BLOCK, 1), 0)
    limit = jnp.where(
        row < SHORT_ROWS, live_ref[0, 0] * SHORT_LEN, SHORT_ROWS + live_ref[0, 1] * LONG_LEN
    )
    is_live = row < limit
    return is_live, jnp.where(is_live, grad_ref[...].astype(F32), 0.0)


def feed_grads(i, second_t, back_t, act_s, hid_s, ff_grad_ref, up_sum_ref, row, width):
    up = nn(second_t[...], hid_s[i])
    ff_grad_ref[0, :, 0:96, :] = up[:width].astype(BF16).reshape(8, 96, width)
    up_sum_ref[pl.ds(row, 1), :] = up[width : width + 1]
    down = nn(back_t[...], act_s[i])
    ff_grad_ref[0, :, 96:192, :] = down.astype(BF16).reshape(8, 96, width)


def feed_first_kernel(
    live_ref,
    tokens_ref,
    grad_ref,
    mixed_ref,
    out_w_ref,
    own_up_ref,
    own_down_ref,
    near_ref,
    bias_ref,
    vec_ref,
    pieces_ref,
    residual_ref,
    feed_ref,
    back_second_ref,
    ff_grad_ref,
    up_sum_ref,
    ff_late,
    second_t,
    back_t,
    act_s,
    hid_s,
    send,
    recv,
    local,
):
    step = pl.program_id(0)
    width = tokens_ref.shape[1]
    gff = Gather(
        None,
        [None, None, ff_late.at[0], ff_late.at[1]],
        ff_piece,
        96,
        send,
        recv,
        {2: pieces_ref.at[0], 3: pieces_ref.at[1]},
    )
    mine = pltpu.make_async_copy(
        pieces_ref, ff_late.at[:, 4 * gff.y + 2 * gff.x + gff.core], local.at[0]
    )

    def begin():
        signal(group_partners())
        mine.start()
        up_sum_ref[...] = jnp.zeros_like(up_sum_ref)
        second_t[width:, :] = jnp.ones((16, second_t.shape[1]), BF16)

    def end():
        gff.complete(3)
        gff.complete(2)
        gff.finish((2, 3), range(1, 9))
        mine.wait()

    hook = hooks_of(
        {
            (0, "begin"): [begin],
            (1, "begin"): [lambda: meet(group_partners()), lambda: gff.spread(3)],
            (3, "begin"): [lambda: gff.forward(3), lambda: gff.spread(2)],
            (5, "begin"): [lambda: gff.last(3)],
            (6, "begin"): [lambda: gff.forward(2)],
            (7, "begin"): [lambda: gff.last(2)],
            (7, "end"): [end],
        },
        step,
    )
    hook("begin")

    @pl.when(step < FEED_BLOCKS)
    def _():
        out_w = out_w_ref[...].reshape(width, width)
        residual = tokens_ref[...].astype(F32) + tn(mixed_ref[...], out_w) + vec_ref[0:1, :]
        residual_ref[...] = residual
        scaled, _ = normed(residual)
        second = (scaled * vec_ref[1:2, :] + vec_ref[2:3, :]).astype(BF16)
        _, back = live_back(live_ref, grad_ref, step)
        back_low = back.astype(BF16)
        rows = pl.ds(pl.multiple_of(step * BLOCK, BLOCK), BLOCK)
        second_t[0:width, rows] = second.T
        back_t[:, rows] = back_low.T
        feed_ref[...], back_second_ref[...] = feed_rows(
            second,
            back_low,
            (0, 1),
            ((own_up_ref, own_down_ref), near_ref),
            bias_ref,
            act_s,
            hid_s,
            rows,
            width,
            None,
            None,
        )

    @pl.when(step >= FEED_BLOCKS)
    def _():
        i = step - FEED_BLOCKS
        feed_grads(i, second_t, back_t, act_s, hid_s, ff_grad_ref, up_sum_ref, i, width)

    hook("end")


def feed_last_kernel(
    live_ref,
    residual_ref,
    feed_ref,
    back_second_ref,
    grad_ref,
    mixed_ref,
    out_w_ref,
    ff_ref,
    bias_ref,
    vec_ref,
    ff_near_grad,
    output_ref,
    resid_ref,
    back_mixed_ref,
    ff_grad_ref,
    out_grad_ref,
    small_ref,
    part_ref,
    second_t,
    back_t,
    act_s,
    hid_s,
    out_acc,
    ff_total,
    local,
    *scratch,
):
    step = pl.program_id(0)
    width = residual_ref.shape[1]
    dp, base, y, x, core, mp = place()
    ff = reduces_of(
        (0, 1),
        lambda i: ff_near_grad.at[i, :, :, flip(core)],
        lambda i: ff_total.at[i],
        scratch,
        96,
    )

    def own(i):
        return pltpu.make_async_copy(ff_near_grad.at[i, :, :, core], ff_total.at[i], local.at[i])

    def begin():
        own(1).start()
        own(0).start()
        signal(group_partners())
        small_ref[...] = jnp.zeros_like(small_ref)
        second_t[width:, :] = jnp.ones((16, second_t.shape[1]), BF16)

    def chips(slot):
        own(slot).wait()
        ff[slot].chips()

    def end():
        part_ref[...] = ff[0].result() + ff[1].result()
        ff[0].finish()
        ff[1].finish()

    hook = hooks_of(
        {
            (0, "begin"): [begin],
            (1, "begin"): [lambda: meet(group_partners()), ff[1].cores, ff[0].cores],
            (2, "begin"): [lambda: chips(1)],
            (4, "begin"): [ff[1].chips_again, lambda: chips(0)],
            (5, "begin"): [ff[1].along],
            (6, "begin"): [ff[0].chips_again],
            (7, "begin"): [ff[0].along],
            (7, "end"): [end],
        },
        step,
    )
    hook("begin")

    @pl.when(step < FEED_BLOCKS)
    def _():
        out_w = out_w_ref[...].reshape(width, width)
        residual = residual_ref[...]
        scaled, inverse = normed(residual)
        gain = vec_ref[1:2, :]
        second = (scaled * gain + vec_ref[2:3, :]).astype(BF16)
        is_live, back = live_back(live_ref, grad_ref, step)
        back_low = back.astype(BF16)
        rows = pl.ds(pl.multiple_of(step * BLOCK, BLOCK), BLOCK)
        second_t[0:width, rows] = second.T
        back_t[:, rows] = back_low.T
        feed, back_second = feed_rows(
            second,
            back_low,
            (2, 3),
            (ff_ref.at[0], ff_ref.at[1]),
            bias_ref,
            act_s,
            hid_s,
            rows,
            width,
            feed_ref[...],
            back_second_ref[...],
        )
        output_ref[...] = jnp.where(is_live, residual + feed + vec_ref[3:4, :], 0.0).astype(BF16)
        small_ref[1:2, :] += jnp.sum(back_second * scaled, axis=0, keepdims=True)
        small_ref[2:3, :] += jnp.sum(back_second, axis=0, keepdims=True)
        small_ref[3:4, :] += jnp.sum(back, axis=0, keepdims=True)
        back_norm = back_second * gain
        back_resid = back + inverse * (
            back_norm
            - jnp.mean(back_norm, axis=-1, keepdims=True)
            - scaled * jnp.mean(back_norm * scaled, axis=-1, keepdims=True)
        )
        small_ref[0:1, :] += jnp.sum(back_resid, axis=0, keepdims=True)
        resid_ref[...] = back_resid
        branch = back_resid.astype(BF16)
        back_mixed_ref[...] = nt(out_w, branch).astype(BF16)
        part = nn(mixed_ref[...], branch)

        @pl.when(step == 0)
        def _():
            out_acc[...] = part

        @pl.when(step > 0)
        def _():
            out_acc[...] += part

        @pl.when(step == FEED_BLOCKS - 1)
        def _():
            out_grad_ref[...] = out_acc[...].astype(BF16).reshape(out_grad_ref.shape)

    @pl.when(step >= FEED_BLOCKS)
    def _():
        i = step - FEED_BLOCKS
        feed_grads(i, second_t, back_t, act_s, hid_s, ff_grad_ref, small_ref, 6 + i, width)

    hook("end")


def feed_first(
    live, tokens, out_grad, mixed, in_all, up_own, down_own, ff_near, bias_all, vectors, ff_pieces
):
    rows, width = tokens.shape
    anywhere = pl.BlockSpec(memory_space=pl.ANY)
    one = pl.Buffered(1)
    last = FEED_BLOCKS - 1
    row = pl.BlockSpec((BLOCK, width), lambda s: (jnp.minimum(s, last), 0))
    return pl.pallas_call(
        feed_first_kernel,
        grid=(FEED_BLOCKS + 2,),
        in_specs=[
            pl.BlockSpec(memory_space=pltpu.SMEM),
            row,
            row,
            pl.BlockSpec((width, BLOCK), lambda s: (0, jnp.minimum(s, last))),
            pl.BlockSpec((4, 4, 48, width), lambda s: (0, 0, 3, 0), pipeline_mode=one),
            pl.BlockSpec((width, width), lambda s: (0, 0), pipeline_mode=one),
            pl.BlockSpec((width, width), lambda s: (0, 0), pipeline_mode=one),
            pl.BlockSpec((8, 192, width), lambda s: (0, 0, 0), pipeline_mode=one),
            pl.BlockSpec((4, 8, 1024), lambda s: (0, 0, 0), pipeline_mode=one),
            pl.BlockSpec((8, width), lambda s: (0, 0), pipeline_mode=one),
            pl.BlockSpec((2, 192, width), lambda s: (0, 0, 0), pipeline_mode=one),
        ],
        out_specs=[
            row,
            row,
            row,
            pl.BlockSpec(
                (1, 8, 192, width), lambda s: (jnp.maximum(s - FEED_BLOCKS, 0), 0, 0, 0)
            ),
            pl.BlockSpec((8, width), lambda s: (0, 0)),
            anywhere,
        ],
        out_shape=[
            jax.ShapeDtypeStruct((rows, width), F32),
            jax.ShapeDtypeStruct((rows, width), F32),
            jax.ShapeDtypeStruct((rows, width), F32),
            jax.ShapeDtypeStruct((2, 8, 192, width), BF16),
            jax.ShapeDtypeStruct((8, width), F32),
            jax.ShapeDtypeStruct((2, 8, 192, width), BF16),
        ],
        scratch_shapes=[
            pltpu.VMEM((width + 16, rows), BF16),
            pltpu.VMEM((width, rows), BF16),
            pltpu.VMEM((2, rows, width), BF16),
            pltpu.VMEM((2, rows, width), BF16),
            pltpu.SemaphoreType.DMA((4 * GATHER_KINDS,)),
            pltpu.SemaphoreType.DMA((4 * GATHER_KINDS,)),
            pltpu.SemaphoreType.DMA((1,)),
        ],
        compiler_params=pltpu.CompilerParams(
            vmem_limit_bytes=62 << 20, collective_id=3, has_side_effects=True
        ),
        cost_estimate=pl.CostEstimate(
            flops=24_000_000_000, bytes_accessed=45_000_000, transcendentals=5_000_000
        ),
        name="feed_first",
    )(live, tokens, out_grad, mixed, in_all, up_own, down_own, ff_near, bias_all, vectors, ff_pieces)


def feed_last(
    live,
    residual,
    feed,
    back_second,
    out_grad,
    mixed,
    in_all,
    ff_late,
    bias_all,
    vectors,
    ff_near_grad,
):
    rows, width = out_grad.shape
    anywhere = pl.BlockSpec(memory_space=pl.ANY)
    one = pl.Buffered(1)
    last = FEED_BLOCKS - 1
    row = pl.BlockSpec((BLOCK, width), lambda s: (jnp.minimum(s, last), 0))
    column = pl.BlockSpec((width, BLOCK), lambda s: (0, jnp.minimum(s, last)))
    return pl.pallas_call(
        feed_last_kernel,
        grid=(FEED_BLOCKS + 2,),
        in_specs=[
            pl.BlockSpec(memory_space=pltpu.SMEM),
            row,
            row,
            row,
            row,
            column,
            pl.BlockSpec((4, 4, 48, width), lambda s: (0, 0, 3, 0), pipeline_mode=one),
            pl.BlockSpec((2, 8, 192, width), lambda s: (0, 0, 0, 0), pipeline_mode=one),
            pl.BlockSpec((4, 8, 1024), lambda s: (0, 0, 0), pipeline_mode=one),
            pl.BlockSpec((8, width), lambda s: (0, 0), pipeline_mode=one),
            anywhere,
        ],
        out_specs=[
            row,
            row,
            column,
            pl.BlockSpec(
                (1, 8, 192, width), lambda s: (jnp.maximum(s - FEED_BLOCKS, 0), 0, 0, 0)
            ),
            pl.BlockSpec((4, 4, 48, width), lambda s: (0, 0, 0, 0)),
            pl.BlockSpec((8, width), lambda s: (0, 0)),
            pl.BlockSpec((192, width), lambda s: (0, 0)),
        ],
        out_shape=[
            jax.ShapeDtypeStruct((rows, width), BF16),
            jax.ShapeDtypeStruct((rows, width), F32),
            jax.ShapeDtypeStruct((width, rows), BF16),
            jax.ShapeDtypeStruct((2, 8, 192, width), BF16),
            jax.ShapeDtypeStruct((4, 4, 48, width), BF16),
            jax.ShapeDtypeStruct((8, width), F32),
            jax.ShapeDtypeStruct((192, width), F32),
        ],
        scratch_shapes=[
            pltpu.VMEM((width + 16, rows), BF16),
            pltpu.VMEM((width, rows), BF16),
            pltpu.VMEM((2, rows, width), BF16),
            pltpu.VMEM((2, rows, width), BF16),
            pltpu.VMEM((width, width), F32),
            pltpu.VMEM((2, 2, 2, 192, width), BF16),
            pltpu.SemaphoreType.DMA((2,)),
        ]
        + reduce_scratch(2, 192, 96, width),
        compiler_params=pltpu.CompilerParams(
            vmem_limit_bytes=62 << 20, collective_id=4, has_side_effects=True
        ),
        cost_estimate=pl.CostEstimate(
            flops=28_000_000_000, bytes_accessed=55_000_000, transcendentals=5_000_000
        ),
        name="feed_last",
    )(
        live,
        residual,
        feed,
        back_second,
        out_grad,
        mixed,
        in_all,
        ff_late,
        bias_all,
        vectors,
        ff_near_grad.reshape(2, 2, 2, 2, 192, width),
    )


def local(
    tokens,
    out_grad,
    live_images,
    first_gain,
    first_shift,
    project_in,
    query_value_bias,
    project_out,
    output_bias,
    second_gain,
    second_shift,
    up_weight,
    up_bias,
    down_weight,
    down_bias,
):
    width = tokens.shape[1]
    own_heads = project_in.shape[2] // HEAD_DIM
    pair_bias = query_value_bias.astype(F32).reshape(2, own_heads, HEAD_DIM)
    own_bias = jnp.concatenate([pair_bias[0], jnp.zeros_like(pair_bias[0]), pair_bias[1]], axis=1)
    bias_own = jnp.concatenate(
        [
            jnp.pad(own_bias, ((0, 8 - own_heads), (0, 256 - own_bias.shape[1]))),
            jnp.pad(up_bias.astype(F32)[None], ((0, 7), (0, 0))),
        ],
        axis=1,
    )
    row = lax.broadcasted_iota(jnp.int32, (8, width), 0)
    vectors = jnp.zeros((8, width), F32)
    for i, vector in enumerate(
        (output_bias, second_gain, second_shift, down_bias, first_gain, first_shift)
    ):
        vectors = jnp.where(row == i, vector[None], vectors)
    qkv, mixed, logsum, first, in_all, ff_near, ff_pieces, bias_all = attend(
        tokens,
        vectors,
        project_in.transpose(1, 2, 0),
        project_out,
        up_weight.reshape(8, -1, width),
        down_weight.reshape(8, -1, width),
        bias_own,
    )
    residual, feed, back_second, near_grad, up_sums, ff_late = feed_first(
        live_images,
        tokens,
        out_grad,
        mixed,
        in_all,
        up_weight,
        down_weight,
        ff_near,
        bias_all,
        vectors,
        ff_pieces,
    )
    output, resid, back_mixed, late_grad, out_grads, feed_small, ff_part = feed_last(
        live_images,
        residual,
        feed,
        back_second,
        out_grad,
        mixed,
        in_all,
        ff_late,
        bias_all,
        vectors,
        near_grad,
    )
    input_grad, small, grad_up, grad_down, grad_in, grad_out = attend_back(
        qkv,
        back_mixed,
        mixed,
        logsum,
        first,
        out_grads,
        ff_part,
        in_all,
        tokens,
        resid,
        vectors,
        feed_small,
        up_sums,
        late_grad.reshape(2, 2, 2, 2, 192, width),
    )
    grad_up = grad_up.reshape(width, width).astype(F32)
    grad_down, grad_out = grad_down.astype(F32), grad_out.astype(F32)
    grad_in = grad_in.astype(F32).transpose(2, 0, 1)
    pair_sum = small[8, : 4 * IN_ROWS].reshape(own_heads, 3, HEAD_DIM)
    grad_pair = jnp.stack([pair_sum[:, 0].reshape(-1), pair_sum[:, 2].reshape(-1)])
    return (
        output,
        input_grad,
        small[12],
        small[13],
        grad_in,
        grad_pair,
        grad_out,
        small[0],
        small[1],
        small[2],
        grad_up,
        small[4],
        grad_down,
        small[3],
    )


def solution(mesh):
    rows = P(("dp", "mp"), None)
    return jax.shard_map(
        local,
        mesh=mesh,
        in_specs=(
            rows,
            rows,
            rows,
            P(),
            P(),
            P(None, None, "mp"),
            P(None, "mp"),
            P("mp", None),
            P(),
            P(),
            P(),
            P(None, "mp"),
            P("mp"),
            P("mp", None),
            P(),
        ),
        out_specs=(
            rows,
            rows,
            P(),
            P(),
            P(None, None, "mp"),
            P(None, "mp"),
            P("mp", None),
            P(),
            P(),
            P(),
            P(None, "mp"),
            P("mp"),
            P("mp", None),
            P(),
        ),
        check_vma=False,
    )
```

```python
import functools
import math

import jax
import jax.numpy as jnp
from jax import lax
from jax.experimental import pallas as pl
from jax.experimental.pallas import tpu as pltpu
from jax.sharding import PartitionSpec as P

HEAD_DIM = 48
SHORT_LEN = 256
LONG_LEN = 1024
SHORT_SLOTS = 2
LONG_SLOTS = 1
SHORT_ROWS = SHORT_SLOTS * SHORT_LEN
IMAGES = tuple((SHORT_LEN * i, SHORT_LEN) for i in range(SHORT_SLOTS)) + tuple(
    (SHORT_ROWS + LONG_LEN * i, LONG_LEN) for i in range(LONG_SLOTS)
)
SCALE = HEAD_DIM**-0.5
SCALE_LOG2 = SCALE * math.log2(math.e)
BF16 = jnp.bfloat16
F32 = jnp.float32
CHUNK = 512
BACK_CHUNK = 256

epsilon = 1e-05


def layer_norm(rows_in, norm_gain, norm_shift):
    average = jnp.mean(rows_in, axis=-1, keepdims=True)
    centred = rows_in - average
    variance = jnp.mean(centred * centred, axis=-1, keepdims=True)
    return centred * lax.rsqrt(variance + epsilon) * norm_gain + norm_shift


def nn(left, right):
    return lax.dot_general(
        left, right, (((1,), (0,)), ((), ())), preferred_element_type=F32
    )


def nt(left, right):
    return lax.dot_general(
        left, right, (((1,), (1,)), ((), ())), preferred_element_type=F32
    )


def tn(left, right):
    return lax.dot_general(
        left, right, (((0,), (0,)), ((), ())), preferred_element_type=F32
    )


GROUP = 8
MESH = pl.DeviceIdType.MESH
IN_ROWS = 144
HEAD_ROWS = 192


def place():
    dp, mp = lax.axis_index("dp"), lax.axis_index("mp")
    g = lax.rem(dp, GROUP)
    return dp, dp - g, g // 4, lax.rem(g // 2, 2), lax.rem(g, 2), mp


def flip(bit):
    return 1 - bit


class Gather:
    def __init__(self, own, buffers, piece, split, send, recv, pieces=None):
        self.own, self.buffers, self.piece, self.split = own, buffers, piece, split
        self.pieces = pieces or {}
        self.send, self.recv = send, recv
        self.dp, self.base, self.y, self.x, self.core, self.mp = place()

    def device(self, y, x, core):
        return (self.base + 4 * y + 2 * x + core, self.mp)

    def view(self, ref, y, x, core, part=None):
        view = self.piece(ref, 2 * y + x, core)
        if part is None:
            return view
        rows = view.shape[0]
        return view.at[pl.ds(0, self.split)] if part == 0 else view.at[pl.ds(self.split, rows - self.split)]

    def copy(self, kind, slot):
        y, x, core = self.y, self.x, self.core
        mine = (y, x, core)
        buffer = self.buffers[slot]
        if kind in (0, 9):
            ways = lax.axis_size("mp")
            hop = 1 if slot == 2 else slot
            dst = self.pieces[slot] if slot in self.pieces else self.view(buffer, *mine)
            if slot == 2:
                src = self.view(self.buffers[1], *mine)
            elif isinstance(self.own, tuple):
                src = self.view(self.own[kind // 9], *mine)
                dst = dst.at[pl.ds(96 * (kind // 9), 96)]
            else:
                src = self.view(self.own, *mine)
            device = (self.dp, lax.rem(self.mp + ways - hop, ways))
        else:
            return self.shared(kind, buffer, kind * 4 + slot, self.pieces.get(slot))
        return self.remote(src, dst, device, kind * 4 + slot)

    def shared(self, kind, buffer, index, piece=None):
        y, x, core = self.y, self.x, self.core
        mine, near_x, near_y = (y, x, core), (y, flip(x), core), (flip(y), x, core)
        moved, device = {
            1: lambda: (self.view(buffer, *mine), near_x),
            2: lambda: (self.view(buffer, *mine), near_y),
            3: lambda: (self.view(buffer, *near_x, 0), near_y),
            4: lambda: (self.view(buffer, *near_y, 1), near_x),
            5: lambda: (self.view(buffer, *mine), (y, x, flip(core))),
            6: lambda: (self.view(buffer, *near_x), (y, x, flip(core))),
            7: lambda: (self.view(buffer, *near_y), (y, x, flip(core))),
            8: lambda: (self.view(buffer, flip(y), flip(x), core), (y, x, flip(core))),
        }[kind]()
        src = moved if piece is None or kind not in (1, 2, 5) else piece
        return self.remote(src, moved, self.device(*device), index)

    def remote(self, src, dst, device, index):
        return pltpu.make_async_remote_copy(
            src_ref=src,
            dst_ref=dst,
            send_sem=self.send.at[index],
            recv_sem=self.recv.at[index],
            device_id=device,
            device_id_type=MESH,
        )

    def start(self, slot, *kinds):
        for kind in kinds:
            self.copy(kind, slot).start()

    def arrived(self, slot, *kinds):
        for kind in kinds:
            self.copy(kind, slot).wait_recv()

    def along_kinds(self, slot):
        return (0, 9) if isinstance(self.own, tuple) and slot != 2 else (0,)

    def along(self, slot):
        self.start(slot, *self.along_kinds(slot))

    def spread(self, slot):
        if slot not in self.pieces:
            self.arrived(slot, *self.along_kinds(slot))
        self.start(slot, 1, 2, 5)

    def forward(self, slot):
        self.arrived(slot, 1)
        self.start(slot, 3, 6)
        self.arrived(slot, 2)
        self.start(slot, 4, 7)

    def last(self, slot):
        self.arrived(slot, 3, 4)
        self.start(slot, 8)

    def complete(self, slot):
        self.arrived(slot, 5, 6, 7, 8)

    def finish(self, slots, kinds=range(9)):
        for slot in slots:
            for kind in kinds:
                self.copy(kind, slot).wait_send()


GATHER_KINDS = 10


def in_piece(ref, chip, core):
    return ref.at[chip, :, pl.ds(pl.multiple_of(core * 384, 128), 384)]


def ff_piece(ref, chip, core):
    return ref.at[2 * chip + core]


def signal(partners):
    barrier = pltpu.get_barrier_semaphore()
    for partner in partners:
        pl.semaphore_signal(barrier, inc=1, device_id=partner, device_id_type=MESH)


def meet(partners):
    pl.semaphore_wait(pltpu.get_barrier_semaphore(), len(partners))


def chunks_of(images, size):
    return [
        (start, length, first, min(size, length))
        for start, length in images
        for first in range(start, start + length, min(size, length))
    ]


def attend_head(qkv_ref, mixed_ref, logsum_ref):
    held = {}

    def score(start, length, first, chunk):
        if start not in held:
            whole = slice(start, start + length)
            value_t = qkv_ref[96:144, whole]
            held[start] = (
                qkv_ref[48:96, whole].T,
                jnp.concatenate([value_t, jnp.ones((16, length), BF16)], axis=0),
            )
        return nn(held[start][0], qkv_ref[0:48, first : first + chunk])

    def soften(scores):
        top = jnp.max(scores, axis=0, keepdims=True)
        return top, jnp.exp2((scores - top) * SCALE_LOG2).astype(BF16)

    def mix(item, top, weights):
        start, length, first, chunk = item
        cols = slice(first, first + chunk)
        sums = nn(held[start][1], weights)
        total = sums[48:49]
        mixed_ref[:, cols] = (sums[:48] / total).astype(BF16)
        logsum_ref[:, cols] = top * SCALE_LOG2 + jnp.log2(total)

    items = chunks_of(IMAGES, CHUNK)
    early, late = {0: score(*items[0])}, {}
    for i in range(len(items) + 1):
        if i + 1 < len(items):
            early[i + 1] = score(*items[i + 1])
        if i < len(items):
            late[i] = soften(early.pop(i))
        if i > 0:
            mix(items[i - 1], *late.pop(i - 1))


def hooks_of(table, step):
    def hook(name, head=None):
        for (at, where), actions in table.items():
            if where == name if head is None else isinstance(where, int):

                @pl.when(step == at if head is None else (step == at) & (head == where))
                def _(actions=actions):
                    for action in actions:
                        action()

    return hook


def group_partners(wide=False):
    dp, base, y, x, core, mp = place()
    ways = lax.axis_size("mp")
    return (
        [(dp, lax.rem(mp + k, ways)) for k in (1, 2, 3)]
        + [
            (base + 4 * y + 2 * flip(x) + core, mp),
            (base + 4 * flip(y) + 2 * x + core, mp),
            (base + 4 * y + 2 * x + flip(core), mp),
        ]
        + [(other_bit(dp, bit), mp) for bit in wider_bits() if wide]
    )


def attend_kernel(
    tokens_ref,
    vector_ref,
    in_own,
    out_own,
    up_own,
    down_own,
    bias_own,
    qkv_ref,
    mixed_ref,
    logsum_ref,
    first_ref,
    in_out,
    ff_near,
    ff_pieces,
    bias_out,
    in_all,
    bias_all,
    in_send,
    in_recv,
    ff_send,
    ff_recv,
    bias_send,
    bias_recv,
    own_sem,
    local_sem,
):
    step = pl.program_id(0)
    dp, base, y, x, core, mp = place()
    ways = lax.axis_size("mp")
    gin = Gather(in_all.at[0], [in_all.at[k] for k in range(4)], in_piece, 96, in_send, in_recv)
    gff = Gather(
        (up_own, down_own),
        [None, ff_near, None, None],
        ff_piece,
        96,
        ff_send,
        ff_recv,
        {2: ff_pieces.at[0], 3: ff_pieces.at[1]},
    )
    own_copies = [
        pltpu.make_async_copy(
            in_own.at[part, pl.ds(head * 48, 48)] if part < 3 else out_own.at[pl.ds(head * 48, 48)],
            in_all.at[0, head, pl.ds(part * 48, 48)],
            own_sem.at[part * 4 + head],
        )
        for part in range(4)
        for head in range(4)
    ]
    local_bias = pltpu.make_async_copy(bias_own, bias_all.at[0], local_sem.at[1])
    out_in = pltpu.make_async_copy(in_all, in_out, local_sem.at[2])
    out_bias = pltpu.make_async_copy(bias_all, bias_out, local_sem.at[3])

    def bias_copy(slot):
        return pltpu.make_async_remote_copy(
            src_ref=bias_own,
            dst_ref=bias_all.at[slot],
            send_sem=bias_send.at[slot],
            recv_sem=bias_recv.at[slot],
            device_id=(dp, lax.rem(mp + ways - slot, ways)),
            device_id_type=MESH,
        )

    def begin():
        for copy in own_copies:
            copy.start()
        local_bias.start()
        signal(group_partners())
        for i, rows in enumerate(range(0, tokens_ref.shape[0], BLOCK)):
            if i == 2:
                meet(group_partners())
                for copy in own_copies:
                    copy.wait()
                gin.along(1)
            block = slice(rows, rows + BLOCK)
            first_ref[block] = layer_norm(
                tokens_ref[block].astype(F32), vector_ref[4:5], vector_ref[5:6]
            ).astype(BF16)
        local_bias.wait()

    def end():
        gff.complete(1)
        gff.arrived(2, 0)
        gff.arrived(3, 0, 9)
        out_in.wait()
        out_bias.wait()
        for slot in (1, 2, 3):
            bias_copy(slot).wait_send()
        gin.finish((1, 2, 3))
        gff.finish((1,), range(10))
        gff.finish((2,), (0,))
        gff.finish((3,), (0, 9))

    hook = hooks_of(
        {
            (0, "begin"): [begin],
            (0, "heads"): [
                lambda: gin.spread(1),
                lambda: gin.along(3),
                lambda: gin.along(2),
                lambda: [bias_copy(slot).start() for slot in (1, 2, 3)],
            ],
            (0, 2): [lambda: gin.forward(1)],
            (0, "end"): [lambda: gin.last(1), lambda: gin.spread(3)],
            (1, "begin"): [
                lambda: [bias_copy(slot).wait_recv() for slot in (1, 2, 3)],
                lambda: gin.complete(1),
            ],
            (1, "heads"): [lambda: gin.spread(2), lambda: gff.along(1)],
            (1, 1): [lambda: gin.forward(3)],
            (1, 3): [lambda: gin.last(3), lambda: gin.forward(2)],
            (2, "begin"): [lambda: gin.last(2), lambda: gin.complete(3)],
            (2, "heads"): [lambda: gff.spread(1), lambda: gff.along(3), lambda: gff.along(2)],
            (3, "begin"): [
                lambda: gin.complete(2),
                out_in.start,
                out_bias.start,
                lambda: gff.forward(1),
            ],
            (3, 2): [lambda: gff.last(1)],
            (3, "end"): [end],
        },
        step,
    )
    slot = slot_order(step)
    hook("begin")
    bias_t = bias_all[slot, :, 0:256].T
    weight = in_all[slot, :, :IN_ROWS].reshape(4 * IN_ROWS, first_ref.shape[1])
    product = nt(weight, first_ref[...])
    for part in range(4):
        rows = slice(part * IN_ROWS, (part + 1) * IN_ROWS)
        qkv_ref[rows, :] = (product[rows] + bias_t[:IN_ROWS, part : part + 1]).astype(BF16)
    hook("heads")

    def one_head(head, carry):
        hook(None, head)
        attend_head(
            qkv_ref.at[pl.ds(pl.multiple_of(head * IN_ROWS, 16), IN_ROWS)],
            mixed_ref.at[pl.ds(pl.multiple_of(head * 48, 16), 48)],
            logsum_ref.at[head],
        )
        return carry

    lax.fori_loop(0, 4, one_head, 0)
    hook("end")


def slot_order(turn):
    return turn + (turn // 2) * (1 - 2 * (turn % 2))


def attend(tokens, vectors, in_own, out_own, up_own, down_own, bias_own):
    rows, width = tokens.shape
    heads = 16
    anywhere = pl.BlockSpec(memory_space=pl.ANY)
    dma = pltpu.SemaphoreType.DMA
    return pl.pallas_call(
        attend_kernel,
        grid=(4,),
        in_specs=[
            pl.BlockSpec((rows, width), lambda s: (0, 0), pipeline_mode=pl.Buffered(1)),
            pl.BlockSpec((8, width), lambda s: (0, 0)),
            anywhere,
            anywhere,
            anywhere,
            anywhere,
            anywhere,
        ],
        out_specs=[
            pl.BlockSpec((4 * IN_ROWS, rows), lambda s: (slot_order(s), 0)),
            pl.BlockSpec((4 * 48, rows), lambda s: (slot_order(s), 0)),
            pl.BlockSpec((4, 1, rows), lambda s: (slot_order(s), 0, 0)),
            pl.BlockSpec((rows, width), lambda s: (0, 0)),
            anywhere,
            anywhere,
            anywhere,
            anywhere,
        ],
        out_shape=[
            jax.ShapeDtypeStruct((heads * IN_ROWS, rows), BF16),
            jax.ShapeDtypeStruct((heads * 48, rows), BF16),
            jax.ShapeDtypeStruct((heads, 1, rows), F32),
            jax.ShapeDtypeStruct((rows, width), BF16),
            jax.ShapeDtypeStruct((4, 4, HEAD_ROWS, width), BF16),
            jax.ShapeDtypeStruct((8, 192, width), BF16),
            jax.ShapeDtypeStruct((2, 192, width), BF16),
            jax.ShapeDtypeStruct((4, 8, 1024), F32),
        ],
        scratch_shapes=[
            pltpu.VMEM((4, 4, HEAD_ROWS, width), BF16),
            pltpu.VMEM((4, 8, 1024), F32),
            dma((4 * GATHER_KINDS,)),
            dma((4 * GATHER_KINDS,)),
            dma((4 * GATHER_KINDS,)),
            dma((4 * GATHER_KINDS,)),
            dma((4,)),
            dma((4,)),
            dma((16,)),
            dma((4,)),
        ],
        compiler_params=pltpu.CompilerParams(
            vmem_limit_bytes=62 << 20, collective_id=0, has_side_effects=True
        ),
        cost_estimate=pl.CostEstimate(
            flops=30_000_000_000, bytes_accessed=30_000_000, transcendentals=19_000_000
        ),
        name="attend",
    )(tokens, vectors, in_own, out_own, up_own, down_own, bias_own)


class Reduce:
    def __init__(self, slot, other, total, got, split, send, recv):
        self.slot, self.other, self.total, self.got, self.split = slot, other, total, got, split
        self.send, self.recv = send, recv
        self.dp, self.base, self.y, self.x, self.core, self.mp = place()

    def copy(self, kind):
        y, x, core = self.y, self.x, self.core
        first, late = pl.ds(0, self.split), pl.ds(self.split, self.total.shape[2] - self.split)
        got = self.got
        near = lambda y, x, core: (self.base + 4 * y + 2 * x + core, self.mp)
        to_x, to_y = near(y, flip(x), core), near(flip(y), x, core)
        src, dst, device = {
            0: lambda: (self.other, got[0], near(y, x, flip(core))),
            1: lambda: (self.total.at[:, flip(x), first], got[1], to_x),
            2: lambda: (self.total.at[flip(y), :, late], got[2], to_y),
            3: lambda: (self.total.at[flip(y), x, first], got[3], to_y),
            4: lambda: (self.total.at[y, flip(x), late], got[4], to_x),
            5: lambda: (
                self.total.at[y, x],
                got[5],
                (self.dp, lax.rem(self.mp + self.slot, lax.axis_size("mp"))),
            ),
        }[kind]()
        index = kind * 4 + self.slot
        return pltpu.make_async_remote_copy(
            src_ref=src,
            dst_ref=dst,
            send_sem=self.send.at[index],
            recv_sem=self.recv.at[index],
            device_id=device,
            device_id_type=MESH,
        )

    def cores(self):
        self.copy(0).start()

    def chips(self):
        self.copy(0).wait_recv()
        for y in range(2):
            for x in range(2):
                self.total[y, x] = add(self.total[y, x], self.got[0][y, x])
        self.copy(1).start()
        self.copy(2).start()

    def chips_again(self):
        x, y, split = self.x, self.y, self.split
        self.copy(1).wait_recv()
        for i in range(2):
            self.total[i, x, :split] = add(self.total[i, x, :split], self.got[1][i])
        self.copy(2).wait_recv()
        for i in range(2):
            self.total[y, i, split:] = add(self.total[y, i, split:], self.got[2][i])
        self.copy(3).start()
        self.copy(4).start()

    def settle(self):
        x, y, split = self.x, self.y, self.split
        self.copy(3).wait_recv()
        self.total[y, x, :split] = add(self.total[y, x, :split], self.got[3][...])
        self.copy(4).wait_recv()
        self.total[y, x, split:] = add(self.total[y, x, split:], self.got[4][...])

    def along(self):
        self.settle()
        if self.slot:
            self.copy(5).start()

    def finish(self, kinds=6):
        for kind in range(kinds if self.slot else 5):
            self.copy(kind).wait_send()

    def result(self):
        if self.slot:
            self.copy(5).wait_recv()
            return self.got[5][...].astype(F32)
        return self.total[self.y, self.x].astype(F32)


REDUCE_KINDS = 6


def add(left, right):
    return (left.astype(F32) + right.astype(F32)).astype(BF16)


def other_bit(index, bit):
    return index + bit * (1 - 2 * lax.rem(index // bit, 2))


def wider_bits():
    bits, bit = [], GROUP
    while bit < lax.axis_size("dp"):
        bits.append(bit)
        bit *= 2
    return bits


class Share:
    def __init__(self, pieces, split, send, recv):
        self.inner = Gather(None, None, ff_piece, split, send, recv)
        self.pieces = pieces

    def copy(self, kind):
        return self.inner.shared(kind, self.pieces, kind)

    def start(self, *kinds):
        for kind in kinds:
            self.copy(kind).start()

    def arrived(self, *kinds):
        for kind in kinds:
            self.copy(kind).wait_recv()

    def spread(self):
        self.start(1, 2, 5)

    def forward(self):
        self.arrived(1)
        self.start(3, 6)
        self.arrived(2)
        self.start(4, 7)

    def last(self):
        self.arrived(3, 4)
        self.start(8)

    def finish(self):
        self.arrived(5, 6, 7, 8)
        for kind in range(1, 9):
            self.copy(kind).wait_send()


class Wide:
    def __init__(self, held, send, recv):
        self.held, self.send, self.recv = held, send, recv

    def copy(self, i, bit):
        dp, mp = lax.axis_index("dp"), lax.axis_index("mp")
        return pltpu.make_async_remote_copy(
            src_ref=self.held.at[2 * i],
            dst_ref=self.held.at[2 * i + 1],
            send_sem=self.send.at[i],
            recv_sem=self.recv.at[i],
            device_id=(other_bit(dp, bit), mp),
            device_id_type=MESH,
        )

    def sum(self, total):
        for i, bit in enumerate(wider_bits()):
            self.held[2 * i] = total.astype(BF16)
            self.copy(i, bit).start()
            self.copy(i, bit).wait()
            total = total + self.held[2 * i + 1].astype(F32)
        return total


def reduce_scratch(slots, rows, split, width):
    dma = pltpu.SemaphoreType.DMA
    late = rows - split
    return [
        pltpu.VMEM((slots, 2, 2, rows, width), BF16),
        pltpu.VMEM((slots, 2, split, width), BF16),
        pltpu.VMEM((slots, 2, late, width), BF16),
        pltpu.VMEM((slots, split, width), BF16),
        pltpu.VMEM((slots, late, width), BF16),
        pltpu.VMEM((slots, rows, width), BF16),
        dma((4 * REDUCE_KINDS,)),
        dma((4 * REDUCE_KINDS,)),
    ]


REDUCE_REFS = 8


def reduces_of(slots, other, total, scratch, split):
    *got, send, recv = scratch
    return {
        slot: Reduce(slot, other(i), total(i), [ref.at[i] for ref in got], split, send, recv)
        for i, slot in enumerate(slots)
    }


def share_scratch(rows, width):
    dma = pltpu.SemaphoreType.DMA
    wide = max(len(wider_bits()), 1)
    return [
        pltpu.VMEM((8, rows, width), BF16),
        pltpu.VMEM((2 * wide, rows, width), BF16),
        dma((GATHER_KINDS,)),
        dma((GATHER_KINDS,)),
        dma((wide,)),
        dma((wide,)),
    ]


SHARE_REFS = 6


class Sums:
    def __init__(self, direct, held, got, along_got, send, recv, along_send, along_recv):
        self.direct, self.held, self.got, self.along_got = direct, held, got, along_got
        self.send, self.recv, self.along_send, self.along_recv = send, recv, along_send, along_recv
        self.dp, self.base, self.y, self.x, self.core, self.mp = place()
        self.bits = ([] if direct else [1, 2, 4]) + wider_bits()
        self.near = GROUP - 1 if direct else 0

    def copy(self, src, index, device):
        return pltpu.make_async_remote_copy(
            src_ref=self.held.at[src],
            dst_ref=self.got.at[index],
            send_sem=self.send.at[index],
            recv_sem=self.recv.at[index],
            device_id=(device, self.mp),
            device_id_type=MESH,
        )

    def near_copy(self, k):
        return self.copy(0, k, self.base + near_index(self.y, self.x, self.core, k + 1))

    def bit_copy(self, i):
        first = 1 if self.direct else 0
        return self.copy(first + i, self.near + i, other_bit(self.dp, self.bits[i]))

    def along_copy(self, slot):
        return pltpu.make_async_remote_copy(
            src_ref=self.held.at[self.last()],
            dst_ref=self.along_got.at[slot - 1],
            send_sem=self.along_send.at[slot - 1],
            recv_sem=self.along_recv.at[slot - 1],
            device_id=(self.dp, lax.rem(self.mp + slot, lax.axis_size("mp"))),
            device_id_type=MESH,
        )

    def last(self):
        return len(self.bits) + (1 if self.direct else 0)

    def start(self):
        if self.direct:
            for k in range(self.near):
                self.near_copy(k).start()
        else:
            self.bit_copy(0).start()

    def step(self, i):
        first = 1 if self.direct else 0
        self.bit_copy(i).wait_recv()
        self.held[first + i + 1] = self.held[first + i] + self.got[self.near + i]
        if i + 1 < len(self.bits):
            self.bit_copy(i + 1).start()

    def join(self, begin=0):
        if self.direct:
            total = self.held[0]
            for k in range(self.near):
                self.near_copy(k).wait_recv()
                total = total + self.got[k]
            self.held[1] = total
            if self.bits:
                self.bit_copy(0).start()
        for i in range(begin, len(self.bits)):
            self.step(i)
        for slot in (1, 2, 3):
            self.along_copy(slot).start()

    def result(self):
        return self.held[self.last()]

    def arrived(self, slot):
        self.along_copy(slot).wait_recv()
        return self.along_got[slot - 1]

    def finish(self):
        for k in range(self.near):
            self.near_copy(k).wait_send()
        for i in range(len(self.bits)):
            self.bit_copy(i).wait_send()
        for slot in (1, 2, 3):
            self.along_copy(slot).wait_send()


SUMS_REFS = 7


def sums_scratch(direct, rows, width):
    dma = pltpu.SemaphoreType.DMA
    stages = (GROUP - 1 if direct else 3) + len(wider_bits())
    return [
        pltpu.VMEM(((1 if direct else 3) + len(wider_bits()) + 1, rows, width), F32),
        pltpu.VMEM((stages, rows, width), F32),
        pltpu.VMEM((3, rows, width), F32),
        dma((stages,)),
        dma((stages,)),
        dma((3,)),
        dma((3,)),
    ]


def attend_back_head(qkv_ref, back_ref, mixed_ref, logsum_ref, out_ref, held):
    rows = {}

    def score(start, length, first, chunk):
        if start not in rows:
            whole = slice(start, start + length)
            key_t = qkv_ref[48:96, whole]
            rows[start] = (key_t, key_t.T, qkv_ref[96:144, whole].T)
        cols = slice(first, first + chunk)
        return (
            nn(rows[start][1], qkv_ref[0:48, cols]),
            nn(rows[start][2], back_ref[:, cols]),
        )

    def soften(item, scores, back_probs):
        cols = slice(item[2], item[2] + item[3])
        inner = jnp.sum(
            back_ref[:, cols].astype(F32) * mixed_ref[:, cols].astype(F32), axis=0, keepdims=True
        )
        probs = jnp.exp2(scores * SCALE_LOG2 - logsum_ref[:, cols])
        return probs.astype(BF16), (probs * (back_probs - inner)).astype(BF16)

    def pull(item, probs, back_scores):
        start, length, first, chunk = item
        cols, whole = slice(first, first + chunk), slice(start, start + length)
        query_t, back_t = qkv_ref[0:48, cols], back_ref[:, cols]
        out_ref[0:48, cols] = (nn(rows[start][0], back_scores) * SCALE).astype(BF16)
        back_key = nt(query_t, back_scores)
        back_value = nt(back_t, probs)
        if first > start:
            back_key = back_key + held[0:48, 0:length]
            back_value = back_value + held[48:96, 0:length]
        if first + chunk < start + length:
            held[0:48, 0:length] = back_key
            held[48:96, 0:length] = back_value
        else:
            out_ref[48:96, whole] = (back_key * SCALE).astype(BF16)
            out_ref[96:144, whole] = back_value.astype(BF16)

    items = chunks_of(IMAGES, BACK_CHUNK)
    early = {0: score(*items[0])}
    for i in range(len(items)):
        if i + 1 < len(items):
            early[i + 1] = score(*items[i + 1])
        pull(items[i], *soften(items[i], *early.pop(i)))


def attend_back_kernel(
    qkv_ref,
    back_ref,
    mixed_ref,
    logsum_ref,
    first_any,
    out_grad_ref,
    ff_part_ref,
    in_any,
    tokens_ref,
    resid_ref,
    vector_ref,
    feed_small_ref,
    up_sums_ref,
    ff_grad,
    input_ref,
    small_ref,
    up_out,
    down_out,
    in_out,
    out_out,
    held,
    ff_total,
    grads,
    back_qkv,
    turned,
    first_ref,
    in_ref,
    local,
    *scratch,
    blocks,
):
    step = pl.program_id(0)
    width = tokens_ref.shape[1]
    dp, base, y, x, core, mp = place()
    early, scratch = Sums(False, *scratch[:SUMS_REFS]), scratch[SUMS_REFS:]
    late, scratch = Sums(True, *scratch[:SUMS_REFS]), scratch[SUMS_REFS:]
    sums, late_sums = early.held, late.held
    ff_scratch, scratch = scratch[:REDUCE_REFS], scratch[REDUCE_REFS:]
    in_scratch, scratch = scratch[:REDUCE_REFS], scratch[REDUCE_REFS:]
    ff_final, ff_wide, *ff_sems = scratch[:SHARE_REFS]
    in_final, in_wide, *in_sems = scratch[SHARE_REFS:]
    ff = reduces_of(
        (2, 3),
        lambda i: ff_grad.at[i, :, :, flip(core)],
        lambda i: ff_total.at[i],
        ff_scratch,
        96,
    )
    ins = reduces_of(
        (0, 1, 2, 3),
        lambda i: grads.at[i, :, :, flip(core)],
        lambda i: grads.at[i, :, :, core],
        in_scratch,
        48,
    )
    ff_share = Share(ff_final, 96, *ff_sems[:2])
    in_share = Share(in_final, 48, *in_sems[:2])
    me = 4 * y + 2 * x + core

    def own(i):
        return pltpu.make_async_copy(ff_grad.at[i, :, :, core], ff_total.at[i], local.at[i])

    up_written = pltpu.make_async_copy(ff_final.at[:, pl.ds(0, 96)], up_out, local.at[2])
    down_written = pltpu.make_async_copy(turned, down_out, local.at[3])

    def in_written():
        copies = []
        for head in range(4):
            rows = pl.ds(48 * head, 48)
            for part in range(4):
                src = in_final.at[2 * head + part // 2, pl.ds(48 * (part % 2), 48)]
                dst = in_out.at[part, rows] if part < 3 else out_out.at[rows]
                copies.append(pltpu.make_async_copy(src, dst, local.at[4 + 4 * head + part]))
        return copies

    first_read = pltpu.make_async_copy(first_any, first_ref, local.at[20])
    in_read = pltpu.make_async_copy(in_any, in_ref, local.at[21])

    def begin():
        own(0).start()
        own(1).start()
        first_read.start()
        in_read.start()
        signal(every_partner())
        sums[0] = jnp.zeros_like(sums[0])
        late_sums[0] = jnp.zeros_like(late_sums[0])
        sums[0, 0:8, :] = feed_small_ref[...]
        sums[0, 4:6, :] = up_sums_ref[0:2, :]

    def chips(slot):
        own(slot - 2).wait()
        ff[slot].chips()

    def finish_ff():
        total = ff_part_ref[...] + ff[2].result() + ff[3].result()
        ff_final[me] = Wide(ff_wide, *ff_sems[2:]).sum(total).astype(BF16)
        ff_share.spread()

    def write_ff():
        ff_share.finish()
        up_written.start()
        turned[...] = ff_final[:, 96:].reshape(width, width).T
        down_written.start()

    def finish_in():
        ins[0].along()
        total = ins[0].result() + ins[1].result() + ins[2].result() + ins[3].result()
        in_final[me] = Wide(in_wide, *in_sems[2:]).sum(total).astype(BF16)
        in_share.spread()

    def late_start():
        late.start()
        in_share.forward()

    def end_early():
        small_ref[0:12] = early.result()[0:12]
        for slot in (1, 2, 3):
            more = early.arrived(slot)
            small_ref[0:4] += more[0:4]
            small_ref[4:5] += more[4 + slot : 5 + slot]
            small_ref[8:9] += more[8 + slot : 9 + slot]

    def end():
        late_start()
        late.join()
        in_share.last()
        in_share.finish()
        for copy in in_written():
            copy.start()
        total = late.result() + late.arrived(1) + late.arrived(2) + late.arrived(3)
        third = width // 3
        for i in range(3):
            part = slice(third * i, third * (i + 1))
            small_ref[12:13, part] = total[i : i + 1]
            small_ref[13:14, part] = total[3 + i : 4 + i]
        early.finish()
        late.finish()
        for reduce in [*ff.values(), *ins.values()]:
            reduce.finish()
        up_written.wait()
        down_written.wait()
        for copy in in_written():
            copy.wait()

    hook = hooks_of(
        {
            (0, 0): [begin],
            (0, "grads"): [first_read.wait],
            (0, 1): [lambda: meet(every_partner()), ff[2].cores, ff[3].cores],
            (0, 2): [lambda: chips(2)],
            (1, 0): [ff[2].chips_again, lambda: chips(3), ins[2].cores],
            (1, 2): [ff[2].along],
            (1, 3): [ff[3].chips_again, ins[2].chips],
            (2, 0): [ff[3].along, ins[1].cores],
            (2, 1): [ins[2].chips_again, ins[1].chips],
            (2, 3): [ins[2].along, ins[1].chips_again],
            (3, 0): [finish_ff, ins[1].along, ins[3].cores],
            (3, 1): [ins[3].chips],
            (3, 3): [ff_share.forward, ins[3].chips_again],
            (4, "begin"): [in_read.wait, ins[0].cores, early.start, ins[3].along],
            (5, "begin"): [ins[0].chips, ff_share.last, lambda: early.step(0)],
            (6, "begin"): [write_ff, lambda: early.step(1)],
            (6, "end"): [ins[0].chips_again],
            (7, "begin"): [lambda: early.join(2)],
            (7, "end"): [finish_in],
            (9, "begin"): [end_early],
            (9, "end"): [end],
        },
        step,
    )

    @pl.when(step < 4)
    def _():
        slot = back_order(step)

        def one_head(head, carry):
            hook(None, head)
            of_head = pl.ds(pl.multiple_of(head * IN_ROWS, 16), IN_ROWS)
            own_head = pl.ds(pl.multiple_of(head * 48, 16), 48)
            out_rows = pl.ds(pl.multiple_of((4 * slot + head) * IN_ROWS, 16), IN_ROWS)
            attend_back_head(
                qkv_ref.at[of_head],
                back_ref.at[own_head],
                mixed_ref.at[own_head],
                logsum_ref.at[head],
                back_qkv.at[out_rows],
                held,
            )
            return carry

        lax.fori_loop(0, 4, one_head, 0)
        hook("grads")
        rows = back_qkv[pl.ds(pl.multiple_of(4 * slot * IN_ROWS, 16), 4 * IN_ROWS), :]
        slot_grad = nn(rows, first_ref[...]).astype(BF16)
        for head in range(4):
            grad = slot_grad[head * IN_ROWS : (head + 1) * IN_ROWS]
            grads[slot, head // 2, head % 2, 0] = grad[:96]
            grads[slot, head // 2, head % 2, 1, 0:48] = grad[96:]
            grads[slot, head // 2, head % 2, 1, 48:96] = out_grad_ref[0, head]
        row_sums = nt(jnp.ones((8, rows.shape[1]), BF16), rows)
        sums[0, pl.ds(8 + slot, 1), 0 : 4 * IN_ROWS] = row_sums[0:1]

    @pl.when(step >= 4)
    def _():
        hook("begin")
        inputs = tokens_ref[...].astype(F32)
        scaled, inverse = normed(inputs)
        cols = pl.ds(pl.multiple_of((step - 4) * BLOCK, BLOCK), BLOCK)
        back_first = None
        for slot in range(4):
            weight = in_ref[slot, :, :IN_ROWS].reshape(4 * IN_ROWS, width)
            part = tn(back_qkv[slot * 4 * IN_ROWS : (slot + 1) * 4 * IN_ROWS, cols], weight)
            back_first = part if slot == 0 else back_first + part
        gain_sum = jnp.sum(back_first * scaled, axis=0, keepdims=True)
        shift_sum = jnp.sum(back_first, axis=0, keepdims=True)
        third = width // 3
        for i in range(3):
            part = slice(third * i, third * (i + 1))
            late_sums[0, i : i + 1] += gain_sum[:, part]
            late_sums[0, 3 + i : 4 + i] += shift_sum[:, part]
        back_norm = back_first * vector_ref[4:5, :]
        input_ref[...] = resid_ref[...] + inverse * (
            back_norm
            - jnp.mean(back_norm, axis=-1, keepdims=True)
            - scaled * jnp.mean(back_norm * scaled, axis=-1, keepdims=True)
        )
        hook("end")


def near_index(y, x, core, k):
    y = flip(y) if k & 4 else y
    x = flip(x) if k & 2 else x
    core = flip(core) if k & 1 else core
    return 4 * y + 2 * x + core


def every_partner():
    dp, base, y, x, core, mp = place()
    ways = lax.axis_size("mp")
    return (
        [(dp, lax.rem(mp + k, ways)) for k in (1, 2, 3)]
        + [(base + near_index(y, x, core, k), mp) for k in range(1, GROUP)]
        + [(other_bit(dp, bit), mp) for bit in wider_bits()]
    )


def back_order(turn):
    turn = jnp.minimum(turn, 3)
    return 2 - turn + (turn // 2) * (3 - 2 * (turn // 3))


BLOCK = 256


def attend_back(
    qkv,
    back_mixed,
    mixed,
    logsum,
    first,
    out_grad,
    ff_part,
    in_all,
    tokens,
    resid,
    vectors,
    feed_small,
    up_sums,
    ff_grad,
):
    rows, width = first.shape
    blocks = rows // BLOCK
    anywhere = pl.BlockSpec(memory_space=pl.ANY)
    one = pl.Buffered(1)
    dma = pltpu.SemaphoreType.DMA
    row = pl.BlockSpec((BLOCK, width), lambda s: (jnp.maximum(s - 4, 0), 0))
    small = pl.BlockSpec((8, width), lambda s: (0, 0))
    return pl.pallas_call(
        functools.partial(attend_back_kernel, blocks=blocks),
        grid=(4 + blocks,),
        in_specs=[
            pl.BlockSpec((4 * IN_ROWS, rows), lambda s: (back_order(s), 0)),
            pl.BlockSpec((4 * 48, rows), lambda s: (back_order(s), 0)),
            pl.BlockSpec((4 * 48, rows), lambda s: (back_order(s), 0)),
            pl.BlockSpec((4, 1, rows), lambda s: (back_order(s), 0, 0)),
            anywhere,
            pl.BlockSpec((1, 4, 48, width), lambda s: (back_order(s), 0, 0, 0)),
            pl.BlockSpec((192, width), lambda s: (0, 0), pipeline_mode=one),
            anywhere,
            row,
            row,
            small,
            small,
            small,
            anywhere,
        ],
        out_specs=[
            row,
            pl.BlockSpec((16, width), lambda s: (0, 0)),
            anywhere,
            anywhere,
            anywhere,
            anywhere,
        ],
        out_shape=[
            jax.ShapeDtypeStruct((rows, width), F32),
            jax.ShapeDtypeStruct((16, width), F32),
            jax.ShapeDtypeStruct((8, 96, width), BF16),
            jax.ShapeDtypeStruct((width, width), BF16),
            jax.ShapeDtypeStruct((3, 192, width), BF16),
            jax.ShapeDtypeStruct((192, width), BF16),
        ],
        scratch_shapes=[
            pltpu.VMEM((96, LONG_LEN), F32),
            pltpu.VMEM((2, 2, 2, 192, width), BF16),
            pltpu.VMEM((4, 2, 2, 2, 96, width), BF16),
            pltpu.VMEM((16 * IN_ROWS, rows), BF16),
            pltpu.VMEM((width, width), BF16),
            pltpu.VMEM((rows, width), BF16),
            pltpu.VMEM((4, 4, HEAD_ROWS, width), BF16),
            dma((22,)),
        ]
        + sums_scratch(False, 16, width)
        + sums_scratch(True, 8, width // 3)
        + reduce_scratch(2, 192, 96, width)
        + reduce_scratch(4, 96, 48, width)
        + share_scratch(192, width)
        + share_scratch(96, width),
        compiler_params=pltpu.CompilerParams(
            vmem_limit_bytes=62 << 20, collective_id=1, has_side_effects=True
        ),
        cost_estimate=pl.CostEstimate(
            flops=50_000_000_000, bytes_accessed=50_000_000, transcendentals=19_000_000
        ),
        name="attend_back",
    )(
        qkv,
        back_mixed,
        mixed,
        logsum,
        first,
        out_grad,
        ff_part,
        in_all,
        tokens,
        resid,
        vectors,
        feed_small,
        up_sums,
        ff_grad,
    )


FEED_BLOCKS = 6


def feed_rows(
    second, back_low, slots, ff_refs, bias_ref, act_s, hid_s, rows, width, feed, back_second
):
    for i, slot in enumerate(slots):
        if isinstance(ff_refs[i], tuple):
            up, down = ff_refs[i][0][...], ff_refs[i][1][...]
        else:
            up = ff_refs[i][:, 0:96, :].reshape(width, width)
            down = ff_refs[i][:, 96:192, :].reshape(width, width)
        hidden = nn(second, up) + bias_ref[slot, 0:1, 256:]
        half = 0.5 + 0.5 * lax.erf(hidden * (0.5**0.5))
        act = (hidden * half).astype(BF16)
        slope = half + hidden * (jnp.exp(hidden * hidden * -0.5) * (1.0 / math.sqrt(2 * math.pi)))
        back_hid = (nt(back_low, down) * slope).astype(BF16)
        act_s[i, rows, :] = act
        hid_s[i, rows, :] = back_hid
        fed, pulled = nn(act, down), nt(back_hid, up)
        feed = fed if feed is None else feed + fed
        back_second = pulled if back_second is None else back_second + pulled
    return feed, back_second


def normed(rows_in):
    average = jnp.mean(rows_in, axis=-1, keepdims=True)
    centred = rows_in - average
    inverse = lax.rsqrt(jnp.mean(centred * centred, axis=-1, keepdims=True) + epsilon)
    return centred * inverse, inverse


def live_back(live_ref, grad_ref, step):
    row = step * BLOCK + lax.broadcasted_iota(jnp.int32, (BLOCK, 1), 0)
    limit = jnp.where(
        row < SHORT_ROWS, live_ref[0, 0] * SHORT_LEN, SHORT_ROWS + live_ref[0, 1] * LONG_LEN
    )
    is_live = row < limit
    return is_live, jnp.where(is_live, grad_ref[...].astype(F32), 0.0)


def feed_grads(i, second_t, back_t, act_s, hid_s, ff_grad_ref, up_sum_ref, row, width):
    up = nn(second_t[...], hid_s[i])
    ff_grad_ref[0, :, 0:96, :] = up[:width].astype(BF16).reshape(8, 96, width)
    up_sum_ref[pl.ds(row, 1), :] = up[width : width + 1]
    down = nn(back_t[...], act_s[i])
    ff_grad_ref[0, :, 96:192, :] = down.astype(BF16).reshape(8, 96, width)


def feed_first_kernel(
    live_ref,
    tokens_ref,
    grad_ref,
    mixed_ref,
    out_w_ref,
    own_up_ref,
    own_down_ref,
    near_ref,
    bias_ref,
    vec_ref,
    pieces_ref,
    residual_ref,
    feed_ref,
    back_second_ref,
    ff_grad_ref,
    up_sum_ref,
    ff_late,
    second_t,
    back_t,
    act_s,
    hid_s,
    send,
    recv,
    local,
):
    step = pl.program_id(0)
    width = tokens_ref.shape[1]
    gff = Gather(
        None,
        [None, None, ff_late.at[0], ff_late.at[1]],
        ff_piece,
        96,
        send,
        recv,
        {2: pieces_ref.at[0], 3: pieces_ref.at[1]},
    )
    mine = pltpu.make_async_copy(
        pieces_ref, ff_late.at[:, 4 * gff.y + 2 * gff.x + gff.core], local.at[0]
    )

    def begin():
        signal(group_partners())
        mine.start()
        up_sum_ref[...] = jnp.zeros_like(up_sum_ref)
        second_t[width:, :] = jnp.ones((16, second_t.shape[1]), BF16)

    def end():
        gff.complete(3)
        gff.complete(2)
        gff.finish((2, 3), range(1, 9))
        mine.wait()

    hook = hooks_of(
        {
            (0, "begin"): [begin],
            (1, "begin"): [lambda: meet(group_partners()), lambda: gff.spread(3)],
            (3, "begin"): [lambda: gff.forward(3), lambda: gff.spread(2)],
            (5, "begin"): [lambda: gff.last(3)],
            (6, "begin"): [lambda: gff.forward(2)],
            (7, "begin"): [lambda: gff.last(2)],
            (7, "end"): [end],
        },
        step,
    )
    hook("begin")

    @pl.when(step < FEED_BLOCKS)
    def _():
        out_w = out_w_ref[...].reshape(width, width)
        residual = tokens_ref[...].astype(F32) + tn(mixed_ref[...], out_w) + vec_ref[0:1, :]
        residual_ref[...] = residual
        scaled, _ = normed(residual)
        second = (scaled * vec_ref[1:2, :] + vec_ref[2:3, :]).astype(BF16)
        _, back = live_back(live_ref, grad_ref, step)
        back_low = back.astype(BF16)
        rows = pl.ds(pl.multiple_of(step * BLOCK, BLOCK), BLOCK)
        second_t[0:width, rows] = second.T
        back_t[:, rows] = back_low.T
        feed_ref[...], back_second_ref[...] = feed_rows(
            second,
            back_low,
            (0, 1),
            ((own_up_ref, own_down_ref), near_ref),
            bias_ref,
            act_s,
            hid_s,
            rows,
            width,
            None,
            None,
        )

    @pl.when(step >= FEED_BLOCKS)
    def _():
        i = step - FEED_BLOCKS
        feed_grads(i, second_t, back_t, act_s, hid_s, ff_grad_ref, up_sum_ref, i, width)

    hook("end")


def feed_last_kernel(
    live_ref,
    residual_ref,
    feed_ref,
    back_second_ref,
    grad_ref,
    mixed_ref,
    out_w_ref,
    ff_ref,
    bias_ref,
    vec_ref,
    ff_near_grad,
    output_ref,
    resid_ref,
    back_mixed_ref,
    ff_grad_ref,
    out_grad_ref,
    small_ref,
    part_ref,
    second_t,
    back_t,
    act_s,
    hid_s,
    out_acc,
    ff_total,
    local,
    *scratch,
):
    step = pl.program_id(0)
    width = residual_ref.shape[1]
    dp, base, y, x, core, mp = place()
    ff = reduces_of(
        (0, 1),
        lambda i: ff_near_grad.at[i, :, :, flip(core)],
        lambda i: ff_total.at[i],
        scratch,
        96,
    )

    def own(i):
        return pltpu.make_async_copy(ff_near_grad.at[i, :, :, core], ff_total.at[i], local.at[i])

    def begin():
        own(1).start()
        own(0).start()
        signal(group_partners())
        small_ref[...] = jnp.zeros_like(small_ref)
        second_t[width:, :] = jnp.ones((16, second_t.shape[1]), BF16)

    def chips(slot):
        own(slot).wait()
        ff[slot].chips()

    def end():
        part_ref[...] = ff[0].result() + ff[1].result()
        ff[0].finish()
        ff[1].finish()

    hook = hooks_of(
        {
            (0, "begin"): [begin],
            (1, "begin"): [lambda: meet(group_partners()), ff[1].cores, ff[0].cores],
            (2, "begin"): [lambda: chips(1)],
            (4, "begin"): [ff[1].chips_again, lambda: chips(0)],
            (5, "begin"): [ff[1].along],
            (6, "begin"): [ff[0].chips_again],
            (7, "begin"): [ff[0].along],
            (7, "end"): [end],
        },
        step,
    )
    hook("begin")

    @pl.when(step < FEED_BLOCKS)
    def _():
        out_w = out_w_ref[...].reshape(width, width)
        residual = residual_ref[...]
        scaled, inverse = normed(residual)
        gain = vec_ref[1:2, :]
        second = (scaled * gain + vec_ref[2:3, :]).astype(BF16)
        is_live, back = live_back(live_ref, grad_ref, step)
        back_low = back.astype(BF16)
        rows = pl.ds(pl.multiple_of(step * BLOCK, BLOCK), BLOCK)
        second_t[0:width, rows] = second.T
        back_t[:, rows] = back_low.T
        feed, back_second = feed_rows(
            second,
            back_low,
            (2, 3),
            (ff_ref.at[0], ff_ref.at[1]),
            bias_ref,
            act_s,
            hid_s,
            rows,
            width,
            feed_ref[...],
            back_second_ref[...],
        )
        output_ref[...] = jnp.where(is_live, residual + feed + vec_ref[3:4, :], 0.0).astype(BF16)
        small_ref[1:2, :] += jnp.sum(back_second * scaled, axis=0, keepdims=True)
        small_ref[2:3, :] += jnp.sum(back_second, axis=0, keepdims=True)
        small_ref[3:4, :] += jnp.sum(back, axis=0, keepdims=True)
        back_norm = back_second * gain
        back_resid = back + inverse * (
            back_norm
            - jnp.mean(back_norm, axis=-1, keepdims=True)
            - scaled * jnp.mean(back_norm * scaled, axis=-1, keepdims=True)
        )
        small_ref[0:1, :] += jnp.sum(back_resid, axis=0, keepdims=True)
        resid_ref[...] = back_resid
        branch = back_resid.astype(BF16)
        back_mixed_ref[...] = nt(out_w, branch).astype(BF16)
        part = nn(mixed_ref[...], branch)

        @pl.when(step == 0)
        def _():
            out_acc[...] = part

        @pl.when(step > 0)
        def _():
            out_acc[...] += part

        @pl.when(step == FEED_BLOCKS - 1)
        def _():
            out_grad_ref[...] = out_acc[...].astype(BF16).reshape(out_grad_ref.shape)

    @pl.when(step >= FEED_BLOCKS)
    def _():
        i = step - FEED_BLOCKS
        feed_grads(i, second_t, back_t, act_s, hid_s, ff_grad_ref, small_ref, 6 + i, width)

    hook("end")


def feed_first(
    live, tokens, out_grad, mixed, in_all, up_own, down_own, ff_near, bias_all, vectors, ff_pieces
):
    rows, width = tokens.shape
    anywhere = pl.BlockSpec(memory_space=pl.ANY)
    one = pl.Buffered(1)
    last = FEED_BLOCKS - 1
    row = pl.BlockSpec((BLOCK, width), lambda s: (jnp.minimum(s, last), 0))
    return pl.pallas_call(
        feed_first_kernel,
        grid=(FEED_BLOCKS + 2,),
        in_specs=[
            pl.BlockSpec(memory_space=pltpu.SMEM),
            row,
            row,
            pl.BlockSpec((width, BLOCK), lambda s: (0, jnp.minimum(s, last))),
            pl.BlockSpec((4, 4, 48, width), lambda s: (0, 0, 3, 0), pipeline_mode=one),
            pl.BlockSpec((width, width), lambda s: (0, 0), pipeline_mode=one),
            pl.BlockSpec((width, width), lambda s: (0, 0), pipeline_mode=one),
            pl.BlockSpec((8, 192, width), lambda s: (0, 0, 0), pipeline_mode=one),
            pl.BlockSpec((4, 8, 1024), lambda s: (0, 0, 0), pipeline_mode=one),
            pl.BlockSpec((8, width), lambda s: (0, 0), pipeline_mode=one),
            pl.BlockSpec((2, 192, width), lambda s: (0, 0, 0), pipeline_mode=one),
        ],
        out_specs=[
            row,
            row,
            row,
            pl.BlockSpec(
                (1, 8, 192, width), lambda s: (jnp.maximum(s - FEED_BLOCKS, 0), 0, 0, 0)
            ),
            pl.BlockSpec((8, width), lambda s: (0, 0)),
            anywhere,
        ],
        out_shape=[
            jax.ShapeDtypeStruct((rows, width), F32),
            jax.ShapeDtypeStruct((rows, width), F32),
            jax.ShapeDtypeStruct((rows, width), F32),
            jax.ShapeDtypeStruct((2, 8, 192, width), BF16),
            jax.ShapeDtypeStruct((8, width), F32),
            jax.ShapeDtypeStruct((2, 8, 192, width), BF16),
        ],
        scratch_shapes=[
            pltpu.VMEM((width + 16, rows), BF16),
            pltpu.VMEM((width, rows), BF16),
            pltpu.VMEM((2, rows, width), BF16),
            pltpu.VMEM((2, rows, width), BF16),
            pltpu.SemaphoreType.DMA((4 * GATHER_KINDS,)),
            pltpu.SemaphoreType.DMA((4 * GATHER_KINDS,)),
            pltpu.SemaphoreType.DMA((1,)),
        ],
        compiler_params=pltpu.CompilerParams(
            vmem_limit_bytes=62 << 20, collective_id=3, has_side_effects=True
        ),
        cost_estimate=pl.CostEstimate(
            flops=24_000_000_000, bytes_accessed=45_000_000, transcendentals=5_000_000
        ),
        name="feed_first",
    )(live, tokens, out_grad, mixed, in_all, up_own, down_own, ff_near, bias_all, vectors, ff_pieces)


def feed_last(
    live,
    residual,
    feed,
    back_second,
    out_grad,
    mixed,
    in_all,
    ff_late,
    bias_all,
    vectors,
    ff_near_grad,
):
    rows, width = out_grad.shape
    anywhere = pl.BlockSpec(memory_space=pl.ANY)
    one = pl.Buffered(1)
    last = FEED_BLOCKS - 1
    row = pl.BlockSpec((BLOCK, width), lambda s: (jnp.minimum(s, last), 0))
    column = pl.BlockSpec((width, BLOCK), lambda s: (0, jnp.minimum(s, last)))
    return pl.pallas_call(
        feed_last_kernel,
        grid=(FEED_BLOCKS + 2,),
        in_specs=[
            pl.BlockSpec(memory_space=pltpu.SMEM),
            row,
            row,
            row,
            row,
            column,
            pl.BlockSpec((4, 4, 48, width), lambda s: (0, 0, 3, 0), pipeline_mode=one),
            pl.BlockSpec((2, 8, 192, width), lambda s: (0, 0, 0, 0), pipeline_mode=one),
            pl.BlockSpec((4, 8, 1024), lambda s: (0, 0, 0), pipeline_mode=one),
            pl.BlockSpec((8, width), lambda s: (0, 0), pipeline_mode=one),
            anywhere,
        ],
        out_specs=[
            row,
            row,
            column,
            pl.BlockSpec(
                (1, 8, 192, width), lambda s: (jnp.maximum(s - FEED_BLOCKS, 0), 0, 0, 0)
            ),
            pl.BlockSpec((4, 4, 48, width), lambda s: (0, 0, 0, 0)),
            pl.BlockSpec((8, width), lambda s: (0, 0)),
            pl.BlockSpec((192, width), lambda s: (0, 0)),
        ],
        out_shape=[
            jax.ShapeDtypeStruct((rows, width), BF16),
            jax.ShapeDtypeStruct((rows, width), F32),
            jax.ShapeDtypeStruct((width, rows), BF16),
            jax.ShapeDtypeStruct((2, 8, 192, width), BF16),
            jax.ShapeDtypeStruct((4, 4, 48, width), BF16),
            jax.ShapeDtypeStruct((8, width), F32),
            jax.ShapeDtypeStruct((192, width), F32),
        ],
        scratch_shapes=[
            pltpu.VMEM((width + 16, rows), BF16),
            pltpu.VMEM((width, rows), BF16),
            pltpu.VMEM((2, rows, width), BF16),
            pltpu.VMEM((2, rows, width), BF16),
            pltpu.VMEM((width, width), F32),
            pltpu.VMEM((2, 2, 2, 192, width), BF16),
            pltpu.SemaphoreType.DMA((2,)),
        ]
        + reduce_scratch(2, 192, 96, width),
        compiler_params=pltpu.CompilerParams(
            vmem_limit_bytes=62 << 20, collective_id=4, has_side_effects=True
        ),
        cost_estimate=pl.CostEstimate(
            flops=28_000_000_000, bytes_accessed=55_000_000, transcendentals=5_000_000
        ),
        name="feed_last",
    )(
        live,
        residual,
        feed,
        back_second,
        out_grad,
        mixed,
        in_all,
        ff_late,
        bias_all,
        vectors,
        ff_near_grad.reshape(2, 2, 2, 2, 192, width),
    )


def local(
    tokens,
    out_grad,
    live_images,
    first_gain,
    first_shift,
    project_in,
    query_value_bias,
    project_out,
    output_bias,
    second_gain,
    second_shift,
    up_weight,
    up_bias,
    down_weight,
    down_bias,
):
    width = tokens.shape[1]
    own_heads = project_in.shape[2] // HEAD_DIM
    pair_bias = query_value_bias.astype(F32).reshape(2, own_heads, HEAD_DIM)
    own_bias = jnp.concatenate([pair_bias[0], jnp.zeros_like(pair_bias[0]), pair_bias[1]], axis=1)
    bias_own = jnp.concatenate(
        [
            jnp.pad(own_bias, ((0, 8 - own_heads), (0, 256 - own_bias.shape[1]))),
            jnp.pad(up_bias.astype(F32)[None], ((0, 7), (0, 0))),
        ],
        axis=1,
    )
    row = lax.broadcasted_iota(jnp.int32, (8, width), 0)
    vectors = jnp.zeros((8, width), F32)
    for i, vector in enumerate(
        (output_bias, second_gain, second_shift, down_bias, first_gain, first_shift)
    ):
        vectors = jnp.where(row == i, vector[None], vectors)
    qkv, mixed, logsum, first, in_all, ff_near, ff_pieces, bias_all = attend(
        tokens,
        vectors,
        project_in.transpose(1, 2, 0),
        project_out,
        up_weight.reshape(8, -1, width),
        down_weight.reshape(8, -1, width),
        bias_own,
    )
    residual, feed, back_second, near_grad, up_sums, ff_late = feed_first(
        live_images,
        tokens,
        out_grad,
        mixed,
        in_all,
        up_weight,
        down_weight,
        ff_near,
        bias_all,
        vectors,
        ff_pieces,
    )
    output, resid, back_mixed, late_grad, out_grads, feed_small, ff_part = feed_last(
        live_images,
        residual,
        feed,
        back_second,
        out_grad,
        mixed,
        in_all,
        ff_late,
        bias_all,
        vectors,
        near_grad,
    )
    input_grad, small, grad_up, grad_down, grad_in, grad_out = attend_back(
        qkv,
        back_mixed,
        mixed,
        logsum,
        first,
        out_grads,
        ff_part,
        in_all,
        tokens,
        resid,
        vectors,
        feed_small,
        up_sums,
        late_grad.reshape(2, 2, 2, 2, 192, width),
    )
    grad_up = grad_up.reshape(width, width).astype(F32)
    grad_down, grad_out = grad_down.astype(F32), grad_out.astype(F32)
    grad_in = grad_in.astype(F32).transpose(2, 0, 1)
    pair_sum = small[8, : 4 * IN_ROWS].reshape(own_heads, 3, HEAD_DIM)
    grad_pair = jnp.stack([pair_sum[:, 0].reshape(-1), pair_sum[:, 2].reshape(-1)])
    return (
        output,
        input_grad,
        small[12],
        small[13],
        grad_in,
        grad_pair,
        grad_out,
        small[0],
        small[1],
        small[2],
        grad_up,
        small[4],
        grad_down,
        small[3],
    )


def solution(mesh):
    rows = P(("dp", "mp"), None)
    return jax.shard_map(
        local,
        mesh=mesh,
        in_specs=(
            rows,
            rows,
            rows,
            P(),
            P(),
            P(None, None, "mp"),
            P(None, "mp"),
            P("mp", None),
            P(),
            P(),
            P(),
            P(None, "mp"),
            P("mp"),
            P("mp", None),
            P(),
        ),
        out_specs=(
            rows,
            rows,
            P(),
            P(),
            P(None, None, "mp"),
            P(None, "mp"),
            P("mp", None),
            P(),
            P(),
            P(),
            P(None, "mp"),
            P("mp"),
            P("mp", None),
            P(),
        ),
        check_vma=False,
    )
```

```python
import functools
import math

import jax
import jax.numpy as jnp
from jax import lax
from jax.experimental import pallas as pl
from jax.experimental.pallas import tpu as pltpu
from jax.sharding import PartitionSpec as P

HEAD_DIM = 48
SHORT_LEN = 256
LONG_LEN = 1024
SHORT_SLOTS = 2
LONG_SLOTS = 1
SHORT_ROWS = SHORT_SLOTS * SHORT_LEN
IMAGES = tuple((SHORT_LEN * i, SHORT_LEN) for i in range(SHORT_SLOTS)) + tuple(
    (SHORT_ROWS + LONG_LEN * i, LONG_LEN) for i in range(LONG_SLOTS)
)
SCALE = HEAD_DIM**-0.5
SCALE_LOG2 = SCALE * math.log2(math.e)
BF16 = jnp.bfloat16
F32 = jnp.float32
CHUNK = 512
BACK_CHUNK = 256

epsilon = 1e-05


def layer_norm(rows_in, norm_gain, norm_shift):
    average = jnp.mean(rows_in, axis=-1, keepdims=True)
    centred = rows_in - average
    variance = jnp.mean(centred * centred, axis=-1, keepdims=True)
    return centred * lax.rsqrt(variance + epsilon) * norm_gain + norm_shift


def nn(left, right):
    return lax.dot_general(
        left, right, (((1,), (0,)), ((), ())), preferred_element_type=F32
    )


def nt(left, right):
    return lax.dot_general(
        left, right, (((1,), (1,)), ((), ())), preferred_element_type=F32
    )


def tn(left, right):
    return lax.dot_general(
        left, right, (((0,), (0,)), ((), ())), preferred_element_type=F32
    )


GROUP = 8
MESH = pl.DeviceIdType.MESH
IN_ROWS = 144
HEAD_ROWS = 192


def place():
    dp, mp = lax.axis_index("dp"), lax.axis_index("mp")
    g = lax.rem(dp, GROUP)
    return dp, dp - g, g // 4, lax.rem(g // 2, 2), lax.rem(g, 2), mp


def flip(bit):
    return 1 - bit


class Gather:
    def __init__(self, own, buffers, piece, split, send, recv, pieces=None):
        self.own, self.buffers, self.piece, self.split = own, buffers, piece, split
        self.pieces = pieces or {}
        self.send, self.recv = send, recv
        self.dp, self.base, self.y, self.x, self.core, self.mp = place()

    def device(self, y, x, core):
        return (self.base + 4 * y + 2 * x + core, self.mp)

    def view(self, ref, y, x, core, part=None):
        view = self.piece(ref, 2 * y + x, core)
        if part is None:
            return view
        rows = view.shape[0]
        return view.at[pl.ds(0, self.split)] if part == 0 else view.at[pl.ds(self.split, rows - self.split)]

    def copy(self, kind, slot):
        y, x, core = self.y, self.x, self.core
        mine = (y, x, core)
        buffer = self.buffers[slot]
        if kind in (0, 9):
            ways = lax.axis_size("mp")
            hop = 1 if slot == 2 else slot
            dst = self.pieces[slot] if slot in self.pieces else self.view(buffer, *mine)
            if slot == 2:
                src = self.view(self.buffers[1], *mine)
            elif isinstance(self.own, tuple):
                src = self.view(self.own[kind // 9], *mine)
                dst = dst.at[pl.ds(96 * (kind // 9), 96)]
            else:
                src = self.view(self.own, *mine)
            device = (self.dp, lax.rem(self.mp + ways - hop, ways))
        else:
            return self.shared(kind, buffer, kind * 4 + slot, self.pieces.get(slot))
        return self.remote(src, dst, device, kind * 4 + slot)

    def shared(self, kind, buffer, index, piece=None):
        y, x, core = self.y, self.x, self.core
        mine, near_x, near_y = (y, x, core), (y, flip(x), core), (flip(y), x, core)
        moved, device = {
            1: lambda: (self.view(buffer, *mine), near_x),
            2: lambda: (self.view(buffer, *mine), near_y),
            3: lambda: (self.view(buffer, *near_x, 0), near_y),
            4: lambda: (self.view(buffer, *near_y, 1), near_x),
            5: lambda: (self.view(buffer, *mine), (y, x, flip(core))),
            6: lambda: (self.view(buffer, *near_x), (y, x, flip(core))),
            7: lambda: (self.view(buffer, *near_y), (y, x, flip(core))),
            8: lambda: (self.view(buffer, flip(y), flip(x), core), (y, x, flip(core))),
        }[kind]()
        src = moved if piece is None or kind not in (1, 2, 5) else piece
        return self.remote(src, moved, self.device(*device), index)

    def remote(self, src, dst, device, index):
        return pltpu.make_async_remote_copy(
            src_ref=src,
            dst_ref=dst,
            send_sem=self.send.at[index],
            recv_sem=self.recv.at[index],
            device_id=device,
            device_id_type=MESH,
        )

    def start(self, slot, *kinds):
        for kind in kinds:
            self.copy(kind, slot).start()

    def arrived(self, slot, *kinds):
        for kind in kinds:
            self.copy(kind, slot).wait_recv()

    def along_kinds(self, slot):
        return (0, 9) if isinstance(self.own, tuple) and slot != 2 else (0,)

    def along(self, slot):
        self.start(slot, *self.along_kinds(slot))

    def spread(self, slot):
        if slot not in self.pieces:
            self.arrived(slot, *self.along_kinds(slot))
        self.start(slot, 1, 2, 5)

    def forward(self, slot):
        self.arrived(slot, 1)
        self.start(slot, 3, 6)
        self.arrived(slot, 2)
        self.start(slot, 4, 7)

    def last(self, slot):
        self.arrived(slot, 3, 4)
        self.start(slot, 8)

    def complete(self, slot):
        self.arrived(slot, 5, 6, 7, 8)

    def finish(self, slots, kinds=range(9)):
        for slot in slots:
            for kind in kinds:
                self.copy(kind, slot).wait_send()


GATHER_KINDS = 10


def in_piece(ref, chip, core):
    return ref.at[chip, :, pl.ds(pl.multiple_of(core * 384, 128), 384)]


def ff_piece(ref, chip, core):
    return ref.at[2 * chip + core]


def signal(partners):
    barrier = pltpu.get_barrier_semaphore()
    for partner in partners:
        pl.semaphore_signal(barrier, inc=1, device_id=partner, device_id_type=MESH)


def meet(partners):
    pl.semaphore_wait(pltpu.get_barrier_semaphore(), len(partners))


def chunks_of(images, size):
    return [
        (start, length, first, min(size, length))
        for start, length in images
        for first in range(start, start + length, min(size, length))
    ]


def attend_head(qkv_ref, mixed_ref, logsum_ref):
    held = {}

    def score(start, length, first, chunk):
        if start not in held:
            whole = slice(start, start + length)
            value_t = qkv_ref[96:144, whole]
            held[start] = (
                qkv_ref[48:96, whole].T,
                jnp.concatenate([value_t, jnp.ones((16, length), BF16)], axis=0),
            )
        return nn(held[start][0], qkv_ref[0:48, first : first + chunk])

    def soften(scores):
        top = jnp.max(scores, axis=0, keepdims=True)
        return top, jnp.exp2((scores - top) * SCALE_LOG2).astype(BF16)

    def mix(item, top, weights):
        start, length, first, chunk = item
        cols = slice(first, first + chunk)
        sums = nn(held[start][1], weights)
        total = sums[48:49]
        mixed_ref[:, cols] = (sums[:48] / total).astype(BF16)
        logsum_ref[:, cols] = top * SCALE_LOG2 + jnp.log2(total)

    items = chunks_of(IMAGES, CHUNK)
    early, late = {0: score(*items[0])}, {}
    for i in range(len(items) + 1):
        if i + 1 < len(items):
            early[i + 1] = score(*items[i + 1])
        if i < len(items):
            late[i] = soften(early.pop(i))
        if i > 0:
            mix(items[i - 1], *late.pop(i - 1))


def hooks_of(table, step):
    def hook(name, head=None):
        for (at, where), actions in table.items():
            if where == name if head is None else isinstance(where, int):

                @pl.when(step == at if head is None else (step == at) & (head == where))
                def _(actions=actions):
                    for action in actions:
                        action()

    return hook


def group_partners(wide=False):
    dp, base, y, x, core, mp = place()
    ways = lax.axis_size("mp")
    return (
        [(dp, lax.rem(mp + k, ways)) for k in (1, 2, 3)]
        + [
            (base + 4 * y + 2 * flip(x) + core, mp),
            (base + 4 * flip(y) + 2 * x + core, mp),
            (base + 4 * y + 2 * x + flip(core), mp),
        ]
        + [(other_bit(dp, bit), mp) for bit in wider_bits() if wide]
    )


def attend_kernel(
    tokens_ref,
    vector_ref,
    in_own,
    out_own,
    up_own,
    down_own,
    bias_own,
    qkv_ref,
    mixed_ref,
    logsum_ref,
    first_ref,
    in_out,
    ff_near,
    ff_pieces,
    bias_out,
    in_all,
    bias_all,
    in_send,
    in_recv,
    ff_send,
    ff_recv,
    bias_send,
    bias_recv,
    own_sem,
    local_sem,
):
    step = pl.program_id(0)
    dp, base, y, x, core, mp = place()
    ways = lax.axis_size("mp")
    gin = Gather(in_all.at[0], [in_all.at[k] for k in range(4)], in_piece, 96, in_send, in_recv)
    gff = Gather(
        (up_own, down_own),
        [None, ff_near, None, None],
        ff_piece,
        96,
        ff_send,
        ff_recv,
        {2: ff_pieces.at[0], 3: ff_pieces.at[1]},
    )
    own_copies = [
        pltpu.make_async_copy(
            in_own.at[part, pl.ds(head * 48, 48)] if part < 3 else out_own.at[pl.ds(head * 48, 48)],
            in_all.at[0, head, pl.ds(part * 48, 48)],
            own_sem.at[part * 4 + head],
        )
        for part in range(4)
        for head in range(4)
    ]
    local_bias = pltpu.make_async_copy(bias_own, bias_all.at[0], local_sem.at[1])
    out_in = pltpu.make_async_copy(in_all, in_out, local_sem.at[2])
    out_bias = pltpu.make_async_copy(bias_all, bias_out, local_sem.at[3])

    def bias_copy(slot):
        return pltpu.make_async_remote_copy(
            src_ref=bias_own,
            dst_ref=bias_all.at[slot],
            send_sem=bias_send.at[slot],
            recv_sem=bias_recv.at[slot],
            device_id=(dp, lax.rem(mp + ways - slot, ways)),
            device_id_type=MESH,
        )

    def begin():
        for copy in own_copies:
            copy.start()
        local_bias.start()
        signal(group_partners())
        for i, rows in enumerate(range(0, tokens_ref.shape[0], BLOCK)):
            if i == 1:
                meet(group_partners())
                for copy in own_copies:
                    copy.wait()
                gin.along(1)
            block = slice(rows, rows + BLOCK)
            first_ref[block] = layer_norm(
                tokens_ref[block].astype(F32), vector_ref[4:5], vector_ref[5:6]
            ).astype(BF16)
        local_bias.wait()

    def end():
        gff.complete(1)
        gff.arrived(2, 0)
        gff.arrived(3, 0, 9)
        out_in.wait()
        out_bias.wait()
        for slot in (1, 2, 3):
            bias_copy(slot).wait_send()
        gin.finish((1, 2, 3))
        gff.finish((1,), range(10))
        gff.finish((2,), (0,))
        gff.finish((3,), (0, 9))

    hook = hooks_of(
        {
            (0, "begin"): [begin],
            (0, "heads"): [
                lambda: gin.spread(1),
                lambda: gin.along(3),
                lambda: gin.along(2),
                lambda: [bias_copy(slot).start() for slot in (1, 2, 3)],
            ],
            (0, 2): [lambda: gin.forward(1)],
            (0, "end"): [lambda: gin.last(1), lambda: gin.spread(3)],
            (1, "begin"): [
                lambda: [bias_copy(slot).wait_recv() for slot in (1, 2, 3)],
                lambda: gin.complete(1),
            ],
            (1, "heads"): [lambda: gin.spread(2), lambda: gff.along(1)],
            (1, 1): [lambda: gin.forward(3)],
            (1, 3): [lambda: gin.last(3), lambda: gin.forward(2)],
            (2, "begin"): [lambda: gin.last(2), lambda: gin.complete(3)],
            (2, "heads"): [lambda: gff.spread(1), lambda: gff.along(3), lambda: gff.along(2)],
            (3, "begin"): [
                lambda: gin.complete(2),
                out_in.start,
                out_bias.start,
                lambda: gff.forward(1),
            ],
            (3, 2): [lambda: gff.last(1)],
            (3, "end"): [end],
        },
        step,
    )
    slot = slot_order(step)
    hook("begin")
    bias_t = bias_all[slot, :, 0:256].T
    weight = in_all[slot, :, :IN_ROWS].reshape(4 * IN_ROWS, first_ref.shape[1])
    product = nt(weight, first_ref[...])
    for part in range(4):
        rows = slice(part * IN_ROWS, (part + 1) * IN_ROWS)
        qkv_ref[rows, :] = (product[rows] + bias_t[:IN_ROWS, part : part + 1]).astype(BF16)
    hook("heads")

    def one_head(head, carry):
        hook(None, head)
        attend_head(
            qkv_ref.at[pl.ds(pl.multiple_of(head * IN_ROWS, 16), IN_ROWS)],
            mixed_ref.at[pl.ds(pl.multiple_of(head * 48, 16), 48)],
            logsum_ref.at[head],
        )
        return carry

    lax.fori_loop(0, 4, one_head, 0)
    hook("end")


def slot_order(turn):
    return turn + (turn // 2) * (1 - 2 * (turn % 2))


def attend(tokens, vectors, in_own, out_own, up_own, down_own, bias_own):
    rows, width = tokens.shape
    heads = 16
    anywhere = pl.BlockSpec(memory_space=pl.ANY)
    dma = pltpu.SemaphoreType.DMA
    return pl.pallas_call(
        attend_kernel,
        grid=(4,),
        in_specs=[
            pl.BlockSpec((rows, width), lambda s: (0, 0), pipeline_mode=pl.Buffered(1)),
            pl.BlockSpec((8, width), lambda s: (0, 0)),
            anywhere,
            anywhere,
            anywhere,
            anywhere,
            anywhere,
        ],
        out_specs=[
            pl.BlockSpec((4 * IN_ROWS, rows), lambda s: (slot_order(s), 0)),
            pl.BlockSpec((4 * 48, rows), lambda s: (slot_order(s), 0)),
            pl.BlockSpec((4, 1, rows), lambda s: (slot_order(s), 0, 0)),
            pl.BlockSpec((rows, width), lambda s: (0, 0)),
            anywhere,
            anywhere,
            anywhere,
            anywhere,
        ],
        out_shape=[
            jax.ShapeDtypeStruct((heads * IN_ROWS, rows), BF16),
            jax.ShapeDtypeStruct((heads * 48, rows), BF16),
            jax.ShapeDtypeStruct((heads, 1, rows), F32),
            jax.ShapeDtypeStruct((rows, width), BF16),
            jax.ShapeDtypeStruct((4, 4, HEAD_ROWS, width), BF16),
            jax.ShapeDtypeStruct((8, 192, width), BF16),
            jax.ShapeDtypeStruct((2, 192, width), BF16),
            jax.ShapeDtypeStruct((4, 8, 1024), F32),
        ],
        scratch_shapes=[
            pltpu.VMEM((4, 4, HEAD_ROWS, width), BF16),
            pltpu.VMEM((4, 8, 1024), F32),
            dma((4 * GATHER_KINDS,)),
            dma((4 * GATHER_KINDS,)),
            dma((4 * GATHER_KINDS,)),
            dma((4 * GATHER_KINDS,)),
            dma((4,)),
            dma((4,)),
            dma((16,)),
            dma((4,)),
        ],
        compiler_params=pltpu.CompilerParams(
            vmem_limit_bytes=62 << 20, collective_id=0, has_side_effects=True
        ),
        cost_estimate=pl.CostEstimate(
            flops=30_000_000_000, bytes_accessed=30_000_000, transcendentals=19_000_000
        ),
        name="attend",
    )(tokens, vectors, in_own, out_own, up_own, down_own, bias_own)


class Reduce:
    def __init__(self, slot, other, total, got, split, send, recv):
        self.slot, self.other, self.total, self.got, self.split = slot, other, total, got, split
        self.send, self.recv = send, recv
        self.dp, self.base, self.y, self.x, self.core, self.mp = place()

    def copy(self, kind):
        y, x, core = self.y, self.x, self.core
        first, late = pl.ds(0, self.split), pl.ds(self.split, self.total.shape[2] - self.split)
        got = self.got
        near = lambda y, x, core: (self.base + 4 * y + 2 * x + core, self.mp)
        to_x, to_y = near(y, flip(x), core), near(flip(y), x, core)
        src, dst, device = {
            0: lambda: (self.other, got[0], near(y, x, flip(core))),
            1: lambda: (self.total.at[:, flip(x), first], got[1], to_x),
            2: lambda: (self.total.at[flip(y), :, late], got[2], to_y),
            3: lambda: (self.total.at[flip(y), x, first], got[3], to_y),
            4: lambda: (self.total.at[y, flip(x), late], got[4], to_x),
            5: lambda: (
                self.total.at[y, x],
                got[5],
                (self.dp, lax.rem(self.mp + self.slot, lax.axis_size("mp"))),
            ),
        }[kind]()
        index = kind * 4 + self.slot
        return pltpu.make_async_remote_copy(
            src_ref=src,
            dst_ref=dst,
            send_sem=self.send.at[index],
            recv_sem=self.recv.at[index],
            device_id=device,
            device_id_type=MESH,
        )

    def cores(self):
        self.copy(0).start()

    def chips(self):
        self.copy(0).wait_recv()
        for y in range(2):
            for x in range(2):
                self.total[y, x] = add(self.total[y, x], self.got[0][y, x])
        self.copy(1).start()
        self.copy(2).start()

    def chips_again(self):
        x, y, split = self.x, self.y, self.split
        self.copy(1).wait_recv()
        for i in range(2):
            self.total[i, x, :split] = add(self.total[i, x, :split], self.got[1][i])
        self.copy(2).wait_recv()
        for i in range(2):
            self.total[y, i, split:] = add(self.total[y, i, split:], self.got[2][i])
        self.copy(3).start()
        self.copy(4).start()

    def settle(self):
        x, y, split = self.x, self.y, self.split
        self.copy(3).wait_recv()
        self.total[y, x, :split] = add(self.total[y, x, :split], self.got[3][...])
        self.copy(4).wait_recv()
        self.total[y, x, split:] = add(self.total[y, x, split:], self.got[4][...])

    def along(self):
        self.settle()
        if self.slot:
            self.copy(5).start()

    def finish(self, kinds=6):
        for kind in range(kinds if self.slot else 5):
            self.copy(kind).wait_send()

    def result(self):
        if self.slot:
            self.copy(5).wait_recv()
            return self.got[5][...].astype(F32)
        return self.total[self.y, self.x].astype(F32)


REDUCE_KINDS = 6


def add(left, right):
    return (left.astype(F32) + right.astype(F32)).astype(BF16)


def other_bit(index, bit):
    return index + bit * (1 - 2 * lax.rem(index // bit, 2))


def wider_bits():
    bits, bit = [], GROUP
    while bit < lax.axis_size("dp"):
        bits.append(bit)
        bit *= 2
    return bits


class Share:
    def __init__(self, pieces, split, send, recv):
        self.inner = Gather(None, None, ff_piece, split, send, recv)
        self.pieces = pieces

    def copy(self, kind):
        return self.inner.shared(kind, self.pieces, kind)

    def start(self, *kinds):
        for kind in kinds:
            self.copy(kind).start()

    def arrived(self, *kinds):
        for kind in kinds:
            self.copy(kind).wait_recv()

    def spread(self):
        self.start(1, 2, 5)

    def forward(self):
        self.arrived(1)
        self.start(3, 6)
        self.arrived(2)
        self.start(4, 7)

    def last(self):
        self.arrived(3, 4)
        self.start(8)

    def finish(self):
        self.arrived(5, 6, 7, 8)
        for kind in range(1, 9):
            self.copy(kind).wait_send()


class Wide:
    def __init__(self, held, send, recv):
        self.held, self.send, self.recv = held, send, recv

    def copy(self, i, bit):
        dp, mp = lax.axis_index("dp"), lax.axis_index("mp")
        return pltpu.make_async_remote_copy(
            src_ref=self.held.at[2 * i],
            dst_ref=self.held.at[2 * i + 1],
            send_sem=self.send.at[i],
            recv_sem=self.recv.at[i],
            device_id=(other_bit(dp, bit), mp),
            device_id_type=MESH,
        )

    def sum(self, total):
        for i, bit in enumerate(wider_bits()):
            self.held[2 * i] = total.astype(BF16)
            self.copy(i, bit).start()
            self.copy(i, bit).wait()
            total = total + self.held[2 * i + 1].astype(F32)
        return total


def reduce_scratch(slots, rows, split, width):
    dma = pltpu.SemaphoreType.DMA
    late = rows - split
    return [
        pltpu.VMEM((slots, 2, 2, rows, width), BF16),
        pltpu.VMEM((slots, 2, split, width), BF16),
        pltpu.VMEM((slots, 2, late, width), BF16),
        pltpu.VMEM((slots, split, width), BF16),
        pltpu.VMEM((slots, late, width), BF16),
        pltpu.VMEM((slots, rows, width), BF16),
        dma((4 * REDUCE_KINDS,)),
        dma((4 * REDUCE_KINDS,)),
    ]


REDUCE_REFS = 8


def reduces_of(slots, other, total, scratch, split):
    *got, send, recv = scratch
    return {
        slot: Reduce(slot, other(i), total(i), [ref.at[i] for ref in got], split, send, recv)
        for i, slot in enumerate(slots)
    }


def share_scratch(rows, width):
    dma = pltpu.SemaphoreType.DMA
    wide = max(len(wider_bits()), 1)
    return [
        pltpu.VMEM((8, rows, width), BF16),
        pltpu.VMEM((2 * wide, rows, width), BF16),
        dma((GATHER_KINDS,)),
        dma((GATHER_KINDS,)),
        dma((wide,)),
        dma((wide,)),
    ]


SHARE_REFS = 6


class Sums:
    def __init__(self, direct, held, got, along_got, send, recv, along_send, along_recv):
        self.direct, self.held, self.got, self.along_got = direct, held, got, along_got
        self.send, self.recv, self.along_send, self.along_recv = send, recv, along_send, along_recv
        self.dp, self.base, self.y, self.x, self.core, self.mp = place()
        self.bits = ([] if direct else [1, 2, 4]) + wider_bits()
        self.near = GROUP - 1 if direct else 0

    def copy(self, src, index, device):
        return pltpu.make_async_remote_copy(
            src_ref=self.held.at[src],
            dst_ref=self.got.at[index],
            send_sem=self.send.at[index],
            recv_sem=self.recv.at[index],
            device_id=(device, self.mp),
            device_id_type=MESH,
        )

    def near_copy(self, k):
        return self.copy(0, k, self.base + near_index(self.y, self.x, self.core, k + 1))

    def bit_copy(self, i):
        first = 1 if self.direct else 0
        return self.copy(first + i, self.near + i, other_bit(self.dp, self.bits[i]))

    def along_copy(self, slot):
        return pltpu.make_async_remote_copy(
            src_ref=self.held.at[self.last()],
            dst_ref=self.along_got.at[slot - 1],
            send_sem=self.along_send.at[slot - 1],
            recv_sem=self.along_recv.at[slot - 1],
            device_id=(self.dp, lax.rem(self.mp + slot, lax.axis_size("mp"))),
            device_id_type=MESH,
        )

    def last(self):
        return len(self.bits) + (1 if self.direct else 0)

    def start(self):
        if self.direct:
            for k in range(self.near):
                self.near_copy(k).start()
        else:
            self.bit_copy(0).start()

    def step(self, i):
        first = 1 if self.direct else 0
        self.bit_copy(i).wait_recv()
        self.held[first + i + 1] = self.held[first + i] + self.got[self.near + i]
        if i + 1 < len(self.bits):
            self.bit_copy(i + 1).start()

    def join(self, begin=0):
        if self.direct:
            total = self.held[0]
            for k in range(self.near):
                self.near_copy(k).wait_recv()
                total = total + self.got[k]
            self.held[1] = total
            if self.bits:
                self.bit_copy(0).start()
        for i in range(begin, len(self.bits)):
            self.step(i)
        for slot in (1, 2, 3):
            self.along_copy(slot).start()

    def result(self):
        return self.held[self.last()]

    def arrived(self, slot):
        self.along_copy(slot).wait_recv()
        return self.along_got[slot - 1]

    def finish(self):
        for k in range(self.near):
            self.near_copy(k).wait_send()
        for i in range(len(self.bits)):
            self.bit_copy(i).wait_send()
        for slot in (1, 2, 3):
            self.along_copy(slot).wait_send()


SUMS_REFS = 7


def sums_scratch(direct, rows, width):
    dma = pltpu.SemaphoreType.DMA
    stages = (GROUP - 1 if direct else 3) + len(wider_bits())
    return [
        pltpu.VMEM(((1 if direct else 3) + len(wider_bits()) + 1, rows, width), F32),
        pltpu.VMEM((stages, rows, width), F32),
        pltpu.VMEM((3, rows, width), F32),
        dma((stages,)),
        dma((stages,)),
        dma((3,)),
        dma((3,)),
    ]


def attend_back_head(qkv_ref, back_ref, mixed_ref, logsum_ref, out_ref, held):
    rows = {}

    def score(start, length, first, chunk):
        if start not in rows:
            whole = slice(start, start + length)
            key_t = qkv_ref[48:96, whole]
            rows[start] = (key_t, key_t.T, qkv_ref[96:144, whole].T)
        cols = slice(first, first + chunk)
        return (
            nn(rows[start][1], qkv_ref[0:48, cols]),
            nn(rows[start][2], back_ref[:, cols]),
        )

    def soften(item, scores, back_probs):
        cols = slice(item[2], item[2] + item[3])
        inner = jnp.sum(
            back_ref[:, cols].astype(F32) * mixed_ref[:, cols].astype(F32), axis=0, keepdims=True
        )
        probs = jnp.exp2(scores * SCALE_LOG2 - logsum_ref[:, cols])
        return probs.astype(BF16), (probs * (back_probs - inner)).astype(BF16)

    def pull(item, probs, back_scores):
        start, length, first, chunk = item
        cols, whole = slice(first, first + chunk), slice(start, start + length)
        query_t, back_t = qkv_ref[0:48, cols], back_ref[:, cols]
        out_ref[0:48, cols] = (nn(rows[start][0], back_scores) * SCALE).astype(BF16)
        back_key = nt(query_t, back_scores)
        back_value = nt(back_t, probs)
        if first > start:
            back_key = back_key + held[0:48, 0:length]
            back_value = back_value + held[48:96, 0:length]
        if first + chunk < start + length:
            held[0:48, 0:length] = back_key
            held[48:96, 0:length] = back_value
        else:
            out_ref[48:96, whole] = (back_key * SCALE).astype(BF16)
            out_ref[96:144, whole] = back_value.astype(BF16)

    items = chunks_of(IMAGES, BACK_CHUNK)
    early = {0: score(*items[0])}
    for i in range(len(items)):
        if i + 1 < len(items):
            early[i + 1] = score(*items[i + 1])
        pull(items[i], *soften(items[i], *early.pop(i)))


def attend_back_kernel(
    qkv_ref,
    back_ref,
    mixed_ref,
    logsum_ref,
    first_any,
    out_grad_ref,
    ff_part_ref,
    in_any,
    tokens_ref,
    resid_ref,
    vector_ref,
    feed_small_ref,
    up_sums_ref,
    ff_grad,
    input_ref,
    small_ref,
    up_out,
    down_out,
    in_out,
    out_out,
    held,
    ff_total,
    grads,
    back_qkv,
    turned,
    first_ref,
    in_ref,
    local,
    *scratch,
    blocks,
):
    step = pl.program_id(0)
    width = tokens_ref.shape[1]
    dp, base, y, x, core, mp = place()
    early, scratch = Sums(False, *scratch[:SUMS_REFS]), scratch[SUMS_REFS:]
    late, scratch = Sums(True, *scratch[:SUMS_REFS]), scratch[SUMS_REFS:]
    sums, late_sums = early.held, late.held
    ff_scratch, scratch = scratch[:REDUCE_REFS], scratch[REDUCE_REFS:]
    in_scratch, scratch = scratch[:REDUCE_REFS], scratch[REDUCE_REFS:]
    ff_final, ff_wide, *ff_sems = scratch[:SHARE_REFS]
    in_final, in_wide, *in_sems = scratch[SHARE_REFS:]
    ff = reduces_of(
        (2, 3),
        lambda i: ff_grad.at[i, :, :, flip(core)],
        lambda i: ff_total.at[i],
        ff_scratch,
        96,
    )
    ins = reduces_of(
        (0, 1, 2, 3),
        lambda i: grads.at[i, :, :, flip(core)],
        lambda i: grads.at[i, :, :, core],
        in_scratch,
        48,
    )
    ff_share = Share(ff_final, 96, *ff_sems[:2])
    in_share = Share(in_final, 48, *in_sems[:2])
    me = 4 * y + 2 * x + core

    def own(i):
        return pltpu.make_async_copy(ff_grad.at[i, :, :, core], ff_total.at[i], local.at[i])

    up_written = pltpu.make_async_copy(ff_final.at[:, pl.ds(0, 96)], up_out, local.at[2])
    down_written = pltpu.make_async_copy(turned, down_out, local.at[3])

    def in_written():
        copies = []
        for head in range(4):
            rows = pl.ds(48 * head, 48)
            for part in range(4):
                src = in_final.at[2 * head + part // 2, pl.ds(48 * (part % 2), 48)]
                dst = in_out.at[part, rows] if part < 3 else out_out.at[rows]
                copies.append(pltpu.make_async_copy(src, dst, local.at[4 + 4 * head + part]))
        return copies

    first_read = pltpu.make_async_copy(first_any, first_ref, local.at[20])
    in_read = pltpu.make_async_copy(in_any, in_ref, local.at[21])

    def begin():
        own(0).start()
        own(1).start()
        first_read.start()
        in_read.start()
        signal(every_partner())
        sums[0] = jnp.zeros_like(sums[0])
        late_sums[0] = jnp.zeros_like(late_sums[0])
        sums[0, 0:8, :] = feed_small_ref[...]
        sums[0, 4:6, :] = up_sums_ref[0:2, :]

    def chips(slot):
        own(slot - 2).wait()
        ff[slot].chips()

    def finish_ff():
        total = ff_part_ref[...] + ff[2].result() + ff[3].result()
        ff_final[me] = Wide(ff_wide, *ff_sems[2:]).sum(total).astype(BF16)
        ff_share.spread()

    def write_ff():
        ff_share.finish()
        up_written.start()
        turned[...] = ff_final[:, 96:].reshape(width, width).T
        down_written.start()

    def finish_in():
        ins[0].along()
        total = ins[0].result() + ins[1].result() + ins[2].result() + ins[3].result()
        in_final[me] = Wide(in_wide, *in_sems[2:]).sum(total).astype(BF16)
        in_share.spread()

    def late_start():
        late.start()
        in_share.forward()

    def end_early():
        small_ref[0:12] = early.result()[0:12]
        for slot in (1, 2, 3):
            more = early.arrived(slot)
            small_ref[0:4] += more[0:4]
            small_ref[4:5] += more[4 + slot : 5 + slot]
            small_ref[8:9] += more[8 + slot : 9 + slot]

    def end():
        late_start()
        late.join()
        in_share.last()
        in_share.finish()
        for copy in in_written():
            copy.start()
        total = late.result() + late.arrived(1) + late.arrived(2) + late.arrived(3)
        third = width // 3
        for i in range(3):
            part = slice(third * i, third * (i + 1))
            small_ref[12:13, part] = total[i : i + 1]
            small_ref[13:14, part] = total[3 + i : 4 + i]
        early.finish()
        late.finish()
        for reduce in [*ff.values(), *ins.values()]:
            reduce.finish()
        up_written.wait()
        down_written.wait()
        for copy in in_written():
            copy.wait()

    hook = hooks_of(
        {
            (0, 0): [begin],
            (0, "grads"): [first_read.wait],
            (0, 1): [lambda: meet(every_partner()), ff[2].cores, ff[3].cores],
            (0, 2): [lambda: chips(2)],
            (1, 0): [ff[2].chips_again, lambda: chips(3), ins[2].cores],
            (1, 2): [ff[2].along],
            (1, 3): [ff[3].chips_again, ins[2].chips],
            (2, 0): [ff[3].along, ins[1].cores],
            (2, 1): [ins[2].chips_again, ins[1].chips],
            (2, 3): [ins[2].along, ins[1].chips_again],
            (3, 0): [finish_ff, ins[1].along, ins[3].cores],
            (3, 1): [ins[3].chips],
            (3, 3): [ff_share.forward, ins[3].chips_again],
            (4, "begin"): [in_read.wait, ins[0].cores, early.start, ins[3].along],
            (5, "begin"): [ins[0].chips, ff_share.last, lambda: early.step(0)],
            (6, "begin"): [write_ff, lambda: early.step(1)],
            (6, "end"): [ins[0].chips_again],
            (7, "begin"): [lambda: early.join(2)],
            (7, "end"): [finish_in],
            (9, "begin"): [end_early],
            (9, "end"): [end],
        },
        step,
    )

    @pl.when(step < 4)
    def _():
        slot = back_order(step)

        def one_head(head, carry):
            hook(None, head)
            of_head = pl.ds(pl.multiple_of(head * IN_ROWS, 16), IN_ROWS)
            own_head = pl.ds(pl.multiple_of(head * 48, 16), 48)
            out_rows = pl.ds(pl.multiple_of((4 * slot + head) * IN_ROWS, 16), IN_ROWS)
            attend_back_head(
                qkv_ref.at[of_head],
                back_ref.at[own_head],
                mixed_ref.at[own_head],
                logsum_ref.at[head],
                back_qkv.at[out_rows],
                held,
            )
            return carry

        lax.fori_loop(0, 4, one_head, 0)
        hook("grads")
        rows = back_qkv[pl.ds(pl.multiple_of(4 * slot * IN_ROWS, 16), 4 * IN_ROWS), :]
        slot_grad = nn(rows, first_ref[...]).astype(BF16)
        for head in range(4):
            grad = slot_grad[head * IN_ROWS : (head + 1) * IN_ROWS]
            grads[slot, head // 2, head % 2, 0] = grad[:96]
            grads[slot, head // 2, head % 2, 1, 0:48] = grad[96:]
            grads[slot, head // 2, head % 2, 1, 48:96] = out_grad_ref[0, head]
        row_sums = nt(jnp.ones((8, rows.shape[1]), BF16), rows)
        sums[0, pl.ds(8 + slot, 1), 0 : 4 * IN_ROWS] = row_sums[0:1]

    @pl.when(step >= 4)
    def _():
        hook("begin")
        inputs = tokens_ref[...].astype(F32)
        scaled, inverse = normed(inputs)
        cols = pl.ds(pl.multiple_of((step - 4) * BLOCK, BLOCK), BLOCK)
        back_first = None
        for slot in range(4):
            weight = in_ref[slot, :, :IN_ROWS].reshape(4 * IN_ROWS, width)
            part = tn(back_qkv[slot * 4 * IN_ROWS : (slot + 1) * 4 * IN_ROWS, cols], weight)
            back_first = part if slot == 0 else back_first + part
        gain_sum = jnp.sum(back_first * scaled, axis=0, keepdims=True)
        shift_sum = jnp.sum(back_first, axis=0, keepdims=True)
        third = width // 3
        for i in range(3):
            part = slice(third * i, third * (i + 1))
            late_sums[0, i : i + 1] += gain_sum[:, part]
            late_sums[0, 3 + i : 4 + i] += shift_sum[:, part]
        back_norm = back_first * vector_ref[4:5, :]
        input_ref[...] = resid_ref[...] + inverse * (
            back_norm
            - jnp.mean(back_norm, axis=-1, keepdims=True)
            - scaled * jnp.mean(back_norm * scaled, axis=-1, keepdims=True)
        )
        hook("end")


def near_index(y, x, core, k):
    y = flip(y) if k & 4 else y
    x = flip(x) if k & 2 else x
    core = flip(core) if k & 1 else core
    return 4 * y + 2 * x + core


def every_partner():
    dp, base, y, x, core, mp = place()
    ways = lax.axis_size("mp")
    return (
        [(dp, lax.rem(mp + k, ways)) for k in (1, 2, 3)]
        + [(base + near_index(y, x, core, k), mp) for k in range(1, GROUP)]
        + [(other_bit(dp, bit), mp) for bit in wider_bits()]
    )


def back_order(turn):
    turn = jnp.minimum(turn, 3)
    return 2 - turn + (turn // 2) * (3 - 2 * (turn // 3))


BLOCK = 256


def attend_back(
    qkv,
    back_mixed,
    mixed,
    logsum,
    first,
    out_grad,
    ff_part,
    in_all,
    tokens,
    resid,
    vectors,
    feed_small,
    up_sums,
    ff_grad,
):
    rows, width = first.shape
    blocks = rows // BLOCK
    anywhere = pl.BlockSpec(memory_space=pl.ANY)
    one = pl.Buffered(1)
    dma = pltpu.SemaphoreType.DMA
    row = pl.BlockSpec((BLOCK, width), lambda s: (jnp.maximum(s - 4, 0), 0))
    small = pl.BlockSpec((8, width), lambda s: (0, 0))
    return pl.pallas_call(
        functools.partial(attend_back_kernel, blocks=blocks),
        grid=(4 + blocks,),
        in_specs=[
            pl.BlockSpec((4 * IN_ROWS, rows), lambda s: (back_order(s), 0)),
            pl.BlockSpec((4 * 48, rows), lambda s: (back_order(s), 0)),
            pl.BlockSpec((4 * 48, rows), lambda s: (back_order(s), 0)),
            pl.BlockSpec((4, 1, rows), lambda s: (back_order(s), 0, 0)),
            anywhere,
            pl.BlockSpec((1, 4, 48, width), lambda s: (back_order(s), 0, 0, 0)),
            pl.BlockSpec((192, width), lambda s: (0, 0), pipeline_mode=one),
            anywhere,
            row,
            row,
            small,
            small,
            small,
            anywhere,
        ],
        out_specs=[
            row,
            pl.BlockSpec((16, width), lambda s: (0, 0)),
            anywhere,
            anywhere,
            anywhere,
            anywhere,
        ],
        out_shape=[
            jax.ShapeDtypeStruct((rows, width), F32),
            jax.ShapeDtypeStruct((16, width), F32),
            jax.ShapeDtypeStruct((8, 96, width), BF16),
            jax.ShapeDtypeStruct((width, width), BF16),
            jax.ShapeDtypeStruct((3, 192, width), BF16),
            jax.ShapeDtypeStruct((192, width), BF16),
        ],
        scratch_shapes=[
            pltpu.VMEM((96, LONG_LEN), F32),
            pltpu.VMEM((2, 2, 2, 192, width), BF16),
            pltpu.VMEM((4, 2, 2, 2, 96, width), BF16),
            pltpu.VMEM((16 * IN_ROWS, rows), BF16),
            pltpu.VMEM((width, width), BF16),
            pltpu.VMEM((rows, width), BF16),
            pltpu.VMEM((4, 4, HEAD_ROWS, width), BF16),
            dma((22,)),
        ]
        + sums_scratch(False, 16, width)
        + sums_scratch(True, 8, width // 3)
        + reduce_scratch(2, 192, 96, width)
        + reduce_scratch(4, 96, 48, width)
        + share_scratch(192, width)
        + share_scratch(96, width),
        compiler_params=pltpu.CompilerParams(
            vmem_limit_bytes=62 << 20, collective_id=1, has_side_effects=True
        ),
        cost_estimate=pl.CostEstimate(
            flops=50_000_000_000, bytes_accessed=50_000_000, transcendentals=19_000_000
        ),
        name="attend_back",
    )(
        qkv,
        back_mixed,
        mixed,
        logsum,
        first,
        out_grad,
        ff_part,
        in_all,
        tokens,
        resid,
        vectors,
        feed_small,
        up_sums,
        ff_grad,
    )


FEED_BLOCKS = 6


def feed_rows(
    second, back_low, slots, ff_refs, bias_ref, act_s, hid_s, rows, width, feed, back_second
):
    for i, slot in enumerate(slots):
        if isinstance(ff_refs[i], tuple):
            up, down = ff_refs[i][0][...], ff_refs[i][1][...]
        else:
            up = ff_refs[i][:, 0:96, :].reshape(width, width)
            down = ff_refs[i][:, 96:192, :].reshape(width, width)
        hidden = nn(second, up) + bias_ref[slot, 0:1, 256:]
        half = 0.5 + 0.5 * lax.erf(hidden * (0.5**0.5))
        act = (hidden * half).astype(BF16)
        slope = half + hidden * (jnp.exp(hidden * hidden * -0.5) * (1.0 / math.sqrt(2 * math.pi)))
        back_hid = (nt(back_low, down) * slope).astype(BF16)
        act_s[i, rows, :] = act
        hid_s[i, rows, :] = back_hid
        fed, pulled = nn(act, down), nt(back_hid, up)
        feed = fed if feed is None else feed + fed
        back_second = pulled if back_second is None else back_second + pulled
    return feed, back_second


def normed(rows_in):
    average = jnp.mean(rows_in, axis=-1, keepdims=True)
    centred = rows_in - average
    inverse = lax.rsqrt(jnp.mean(centred * centred, axis=-1, keepdims=True) + epsilon)
    return centred * inverse, inverse


def live_back(live_ref, grad_ref, step):
    row = step * BLOCK + lax.broadcasted_iota(jnp.int32, (BLOCK, 1), 0)
    limit = jnp.where(
        row < SHORT_ROWS, live_ref[0, 0] * SHORT_LEN, SHORT_ROWS + live_ref[0, 1] * LONG_LEN
    )
    is_live = row < limit
    return is_live, jnp.where(is_live, grad_ref[...].astype(F32), 0.0)


def feed_grads(i, second_t, back_t, act_s, hid_s, ff_grad_ref, up_sum_ref, row, width):
    up = nn(second_t[...], hid_s[i])
    ff_grad_ref[0, :, 0:96, :] = up[:width].astype(BF16).reshape(8, 96, width)
    up_sum_ref[pl.ds(row, 1), :] = up[width : width + 1]
    down = nn(back_t[...], act_s[i])
    ff_grad_ref[0, :, 96:192, :] = down.astype(BF16).reshape(8, 96, width)


def feed_first_kernel(
    live_ref,
    tokens_ref,
    grad_ref,
    mixed_ref,
    out_w_ref,
    own_up_ref,
    own_down_ref,
    near_ref,
    bias_ref,
    vec_ref,
    pieces_ref,
    residual_ref,
    feed_ref,
    back_second_ref,
    ff_grad_ref,
    up_sum_ref,
    ff_late,
    second_t,
    back_t,
    act_s,
    hid_s,
    send,
    recv,
    local,
):
    step = pl.program_id(0)
    width = tokens_ref.shape[1]
    gff = Gather(
        None,
        [None, None, ff_late.at[0], ff_late.at[1]],
        ff_piece,
        96,
        send,
        recv,
        {2: pieces_ref.at[0], 3: pieces_ref.at[1]},
    )
    mine = pltpu.make_async_copy(
        pieces_ref, ff_late.at[:, 4 * gff.y + 2 * gff.x + gff.core], local.at[0]
    )

    def begin():
        signal(group_partners())
        mine.start()
        up_sum_ref[...] = jnp.zeros_like(up_sum_ref)
        second_t[width:, :] = jnp.ones((16, second_t.shape[1]), BF16)

    def end():
        gff.complete(3)
        gff.complete(2)
        gff.finish((2, 3), range(1, 9))
        mine.wait()

    hook = hooks_of(
        {
            (0, "begin"): [begin],
            (1, "begin"): [lambda: meet(group_partners()), lambda: gff.spread(3)],
            (3, "begin"): [lambda: gff.forward(3), lambda: gff.spread(2)],
            (5, "begin"): [lambda: gff.last(3)],
            (6, "begin"): [lambda: gff.forward(2)],
            (7, "begin"): [lambda: gff.last(2)],
            (7, "end"): [end],
        },
        step,
    )
    hook("begin")

    @pl.when(step < FEED_BLOCKS)
    def _():
        out_w = out_w_ref[...].reshape(width, width)
        residual = tokens_ref[...].astype(F32) + tn(mixed_ref[...], out_w) + vec_ref[0:1, :]
        residual_ref[...] = residual
        scaled, _ = normed(residual)
        second = (scaled * vec_ref[1:2, :] + vec_ref[2:3, :]).astype(BF16)
        _, back = live_back(live_ref, grad_ref, step)
        back_low = back.astype(BF16)
        rows = pl.ds(pl.multiple_of(step * BLOCK, BLOCK), BLOCK)
        second_t[0:width, rows] = second.T
        back_t[:, rows] = back_low.T
        feed_ref[...], back_second_ref[...] = feed_rows(
            second,
            back_low,
            (0, 1),
            ((own_up_ref, own_down_ref), near_ref),
            bias_ref,
            act_s,
            hid_s,
            rows,
            width,
            None,
            None,
        )

    @pl.when(step >= FEED_BLOCKS)
    def _():
        i = step - FEED_BLOCKS
        feed_grads(i, second_t, back_t, act_s, hid_s, ff_grad_ref, up_sum_ref, i, width)

    hook("end")


def feed_last_kernel(
    live_ref,
    residual_ref,
    feed_ref,
    back_second_ref,
    grad_ref,
    mixed_ref,
    out_w_ref,
    ff_ref,
    bias_ref,
    vec_ref,
    ff_near_grad,
    output_ref,
    resid_ref,
    back_mixed_ref,
    ff_grad_ref,
    out_grad_ref,
    small_ref,
    part_ref,
    second_t,
    back_t,
    act_s,
    hid_s,
    out_acc,
    ff_total,
    local,
    *scratch,
):
    step = pl.program_id(0)
    width = residual_ref.shape[1]
    dp, base, y, x, core, mp = place()
    ff = reduces_of(
        (0, 1),
        lambda i: ff_near_grad.at[i, :, :, flip(core)],
        lambda i: ff_total.at[i],
        scratch,
        96,
    )

    def own(i):
        return pltpu.make_async_copy(ff_near_grad.at[i, :, :, core], ff_total.at[i], local.at[i])

    def begin():
        own(1).start()
        own(0).start()
        signal(group_partners())
        small_ref[...] = jnp.zeros_like(small_ref)
        second_t[width:, :] = jnp.ones((16, second_t.shape[1]), BF16)

    def chips(slot):
        own(slot).wait()
        ff[slot].chips()

    def end():
        part_ref[...] = ff[0].result() + ff[1].result()
        ff[0].finish()
        ff[1].finish()

    hook = hooks_of(
        {
            (0, "begin"): [begin],
            (1, "begin"): [lambda: meet(group_partners()), ff[1].cores, ff[0].cores],
            (2, "begin"): [lambda: chips(1)],
            (4, "begin"): [ff[1].chips_again, lambda: chips(0)],
            (5, "begin"): [ff[1].along],
            (6, "begin"): [ff[0].chips_again],
            (7, "begin"): [ff[0].along],
            (7, "end"): [end],
        },
        step,
    )
    hook("begin")

    @pl.when(step < FEED_BLOCKS)
    def _():
        out_w = out_w_ref[...].reshape(width, width)
        residual = residual_ref[...]
        scaled, inverse = normed(residual)
        gain = vec_ref[1:2, :]
        second = (scaled * gain + vec_ref[2:3, :]).astype(BF16)
        is_live, back = live_back(live_ref, grad_ref, step)
        back_low = back.astype(BF16)
        rows = pl.ds(pl.multiple_of(step * BLOCK, BLOCK), BLOCK)
        second_t[0:width, rows] = second.T
        back_t[:, rows] = back_low.T
        feed, back_second = feed_rows(
            second,
            back_low,
            (2, 3),
            (ff_ref.at[0], ff_ref.at[1]),
            bias_ref,
            act_s,
            hid_s,
            rows,
            width,
            feed_ref[...],
            back_second_ref[...],
        )
        output_ref[...] = jnp.where(is_live, residual + feed + vec_ref[3:4, :], 0.0).astype(BF16)
        small_ref[1:2, :] += jnp.sum(back_second * scaled, axis=0, keepdims=True)
        small_ref[2:3, :] += jnp.sum(back_second, axis=0, keepdims=True)
        small_ref[3:4, :] += jnp.sum(back, axis=0, keepdims=True)
        back_norm = back_second * gain
        back_resid = back + inverse * (
            back_norm
            - jnp.mean(back_norm, axis=-1, keepdims=True)
            - scaled * jnp.mean(back_norm * scaled, axis=-1, keepdims=True)
        )
        small_ref[0:1, :] += jnp.sum(back_resid, axis=0, keepdims=True)
        resid_ref[...] = back_resid
        branch = back_resid.astype(BF16)
        back_mixed_ref[...] = nt(out_w, branch).astype(BF16)
        part = nn(mixed_ref[...], branch)

        @pl.when(step == 0)
        def _():
            out_acc[...] = part

        @pl.when(step > 0)
        def _():
            out_acc[...] += part

        @pl.when(step == FEED_BLOCKS - 1)
        def _():
            out_grad_ref[...] = out_acc[...].astype(BF16).reshape(out_grad_ref.shape)

    @pl.when(step >= FEED_BLOCKS)
    def _():
        i = step - FEED_BLOCKS
        feed_grads(i, second_t, back_t, act_s, hid_s, ff_grad_ref, small_ref, 6 + i, width)

    hook("end")


def feed_first(
    live, tokens, out_grad, mixed, in_all, up_own, down_own, ff_near, bias_all, vectors, ff_pieces
):
    rows, width = tokens.shape
    anywhere = pl.BlockSpec(memory_space=pl.ANY)
    one = pl.Buffered(1)
    last = FEED_BLOCKS - 1
    row = pl.BlockSpec((BLOCK, width), lambda s: (jnp.minimum(s, last), 0))
    return pl.pallas_call(
        feed_first_kernel,
        grid=(FEED_BLOCKS + 2,),
        in_specs=[
            pl.BlockSpec(memory_space=pltpu.SMEM),
            row,
            row,
            pl.BlockSpec((width, BLOCK), lambda s: (0, jnp.minimum(s, last))),
            pl.BlockSpec((4, 4, 48, width), lambda s: (0, 0, 3, 0), pipeline_mode=one),
            pl.BlockSpec((width, width), lambda s: (0, 0), pipeline_mode=one),
            pl.BlockSpec((width, width), lambda s: (0, 0), pipeline_mode=one),
            pl.BlockSpec((8, 192, width), lambda s: (0, 0, 0), pipeline_mode=one),
            pl.BlockSpec((4, 8, 1024), lambda s: (0, 0, 0), pipeline_mode=one),
            pl.BlockSpec((8, width), lambda s: (0, 0), pipeline_mode=one),
            pl.BlockSpec((2, 192, width), lambda s: (0, 0, 0), pipeline_mode=one),
        ],
        out_specs=[
            row,
            row,
            row,
            pl.BlockSpec(
                (1, 8, 192, width), lambda s: (jnp.maximum(s - FEED_BLOCKS, 0), 0, 0, 0)
            ),
            pl.BlockSpec((8, width), lambda s: (0, 0)),
            anywhere,
        ],
        out_shape=[
            jax.ShapeDtypeStruct((rows, width), F32),
            jax.ShapeDtypeStruct((rows, width), F32),
            jax.ShapeDtypeStruct((rows, width), F32),
            jax.ShapeDtypeStruct((2, 8, 192, width), BF16),
            jax.ShapeDtypeStruct((8, width), F32),
            jax.ShapeDtypeStruct((2, 8, 192, width), BF16),
        ],
        scratch_shapes=[
            pltpu.VMEM((width + 16, rows), BF16),
            pltpu.VMEM((width, rows), BF16),
            pltpu.VMEM((2, rows, width), BF16),
            pltpu.VMEM((2, rows, width), BF16),
            pltpu.SemaphoreType.DMA((4 * GATHER_KINDS,)),
            pltpu.SemaphoreType.DMA((4 * GATHER_KINDS,)),
            pltpu.SemaphoreType.DMA((1,)),
        ],
        compiler_params=pltpu.CompilerParams(
            vmem_limit_bytes=62 << 20, collective_id=3, has_side_effects=True
        ),
        cost_estimate=pl.CostEstimate(
            flops=24_000_000_000, bytes_accessed=45_000_000, transcendentals=5_000_000
        ),
        name="feed_first",
    )(live, tokens, out_grad, mixed, in_all, up_own, down_own, ff_near, bias_all, vectors, ff_pieces)


def feed_last(
    live,
    residual,
    feed,
    back_second,
    out_grad,
    mixed,
    in_all,
    ff_late,
    bias_all,
    vectors,
    ff_near_grad,
):
    rows, width = out_grad.shape
    anywhere = pl.BlockSpec(memory_space=pl.ANY)
    one = pl.Buffered(1)
    last = FEED_BLOCKS - 1
    row = pl.BlockSpec((BLOCK, width), lambda s: (jnp.minimum(s, last), 0))
    column = pl.BlockSpec((width, BLOCK), lambda s: (0, jnp.minimum(s, last)))
    return pl.pallas_call(
        feed_last_kernel,
        grid=(FEED_BLOCKS + 2,),
        in_specs=[
            pl.BlockSpec(memory_space=pltpu.SMEM),
            row,
            row,
            row,
            row,
            column,
            pl.BlockSpec((4, 4, 48, width), lambda s: (0, 0, 3, 0), pipeline_mode=one),
            pl.BlockSpec((2, 8, 192, width), lambda s: (0, 0, 0, 0), pipeline_mode=one),
            pl.BlockSpec((4, 8, 1024), lambda s: (0, 0, 0), pipeline_mode=one),
            pl.BlockSpec((8, width), lambda s: (0, 0), pipeline_mode=one),
            anywhere,
        ],
        out_specs=[
            row,
            row,
            column,
            pl.BlockSpec(
                (1, 8, 192, width), lambda s: (jnp.maximum(s - FEED_BLOCKS, 0), 0, 0, 0)
            ),
            pl.BlockSpec((4, 4, 48, width), lambda s: (0, 0, 0, 0)),
            pl.BlockSpec((8, width), lambda s: (0, 0)),
            pl.BlockSpec((192, width), lambda s: (0, 0)),
        ],
        out_shape=[
            jax.ShapeDtypeStruct((rows, width), BF16),
            jax.ShapeDtypeStruct((rows, width), F32),
            jax.ShapeDtypeStruct((width, rows), BF16),
            jax.ShapeDtypeStruct((2, 8, 192, width), BF16),
            jax.ShapeDtypeStruct((4, 4, 48, width), BF16),
            jax.ShapeDtypeStruct((8, width), F32),
            jax.ShapeDtypeStruct((192, width), F32),
        ],
        scratch_shapes=[
            pltpu.VMEM((width + 16, rows), BF16),
            pltpu.VMEM((width, rows), BF16),
            pltpu.VMEM((2, rows, width), BF16),
            pltpu.VMEM((2, rows, width), BF16),
            pltpu.VMEM((width, width), F32),
            pltpu.VMEM((2, 2, 2, 192, width), BF16),
            pltpu.SemaphoreType.DMA((2,)),
        ]
        + reduce_scratch(2, 192, 96, width),
        compiler_params=pltpu.CompilerParams(
            vmem_limit_bytes=62 << 20, collective_id=4, has_side_effects=True
        ),
        cost_estimate=pl.CostEstimate(
            flops=28_000_000_000, bytes_accessed=55_000_000, transcendentals=5_000_000
        ),
        name="feed_last",
    )(
        live,
        residual,
        feed,
        back_second,
        out_grad,
        mixed,
        in_all,
        ff_late,
        bias_all,
        vectors,
        ff_near_grad.reshape(2, 2, 2, 2, 192, width),
    )


def local(
    tokens,
    out_grad,
    live_images,
    first_gain,
    first_shift,
    project_in,
    query_value_bias,
    project_out,
    output_bias,
    second_gain,
    second_shift,
    up_weight,
    up_bias,
    down_weight,
    down_bias,
):
    width = tokens.shape[1]
    own_heads = project_in.shape[2] // HEAD_DIM
    pair_bias = query_value_bias.reshape(2, own_heads, HEAD_DIM)
    place_of = lambda value, top, left: jnp.pad(
        value, ((top, 8 - top - value.shape[0]), (left, 1024 - left - value.shape[1]))
    )
    bias_own = place_of(pair_bias[0], 0, 0) + place_of(pair_bias[1], 0, 2 * HEAD_DIM)
    bias_own = (bias_own + place_of(up_bias[None], 0, 256)).astype(F32)
    row = lax.broadcasted_iota(jnp.int32, (8, width), 0)
    vectors = jnp.zeros((8, width), F32)
    for i, vector in enumerate(
        (output_bias, second_gain, second_shift, down_bias, first_gain, first_shift)
    ):
        vectors = jnp.where(row == i, vector[None], vectors)
    qkv, mixed, logsum, first, in_all, ff_near, ff_pieces, bias_all = attend(
        tokens,
        vectors,
        project_in.transpose(1, 2, 0),
        project_out,
        up_weight.reshape(8, -1, width),
        down_weight.reshape(8, -1, width),
        bias_own,
    )
    residual, feed, back_second, near_grad, up_sums, ff_late = feed_first(
        live_images,
        tokens,
        out_grad,
        mixed,
        in_all,
        up_weight,
        down_weight,
        ff_near,
        bias_all,
        vectors,
        ff_pieces,
    )
    output, resid, back_mixed, late_grad, out_grads, feed_small, ff_part = feed_last(
        live_images,
        residual,
        feed,
        back_second,
        out_grad,
        mixed,
        in_all,
        ff_late,
        bias_all,
        vectors,
        near_grad,
    )
    input_grad, small, grad_up, grad_down, grad_in, grad_out = attend_back(
        qkv,
        back_mixed,
        mixed,
        logsum,
        first,
        out_grads,
        ff_part,
        in_all,
        tokens,
        resid,
        vectors,
        feed_small,
        up_sums,
        late_grad.reshape(2, 2, 2, 2, 192, width),
    )
    grad_up = grad_up.reshape(width, width).astype(F32)
    grad_down, grad_out = grad_down.astype(F32), grad_out.astype(F32)
    grad_in = grad_in.astype(F32).transpose(2, 0, 1)
    pair_sum = small[8, : 4 * IN_ROWS].reshape(own_heads, 3, HEAD_DIM)
    grad_pair = jnp.stack([pair_sum[:, 0].reshape(-1), pair_sum[:, 2].reshape(-1)])
    return (
        output,
        input_grad,
        small[12],
        small[13],
        grad_in,
        grad_pair,
        grad_out,
        small[0],
        small[1],
        small[2],
        grad_up,
        small[4],
        grad_down,
        small[3],
    )


def solution(mesh):
    rows = P(("dp", "mp"), None)
    return jax.shard_map(
        local,
        mesh=mesh,
        in_specs=(
            rows,
            rows,
            rows,
            P(),
            P(),
            P(None, None, "mp"),
            P(None, "mp"),
            P("mp", None),
            P(),
            P(),
            P(),
            P(None, "mp"),
            P("mp"),
            P("mp", None),
            P(),
        ),
        out_specs=(
            rows,
            rows,
            P(),
            P(),
            P(None, None, "mp"),
            P(None, "mp"),
            P("mp", None),
            P(),
            P(),
            P(),
            P(None, "mp"),
            P("mp"),
            P("mp", None),
            P(),
        ),
        check_vma=False,
    )
```
